32 devices in a mesh: dp: 2 (over core), ctx: 4 (over y, x), tp: 4 (over z).
Axes of the slice: x: 2, y: 2, z: 4, core: 2. Of those that a mesh axis runs over, the one named last changes fastest.
Arguments:
- inputs: bfloat16 [24, 1024, 512], P('dp', 'ctx'), may hold values from -6 to 6
- lengths: int32 [24], P('dp'), may hold values from 256 to 1024, as said below
- norm_gain: float32 [512], P('dp'), may hold values from 0.5 to 1.5
- skip_weight: float32 [512], P('dp'), may hold values from -3 to 3
- lambda_re: float32 [384], P(('tp', 'dp')), may hold values from -1 to -0.1
- lambda_im: float32 [384], P(('tp', 'dp')), may hold values from -20 to 20
- log_step: float32 [384], P(('tp', 'dp')), may hold values from -6.9 to -3
- b_re: bfloat16 [384, 512], P('tp', 'dp'), may hold values from -0.25 to 0.25
- b_im: bfloat16 [384, 512], P('tp', 'dp'), may hold values from -0.25 to 0.25
- c_re: bfloat16 [512, 384], P('dp', 'tp'), may hold values from -0.875 to 0.875
- c_im: bfloat16 [512, 384], P('dp', 'tp'), may hold values from -0.875 to 0.875
- glu_weight: bfloat16 [512, 512], P('dp', 'tp'), may hold values from -0.25 to 0.25
- glu_bias: float32 [512], P(('tp', 'dp')), may hold values from -3 to 3
- out_grad: bfloat16 [24, 1024, 512], P('dp', 'ctx', 'tp'), may hold values from -6 to 6
Outputs:
- output: bfloat16 [24, 1024, 512], P('dp', 'ctx', 'tp')
- input_grad: float32 [24, 1024, 512], P('dp', 'ctx', 'tp')
- grad_norm_gain: float32 [512], P('dp')
- grad_skip: float32 [512], P('dp')
- grad_lambda_re: float32 [384], P(('tp', 'dp'))
- grad_lambda_im: float32 [384], P(('tp', 'dp'))
- grad_log_step: float32 [384], P(('tp', 'dp'))
- grad_b_re: float32 [384, 512], P('tp', 'dp')
- grad_b_im: float32 [384, 512], P('tp', 'dp')
- grad_c_re: float32 [512, 384], P('dp', 'tp')
- grad_c_im: float32 [512, 384], P('dp', 'tp')
- grad_glu_weight: float32 [512, 512], P('dp', 'tp')
- grad_glu_bias: float32 [512], P(('tp', 'dp'))
The draws below stay inside these ranges and needn't reach their ends.
Inputs may be any that keep to these rules, and one draw needn't show every extreme that they name: `lengths`: each sequence's valid length lies between 256 and 1024; some sequence has exactly 1024.
All inputs are finite; a program needn't handle non-finite values.
Results may differ from the reference program's by a relative error of at most 0.02.
Values may be sent and summed in bfloat16 or wider, within the bound.
A program may use at most 128 MiB of HBM per device.

```python
import jax
import jax.numpy as jnp
from jax import lax

H = 512
P_SIZE = 384
LMAX = 1024
LMIN = 256
SEQS = 24


def draw_lengths(key, part):
    first_key, second_key = jax.random.split(key)
    drawn = jax.random.randint(first_key, (SEQS,), LMIN, LMAX + 1)
    chosen = jax.random.randint(second_key, (), 0, SEQS)
    return jnp.where(jnp.arange(SEQS) == chosen, LMAX, drawn).astype(jnp.int32)


def block_levels(key, shape, shards, smallest, largest):
    loudness, own = 1.0, jax.random.fold_in(key, 6)
    for axis_at, blocks in shards:
        draws = jnp.exp(jax.random.uniform(jax.random.fold_in(own, axis_at), (blocks,), jnp.float32, smallest / len(shards), largest / len(shards)))
        loudness = loudness * jnp.repeat(draws, shape[axis_at] // blocks).reshape([-1 if axis == axis_at else 1 for axis in range(len(shape))])
    return loudness


def noise(rng, shape, deviation, bound, pieces=(), kind=jnp.bfloat16):
    entries = deviation * jax.random.normal(rng, shape, jnp.float32)
    if pieces:
        entries = entries * block_levels(rng, shape, pieces, -0.22, 0.18)
    return jnp.clip(entries, -bound, bound).astype(kind)


def setup_inputs(seed: int = 0) -> dict:
    arg_keys = jax.random.split(jax.random.key(seed), 15)
    return {
        "inputs": noise(arg_keys[0], (SEQS, LMAX, H), 1.0, 6.0, ((0, 2), (1, 4))),
        "lengths": draw_lengths(jax.random.fold_in(arg_keys[14], 71), 0),
        "norm_gain": jnp.clip(1.0 + 0.1 * jax.random.normal(arg_keys[2], (H,), jnp.float32), 0.5, 1.5),
        "skip_weight": noise(arg_keys[3], (H,), 1.0, 3.0, ((0, 2),), jnp.float32),
        "lambda_re": jnp.clip(-1.0 + 0.9 * jax.random.uniform(arg_keys[4], (P_SIZE,), jnp.float32) ** block_levels(arg_keys[4], (P_SIZE,), ((0, 8),), -0.2, 0.2), -1.0, -0.1),
        "lambda_im": jnp.clip(jax.random.uniform(arg_keys[5], (P_SIZE,), jnp.float32, -20.0, 20.0) * block_levels(arg_keys[5], (P_SIZE,), ((0, 8),), -0.4, 0.0), -20.0, 20.0),
        "log_step": jnp.clip(-6.9 + 3.9 * jax.random.uniform(arg_keys[6], (P_SIZE,), jnp.float32) ** block_levels(arg_keys[6], (P_SIZE,), ((0, 8),), -0.2, 0.2), -6.9, -3.0),
        "b_re": noise(arg_keys[7], (P_SIZE, H), H ** -0.5, 0.25, ((0, 4), (1, 2))),
        "b_im": noise(arg_keys[8], (P_SIZE, H), H ** -0.5, 0.25, ((0, 4), (1, 2))),
        "c_re": noise(arg_keys[9], (H, P_SIZE), (P_SIZE // 8) ** -0.5, 0.875, ((0, 2), (1, 4))),
        "c_im": noise(arg_keys[10], (H, P_SIZE), (P_SIZE // 8) ** -0.5, 0.875, ((0, 2), (1, 4))),
        "glu_weight": noise(arg_keys[11], (H, H), H ** -0.5, 0.25, ((0, 2), (1, 4))),
        "glu_bias": noise(arg_keys[12], (H,), 0.5, 3.0, ((0, 8),), jnp.float32),
        "out_grad": noise(arg_keys[13], (SEQS, LMAX, H), 1.0, 6.0, ((0, 2), (1, 4), (2, 4))),
    }


@jax.custom_vjp
def low(v):
    return lax.optimization_barrier(v.astype(jnp.bfloat16)).astype(jnp.float32)

@jax.custom_vjp
def low_back(v):
    return v

def low_keep(v):
    return (low(v), None)

def low_pass(kept, grad):
    return (grad,)

def back_keep(v):
    return (v, None)

def back_low(kept, grad):
    return (low(grad),)
low.defvjp(low_keep, low_pass)
low_back.defvjp(back_keep, back_low)
epsilon = 1e-05

def matmul_hi(left, right):
    return jnp.dot(left, right, precision=lax.Precision.HIGHEST, preferred_element_type=jnp.float32)

def combine(earlier, later):
    e_re, e_im, eb_re, eb_im = earlier
    l_re, l_im, lb_re, lb_im = later
    return (e_re * l_re - e_im * l_im, e_re * l_im + e_im * l_re, l_re * eb_re - l_im * eb_im + lb_re, l_re * eb_im + l_im * eb_re + lb_im)

def discretize(lam_re, lam_im, step_log, mat_re, mat_im):
    step = jnp.exp(step_log)
    magnitude = jnp.exp(lam_re * step)
    decay_re = magnitude * jnp.cos(lam_im * step)
    decay_im = magnitude * jnp.sin(lam_im * step)
    denom = lam_re * lam_re + lam_im * lam_im
    coef_re = ((decay_re - 1.0) * lam_re + decay_im * lam_im) / denom
    coef_im = (decay_im * lam_re - (decay_re - 1.0) * lam_im) / denom
    bar_re = coef_re[:, None] * mat_re - coef_im[:, None] * mat_im
    bar_im = coef_re[:, None] * mat_im + coef_im[:, None] * mat_re
    return (decay_re, decay_im, jnp.concatenate([bar_re, bar_im], 0))

def normalize(tokens, gain):
    mean_val = lax.optimization_barrier(jnp.mean(tokens, -1, keepdims=True))
    centered = tokens - mean_val
    var_val = lax.optimization_barrier(jnp.mean(centered * centered, -1, keepdims=True))
    return centered * lax.rsqrt(var_val + epsilon) * gain

def layer_fwd(tokens, gain, skip_vec, lam_re, lam_im, step_log, mat_bre, mat_bim, mat_cre, mat_cim, glu_mat, glu_vec, valid_row):
    normed = low(normalize(tokens, gain))
    decay_re, decay_im, b_bar = discretize(lam_re, lam_im, step_log, mat_bre, mat_bim)
    b_bar = low(b_bar)
    drive = low_back(matmul_hi(normed, b_bar.T))
    state_count = lam_re.shape[0]
    length = tokens.shape[0]
    full_re = jnp.broadcast_to(decay_re, (length, state_count))
    full_im = jnp.broadcast_to(decay_im, (length, state_count))
    scanned = lax.associative_scan(combine, (full_re, full_im, drive[:, :state_count], drive[:, state_count:]), axis=0)
    states = low(jnp.concatenate([scanned[2], scanned[3]], -1))
    c_stack = jnp.concatenate([mat_cre, -mat_cim], 1)
    ssm_out = low_back(matmul_hi(states, c_stack.T))
    pre_act = ssm_out + skip_vec * normed
    act_low = low(jax.nn.gelu(pre_act))
    gate = low_back(matmul_hi(act_low, glu_mat)) + glu_vec
    branch = act_low * jax.nn.sigmoid(gate)
    return valid_row[:, None] * (tokens + branch)

def reference(inputs, lengths, norm_gain, skip_weight, lambda_re, lambda_im, log_step, b_re, b_im, c_re, c_im, glu_weight, glu_bias, out_grad):
    params = tuple((member.astype(jnp.float32) for member in (norm_gain, skip_weight, lambda_re, lambda_im, log_step, b_re, b_im, c_re, c_im, glu_weight, glu_bias)))
    positions = jnp.arange(inputs.shape[1], dtype=jnp.int32)
    valid_mask = (positions[None, :] < lengths[:, None]).astype(jnp.float32)
    zero_grads = tuple((jnp.zeros_like(member) for member in params))

    def per_sequence(totals, scan_item):
        tokens, valid_row, cotangent = scan_item

        def apply_layer(tokens_in, *weights):
            return layer_fwd(tokens_in, *weights, valid_row)
        result, pull_back = jax.vjp(apply_layer, tokens, *params)
        gradients = pull_back(cotangent)
        new_totals = tuple((first + second for first, second in zip(totals, gradients[1:])))
        return (new_totals, (result.astype(jnp.bfloat16), gradients[0]))
    totals, (output, input_grad) = lax.scan(per_sequence, zero_grads, (inputs.astype(jnp.float32), valid_mask, out_grad.astype(jnp.float32)))
    return (output, input_grad, totals[0], totals[1], totals[2], totals[3], totals[4], totals[5], totals[6], totals[7], totals[8], totals[9], totals[10])
```

```python
import functools

import jax
import jax.numpy as jnp
from jax import lax
from jax.experimental import pallas as pl
from jax.experimental.pallas import tpu as pltpu
from jax.sharding import PartitionSpec as P

epsilon = 1e-05


def carried_in(value, axis, combine, identity, reverse):
    count, index = (lax.axis_size(axis), lax.axis_index(axis))
    everything = jax.tree.map(lambda part: lax.all_gather(part, axis), value)
    start = jax.tree.map(
        lambda part, zero: jnp.broadcast_to(jnp.asarray(zero, part.dtype), part.shape),
        value,
        identity,
    )

    def lap(k, before):
        at = count - 1 - k if reverse else k
        reached = at > index if reverse else at < index
        new = combine(before, jax.tree.map(lambda part: part[at], everything))
        return jax.tree.map(lambda a, b: jnp.where(reached, a, b), new, before)

    return lax.fori_loop(0, count, lap, start)


def contract(left, right, left_dim, right_dim):
    return lax.dot_general(
        left, right, (((left_dim,), (right_dim,)), ((), ())), preferred_element_type=jnp.float32
    )


def combine(earlier, later):
    e_re, e_im, eb_re, eb_im = earlier
    l_re, l_im, lb_re, lb_im = later
    return (
        e_re * l_re - e_im * l_im,
        e_re * l_im + e_im * l_re,
        l_re * eb_re - l_im * eb_im + lb_re,
        l_re * eb_im + l_im * eb_re + lb_im,
    )


def discretize(lam_re, lam_im, step_log, mat_re, mat_im):
    step = jnp.exp(step_log)
    magnitude = jnp.exp(lam_re * step)
    decay_re = magnitude * jnp.cos(lam_im * step)
    decay_im = magnitude * jnp.sin(lam_im * step)
    denom = lam_re * lam_re + lam_im * lam_im
    coef_re = ((decay_re - 1.0) * lam_re + decay_im * lam_im) / denom
    coef_im = (decay_im * lam_re - (decay_re - 1.0) * lam_im) / denom
    bar_re = coef_re[:, None] * mat_re - coef_im[:, None] * mat_im
    bar_im = coef_re[:, None] * mat_im + coef_im[:, None] * mat_re
    return (decay_re, decay_im, jnp.concatenate([bar_re, bar_im], 0))


def normalize(tokens, gain):
    mean_val = jnp.mean(tokens, -1, keepdims=True)
    centered = tokens - mean_val
    var_val = jnp.mean(centered * centered, -1, keepdims=True)
    return centered * lax.rsqrt(var_val + epsilon) * gain


def powers(lam_re, lam_im, step_log, count):
    step = jnp.exp(step_log)
    exponent = (jnp.arange(count, dtype=jnp.float32) + 1.0)[:, None]
    magnitude = jnp.exp(exponent * lam_re * step)
    return (
        magnitude * jnp.cos(exponent * lam_im * step),
        magnitude * jnp.sin(exponent * lam_im * step),
    )


def on_device(
    inputs,
    lengths,
    norm_gain,
    skip_weight,
    lambda_re,
    lambda_im,
    log_step,
    b_re,
    b_im,
    c_re,
    c_im,
    glu_weight,
    glu_bias,
    out_grad,
):
    full_bre, full_bim, full_cre, full_cim, full_glu = (
        lax.all_gather(b_re, "dp", axis=1, tiled=True),
        lax.all_gather(b_im, "dp", axis=1, tiled=True),
        lax.all_gather(c_re, "dp", axis=0, tiled=True),
        lax.all_gather(c_im, "dp", axis=0, tiled=True),
        lax.all_gather(glu_weight, "dp", axis=0, tiled=True),
    )
    gain, skip_full, lam_re, lam_im, step_log, bias_vec = (
        lax.all_gather(norm_gain, "dp", axis=0, tiled=True),
        lax.all_gather(skip_weight, "dp", axis=0, tiled=True),
        lax.all_gather(lambda_re, "dp", axis=0, tiled=True),
        lax.all_gather(lambda_im, "dp", axis=0, tiled=True),
        lax.all_gather(log_step, "dp", axis=0, tiled=True),
        lax.all_gather(glu_bias, "dp", axis=0, tiled=True),
    )
    seq_count, blk_len, feat_dim = inputs.shape
    row_count = seq_count * blk_len
    state_count = full_bre.shape[0]
    unit_count = full_glu.shape[1]
    tp_rank = lax.axis_index("tp")
    unit_start = tp_rank * unit_count
    positions = lax.axis_index("ctx") * blk_len + jnp.arange(blk_len, dtype=jnp.int32)
    valid_mask = (positions[None, :] < lengths[:, None]).astype(jnp.float32).reshape(row_count, 1)
    tokens = inputs.astype(jnp.float32).reshape(row_count, feat_dim)
    tokens_mine = lax.dynamic_slice_in_dim(tokens, unit_start, unit_count, 1)
    cotangent = out_grad.astype(jnp.float32).reshape(row_count, unit_count)
    normed_f, norm_pull = jax.vjp(normalize, tokens, gain)
    normed_b = normed_f.astype(jnp.bfloat16)
    normed_r = normed_b.astype(jnp.float32)
    (decay_re, decay_im, bar_full), disc_pull = jax.vjp(
        discretize,
        lam_re,
        lam_im,
        step_log,
        full_bre.astype(jnp.float32),
        full_bim.astype(jnp.float32),
    )
    bar_b = bar_full.astype(jnp.bfloat16)
    drive = contract(normed_b, bar_b, 1, 1).reshape(seq_count, blk_len, 2 * state_count)
    full_re = jnp.broadcast_to(decay_re, (seq_count, blk_len, state_count))
    full_im = jnp.broadcast_to(decay_im, (seq_count, blk_len, state_count))
    local_states = lax.associative_scan(
        combine, (full_re, full_im, drive[..., :state_count], drive[..., state_count:]), axis=1
    )
    pow_re, pow_im = powers(lam_re, lam_im, step_log, blk_len)
    identity = (
        jnp.ones((1, state_count), jnp.float32),
        jnp.zeros((1, state_count), jnp.float32),
        jnp.zeros((seq_count, state_count), jnp.float32),
        jnp.zeros((seq_count, state_count), jnp.float32),
    )
    incoming = carried_in(
        (pow_re[-1:], pow_im[-1:], local_states[2][:, -1], local_states[3][:, -1]),
        "ctx",
        combine,
        identity,
        False,
    )
    in_re = incoming[2][:, None, :]
    in_im = incoming[3][:, None, :]
    state_re = local_states[2] + pow_re * in_re - pow_im * in_im
    state_im = local_states[3] + pow_re * in_im + pow_im * in_re
    states_b = (
        jnp.concatenate([state_re, state_im], -1)
        .reshape(row_count, 2 * state_count)
        .astype(jnp.bfloat16)
    )
    c_stack = jnp.concatenate([full_cre, -full_cim], 1)
    ssm_part = contract(states_b, c_stack, 1, 1)
    ssm_full = lax.psum(ssm_part.astype(jnp.bfloat16), "tp").astype(jnp.float32)
    pre_full = ssm_full + skip_full * normed_r
    gelu_full, gelu_pull = jax.vjp(jax.nn.gelu, pre_full)
    gelu_b = gelu_full.astype(jnp.bfloat16)
    gelu_part = lax.dynamic_slice_in_dim(gelu_b, unit_start, unit_count, 1)
    gelu_mine = gelu_part.astype(jnp.float32)
    gate = contract(gelu_b, full_glu, 1, 0) + bias_vec
    gate_sig = jax.nn.sigmoid(gate)
    output = (
        (valid_mask * (tokens_mine + gelu_mine * gate_sig))
        .astype(jnp.bfloat16)
        .reshape(seq_count, blk_len, unit_count)
    )
    branch_grad = valid_mask * cotangent
    gate_grad = branch_grad * gelu_mine * gate_sig * (1.0 - gate_sig)
    bias_grad = jnp.sum(gate_grad, 0)
    gate_b = gate_grad.astype(jnp.bfloat16)
    glu_grad = contract(gelu_b, gate_b, 0, 0)
    gelu_grad = contract(gate_b, full_glu, 1, 1)
    own_cols = (
        lax.dynamic_slice_in_dim(gelu_grad, unit_start, unit_count, 1) + branch_grad * gate_sig
    )
    gelu_grad = lax.dynamic_update_slice_in_dim(gelu_grad, own_cols, unit_start, 1)
    gelu_back = lax.psum(gelu_grad, "tp")
    (pre_grad,) = gelu_pull(gelu_back)
    skip_grad = jnp.sum(pre_grad * normed_r, 0)
    pre_b = pre_grad.astype(jnp.bfloat16)
    state_grad = contract(pre_b, c_stack, 1, 0).reshape(seq_count, blk_len, 2 * state_count)
    c_grad = contract(pre_b, states_b, 0, 0)
    back_local = lax.associative_scan(
        combine,
        (full_re, -full_im, state_grad[..., :state_count], state_grad[..., state_count:]),
        axis=1,
        reverse=True,
    )
    later_adj = carried_in(
        (pow_re[-1:], -pow_im[-1:], back_local[2][:, 0], back_local[3][:, 0]),
        "ctx",
        combine,
        identity,
        True,
    )
    rev_re = pow_re[::-1]
    rev_im = -pow_im[::-1]
    next_re = later_adj[2][:, None, :]
    next_im = later_adj[3][:, None, :]
    adj_re = back_local[2] + rev_re * next_re - rev_im * next_im
    adj_im = back_local[3] + rev_re * next_im + rev_im * next_re
    prev_re = jnp.concatenate([in_re, state_re[:, :-1]], 1)
    prev_im = jnp.concatenate([in_im, state_im[:, :-1]], 1)
    decay_grad_re = jnp.sum(adj_re * prev_re + adj_im * prev_im, (0, 1))
    decay_grad_im = jnp.sum(adj_im * prev_re - adj_re * prev_im, (0, 1))
    adj_b = (
        jnp.concatenate([adj_re, adj_im], -1)
        .reshape(row_count, 2 * state_count)
        .astype(jnp.bfloat16)
    )
    bar_grad = contract(adj_b, normed_b, 0, 0)
    normed_part = contract(adj_b, bar_b, 1, 0)
    normed_sum = lax.psum(normed_part.astype(jnp.bfloat16), "tp").astype(jnp.float32)
    normed_grad = normed_sum + skip_full * pre_grad
    token_grad, gain_grad = norm_pull(normed_grad)
    input_grad = (
        valid_mask * cotangent + lax.dynamic_slice_in_dim(token_grad, unit_start, unit_count, 1)
    ).reshape(seq_count, blk_len, unit_count)
    grad_cre = c_grad[:, :state_count]
    grad_cim = -c_grad[:, state_count:]
    lre_grad, lim_grad, step_grad, bre_grad, bim_grad = disc_pull(
        (decay_grad_re, decay_grad_im, bar_grad)
    )
    shards = (
        lax.psum_scatter(
            gain_grad.astype(jnp.bfloat16), "dp", scatter_dimension=0, tiled=True
        ).astype(jnp.float32),
        lax.psum_scatter(
            skip_grad.astype(jnp.bfloat16), "dp", scatter_dimension=0, tiled=True
        ).astype(jnp.float32),
        lax.psum_scatter(
            lre_grad.astype(jnp.bfloat16), "dp", scatter_dimension=0, tiled=True
        ).astype(jnp.float32),
        lax.psum_scatter(
            lim_grad.astype(jnp.bfloat16), "dp", scatter_dimension=0, tiled=True
        ).astype(jnp.float32),
        lax.psum_scatter(
            step_grad.astype(jnp.bfloat16), "dp", scatter_dimension=0, tiled=True
        ).astype(jnp.float32),
        lax.psum_scatter(
            bias_grad.astype(jnp.bfloat16), "dp", scatter_dimension=0, tiled=True
        ).astype(jnp.float32),
        lax.psum_scatter(
            bre_grad.astype(jnp.bfloat16), "dp", scatter_dimension=1, tiled=True
        ).astype(jnp.float32),
        lax.psum_scatter(
            bim_grad.astype(jnp.bfloat16), "dp", scatter_dimension=1, tiled=True
        ).astype(jnp.float32),
        lax.psum_scatter(
            grad_cre.astype(jnp.bfloat16), "dp", scatter_dimension=0, tiled=True
        ).astype(jnp.float32),
        lax.psum_scatter(
            grad_cim.astype(jnp.bfloat16), "dp", scatter_dimension=0, tiled=True
        ).astype(jnp.float32),
        lax.psum_scatter(
            glu_grad.astype(jnp.bfloat16), "dp", scatter_dimension=0, tiled=True
        ).astype(jnp.float32),
    )
    summed = (
        lax.psum(shards[0].astype(jnp.bfloat16), "ctx").astype(jnp.float32),
        lax.psum(shards[1].astype(jnp.bfloat16), "ctx").astype(jnp.float32),
        lax.psum(shards[2].astype(jnp.bfloat16), "ctx").astype(jnp.float32),
        lax.psum(shards[3].astype(jnp.bfloat16), "ctx").astype(jnp.float32),
        lax.psum(shards[4].astype(jnp.bfloat16), "ctx").astype(jnp.float32),
        lax.psum(shards[5].astype(jnp.bfloat16), "ctx").astype(jnp.float32),
        lax.psum(shards[6].astype(jnp.bfloat16), "ctx").astype(jnp.float32),
        lax.psum(shards[7].astype(jnp.bfloat16), "ctx").astype(jnp.float32),
        lax.psum(shards[8].astype(jnp.bfloat16), "ctx").astype(jnp.float32),
        lax.psum(shards[9].astype(jnp.bfloat16), "ctx").astype(jnp.float32),
        lax.psum(shards[10].astype(jnp.bfloat16), "ctx").astype(jnp.float32),
    )
    return (
        output,
        input_grad,
        summed[0],
        summed[1],
        summed[2],
        summed[3],
        summed[4],
        summed[6],
        summed[7],
        summed[8],
        summed[9],
        summed[10],
        summed[5],
    )


MESH = pl.DeviceIdType.MESH
SQ2PI = 0.7978845608028654


def nt(a, b):
    return lax.dot_general(a, b, (((1,), (1,)), ((), ())), preferred_element_type=jnp.float32)


def nn(a, b):
    return lax.dot_general(a, b, (((1,), (0,)), ((), ())), preferred_element_type=jnp.float32)


def tn(a, b):
    return lax.dot_general(a, b, (((0,), (0,)), ((), ())), preferred_element_type=jnp.float32)


def cmul(ar, ai, br, bi):
    return ar * br - ai * bi, ar * bi + ai * br


def lane(start, size):
    return pl.ds(pl.multiple_of(start, 128), size)


def fused_body(geo, *refs):
    D, C, T, S, L, H, N, U = geo
    R = S * L
    NS = N // T
    HD = H // D
    f32, bf16 = jnp.float32, jnp.bfloat16
    (len_ref, x_hbm, og_hbm, pk1, pk2, sm_ref, out_hbm, tg_hbm, fc_ref, fg_ref, fb_ref, fv_ref) = refs[:12]
    (xv, nrm, xh, rs, raw, st, sb, tmp, act, gp, sig, ogv, ob, gl, pg, plb, mu, nb, tgb,
     w4, gt, smr, cst, ce, cer, cbr, gc, gg, gb, r1c, r1g, r1b, s1c, s1g, s1b, r2c, r2g, r2b,
     s2c, s2g, s2b, r3c, r3g, r3b, vv, vr1, vr2, vr3, lsem, ssem, rsem) = refs[12:]
    d, c, t = lax.axis_index("dp"), lax.axis_index("ctx"), lax.axis_index("tp")
    zpeer = [(d, c, lax.rem(t + k, T)) for k in range(1, T)]
    cpeer = [(d, lax.rem(c + k, C), t) for k in range(1, C)]
    sib = (1 - d, c, t)
    xpeer = [(1 - d, c, lax.rem(t + k, T)) for k in range(1, T)]
    everyone = zpeer + cpeer + [sib] + xpeer

    count = [0]
    started = []

    def remote(src, dst, peer):
        i = count[0]
        count[0] += 1
        cp = pltpu.make_async_remote_copy(
            src_ref=src, dst_ref=dst, send_sem=ssem.at[i], recv_sem=rsem.at[i],
            device_id=peer, device_id_type=MESH)
        cp.start()
        started.append(cp)
        return cp

    cx = pltpu.make_async_copy(x_hbm.at[pl.ds(pl.multiple_of(R * t, R), R)], xv, lsem.at[0])
    cx.start()
    co = pltpu.make_async_copy(
        og_hbm.at[pl.ds(pl.multiple_of(R * t, R), R)], ogv.at[:, lane(U * t, U)], lsem.at[1])
    co.start()
    barrier = pltpu.get_barrier_semaphore()
    for p in everyone:
        pl.semaphore_signal(barrier, inc=1, device_id=p, device_id_type=MESH)
    pl.semaphore_wait(barrier, len(everyone))

    me8 = d * T + t
    small = [remote(sm_ref, smr.at[me8], p) for p in zpeer + [sib] + xpeer]
    gq, hq = c // 2, lax.rem(c, 2)
    wl = lane(HD * d + 128 * hq, 128)
    w1b = [remote(pk1.at[gq, :, lane(128 * hq, 128)], w4.at[gq, t, :, wl], p) for p in zpeer]
    w1c = [remote(pk1.at[2 + gq, :, lane(128 * hq, 128)], w4.at[2 + gq, t, :, wl], p) for p in zpeer]
    uq = U // C
    grow = pl.ds(pl.multiple_of(uq * c, uq), uq)
    dl = lane(HD * d, HD)
    w1g = [remote(pk2.at[grow], gt.at[t, grow, dl], p) for p in zpeer]
    w4[gq, t, :, wl] = pk1[gq, :, lane(128 * hq, 128)]
    w4[2 + gq, t, :, wl] = pk1[2 + gq, :, lane(128 * hq, 128)]
    gt[t, grow, dl] = pk2[grow]
    smr[me8] = sm_ref[...]

    cx.wait()

    def ln_tile(i, _):
        rows = pl.ds(pl.multiple_of(i * 32, 32), 32)
        x = xv[rows, :].astype(f32)
        cen = x - jnp.mean(x, -1, keepdims=True)
        rstd = lax.rsqrt(jnp.mean(cen * cen, -1, keepdims=True) + epsilon)
        xh[rows, :] = cen * rstd
        rs[rows, :] = jnp.broadcast_to(rstd, (32, 128))
        return 0

    lax.fori_loop(0, R // 32, ln_tile, 0)

    for cp in small:
        cp.wait_recv()
    zero = jnp.zeros((8, H - HD), f32)
    vec = jnp.zeros((8, H), f32)
    bias = jnp.zeros((8, H), f32)
    for dd in range(D):
        for tt in range(T):
            ext = jnp.concatenate([smr[dd * T + tt], zero], 1)
            place = tt * D + dd
            vec = vec + (pltpu.roll(ext, place * (NS // D), 1) if place else ext)
            bias = bias + (pltpu.roll(ext, place * (U // D), 1) if place else ext)
    both = jnp.concatenate([smr[t], smr[T + t]], 1)
    row8 = lax.broadcasted_iota(jnp.int32, (8, N), 0)
    full = lambda v, k, n: jnp.broadcast_to(v[k:k + 1, :n], (8, n))
    dr, di = full(vec, 0, N), full(vec, 1, N)
    cr, ci = full(vec, 2, N), full(vec, 3, N)
    pows = {1: (dr, di)}
    for k in range(2, 9):
        pows[k] = cmul(*pows[k - 1], dr, di)
    for n_, k in ((0, 1), (1, 2), (2, 4)):
        keep = row8 >= k
        cst[2 * n_] = jnp.where(keep, pows[k][0], 0.0)
        cst[2 * n_ + 1] = jnp.where(keep, pows[k][1], 0.0)
        keep = row8 < 8 - k
        cst[8 + 2 * n_] = jnp.where(keep, pows[k][0], 0.0)
        cst[8 + 2 * n_ + 1] = jnp.where(keep, -pows[k][1], 0.0)
    pr, pi, qr, qi = pows[1][0], pows[1][1], pows[8][0], -pows[8][1]
    for r in range(1, 8):
        pr = jnp.where(row8 == r, pows[r + 1][0], pr)
        pi = jnp.where(row8 == r, pows[r + 1][1], pi)
        qr = jnp.where(row8 == r, pows[8 - r][0], qr)
        qi = jnp.where(row8 == r, -pows[8 - r][1], qi)
    cst[6], cst[7], cst[14], cst[15] = pr, pi, qr, qi
    cst[16], cst[17] = pows[8]
    cst[18], cst[19] = cr, ci
    big = pows[8]
    n_ = 8
    while n_ < L:
        big = cmul(*big, *big)
        n_ *= 2
    cst[20], cst[21] = big
    gain_r, skip_r, bias_r = both[5:6, :], both[6:7, :], bias[4:5, :]

    def nrm_tile(i, _):
        rows = pl.ds(pl.multiple_of(i * 32, 32), 32)
        nrm[rows, :] = (xh[rows, :] * gain_r).astype(bf16)
        return 0

    lax.fori_loop(0, R // 32, nrm_tile, 0)

    for cp in w1b:
        cp.wait_recv()
    w2b = [remote(w4.at[gq, :, :, wl], w4.at[gq, :, :, wl], p) for p in cpeer]
    for cp in w1c:
        cp.wait_recv()
    w2c = [remote(w4.at[2 + gq, :, :, wl], w4.at[2 + gq, :, :, wl], p) for p in cpeer]
    for cp in w1g:
        cp.wait_recv()
    w2g = [remote(gt.at[:, grow, dl], gt.at[:, grow, dl], p) for p in cpeer]
    og = [remote(og_hbm.at[pl.ds(pl.multiple_of(R * p[2], R), R)], ogv.at[:, lane(U * t, U)], p)
          for p in zpeer]
    for cp in w2b:
        cp.wait_recv()
    w3b = remote(w4.at[0:2, :, :, dl], w4.at[0:2, :, :, dl], sib)
    for cp in w2c:
        cp.wait_recv()
    w3c = remote(w4.at[2:4, :, :, dl], w4.at[2:4, :, :, dl], sib)
    for cp in w2g:
        cp.wait_recv()
    w3g = remote(gt.at[:, :, dl], gt.at[:, :, dl], sib)

    w3b.wait_recv()

    def seq_rows(s):
        return pl.ds(pl.multiple_of(s * L, L), L)

    def drive_seq(s, _):
        raw[seq_rows(s), :] = nt(nrm[seq_rows(s), :], w4[0:2].reshape(2 * N, H))
        return 0

    lax.fori_loop(0, S, drive_seq, 0)

    def scan_lanes(src, dst, base, coef, reverse, end_ref):
        def lanes_step(j, _):
            lr_, li_ = lane(128 * j, 128), lane(N + 128 * j, 128)
            con = [cst[base + k, :, lr_] for k in range(8)]
            cfr, cfi = cst[18, :, lr_], cst[19, :, lr_]

            def tile(i, carry):
                ii = L // 8 - 1 - i if reverse else i
                out = []
                for s in range(S):
                    rows = pl.ds(pl.multiple_of(s * L + ii * 8, 8), 8)
                    ar, ai = src[rows, lr_], src[rows, li_]
                    if coef:
                        ar, ai = cmul(cfr, cfi, ar, ai)
                    for n_, k in ((0, 1), (1, 2), (2, 4)):
                        sh = 8 - k if reverse else k
                        br, bi = pltpu.roll(ar, sh, 0), pltpu.roll(ai, sh, 0)
                        mr, mi = con[2 * n_], con[2 * n_ + 1]
                        ar, ai = ar + mr * br - mi * bi, ai + mr * bi + mi * br
                    kr, ki = carry[2 * s], carry[2 * s + 1]
                    ar, ai = ar + con[6] * kr - con[7] * ki, ai + con[6] * ki + con[7] * kr
                    dst[rows, lr_] = ar
                    dst[rows, li_] = ai
                    e = 0 if reverse else 7
                    out.append(jnp.broadcast_to(ar[e:e + 1, :], (8, 128)))
                    out.append(jnp.broadcast_to(ai[e:e + 1, :], (8, 128)))
                return tuple(out)

            z = jnp.zeros((8, 128), f32)
            fin = lax.fori_loop(0, L // 8, tile, (z,) * (2 * S))
            for s in range(S):
                end_ref[pl.ds(s, 1), lr_] = fin[2 * s][0:1, :]
                end_ref[pl.ds(S + s, 1), lr_] = fin[2 * s + 1][0:1, :]
            return 0

        lax.fori_loop(0, N // 128, lanes_step, 0)

    scan_lanes(raw, st, 0, True, False, ce.at[0])
    fce = [remote(ce.at[0], cer.at[k], p) for k, p in enumerate(cpeer)]
    for cp in fce:
        cp.wait_recv()

    def incoming(buf, forward):
        bg = (cst[20, 0:1, :], cst[21, 0:1, :])
        wt = (jnp.ones((1, N), f32), jnp.zeros((1, N), f32))
        accr = jnp.zeros((S, N), f32)
        acci = jnp.zeros((S, N), f32)
        for k in range(1, C):
            got = buf[k - 1] if forward else buf[C - 1 - k]
            has = (c >= k) if forward else (c + k < C)
            w = jnp.where(has, 1.0, 0.0)
            vr, vi = got[0:S, :], got[S:2 * S, :]
            wi = wt[1] if forward else -wt[1]
            ur, ui = cmul(wt[0], wi, vr, vi)
            accr = accr + w * ur
            acci = acci + w * ui
            wt = cmul(*wt, *bg)
        return accr, acci

    inr, ini = incoming(cer, True)
    ce[2, 0:S, :] = inr
    ce[2, S:2 * S, :] = ini

    def fix_lanes(j, _):
        lr_, li_ = lane(128 * j, 128), lane(N + 128 * j, 128)
        p0, p1 = cst[6, :, lr_], cst[7, :, lr_]
        e0, e1 = cst[16, :, lr_], cst[17, :, lr_]
        q0 = tuple(jnp.broadcast_to(ce[2, pl.ds(k * S + s, 1), lr_], (8, 128))
                   for s in range(S) for k in range(2))

        def tile(i, q):
            q = list(q)
            for s in range(S):
                rr, ri = [], []
                for h in range(2):
                    rows = pl.ds(pl.multiple_of(s * L + i * 16 + 8 * h, 8), 8)
                    vr, vi = cmul(p0, p1, q[2 * s], q[2 * s + 1])
                    ar, ai = st[rows, lr_] + vr, st[rows, li_] + vi
                    st[rows, lr_] = ar
                    st[rows, li_] = ai
                    rr.append(ar)
                    ri.append(ai)
                    q[2 * s], q[2 * s + 1] = cmul(q[2 * s], q[2 * s + 1], e0, e1)
                rows = pl.ds(pl.multiple_of(s * L + i * 16, 16), 16)
                sb[rows, lr_] = jnp.concatenate(rr, 0).astype(bf16)
                sb[rows, li_] = jnp.concatenate(ri, 0).astype(bf16)
            return tuple(q)

        lax.fori_loop(0, L // 16, tile, q0)
        return 0

    lax.fori_loop(0, N // 128, fix_lanes, 0)

    w3c.wait_recv()

    def ssm_seq(s, _):
        tmp[seq_rows(s), :] = nn(sb[seq_rows(s), :], w4[2:4].reshape(2 * N, H))
        return 0

    lax.fori_loop(0, S, ssm_seq, 0)

    def gelu_tile(i, _):
        rows = pl.ds(pl.multiple_of(i * 32, 32), 32)
        pre = tmp[rows, :] + skip_r * nrm[rows, :].astype(f32)
        sq = pre * pre
        th = jnp.tanh(pre * (SQ2PI + (SQ2PI * 0.044715) * sq))
        half = 0.5 + 0.5 * th
        act[rows, :] = (pre * half).astype(bf16)
        gp[rows, :] = half + 0.5 * pre * (1.0 - th * th) * (SQ2PI + (3 * 0.044715 * SQ2PI) * sq)
        return 0

    lax.fori_loop(0, R // 32, gelu_tile, 0)
    w3g.wait_recv()

    def gate_seq(s, _):
        tmp[seq_rows(s), :] = nt(act[seq_rows(s), :], gt[...].reshape(H, H))
        return 0

    lax.fori_loop(0, S, gate_seq, 0)

    def valid_of(i):
        s = i // (L // 32)
        pos = c * L + lax.rem(i, L // 32) * 32 + lax.broadcasted_iota(jnp.int32, (32, 1), 0)
        return jnp.where(pos < len_ref[S * t + s], 1.0, 0.0)

    def out_tile(i, _):
        rows = pl.ds(pl.multiple_of(i * 32, 32), 32)
        sg = 0.5 + 0.5 * jnp.tanh(0.5 * (tmp[rows, :] + bias_r))
        sig[rows, :] = sg
        o = valid_of(i) * (xv[rows, :].astype(f32) + act[rows, :].astype(f32) * sg)
        ob[rows, :] = o.astype(bf16)
        return 0

    lax.fori_loop(0, R // 32, out_tile, 0)
    mine = pl.ds(pl.multiple_of(R * t, R), R)
    outc = [remote(ob.at[:, lane(U * p[2], U)], out_hbm.at[mine, :], p) for p in zpeer]
    oc = pltpu.make_async_copy(ob.at[:, lane(U * t, U)], out_hbm.at[mine, :], lsem.at[2])
    oc.start()

    co.wait()
    for cp in og:
        cp.wait_recv()

    def fold(v):
        return jnp.sum(v.reshape(4, 8, v.shape[-1]), 0)

    def gate_tile(i, acc):
        rows = pl.ds(pl.multiple_of(i * 32, 32), 32)
        sg = sig[rows, :]
        direct = valid_of(i) * ogv[rows, :].astype(f32) * sg
        gg_ = direct * act[rows, :].astype(f32) * (1.0 - sg)
        gl[rows, :] = gg_.astype(bf16)
        sig[rows, :] = direct
        return acc + fold(gg_)

    bias_g = lax.fori_loop(0, R // 32, gate_tile, jnp.zeros((8, H), f32))

    def actg_seq(s, _):
        tmp[seq_rows(s), :] = nn(gl[seq_rows(s), :], gt[...].reshape(H, H))
        return 0

    lax.fori_loop(0, S, actg_seq, 0)

    def pre_tile(i, acc):
        rows = pl.ds(pl.multiple_of(i * 32, 32), 32)
        p = (tmp[rows, :] + sig[rows, :]) * gp[rows, :]
        pg[rows, :] = p
        plb[rows, :] = p.astype(bf16)
        return acc + fold(p * nrm[rows, :].astype(f32))

    skip_g = lax.fori_loop(0, R // 32, pre_tile, jnp.zeros((8, H), f32))

    def sgrad_seq(s, _):
        mu[seq_rows(s), :] = nt(plb[seq_rows(s), :], w4[2:4].reshape(2 * N, H))
        return 0

    lax.fori_loop(0, S, sgrad_seq, 0)
    scan_lanes(mu, mu, 8, False, True, ce.at[1])
    bce = [remote(ce.at[1], cbr.at[k], p) for k, p in enumerate(cpeer)]

    gcf, gbf, ggf = gc.reshape(2 * N, H), gb.reshape(2 * N, H), gg.reshape(H, H)

    def gc_step(j, _):
        gcf[pl.ds(pl.multiple_of(j * 128, 128), 128), :] = tn(sb[:, lane(j * 128, 128)], plb[...]).astype(bf16)
        return 0

    lax.fori_loop(0, 2 * N // 128, gc_step, 0)
    ol = lane(HD * (1 - d), HD)
    d1c = remote(gc.at[:, :, :, ol], r1c, sib)

    def gg_step(j, _):
        ggf[pl.ds(pl.multiple_of(j * 128, 128), 128), :] = tn(gl[:, lane(j * 128, 128)], act[...]).astype(bf16)
        return 0

    lax.fori_loop(0, H // 128, gg_step, 0)
    d1g = remote(gg.at[:, :, ol], r1g, sib)

    for cp in bce:
        cp.wait_recv()
    inr, ini = incoming(cbr, False)
    ce[2, 0:S, :] = inr
    ce[2, S:2 * S, :] = ini
    row1 = lax.broadcasted_iota(jnp.int32, (8, 128), 0)

    def adj_lanes(j, _):
        lr_, li_ = lane(128 * j, 128), lane(N + 128 * j, 128)
        p0, p1 = cst[14, :, lr_], cst[15, :, lr_]
        e0, e1 = cst[16, :, lr_], -cst[17, :, lr_]
        cfr, cfi = cst[18, :, lr_], cst[19, :, lr_]
        q0 = tuple(jnp.broadcast_to(ce[2, pl.ds(k * S + s, 1), lr_], (8, 128))
                   for s in range(S) for k in range(2))
        z = jnp.zeros((8, 128), f32)

        def tile(i, carry):
            q, m, acc = list(carry[:2 * S]), list(carry[2 * S:4 * S]), list(carry[4 * S:])
            ii = L // 16 - 1 - i
            for s in range(S):
                rr, ri = [None, None], [None, None]
                for h in (1, 0):
                    rows = pl.ds(pl.multiple_of(s * L + ii * 16 + 8 * h, 8), 8)
                    vr, vi = cmul(p0, p1, q[2 * s], q[2 * s + 1])
                    ar, ai = mu[rows, lr_] + vr, mu[rows, li_] + vi
                    q[2 * s], q[2 * s + 1] = cmul(q[2 * s], q[2 * s + 1], e0, e1)
                    nr = jnp.where(row1 == 7, m[2 * s], pltpu.roll(ar, 7, 0))
                    ni = jnp.where(row1 == 7, m[2 * s + 1], pltpu.roll(ai, 7, 0))
                    m[2 * s] = jnp.broadcast_to(ar[0:1, :], (8, 128))
                    m[2 * s + 1] = jnp.broadcast_to(ai[0:1, :], (8, 128))
                    xr, xi = st[rows, lr_], st[rows, li_]
                    acc[0] = acc[0] + nr * xr + ni * xi
                    acc[1] = acc[1] + ni * xr - nr * xi
                    ur, ui = raw[rows, lr_], raw[rows, li_]
                    acc[2] = acc[2] + ar * ur + ai * ui
                    acc[3] = acc[3] + ai * ur - ar * ui
                    rr[h] = cfr * ar + cfi * ai
                    ri[h] = cfr * ai - cfi * ar
                rows = pl.ds(pl.multiple_of(s * L + ii * 16, 16), 16)
                nb[rows, lr_] = jnp.concatenate(rr, 0).astype(bf16)
                nb[rows, li_] = jnp.concatenate(ri, 0).astype(bf16)
            return tuple(q) + tuple(m) + tuple(acc)

        fin = lax.fori_loop(0, L // 16, tile, q0 + q0 + (z,) * 4)
        for k in range(4):
            vv[3 + k:4 + k, lr_] = jnp.sum(fin[4 * S + k], 0, keepdims=True)
        return 0

    vv[...] = jnp.zeros_like(vv)
    lax.fori_loop(0, N // 128, adj_lanes, 0)

    def gb_step(j, _):
        gbf[pl.ds(pl.multiple_of(j * 128, 128), 128), :] = tn(nb[:, lane(j * 128, 128)], nrm[...]).astype(bf16)
        return 0

    lax.fori_loop(0, 2 * N // 128, gb_step, 0)
    d1b = remote(gb.at[:, :, :, ol], r1b, sib)

    def rs_ctx(p):
        return p // 2, pl.ds(pl.multiple_of((NS // 2) * lax.rem(p, 2), NS // 2), NS // 2)

    d1c.wait_recv()
    s1c[...] = (gc[:, :, :, dl].astype(f32) + r1c[...].astype(f32)).astype(bf16)
    d2c = [remote(s1c.at[rs_ctx(p[1])[0], :, rs_ctx(p[1])[1], :], r2c.at[k], p) for k, p in enumerate(cpeer)]
    d1g.wait_recv()
    s1g[...] = (gg[:, :, dl].astype(f32) + r1g[...].astype(f32)).astype(bf16)
    gr = lambda p: pl.ds(pl.multiple_of(uq * p, uq), uq)
    d2g = [remote(s1g.at[:, gr(p[1]), :], r2g.at[k], p) for k, p in enumerate(cpeer)]

    def ng_seq(s, _):
        tmp[seq_rows(s), :] = nn(nb[seq_rows(s), :], w4[0:2].reshape(2 * N, H))
        return 0

    lax.fori_loop(0, S, ng_seq, 0)

    def tok_tile(i, acc):
        rows = pl.ds(pl.multiple_of(i * 32, 32), 32)
        n = tmp[rows, :] + skip_r * pg[rows, :]
        xt = xh[rows, :]
        h = n * gain_r
        m1 = jnp.mean(h, -1, keepdims=True)
        m2 = jnp.mean(h * xt, -1, keepdims=True)
        tgb[rows, :] = ((h - m1 - xt * m2) * rs[rows, 0:1]).astype(bf16)
        return acc + fold(n * xt)

    gain_g = lax.fori_loop(0, R // 32, tok_tile, jnp.zeros((8, H), f32))
    tgc = [remote(tgb.at[:, lane(U * p[2], U)], tg_hbm.at[mine, :], p) for p in zpeer]
    tc = pltpu.make_async_copy(tgb.at[:, lane(U * t, U)], tg_hbm.at[mine, :], lsem.at[3])
    tc.start()
    vv[0:1, :] = jnp.sum(gain_g, 0, keepdims=True)
    vv[1:2, :] = jnp.sum(skip_g, 0, keepdims=True)
    vv[2:3, :] = jnp.sum(bias_g, 0, keepdims=True)

    d1v = remote(vv, vr1, sib)
    d1b.wait_recv()
    s1b[...] = (gb[:, :, :, dl].astype(f32) + r1b[...].astype(f32)).astype(bf16)
    d2b = [remote(s1b.at[rs_ctx(p[1])[0], :, rs_ctx(p[1])[1], :], r2b.at[k], p) for k, p in enumerate(cpeer)]
    d1v.wait_recv()
    vr2[0] = vv[...] + vr1[...]
    d2v = [remote(vr2.at[0], vr2.at[k + 1], p) for k, p in enumerate(cpeer)]

    def total(first, buf, n):
        acc = first.astype(f32)
        for k in range(n):
            acc = acc + buf[k].astype(f32)
        return acc

    for cp in d2c:
        cp.wait_recv()
    s2c[...] = total(s1c[rs_ctx(c)[0], :, rs_ctx(c)[1], :], r2c, C - 1).astype(bf16)
    d3c = [remote(s2c.at[p[2]], r3c.at[k], p) for k, p in enumerate(zpeer)]
    for cp in d2g:
        cp.wait_recv()
    s2g[...] = total(s1g[:, gr(c), :], r2g, C - 1).astype(bf16)
    d3g = [remote(s2g.at[p[2]], r3g.at[k], p) for k, p in enumerate(zpeer)]
    for cp in d2b:
        cp.wait_recv()
    s2b[...] = total(s1b[rs_ctx(c)[0], :, rs_ctx(c)[1], :], r2b, C - 1).astype(bf16)
    d3b = [remote(s2b.at[p[2]], r3b.at[k], p) for k, p in enumerate(zpeer)]
    for cp in d2v:
        cp.wait_recv()
    vr3[0] = vr2[0] + vr2[1] + vr2[2] + vr2[3]
    d3v = [remote(vr3.at[0], vr3.at[k + 1], p) for k, p in enumerate(zpeer)]

    for cp in d3c:
        cp.wait_recv()
    fc_ref[c] = total(s2c[t], r3c, T - 1).astype(bf16)
    d4 = [remote(fc_ref.at[c], fc_ref.at[c], p) for p in cpeer]
    for cp in d3g:
        cp.wait_recv()
    fg_ref[c] = total(s2g[t], r3g, T - 1).astype(bf16)
    d4 += [remote(fg_ref.at[c], fg_ref.at[c], p) for p in cpeer]
    for cp in d3b:
        cp.wait_recv()
    fb_ref[c] = total(s2b[t], r3b, T - 1).astype(bf16)
    d4 += [remote(fb_ref.at[c], fb_ref.at[c], p) for p in cpeer]
    for cp in d3v:
        cp.wait_recv()
    fv_ref[...] = vr3[0] + vr3[1] + vr3[2] + vr3[3]
    for cp in d4 + tgc + outc:
        cp.wait_recv()
    oc.wait()
    tc.wait()
    for cp in started:
        cp.wait_send()


def fused_call(geo, lens, x2, og2, pk1, pk2, sm):
    D, C, T, S, L, H, N, U = geo
    R, NS, HD = S * L, N // T, H // D
    f32, bf16 = jnp.float32, jnp.bfloat16
    uq, hs = U // C, NS // 2
    V = pltpu.VMEM
    nsem = 7 + 9 + 9 + 3 + 3 + 6 + 3 + 3 + 4 + 12 + 12 + 9
    any_, vm = pl.BlockSpec(memory_space=pl.ANY), pl.BlockSpec(memory_space=pltpu.VMEM)
    scratch = [
        V((R, H), bf16), V((R, H), bf16), V((R, H), f32), V((R, 128), f32),
        V((R, 2 * N), f32), V((R, 2 * N), f32), V((R, 2 * N), bf16),
        V((R, H), f32), V((R, H), bf16), V((R, H), f32), V((R, H), f32),
        V((R, H), bf16), V((R, H), bf16), V((R, H), bf16), V((R, H), f32), V((R, H), bf16),
        V((R, 2 * N), f32), V((R, 2 * N), bf16), V((R, H), bf16),
        V((4, T, NS, H), bf16), V((T, U, H), bf16), V((D * T, 8, HD), f32),
        V((22, 8, N), f32), V((3, 8, N), f32), V((C - 1, 8, N), f32), V((C - 1, 8, N), f32),
        V((2, T, NS, H), bf16), V((T, U, H), bf16), V((2, T, NS, H), bf16),
        V((2, T, NS, HD), bf16), V((T, U, HD), bf16), V((2, T, NS, HD), bf16),
        V((2, T, NS, HD), bf16), V((T, U, HD), bf16), V((2, T, NS, HD), bf16),
        V((C - 1, T, hs, HD), bf16), V((C - 1, T, uq, HD), bf16), V((C - 1, T, hs, HD), bf16),
        V((T, hs, HD), bf16), V((T, uq, HD), bf16), V((T, hs, HD), bf16),
        V((T - 1, hs, HD), bf16), V((T - 1, uq, HD), bf16), V((T - 1, hs, HD), bf16),
        V((8, H), f32), V((8, H), f32), V((C, 8, H), f32), V((T, 8, H), f32),
        pltpu.SemaphoreType.DMA((4,)), pltpu.SemaphoreType.DMA((nsem,)), pltpu.SemaphoreType.DMA((nsem,)),
    ]
    rows = x2.shape[0]
    return pl.pallas_call(
        functools.partial(fused_body, geo),
        out_shape=(
            jax.ShapeDtypeStruct((rows, U), bf16), jax.ShapeDtypeStruct((rows, U), bf16),
            jax.ShapeDtypeStruct((C, hs, HD), bf16), jax.ShapeDtypeStruct((C, uq, HD), bf16),
            jax.ShapeDtypeStruct((C, hs, HD), bf16), jax.ShapeDtypeStruct((8, H), f32)),
        in_specs=[pl.BlockSpec(memory_space=pltpu.SMEM), any_, any_, vm, vm, vm],
        out_specs=(any_, any_, vm, vm, vm, vm),
        scratch_shapes=scratch,
        compiler_params=pltpu.CompilerParams(
            collective_id=0, has_side_effects=True, vmem_limit_bytes=58 * 1024 * 1024),
        name="block",
    )(lens, x2, og2, pk1, pk2, sm)


def coefficients(lam_re, lam_im, step_log):
    step = jnp.exp(step_log)
    magnitude = jnp.exp(lam_re * step)
    decay_re = magnitude * jnp.cos(lam_im * step)
    decay_im = magnitude * jnp.sin(lam_im * step)
    denom = lam_re * lam_re + lam_im * lam_im
    coef_re = ((decay_re - 1.0) * lam_re + decay_im * lam_im) / denom
    coef_im = (decay_im * lam_re - (decay_re - 1.0) * lam_im) / denom
    return decay_re, decay_im, coef_re, coef_im


def token_split(sizes, inputs, lengths, norm_gain, skip_weight, lambda_re, lambda_im, log_step,
                b_re, b_im, c_re, c_im, glu_weight, glu_bias, out_grad):
    D, C, T = sizes
    seqs, L, H = inputs.shape
    NS, HD = b_re.shape
    U = glu_weight.shape[1]
    geo = (D, C, T, seqs // T, L, H, NS * T, U)
    d, c, t = lax.axis_index("dp"), lax.axis_index("ctx"), lax.axis_index("tp")
    derived, pull = jax.vjp(coefficients, lambda_re, lambda_im, log_step)
    wide = lambda v: jnp.pad(v, (0, HD - v.shape[0]))
    sm = jnp.stack([wide(v) for v in derived + (glu_bias, norm_gain, skip_weight)] + [jnp.zeros((HD,), jnp.float32)])
    pk1 = jnp.stack([b_re, b_im, c_re.T, -c_im.T])
    pk2 = glu_weight.T
    out, tok, fc, fg, fb, fv = fused_call(
        geo, lengths, inputs.reshape(seqs * L, H), out_grad.reshape(seqs * L, U), pk1, pk2, sm)
    pos = c * L + jnp.arange(L, dtype=jnp.int32)
    valid = (pos[None, :] < lengths[:, None])[:, :, None]
    input_grad = jnp.where(valid, out_grad.astype(jnp.float32), 0.0) + tok.reshape(seqs, L, U).astype(jnp.float32)
    place = t * D + d
    own = lambda row, n: lax.dynamic_slice_in_dim(fv[row], place * n, n)
    gl_re, gl_im, g_step = pull(tuple(own(3 + k, NS // D) for k in range(4)))
    gain_g = lax.dynamic_slice_in_dim(fv[0], d * HD, HD)
    skip_g = lax.dynamic_slice_in_dim(fv[1], d * HD, HD)
    up = lambda v: v.astype(jnp.float32)
    fc, fb = up(fc).reshape(2, NS, HD), up(fb).reshape(2, NS, HD)
    return (out.reshape(seqs, L, U), input_grad, gain_g, skip_g, gl_re, gl_im, g_step,
            fb[0], fb[1], fc[0].T, -fc[1].T, up(fg).reshape(U, HD).T, own(2, U // D))


def solution(mesh):
    in_specs = (
        P("dp", "ctx", None),
        P("dp"),
        P("dp"),
        P("dp"),
        P(("tp", "dp")),
        P(("tp", "dp")),
        P(("tp", "dp")),
        P("tp", "dp"),
        P("tp", "dp"),
        P("dp", "tp"),
        P("dp", "tp"),
        P("dp", "tp"),
        P(("tp", "dp")),
        P("dp", "ctx", "tp"),
    )
    out_specs = (
        P("dp", "ctx", "tp"),
        P("dp", "ctx", "tp"),
        P("dp"),
        P("dp"),
        P(("tp", "dp")),
        P(("tp", "dp")),
        P(("tp", "dp")),
        P("tp", "dp"),
        P("tp", "dp"),
        P("dp", "tp"),
        P("dp", "tp"),
        P("dp", "tp"),
        P(("tp", "dp")),
    )
    sizes = tuple(mesh.shape[name] for name in ("dp", "ctx", "tp"))

    def block(*args):
        seqs, _, feat = args[0].shape
        units = args[11].shape[1]
        if sizes == (2, 4, 4) and seqs % sizes[2] == 0 and units % 128 == 0:
            return token_split(sizes, *args)
        return on_device(*args)

    return jax.shard_map(
        block, mesh=mesh, in_specs=in_specs, out_specs=out_specs, check_vma=False
    )
```

```python
import functools

import jax
import jax.numpy as jnp
from jax import lax
from jax.experimental import pallas as pl
from jax.experimental.pallas import tpu as pltpu
from jax.sharding import PartitionSpec as P

epsilon = 1e-05


def carried_in(value, axis, combine, identity, reverse):
    count, index = (lax.axis_size(axis), lax.axis_index(axis))
    everything = jax.tree.map(lambda part: lax.all_gather(part, axis), value)
    start = jax.tree.map(
        lambda part, zero: jnp.broadcast_to(jnp.asarray(zero, part.dtype), part.shape),
        value,
        identity,
    )

    def lap(k, before):
        at = count - 1 - k if reverse else k
        reached = at > index if reverse else at < index
        new = combine(before, jax.tree.map(lambda part: part[at], everything))
        return jax.tree.map(lambda a, b: jnp.where(reached, a, b), new, before)

    return lax.fori_loop(0, count, lap, start)


def contract(left, right, left_dim, right_dim):
    return lax.dot_general(
        left, right, (((left_dim,), (right_dim,)), ((), ())), preferred_element_type=jnp.float32
    )


def combine(earlier, later):
    e_re, e_im, eb_re, eb_im = earlier
    l_re, l_im, lb_re, lb_im = later
    return (
        e_re * l_re - e_im * l_im,
        e_re * l_im + e_im * l_re,
        l_re * eb_re - l_im * eb_im + lb_re,
        l_re * eb_im + l_im * eb_re + lb_im,
    )


def discretize(lam_re, lam_im, step_log, mat_re, mat_im):
    step = jnp.exp(step_log)
    magnitude = jnp.exp(lam_re * step)
    decay_re = magnitude * jnp.cos(lam_im * step)
    decay_im = magnitude * jnp.sin(lam_im * step)
    denom = lam_re * lam_re + lam_im * lam_im
    coef_re = ((decay_re - 1.0) * lam_re + decay_im * lam_im) / denom
    coef_im = (decay_im * lam_re - (decay_re - 1.0) * lam_im) / denom
    bar_re = coef_re[:, None] * mat_re - coef_im[:, None] * mat_im
    bar_im = coef_re[:, None] * mat_im + coef_im[:, None] * mat_re
    return (decay_re, decay_im, jnp.concatenate([bar_re, bar_im], 0))


def normalize(tokens, gain):
    mean_val = jnp.mean(tokens, -1, keepdims=True)
    centered = tokens - mean_val
    var_val = jnp.mean(centered * centered, -1, keepdims=True)
    return centered * lax.rsqrt(var_val + epsilon) * gain


def powers(lam_re, lam_im, step_log, count):
    step = jnp.exp(step_log)
    exponent = (jnp.arange(count, dtype=jnp.float32) + 1.0)[:, None]
    magnitude = jnp.exp(exponent * lam_re * step)
    return (
        magnitude * jnp.cos(exponent * lam_im * step),
        magnitude * jnp.sin(exponent * lam_im * step),
    )


def on_device(
    inputs,
    lengths,
    norm_gain,
    skip_weight,
    lambda_re,
    lambda_im,
    log_step,
    b_re,
    b_im,
    c_re,
    c_im,
    glu_weight,
    glu_bias,
    out_grad,
):
    full_bre, full_bim, full_cre, full_cim, full_glu = (
        lax.all_gather(b_re, "dp", axis=1, tiled=True),
        lax.all_gather(b_im, "dp", axis=1, tiled=True),
        lax.all_gather(c_re, "dp", axis=0, tiled=True),
        lax.all_gather(c_im, "dp", axis=0, tiled=True),
        lax.all_gather(glu_weight, "dp", axis=0, tiled=True),
    )
    gain, skip_full, lam_re, lam_im, step_log, bias_vec = (
        lax.all_gather(norm_gain, "dp", axis=0, tiled=True),
        lax.all_gather(skip_weight, "dp", axis=0, tiled=True),
        lax.all_gather(lambda_re, "dp", axis=0, tiled=True),
        lax.all_gather(lambda_im, "dp", axis=0, tiled=True),
        lax.all_gather(log_step, "dp", axis=0, tiled=True),
        lax.all_gather(glu_bias, "dp", axis=0, tiled=True),
    )
    seq_count, blk_len, feat_dim = inputs.shape
    row_count = seq_count * blk_len
    state_count = full_bre.shape[0]
    unit_count = full_glu.shape[1]
    tp_rank = lax.axis_index("tp")
    unit_start = tp_rank * unit_count
    positions = lax.axis_index("ctx") * blk_len + jnp.arange(blk_len, dtype=jnp.int32)
    valid_mask = (positions[None, :] < lengths[:, None]).astype(jnp.float32).reshape(row_count, 1)
    tokens = inputs.astype(jnp.float32).reshape(row_count, feat_dim)
    tokens_mine = lax.dynamic_slice_in_dim(tokens, unit_start, unit_count, 1)
    cotangent = out_grad.astype(jnp.float32).reshape(row_count, unit_count)
    normed_f, norm_pull = jax.vjp(normalize, tokens, gain)
    normed_b = normed_f.astype(jnp.bfloat16)
    normed_r = normed_b.astype(jnp.float32)
    (decay_re, decay_im, bar_full), disc_pull = jax.vjp(
        discretize,
        lam_re,
        lam_im,
        step_log,
        full_bre.astype(jnp.float32),
        full_bim.astype(jnp.float32),
    )
    bar_b = bar_full.astype(jnp.bfloat16)
    drive = contract(normed_b, bar_b, 1, 1).reshape(seq_count, blk_len, 2 * state_count)
    full_re = jnp.broadcast_to(decay_re, (seq_count, blk_len, state_count))
    full_im = jnp.broadcast_to(decay_im, (seq_count, blk_len, state_count))
    local_states = lax.associative_scan(
        combine, (full_re, full_im, drive[..., :state_count], drive[..., state_count:]), axis=1
    )
    pow_re, pow_im = powers(lam_re, lam_im, step_log, blk_len)
    identity = (
        jnp.ones((1, state_count), jnp.float32),
        jnp.zeros((1, state_count), jnp.float32),
        jnp.zeros((seq_count, state_count), jnp.float32),
        jnp.zeros((seq_count, state_count), jnp.float32),
    )
    incoming = carried_in(
        (pow_re[-1:], pow_im[-1:], local_states[2][:, -1], local_states[3][:, -1]),
        "ctx",
        combine,
        identity,
        False,
    )
    in_re = incoming[2][:, None, :]
    in_im = incoming[3][:, None, :]
    state_re = local_states[2] + pow_re * in_re - pow_im * in_im
    state_im = local_states[3] + pow_re * in_im + pow_im * in_re
    states_b = (
        jnp.concatenate([state_re, state_im], -1)
        .reshape(row_count, 2 * state_count)
        .astype(jnp.bfloat16)
    )
    c_stack = jnp.concatenate([full_cre, -full_cim], 1)
    ssm_part = contract(states_b, c_stack, 1, 1)
    ssm_full = lax.psum(ssm_part.astype(jnp.bfloat16), "tp").astype(jnp.float32)
    pre_full = ssm_full + skip_full * normed_r
    gelu_full, gelu_pull = jax.vjp(jax.nn.gelu, pre_full)
    gelu_b = gelu_full.astype(jnp.bfloat16)
    gelu_part = lax.dynamic_slice_in_dim(gelu_b, unit_start, unit_count, 1)
    gelu_mine = gelu_part.astype(jnp.float32)
    gate = contract(gelu_b, full_glu, 1, 0) + bias_vec
    gate_sig = jax.nn.sigmoid(gate)
    output = (
        (valid_mask * (tokens_mine + gelu_mine * gate_sig))
        .astype(jnp.bfloat16)
        .reshape(seq_count, blk_len, unit_count)
    )
    branch_grad = valid_mask * cotangent
    gate_grad = branch_grad * gelu_mine * gate_sig * (1.0 - gate_sig)
    bias_grad = jnp.sum(gate_grad, 0)
    gate_b = gate_grad.astype(jnp.bfloat16)
    glu_grad = contract(gelu_b, gate_b, 0, 0)
    gelu_grad = contract(gate_b, full_glu, 1, 1)
    own_cols = (
        lax.dynamic_slice_in_dim(gelu_grad, unit_start, unit_count, 1) + branch_grad * gate_sig
    )
    gelu_grad = lax.dynamic_update_slice_in_dim(gelu_grad, own_cols, unit_start, 1)
    gelu_back = lax.psum(gelu_grad, "tp")
    (pre_grad,) = gelu_pull(gelu_back)
    skip_grad = jnp.sum(pre_grad * normed_r, 0)
    pre_b = pre_grad.astype(jnp.bfloat16)
    state_grad = contract(pre_b, c_stack, 1, 0).reshape(seq_count, blk_len, 2 * state_count)
    c_grad = contract(pre_b, states_b, 0, 0)
    back_local = lax.associative_scan(
        combine,
        (full_re, -full_im, state_grad[..., :state_count], state_grad[..., state_count:]),
        axis=1,
        reverse=True,
    )
    later_adj = carried_in(
        (pow_re[-1:], -pow_im[-1:], back_local[2][:, 0], back_local[3][:, 0]),
        "ctx",
        combine,
        identity,
        True,
    )
    rev_re = pow_re[::-1]
    rev_im = -pow_im[::-1]
    next_re = later_adj[2][:, None, :]
    next_im = later_adj[3][:, None, :]
    adj_re = back_local[2] + rev_re * next_re - rev_im * next_im
    adj_im = back_local[3] + rev_re * next_im + rev_im * next_re
    prev_re = jnp.concatenate([in_re, state_re[:, :-1]], 1)
    prev_im = jnp.concatenate([in_im, state_im[:, :-1]], 1)
    decay_grad_re = jnp.sum(adj_re * prev_re + adj_im * prev_im, (0, 1))
    decay_grad_im = jnp.sum(adj_im * prev_re - adj_re * prev_im, (0, 1))
    adj_b = (
        jnp.concatenate([adj_re, adj_im], -1)
        .reshape(row_count, 2 * state_count)
        .astype(jnp.bfloat16)
    )
    bar_grad = contract(adj_b, normed_b, 0, 0)
    normed_part = contract(adj_b, bar_b, 1, 0)
    normed_sum = lax.psum(normed_part.astype(jnp.bfloat16), "tp").astype(jnp.float32)
    normed_grad = normed_sum + skip_full * pre_grad
    token_grad, gain_grad = norm_pull(normed_grad)
    input_grad = (
        valid_mask * cotangent + lax.dynamic_slice_in_dim(token_grad, unit_start, unit_count, 1)
    ).reshape(seq_count, blk_len, unit_count)
    grad_cre = c_grad[:, :state_count]
    grad_cim = -c_grad[:, state_count:]
    lre_grad, lim_grad, step_grad, bre_grad, bim_grad = disc_pull(
        (decay_grad_re, decay_grad_im, bar_grad)
    )
    shards = (
        lax.psum_scatter(
            gain_grad.astype(jnp.bfloat16), "dp", scatter_dimension=0, tiled=True
        ).astype(jnp.float32),
        lax.psum_scatter(
            skip_grad.astype(jnp.bfloat16), "dp", scatter_dimension=0, tiled=True
        ).astype(jnp.float32),
        lax.psum_scatter(
            lre_grad.astype(jnp.bfloat16), "dp", scatter_dimension=0, tiled=True
        ).astype(jnp.float32),
        lax.psum_scatter(
            lim_grad.astype(jnp.bfloat16), "dp", scatter_dimension=0, tiled=True
        ).astype(jnp.float32),
        lax.psum_scatter(
            step_grad.astype(jnp.bfloat16), "dp", scatter_dimension=0, tiled=True
        ).astype(jnp.float32),
        lax.psum_scatter(
            bias_grad.astype(jnp.bfloat16), "dp", scatter_dimension=0, tiled=True
        ).astype(jnp.float32),
        lax.psum_scatter(
            bre_grad.astype(jnp.bfloat16), "dp", scatter_dimension=1, tiled=True
        ).astype(jnp.float32),
        lax.psum_scatter(
            bim_grad.astype(jnp.bfloat16), "dp", scatter_dimension=1, tiled=True
        ).astype(jnp.float32),
        lax.psum_scatter(
            grad_cre.astype(jnp.bfloat16), "dp", scatter_dimension=0, tiled=True
        ).astype(jnp.float32),
        lax.psum_scatter(
            grad_cim.astype(jnp.bfloat16), "dp", scatter_dimension=0, tiled=True
        ).astype(jnp.float32),
        lax.psum_scatter(
            glu_grad.astype(jnp.bfloat16), "dp", scatter_dimension=0, tiled=True
        ).astype(jnp.float32),
    )
    summed = (
        lax.psum(shards[0].astype(jnp.bfloat16), "ctx").astype(jnp.float32),
        lax.psum(shards[1].astype(jnp.bfloat16), "ctx").astype(jnp.float32),
        lax.psum(shards[2].astype(jnp.bfloat16), "ctx").astype(jnp.float32),
        lax.psum(shards[3].astype(jnp.bfloat16), "ctx").astype(jnp.float32),
        lax.psum(shards[4].astype(jnp.bfloat16), "ctx").astype(jnp.float32),
        lax.psum(shards[5].astype(jnp.bfloat16), "ctx").astype(jnp.float32),
        lax.psum(shards[6].astype(jnp.bfloat16), "ctx").astype(jnp.float32),
        lax.psum(shards[7].astype(jnp.bfloat16), "ctx").astype(jnp.float32),
        lax.psum(shards[8].astype(jnp.bfloat16), "ctx").astype(jnp.float32),
        lax.psum(shards[9].astype(jnp.bfloat16), "ctx").astype(jnp.float32),
        lax.psum(shards[10].astype(jnp.bfloat16), "ctx").astype(jnp.float32),
    )
    return (
        output,
        input_grad,
        summed[0],
        summed[1],
        summed[2],
        summed[3],
        summed[4],
        summed[6],
        summed[7],
        summed[8],
        summed[9],
        summed[10],
        summed[5],
    )


MESH = pl.DeviceIdType.MESH
SQ2PI = 0.7978845608028654


def nt(a, b):
    return lax.dot_general(a, b, (((1,), (1,)), ((), ())), preferred_element_type=jnp.float32)


def nn(a, b):
    return lax.dot_general(a, b, (((1,), (0,)), ((), ())), preferred_element_type=jnp.float32)


def tn(a, b):
    return lax.dot_general(a, b, (((0,), (0,)), ((), ())), preferred_element_type=jnp.float32)


def cmul(ar, ai, br, bi):
    return ar * br - ai * bi, ar * bi + ai * br


def lane(start, size):
    return pl.ds(pl.multiple_of(start, 128), size)


def fused_body(geo, *refs):
    D, C, T, S, L, H, N, U = geo
    R = S * L
    NS = N // T
    HD = H // D
    f32, bf16 = jnp.float32, jnp.bfloat16
    (len_ref, x_hbm, og_hbm, bre, bim, cre, cim, glu, gain_in, skip_in, lre_in, lim_in, stp_in, bias_in,
     out_hbm, tg_hbm, fc_ref, fg_ref, fb_ref, fv_ref) = refs[:20]
    (xv, nrm, xh, rs, raw, st, sb, tmp, act, gp, sig, ogv, ob, gl, pg, plb, mu, nb, tgb,
     w4, gt, smr, cst, ce, cer, cbr, gc, gg, gb, r1c, r1g, r1b, s1c, s1g, s1b, r2c, r2g, r2b,
     s2c, s2g, s2b, r3c, r3g, r3b, vv, vr1, vr2, vr3, vf, pk, sm_ref, lsem, ssem, rsem) = refs[20:]
    d, c, t = lax.axis_index("dp"), lax.axis_index("ctx"), lax.axis_index("tp")
    zpeer = [(d, c, lax.rem(t + k, T)) for k in range(1, T)]
    cpeer = [(d, lax.rem(c + k, C), t) for k in range(1, C)]
    sib = (1 - d, c, t)
    xpeer = [(1 - d, c, lax.rem(t + k, T)) for k in range(1, T)]
    everyone = zpeer + cpeer + [sib] + xpeer

    count = [0]
    started = []

    def remote(src, dst, peer):
        i = count[0]
        count[0] += 1
        cp = pltpu.make_async_remote_copy(
            src_ref=src, dst_ref=dst, send_sem=ssem.at[i], recv_sem=rsem.at[i],
            device_id=peer, device_id_type=MESH)
        cp.start()
        started.append(cp)
        return cp

    cx = pltpu.make_async_copy(x_hbm.at[pl.ds(pl.multiple_of(R * t, R), R)], xv, lsem.at[0])
    cx.start()
    co = pltpu.make_async_copy(
        og_hbm.at[pl.ds(pl.multiple_of(R * t, R), R)], ogv.at[:, lane(U * t, U)], lsem.at[1])
    co.start()
    barrier = pltpu.get_barrier_semaphore()
    for p in everyone:
        pl.semaphore_signal(barrier, inc=1, device_id=p, device_id_type=MESH)
    pk[0], pk[1], pk[2], pk[3] = bre[...], bim[...], cre[...], cim[...]
    sm_ref[...] = jnp.zeros_like(sm_ref)
    own = coefficients(lre_in[...], lim_in[...], stp_in[...])
    for k in range(4):
        sm_ref[k:k + 1, 0:NS // D] = own[k]
    sm_ref[4:5, 0:U // D] = bias_in[...]
    sm_ref[5:6, :] = gain_in[...]
    sm_ref[6:7, :] = skip_in[...]
    pl.semaphore_wait(barrier, len(everyone))

    me8 = d * T + t
    small = [remote(sm_ref, smr.at[me8], p) for p in zpeer + [sib] + xpeer]
    gq, hq = c // 2, lax.rem(c, 2)
    wl = lane(HD * d + 128 * hq, 128)
    w1b = [remote(pk.at[gq, :, lane(128 * hq, 128)], w4.at[gq, t, :, wl], p) for p in zpeer]
    w1c = [remote(pk.at[2 + gq, :, lane(128 * hq, 128)], w4.at[2 + gq, t, :, wl], p) for p in zpeer]
    uq = HD // C
    gown = pl.ds(pl.multiple_of(uq * c, uq), uq)
    grow = pl.ds(pl.multiple_of(HD * d + uq * c, uq), uq)
    dr_ = pl.ds(pl.multiple_of(HD * d, HD), HD)
    dl = lane(HD * d, HD)
    tl = lane(U * t, U)
    w1g = [remote(glu.at[gown], gt.at[grow, tl], p) for p in zpeer]
    w4[gq, t, :, wl] = pk[gq, :, lane(128 * hq, 128)]
    w4[2 + gq, t, :, wl] = pk[2 + gq, :, lane(128 * hq, 128)]
    gt[grow, tl] = glu[gown]
    smr[me8] = sm_ref[...]

    cx.wait()

    def ln_tile(i, _):
        for u in range(4):
            rows = pl.ds(pl.multiple_of(i * 128 + u * 32, 32), 32)
            x = xv[rows, :].astype(f32)
            cen = x - jnp.mean(x, -1, keepdims=True)
            rstd = lax.rsqrt(jnp.mean(cen * cen, -1, keepdims=True) + epsilon)
            xh[rows, :] = cen * rstd
            rs[rows, :] = jnp.broadcast_to(rstd, (32, 128))
        return 0

    lax.fori_loop(0, R // 128, ln_tile, 0)

    for cp in small:
        cp.wait_recv()
    zero = jnp.zeros((8, H - HD), f32)
    vec = jnp.zeros((8, H), f32)
    bias = jnp.zeros((8, H), f32)
    for dd in range(D):
        for tt in range(T):
            ext = jnp.concatenate([smr[dd * T + tt], zero], 1)
            place = tt * D + dd
            vec = vec + (pltpu.roll(ext, place * (NS // D), 1) if place else ext)
            bias = bias + (pltpu.roll(ext, place * (U // D), 1) if place else ext)
    both = jnp.concatenate([smr[t], smr[T + t]], 1)
    row8 = lax.broadcasted_iota(jnp.int32, (8, N), 0)
    full = lambda v, k, n: jnp.broadcast_to(v[k:k + 1, :n], (8, n))
    dr, di = full(vec, 0, N), full(vec, 1, N)
    cr, ci = full(vec, 2, N), full(vec, 3, N)
    pows = {1: (dr, di)}
    for k in range(2, 9):
        pows[k] = cmul(*pows[k - 1], dr, di)
    for n_, k in ((0, 1), (1, 2), (2, 4)):
        keep = row8 >= k
        cst[2 * n_] = jnp.where(keep, pows[k][0], 0.0)
        cst[2 * n_ + 1] = jnp.where(keep, pows[k][1], 0.0)
        keep = row8 < 8 - k
        cst[8 + 2 * n_] = jnp.where(keep, pows[k][0], 0.0)
        cst[8 + 2 * n_ + 1] = jnp.where(keep, -pows[k][1], 0.0)
    pr, pi, qr, qi = pows[1][0], pows[1][1], pows[8][0], -pows[8][1]
    for r in range(1, 8):
        pr = jnp.where(row8 == r, pows[r + 1][0], pr)
        pi = jnp.where(row8 == r, pows[r + 1][1], pi)
        qr = jnp.where(row8 == r, pows[8 - r][0], qr)
        qi = jnp.where(row8 == r, -pows[8 - r][1], qi)
    cst[6], cst[7], cst[14], cst[15] = pr, pi, qr, qi
    cst[16], cst[17] = pows[8]
    cst[18], cst[19] = cr, ci
    big = pows[8]
    n_ = 8
    while n_ < L:
        big = cmul(*big, *big)
        n_ *= 2
    cst[20], cst[21] = big
    gain_r, skip_r, bias_r = both[5:6, :], both[6:7, :], bias[4:5, :]

    def nrm_tile(i, _):
        rows = pl.ds(pl.multiple_of(i * 32, 32), 32)
        nrm[rows, :] = (xh[rows, :] * gain_r).astype(bf16)
        return 0

    lax.fori_loop(0, R // 32, nrm_tile, 0)

    for cp in w1b:
        cp.wait_recv()
    w2b = [remote(w4.at[gq, :, :, wl], w4.at[gq, :, :, wl], p) for p in cpeer]
    og = [remote(og_hbm.at[pl.ds(pl.multiple_of(R * p[2], R), R)], ogv.at[:, lane(U * t, U)], p)
          for p in zpeer]
    for cp in w1c:
        cp.wait_recv()
    w2c = [remote(w4.at[2 + gq, :, :, wl], w4.at[2 + gq, :, :, wl], p) for p in cpeer]
    for cp in w1g:
        cp.wait_recv()
    w2g = [remote(gt.at[grow, :], gt.at[grow, :], p) for p in cpeer]
    for cp in w2b:
        cp.wait_recv()
    w3b = remote(w4.at[0:2, :, :, dl], w4.at[0:2, :, :, dl], sib)
    for cp in w2c:
        cp.wait_recv()
    w3c = remote(w4.at[2:4, :, :, dl], w4.at[2:4, :, :, dl], sib)
    for cp in w2g:
        cp.wait_recv()
    w3g = remote(gt.at[dr_, :], gt.at[dr_, :], sib)

    w3b.wait_recv()

    def seq_rows(s):
        return pl.ds(pl.multiple_of(s * L, L), L)

    def drive_seq(s, _):
        raw[seq_rows(s), :] = nt(nrm[seq_rows(s), :], w4[0:2].reshape(2 * N, H))
        return 0

    lax.fori_loop(0, S, drive_seq, 0)

    def scan_lanes(src, dst, base, coef, reverse, end_ref):
        def lanes_step(j, _):
            lr_, li_ = lane(128 * j, 128), lane(N + 128 * j, 128)
            con = [cst[base + k, :, lr_] for k in range(8)]
            cfr, cfi = cst[18, :, lr_], cst[19, :, lr_]

            e = 0 if reverse else 7
            e0 = cst[16, :, lr_]
            e1 = -cst[17, :, lr_] if reverse else cst[17, :, lr_]

            def tile(i, carry):
                carry = list(carry)
                ii = L // 32 - 1 - i if reverse else i
                for s in range(S):
                    loc = []
                    for u in range(4):
                        uu = 3 - u if reverse else u
                        rows = pl.ds(pl.multiple_of(s * L + ii * 32 + uu * 8, 8), 8)
                        ar, ai = src[rows, lr_], src[rows, li_]
                        if coef:
                            ar, ai = cmul(cfr, cfi, ar, ai)
                        else:
                            ai = -ai
                        for n_, k in ((0, 1), (1, 2), (2, 4)):
                            sh = 8 - k if reverse else k
                            br, bi = pltpu.roll(ar, sh, 0), pltpu.roll(ai, sh, 0)
                            mr, mi = con[2 * n_], con[2 * n_ + 1]
                            ar, ai = ar + mr * br - mi * bi, ai + mr * bi + mi * br
                        loc.append((rows, ar, ai))
                    kr, ki = carry[2 * s], carry[2 * s + 1]
                    for rows, ar, ai in loc:
                        dst[rows, lr_] = ar + con[6] * kr - con[7] * ki
                        dst[rows, li_] = ai + con[6] * ki + con[7] * kr
                        endr = jnp.broadcast_to(ar[e:e + 1, :], (8, 128))
                        endi = jnp.broadcast_to(ai[e:e + 1, :], (8, 128))
                        kr, ki = endr + e0 * kr - e1 * ki, endi + e0 * ki + e1 * kr
                    carry[2 * s], carry[2 * s + 1] = kr, ki
                return tuple(carry)

            z = jnp.zeros((8, 128), f32)
            fin = lax.fori_loop(0, L // 32, tile, (z,) * (2 * S))
            for s in range(S):
                end_ref[pl.ds(s, 1), lr_] = fin[2 * s][0:1, :]
                end_ref[pl.ds(S + s, 1), lr_] = fin[2 * s + 1][0:1, :]
            return 0

        lax.fori_loop(0, N // 128, lanes_step, 0)

    scan_lanes(raw, st, 0, True, False, ce.at[0])
    fce = [remote(ce.at[0], cer.at[k], p) for k, p in enumerate(cpeer)]
    for cp in fce:
        cp.wait_recv()

    def incoming(buf, forward):
        bg = (cst[20, 0:1, :], cst[21, 0:1, :])
        wt = (jnp.ones((1, N), f32), jnp.zeros((1, N), f32))
        accr = jnp.zeros((S, N), f32)
        acci = jnp.zeros((S, N), f32)
        for k in range(1, C):
            got = buf[k - 1] if forward else buf[C - 1 - k]
            has = (c >= k) if forward else (c + k < C)
            w = jnp.where(has, 1.0, 0.0)
            vr, vi = got[0:S, :], got[S:2 * S, :]
            wi = wt[1] if forward else -wt[1]
            ur, ui = cmul(wt[0], wi, vr, vi)
            accr = accr + w * ur
            acci = acci + w * ui
            wt = cmul(*wt, *bg)
        return accr, acci

    inr, ini = incoming(cer, True)
    ce[2, 0:S, :] = inr
    ce[2, S:2 * S, :] = ini

    def fix_lanes(j, _):
        lr_, li_ = lane(128 * j, 128), lane(N + 128 * j, 128)
        p0, p1 = cst[6, :, lr_], cst[7, :, lr_]
        e0, e1 = cst[16, :, lr_], cst[17, :, lr_]
        q0 = tuple(jnp.broadcast_to(ce[2, pl.ds(k * S + s, 1), lr_], (8, 128))
                   for s in range(S) for k in range(2))

        def tile(i, q):
            q = list(q)
            for s in range(S):
                rr, ri = [], []
                for h in range(2):
                    rows = pl.ds(pl.multiple_of(s * L + i * 16 + 8 * h, 8), 8)
                    vr, vi = cmul(p0, p1, q[2 * s], q[2 * s + 1])
                    ar, ai = st[rows, lr_] + vr, st[rows, li_] + vi
                    st[rows, lr_] = ar
                    st[rows, li_] = ai
                    rr.append(ar)
                    ri.append(ai)
                    q[2 * s], q[2 * s + 1] = cmul(q[2 * s], q[2 * s + 1], e0, e1)
                rows = pl.ds(pl.multiple_of(s * L + i * 16, 16), 16)
                sb[rows, lr_] = jnp.concatenate(rr, 0).astype(bf16)
                sb[rows, li_] = (-jnp.concatenate(ri, 0)).astype(bf16)
            return tuple(q)

        lax.fori_loop(0, L // 16, tile, q0)
        return 0

    lax.fori_loop(0, N // 128, fix_lanes, 0)

    w3c.wait_recv()

    def ssm_seq(s, _):
        tmp[seq_rows(s), :] = nn(sb[seq_rows(s), :], w4[2:4].reshape(2 * N, H))
        return 0

    lax.fori_loop(0, S, ssm_seq, 0)

    def gelu_tile(i, _):
        rows = pl.ds(pl.multiple_of(i * 32, 32), 32)
        pre = tmp[rows, :] + skip_r * nrm[rows, :].astype(f32)
        sq = pre * pre
        th = jnp.tanh(pre * (SQ2PI + (SQ2PI * 0.044715) * sq))
        half = 0.5 + 0.5 * th
        act[rows, :] = (pre * half).astype(bf16)
        gp[rows, :] = half + 0.5 * pre * (1.0 - th * th) * (SQ2PI + (3 * 0.044715 * SQ2PI) * sq)
        return 0

    lax.fori_loop(0, R // 32, gelu_tile, 0)
    w3g.wait_recv()

    def gate_seq(s, _):
        tmp[seq_rows(s), :] = nn(act[seq_rows(s), :], gt[...])
        return 0

    lax.fori_loop(0, S, gate_seq, 0)

    def valid_of(i):
        s = i // (L // 32)
        pos = c * L + lax.rem(i, L // 32) * 32 + lax.broadcasted_iota(jnp.int32, (32, 1), 0)
        return jnp.where(pos < len_ref[S * t + s], 1.0, 0.0)

    def out_tile(i, _):
        rows = pl.ds(pl.multiple_of(i * 32, 32), 32)
        sg = 0.5 + 0.5 * jnp.tanh(0.5 * (tmp[rows, :] + bias_r))
        sig[rows, :] = sg
        o = valid_of(i) * (xv[rows, :].astype(f32) + act[rows, :].astype(f32) * sg)
        ob[rows, :] = o.astype(bf16)
        return 0

    lax.fori_loop(0, R // 32, out_tile, 0)
    mine = pl.ds(pl.multiple_of(R * t, R), R)
    outc = [remote(ob.at[:, lane(U * p[2], U)], out_hbm.at[mine, :], p) for p in zpeer]
    oc = pltpu.make_async_copy(ob.at[:, lane(U * t, U)], out_hbm.at[mine, :], lsem.at[2])
    oc.start()

    co.wait()
    for cp in og:
        cp.wait_recv()

    def fold(v):
        return jnp.sum(v.reshape(4, 8, v.shape[-1]), 0)

    def gate_tile(i, acc):
        rows = pl.ds(pl.multiple_of(i * 32, 32), 32)
        sg = sig[rows, :]
        direct = valid_of(i) * ogv[rows, :].astype(f32) * sg
        gg_ = direct * act[rows, :].astype(f32) * (1.0 - sg)
        gl[rows, :] = gg_.astype(bf16)
        sig[rows, :] = direct
        return acc + fold(gg_)

    bias_g = lax.fori_loop(0, R // 32, gate_tile, jnp.zeros((8, H), f32))

    def actg_seq(s, _):
        tmp[seq_rows(s), :] = nt(gl[seq_rows(s), :], gt[...])
        return 0

    lax.fori_loop(0, S, actg_seq, 0)

    def pre_tile(i, acc):
        rows = pl.ds(pl.multiple_of(i * 32, 32), 32)
        p = (tmp[rows, :] + sig[rows, :]) * gp[rows, :]
        pg[rows, :] = p
        plb[rows, :] = p.astype(bf16)
        return acc + fold(p * nrm[rows, :].astype(f32))

    skip_g = lax.fori_loop(0, R // 32, pre_tile, jnp.zeros((8, H), f32))

    def sgrad_seq(s, _):
        mu[seq_rows(s), :] = nt(plb[seq_rows(s), :], w4[2:4].reshape(2 * N, H))
        return 0

    lax.fori_loop(0, S, sgrad_seq, 0)
    scan_lanes(mu, mu, 8, False, True, ce.at[1])
    bce = [remote(ce.at[1], cbr.at[k], p) for k, p in enumerate(cpeer)]

    gcf, gbf = gc.reshape(2 * N, H), gb.reshape(2 * N, H)

    def gc_step(j, _):
        gcf[pl.ds(pl.multiple_of(j * 256, 256), 256), :] = tn(sb[:, lane(j * 256, 256)], plb[...]).astype(bf16)
        return 0

    lax.fori_loop(0, 2 * N // 256, gc_step, 0)
    ol = lane(HD * (1 - d), HD)
    d1c = remote(gc.at[:, :, :, ol], r1c, sib)

    def gg_step(j, _):
        gg[pl.ds(pl.multiple_of(j * 256, 256), 256), :] = tn(act[:, lane(j * 256, 256)], gl[...]).astype(bf16)
        return 0

    lax.fori_loop(0, H // 256, gg_step, 0)
    d1g = remote(gg.at[pl.ds(pl.multiple_of(HD * (1 - d), HD), HD), :], r1g, sib)

    for cp in bce:
        cp.wait_recv()
    inr, ini = incoming(cbr, False)
    ce[2, 0:S, :] = inr
    ce[2, S:2 * S, :] = ini
    row1 = lax.broadcasted_iota(jnp.int32, (8, 128), 0)

    def adj_lanes(j, _):
        lr_, li_ = lane(128 * j, 128), lane(N + 128 * j, 128)
        p0, p1 = cst[14, :, lr_], cst[15, :, lr_]
        e0, e1 = cst[16, :, lr_], -cst[17, :, lr_]
        cfr, cfi = cst[18, :, lr_], cst[19, :, lr_]
        q0 = tuple(jnp.broadcast_to(ce[2, pl.ds(k * S + s, 1), lr_], (8, 128))
                   for s in range(S) for k in range(2))
        z = jnp.zeros((8, 128), f32)

        def tile(i, carry):
            q, m, acc = list(carry[:2 * S]), list(carry[2 * S:4 * S]), list(carry[4 * S:])
            ii = L // 16 - 1 - i
            for s in range(S):
                rr, ri = [None, None], [None, None]
                for h in (1, 0):
                    rows = pl.ds(pl.multiple_of(s * L + ii * 16 + 8 * h, 8), 8)
                    vr, vi = cmul(p0, p1, q[2 * s], q[2 * s + 1])
                    ar, ai = mu[rows, lr_] + vr, mu[rows, li_] + vi
                    q[2 * s], q[2 * s + 1] = cmul(q[2 * s], q[2 * s + 1], e0, e1)
                    nr = jnp.where(row1 == 7, m[2 * s], pltpu.roll(ar, 7, 0))
                    ni = jnp.where(row1 == 7, m[2 * s + 1], pltpu.roll(ai, 7, 0))
                    m[2 * s] = jnp.broadcast_to(ar[0:1, :], (8, 128))
                    m[2 * s + 1] = jnp.broadcast_to(ai[0:1, :], (8, 128))
                    xr, xi = st[rows, lr_], st[rows, li_]
                    acc[0] = acc[0] + nr * xr + ni * xi
                    acc[1] = acc[1] + ni * xr - nr * xi
                    ur, ui = raw[rows, lr_], raw[rows, li_]
                    acc[2] = acc[2] + ar * ur + ai * ui
                    acc[3] = acc[3] + ai * ur - ar * ui
                    rr[h] = cfr * ar + cfi * ai
                    ri[h] = cfr * ai - cfi * ar
                rows = pl.ds(pl.multiple_of(s * L + ii * 16, 16), 16)
                nb[rows, lr_] = jnp.concatenate(rr, 0).astype(bf16)
                nb[rows, li_] = jnp.concatenate(ri, 0).astype(bf16)
            return tuple(q) + tuple(m) + tuple(acc)

        fin = lax.fori_loop(0, L // 16, tile, q0 + q0 + (z,) * 4)
        for k in range(4):
            vv[3 + k:4 + k, lr_] = jnp.sum(fin[4 * S + k], 0, keepdims=True)
        return 0

    vv[...] = jnp.zeros_like(vv)
    lax.fori_loop(0, N // 128, adj_lanes, 0)

    def gb_step(j, _):
        gbf[pl.ds(pl.multiple_of(j * 256, 256), 256), :] = tn(nb[:, lane(j * 256, 256)], nrm[...]).astype(bf16)
        return 0

    lax.fori_loop(0, 2 * N // 256, gb_step, 0)
    d1b = remote(gb.at[:, :, :, ol], r1b, sib)

    def rs_ctx(p):
        return p // 2, pl.ds(pl.multiple_of((NS // 2) * lax.rem(p, 2), NS // 2), NS // 2)

    d1c.wait_recv()
    s1c[...] = (gc[:, :, :, dl].astype(f32) + r1c[...].astype(f32)).astype(bf16)
    d2c = [remote(s1c.at[rs_ctx(p[1])[0], :, rs_ctx(p[1])[1], :], r2c.at[k], p) for k, p in enumerate(cpeer)]
    d1g.wait_recv()
    s1g[...] = (gg[dr_, :].astype(f32) + r1g[...].astype(f32)).astype(bf16)
    gr = lambda p: pl.ds(pl.multiple_of(uq * p, uq), uq)
    d2g = [remote(s1g.at[gr(p[1]), :], r2g.at[k], p) for k, p in enumerate(cpeer)]

    def ng_seq(s, _):
        tmp[seq_rows(s), :] = nn(nb[seq_rows(s), :], w4[0:2].reshape(2 * N, H))
        return 0

    lax.fori_loop(0, S, ng_seq, 0)

    def tok_tile(i, acc):
        for u in range(4):
            rows = pl.ds(pl.multiple_of(i * 128 + u * 32, 32), 32)
            n = tmp[rows, :] + skip_r * pg[rows, :]
            xt = xh[rows, :]
            h = n * gain_r
            m1 = jnp.mean(h, -1, keepdims=True)
            m2 = jnp.mean(h * xt, -1, keepdims=True)
            tgb[rows, :] = ((h - m1 - xt * m2) * rs[rows, 0:1]).astype(bf16)
            acc = acc + fold(n * xt)
        return acc

    gain_g = lax.fori_loop(0, R // 128, tok_tile, jnp.zeros((8, H), f32))
    tgc = [remote(tgb.at[:, lane(U * p[2], U)], tg_hbm.at[mine, :], p) for p in zpeer]
    tc = pltpu.make_async_copy(tgb.at[:, lane(U * t, U)], tg_hbm.at[mine, :], lsem.at[3])
    tc.start()
    vv[0:1, :] = jnp.sum(gain_g, 0, keepdims=True)
    vv[1:2, :] = jnp.sum(skip_g, 0, keepdims=True)
    vv[2:3, :] = jnp.sum(bias_g, 0, keepdims=True)

    d1v = remote(vv, vr1, sib)
    d1b.wait_recv()
    s1b[...] = (gb[:, :, :, dl].astype(f32) + r1b[...].astype(f32)).astype(bf16)
    d2b = [remote(s1b.at[rs_ctx(p[1])[0], :, rs_ctx(p[1])[1], :], r2b.at[k], p) for k, p in enumerate(cpeer)]
    d1v.wait_recv()
    vr2[0] = vv[...] + vr1[...]
    d2v = [remote(vr2.at[0], vr2.at[k + 1], p) for k, p in enumerate(cpeer)]

    def total(first, buf, n):
        acc = first.astype(f32)
        for k in range(n):
            acc = acc + buf[k].astype(f32)
        return acc

    for cp in d2c:
        cp.wait_recv()
    s2c[...] = total(s1c[rs_ctx(c)[0], :, rs_ctx(c)[1], :], r2c, C - 1).astype(bf16)
    d3c = [remote(s2c.at[p[2]], r3c.at[k], p) for k, p in enumerate(zpeer)]
    for cp in d2g:
        cp.wait_recv()
    s2g[...] = total(s1g[gr(c), :], r2g, C - 1).astype(bf16)
    d3g = [remote(s2g.at[:, lane(U * p[2], U)], r3g.at[k], p) for k, p in enumerate(zpeer)]
    for cp in d2b:
        cp.wait_recv()
    s2b[...] = total(s1b[rs_ctx(c)[0], :, rs_ctx(c)[1], :], r2b, C - 1).astype(bf16)
    d3b = [remote(s2b.at[p[2]], r3b.at[k], p) for k, p in enumerate(zpeer)]
    for cp in d2v:
        cp.wait_recv()
    vr3[0] = vr2[0] + vr2[1] + vr2[2] + vr2[3]
    d3v = [remote(vr3.at[0], vr3.at[k + 1], p) for k, p in enumerate(zpeer)]

    for cp in d3c:
        cp.wait_recv()
    fc_ref[c] = total(s2c[t], r3c, T - 1).astype(bf16)
    d4 = [remote(fc_ref.at[c], fc_ref.at[c], p) for p in cpeer]
    for cp in d3g:
        cp.wait_recv()
    fg_ref[c] = total(s2g[:, tl], r3g, T - 1).astype(bf16)
    d4 += [remote(fg_ref.at[c], fg_ref.at[c], p) for p in cpeer]
    for cp in d3b:
        cp.wait_recv()
    fb_ref[c] = total(s2b[t], r3b, T - 1).astype(bf16)
    d4 += [remote(fb_ref.at[c], fb_ref.at[c], p) for p in cpeer]
    for cp in d3v:
        cp.wait_recv()
    vf[...] = vr3[0] + vr3[1] + vr3[2] + vr3[3]
    place = t * D + d
    back = lambda n: lax.rem(H - n * place, H)
    st8 = pltpu.roll(vf[...], back(NS // D), 1)[:, 0:NS // D]
    ub8 = pltpu.roll(vf[...], back(U // D), 1)[:, 0:U // D]
    lr1, li1, step1 = lre_in[...], lim_in[...], jnp.exp(stp_in[...])
    dr1, di1, cr1, ci1 = (sm_ref[k:k + 1, 0:NS // D] for k in range(4))
    gdr, gdi, gcr, gci = (st8[k:k + 1] for k in range(3, 7))
    inv = 1.0 / (lr1 * lr1 + li1 * li1)
    hdr = gdr + (gcr * lr1 - gci * li1) * inv
    hdi = gdi + (gcr * li1 + gci * lr1) * inv
    pull = 2.0 * (gcr * cr1 + gci * ci1)
    e1, e2 = dr1 - 1.0, hdr * dr1 + hdi * di1
    e3 = hdi * dr1 - hdr * di1
    fv_ref[...] = jnp.zeros_like(fv_ref)
    fv_ref[0:1, :] = vf[0:1, dl]
    fv_ref[1:2, :] = vf[1:2, dl]
    fv_ref[2:3, 0:U // D] = ub8[2:3]
    fv_ref[3:4, 0:NS // D] = (gcr * e1 + gci * di1 - pull * lr1) * inv + step1 * e2
    fv_ref[4:5, 0:NS // D] = (gcr * di1 - gci * e1 - pull * li1) * inv + step1 * e3
    fv_ref[5:6, 0:NS // D] = step1 * (lr1 * e2 + li1 * e3)
    for cp in d4 + tgc + outc:
        cp.wait_recv()
    oc.wait()
    tc.wait()
    for cp in started:
        cp.wait_send()


def fused_call(geo, lens, x2, og2, *params):
    D, C, T, S, L, H, N, U = geo
    R, NS, HD = S * L, N // T, H // D
    f32, bf16 = jnp.float32, jnp.bfloat16
    uq, hs = HD // C, NS // 2
    V = pltpu.VMEM
    nsem = 7 + 9 + 9 + 3 + 3 + 6 + 3 + 3 + 4 + 12 + 12 + 9
    any_, vm = pl.BlockSpec(memory_space=pl.ANY), pl.BlockSpec(memory_space=pltpu.VMEM)
    scratch = [
        V((R, H), bf16), V((R, H), bf16), V((R, H), f32), V((R, 128), f32),
        V((R, 2 * N), f32), V((R, 2 * N), f32), V((R, 2 * N), bf16),
        V((R, H), f32), V((R, H), bf16), V((R, H), f32), V((R, H), f32),
        V((R, H), bf16), V((R, H), bf16), V((R, H), bf16), V((R, H), f32), V((R, H), bf16),
        V((R, 2 * N), f32), V((R, 2 * N), bf16), V((R, H), bf16),
        V((4, T, NS, H), bf16), V((H, H), bf16), V((D * T, 8, HD), f32),
        V((22, 8, N), f32), V((3, 8, N), f32), V((C - 1, 8, N), f32), V((C - 1, 8, N), f32),
        V((2, T, NS, H), bf16), V((H, H), bf16), V((2, T, NS, H), bf16),
        V((2, T, NS, HD), bf16), V((HD, H), bf16), V((2, T, NS, HD), bf16),
        V((2, T, NS, HD), bf16), V((HD, H), bf16), V((2, T, NS, HD), bf16),
        V((C - 1, T, hs, HD), bf16), V((C - 1, uq, H), bf16), V((C - 1, T, hs, HD), bf16),
        V((T, hs, HD), bf16), V((uq, H), bf16), V((T, hs, HD), bf16),
        V((T - 1, hs, HD), bf16), V((T - 1, uq, U), bf16), V((T - 1, hs, HD), bf16),
        V((8, H), f32), V((8, H), f32), V((C, 8, H), f32), V((T, 8, H), f32), V((8, H), f32),
        V((4, NS, HD), bf16), V((8, HD), f32),
        pltpu.SemaphoreType.DMA((4,)), pltpu.SemaphoreType.DMA((nsem,)), pltpu.SemaphoreType.DMA((nsem,)),
    ]
    rows = x2.shape[0]
    return pl.pallas_call(
        functools.partial(fused_body, geo),
        out_shape=(
            jax.ShapeDtypeStruct((rows, U), bf16), jax.ShapeDtypeStruct((rows, U), bf16),
            jax.ShapeDtypeStruct((C, hs, HD), bf16), jax.ShapeDtypeStruct((C, uq, U), bf16),
            jax.ShapeDtypeStruct((C, hs, HD), bf16), jax.ShapeDtypeStruct((8, HD), f32)),
        in_specs=[pl.BlockSpec(memory_space=pltpu.SMEM), any_, any_] + [vm] * 11,
        out_specs=(any_, any_, vm, vm, vm, vm),
        scratch_shapes=scratch,
        compiler_params=pltpu.CompilerParams(
            collective_id=0, has_side_effects=True, vmem_limit_bytes=58 * 1024 * 1024),
        name="block",
    )(lens, x2, og2, *params)


def finish_body(geo, group, len_ref, out_in, tok_in, og_in, fc, fg, fb, fv, out, ingrad, gain_g, skip_g,
                lre_g, lim_g, step_g, bre_g, bim_g, cre_g, cim_g, glu_g, bias_g):
    D, C, T, S, L, H, N, U = geo
    NS = N // T
    f32 = jnp.float32
    i = pl.program_id(0)
    out[...] = out_in[...]
    pos = lax.axis_index("ctx") * L + lax.broadcasted_iota(jnp.int32, (L, 1), 0)
    for s in range(group):
        keep = jnp.where(pos < len_ref[i * group + s], 1.0, 0.0)
        ingrad[s] = keep * og_in[s].astype(f32) + tok_in[s].astype(f32)

    @pl.when(i == 0)
    def _():
        h = C // 2
        for k in range(C):
            rows = pl.ds((k % h) * (NS // h), NS // h)
            (bre_g if k < h else bim_g)[rows, :] = fb[k].astype(f32)
            (cre_g if k < h else cim_g)[rows, :] = fc[k].astype(f32)
        glu_g[...] = fg[...].reshape(glu_g.shape).astype(f32)
        gain_g[...] = fv[0:1, :]
        skip_g[...] = fv[1:2, :]
        bias_g[...] = fv[2:3, 0:U // D]
        lre_g[...] = fv[3:4, 0:NS // D]
        lim_g[...] = fv[4:5, 0:NS // D]
        step_g[...] = fv[5:6, 0:NS // D]


def finish_call(geo, lens, out, tok, og, fc, fg, fb, fv):
    D, C, T, S, L, H, N, U = geo
    NS, HD = N // T, H // D
    f32 = jnp.float32
    seqs = S * T
    group = 2
    big = pl.BlockSpec((group, L, U), lambda i: (i, 0, 0))
    vm = pl.BlockSpec(memory_space=pltpu.VMEM)
    const = lambda *shape: pl.BlockSpec(shape, lambda i: (0,) * len(shape))
    small = [(1, HD), (1, HD)] + [(1, NS // D)] * 3 + [(NS, HD)] * 4 + [(HD, U), (1, U // D)]
    return pl.pallas_call(
        functools.partial(finish_body, geo, group),
        grid=(seqs // group,),
        out_shape=[jax.ShapeDtypeStruct((seqs, L, U), jnp.bfloat16), jax.ShapeDtypeStruct((seqs, L, U), f32)]
        + [jax.ShapeDtypeStruct(s, f32) for s in small],
        in_specs=[pl.BlockSpec(memory_space=pltpu.SMEM), big, big, big] + [const(*a.shape) for a in (fc, fg, fb, fv)],
        out_specs=[big, big] + [const(*s) for s in small],
        compiler_params=pltpu.CompilerParams(vmem_limit_bytes=60 * 1024 * 1024),
        name="finish",
    )(lens, out.reshape(seqs, L, U), tok.reshape(seqs, L, U), og, fc, fg, fb, fv)


def coefficients(lam_re, lam_im, step_log):
    step = jnp.exp(step_log)
    magnitude = jnp.exp(lam_re * step)
    decay_re = magnitude * jnp.cos(lam_im * step)
    decay_im = magnitude * jnp.sin(lam_im * step)
    inv = 1.0 / (lam_re * lam_re + lam_im * lam_im)
    coef_re = ((decay_re - 1.0) * lam_re + decay_im * lam_im) * inv
    coef_im = (decay_im * lam_re - (decay_re - 1.0) * lam_im) * inv
    return decay_re, decay_im, coef_re, coef_im


def token_split(sizes, inputs, lengths, norm_gain, skip_weight, lambda_re, lambda_im, log_step,
                b_re, b_im, c_re, c_im, glu_weight, glu_bias, out_grad):
    D, C, T = sizes
    seqs, L, H = inputs.shape
    NS, HD = b_re.shape
    U = glu_weight.shape[1]
    geo = (D, C, T, seqs // T, L, H, NS * T, U)
    row = lambda v: v.reshape(1, -1)
    out, tok, fc, fg, fb, fv = fused_call(
        geo, lengths, inputs.reshape(seqs * L, H), out_grad.reshape(seqs * L, U),
        b_re, b_im, c_re.T, c_im.T, glu_weight,
        *(row(v) for v in (norm_gain, skip_weight, lambda_re, lambda_im, log_step, glu_bias)))
    res = finish_call(geo, lengths, out, tok, out_grad, fc, fg, fb, fv)
    out, ingrad, gain_g, skip_g, lre_g, lim_g, step_g, bre_g, bim_g, cre_g, cim_g, glu_g, bias_g = res
    flat = lambda v: v.reshape(-1)
    return (out, ingrad, flat(gain_g), flat(skip_g), flat(lre_g), flat(lim_g), flat(step_g),
            bre_g, bim_g, cre_g.T, cim_g.T, glu_g, flat(bias_g))


def solution(mesh):
    in_specs = (
        P("dp", "ctx", None),
        P("dp"),
        P("dp"),
        P("dp"),
        P(("tp", "dp")),
        P(("tp", "dp")),
        P(("tp", "dp")),
        P("tp", "dp"),
        P("tp", "dp"),
        P("dp", "tp"),
        P("dp", "tp"),
        P("dp", "tp"),
        P(("tp", "dp")),
        P("dp", "ctx", "tp"),
    )
    out_specs = (
        P("dp", "ctx", "tp"),
        P("dp", "ctx", "tp"),
        P("dp"),
        P("dp"),
        P(("tp", "dp")),
        P(("tp", "dp")),
        P(("tp", "dp")),
        P("tp", "dp"),
        P("tp", "dp"),
        P("dp", "tp"),
        P("dp", "tp"),
        P("dp", "tp"),
        P(("tp", "dp")),
    )
    sizes = tuple(mesh.shape[name] for name in ("dp", "ctx", "tp"))

    def block(*args):
        seqs, _, feat = args[0].shape
        units = args[11].shape[1]
        if sizes == (2, 4, 4) and seqs % sizes[2] == 0 and units % 128 == 0:
            return token_split(sizes, *args)
        return on_device(*args)

    return jax.shard_map(
        block, mesh=mesh, in_specs=in_specs, out_specs=out_specs, check_vma=False
    )
```

```python
import functools

import jax
import jax.numpy as jnp
from jax import lax
from jax.experimental import pallas as pl
from jax.experimental.pallas import tpu as pltpu
from jax.sharding import PartitionSpec as P

epsilon = 1e-05


def carried_in(value, axis, combine, identity, reverse):
    count, index = (lax.axis_size(axis), lax.axis_index(axis))
    everything = jax.tree.map(lambda part: lax.all_gather(part, axis), value)
    start = jax.tree.map(
        lambda part, zero: jnp.broadcast_to(jnp.asarray(zero, part.dtype), part.shape),
        value,
        identity,
    )

    def lap(k, before):
        at = count - 1 - k if reverse else k
        reached = at > index if reverse else at < index
        new = combine(before, jax.tree.map(lambda part: part[at], everything))
        return jax.tree.map(lambda a, b: jnp.where(reached, a, b), new, before)

    return lax.fori_loop(0, count, lap, start)


def contract(left, right, left_dim, right_dim):
    return lax.dot_general(
        left, right, (((left_dim,), (right_dim,)), ((), ())), preferred_element_type=jnp.float32
    )


def combine(earlier, later):
    e_re, e_im, eb_re, eb_im = earlier
    l_re, l_im, lb_re, lb_im = later
    return (
        e_re * l_re - e_im * l_im,
        e_re * l_im + e_im * l_re,
        l_re * eb_re - l_im * eb_im + lb_re,
        l_re * eb_im + l_im * eb_re + lb_im,
    )


def discretize(lam_re, lam_im, step_log, mat_re, mat_im):
    step = jnp.exp(step_log)
    magnitude = jnp.exp(lam_re * step)
    decay_re = magnitude * jnp.cos(lam_im * step)
    decay_im = magnitude * jnp.sin(lam_im * step)
    denom = lam_re * lam_re + lam_im * lam_im
    coef_re = ((decay_re - 1.0) * lam_re + decay_im * lam_im) / denom
    coef_im = (decay_im * lam_re - (decay_re - 1.0) * lam_im) / denom
    bar_re = coef_re[:, None] * mat_re - coef_im[:, None] * mat_im
    bar_im = coef_re[:, None] * mat_im + coef_im[:, None] * mat_re
    return (decay_re, decay_im, jnp.concatenate([bar_re, bar_im], 0))


def normalize(tokens, gain):
    mean_val = jnp.mean(tokens, -1, keepdims=True)
    centered = tokens - mean_val
    var_val = jnp.mean(centered * centered, -1, keepdims=True)
    return centered * lax.rsqrt(var_val + epsilon) * gain


def powers(lam_re, lam_im, step_log, count):
    step = jnp.exp(step_log)
    exponent = (jnp.arange(count, dtype=jnp.float32) + 1.0)[:, None]
    magnitude = jnp.exp(exponent * lam_re * step)
    return (
        magnitude * jnp.cos(exponent * lam_im * step),
        magnitude * jnp.sin(exponent * lam_im * step),
    )


def on_device(
    inputs,
    lengths,
    norm_gain,
    skip_weight,
    lambda_re,
    lambda_im,
    log_step,
    b_re,
    b_im,
    c_re,
    c_im,
    glu_weight,
    glu_bias,
    out_grad,
):
    full_bre, full_bim, full_cre, full_cim, full_glu = (
        lax.all_gather(b_re, "dp", axis=1, tiled=True),
        lax.all_gather(b_im, "dp", axis=1, tiled=True),
        lax.all_gather(c_re, "dp", axis=0, tiled=True),
        lax.all_gather(c_im, "dp", axis=0, tiled=True),
        lax.all_gather(glu_weight, "dp", axis=0, tiled=True),
    )
    gain, skip_full, lam_re, lam_im, step_log, bias_vec = (
        lax.all_gather(norm_gain, "dp", axis=0, tiled=True),
        lax.all_gather(skip_weight, "dp", axis=0, tiled=True),
        lax.all_gather(lambda_re, "dp", axis=0, tiled=True),
        lax.all_gather(lambda_im, "dp", axis=0, tiled=True),
        lax.all_gather(log_step, "dp", axis=0, tiled=True),
        lax.all_gather(glu_bias, "dp", axis=0, tiled=True),
    )
    seq_count, blk_len, feat_dim = inputs.shape
    row_count = seq_count * blk_len
    state_count = full_bre.shape[0]
    unit_count = full_glu.shape[1]
    tp_rank = lax.axis_index("tp")
    unit_start = tp_rank * unit_count
    positions = lax.axis_index("ctx") * blk_len + jnp.arange(blk_len, dtype=jnp.int32)
    valid_mask = (positions[None, :] < lengths[:, None]).astype(jnp.float32).reshape(row_count, 1)
    tokens = inputs.astype(jnp.float32).reshape(row_count, feat_dim)
    tokens_mine = lax.dynamic_slice_in_dim(tokens, unit_start, unit_count, 1)
    cotangent = out_grad.astype(jnp.float32).reshape(row_count, unit_count)
    normed_f, norm_pull = jax.vjp(normalize, tokens, gain)
    normed_b = normed_f.astype(jnp.bfloat16)
    normed_r = normed_b.astype(jnp.float32)
    (decay_re, decay_im, bar_full), disc_pull = jax.vjp(
        discretize,
        lam_re,
        lam_im,
        step_log,
        full_bre.astype(jnp.float32),
        full_bim.astype(jnp.float32),
    )
    bar_b = bar_full.astype(jnp.bfloat16)
    drive = contract(normed_b, bar_b, 1, 1).reshape(seq_count, blk_len, 2 * state_count)
    full_re = jnp.broadcast_to(decay_re, (seq_count, blk_len, state_count))
    full_im = jnp.broadcast_to(decay_im, (seq_count, blk_len, state_count))
    local_states = lax.associative_scan(
        combine, (full_re, full_im, drive[..., :state_count], drive[..., state_count:]), axis=1
    )
    pow_re, pow_im = powers(lam_re, lam_im, step_log, blk_len)
    identity = (
        jnp.ones((1, state_count), jnp.float32),
        jnp.zeros((1, state_count), jnp.float32),
        jnp.zeros((seq_count, state_count), jnp.float32),
        jnp.zeros((seq_count, state_count), jnp.float32),
    )
    incoming = carried_in(
        (pow_re[-1:], pow_im[-1:], local_states[2][:, -1], local_states[3][:, -1]),
        "ctx",
        combine,
        identity,
        False,
    )
    in_re = incoming[2][:, None, :]
    in_im = incoming[3][:, None, :]
    state_re = local_states[2] + pow_re * in_re - pow_im * in_im
    state_im = local_states[3] + pow_re * in_im + pow_im * in_re
    states_b = (
        jnp.concatenate([state_re, state_im], -1)
        .reshape(row_count, 2 * state_count)
        .astype(jnp.bfloat16)
    )
    c_stack = jnp.concatenate([full_cre, -full_cim], 1)
    ssm_part = contract(states_b, c_stack, 1, 1)
    ssm_full = lax.psum(ssm_part.astype(jnp.bfloat16), "tp").astype(jnp.float32)
    pre_full = ssm_full + skip_full * normed_r
    gelu_full, gelu_pull = jax.vjp(jax.nn.gelu, pre_full)
    gelu_b = gelu_full.astype(jnp.bfloat16)
    gelu_part = lax.dynamic_slice_in_dim(gelu_b, unit_start, unit_count, 1)
    gelu_mine = gelu_part.astype(jnp.float32)
    gate = contract(gelu_b, full_glu, 1, 0) + bias_vec
    gate_sig = jax.nn.sigmoid(gate)
    output = (
        (valid_mask * (tokens_mine + gelu_mine * gate_sig))
        .astype(jnp.bfloat16)
        .reshape(seq_count, blk_len, unit_count)
    )
    branch_grad = valid_mask * cotangent
    gate_grad = branch_grad * gelu_mine * gate_sig * (1.0 - gate_sig)
    bias_grad = jnp.sum(gate_grad, 0)
    gate_b = gate_grad.astype(jnp.bfloat16)
    glu_grad = contract(gelu_b, gate_b, 0, 0)
    gelu_grad = contract(gate_b, full_glu, 1, 1)
    own_cols = (
        lax.dynamic_slice_in_dim(gelu_grad, unit_start, unit_count, 1) + branch_grad * gate_sig
    )
    gelu_grad = lax.dynamic_update_slice_in_dim(gelu_grad, own_cols, unit_start, 1)
    gelu_back = lax.psum(gelu_grad, "tp")
    (pre_grad,) = gelu_pull(gelu_back)
    skip_grad = jnp.sum(pre_grad * normed_r, 0)
    pre_b = pre_grad.astype(jnp.bfloat16)
    state_grad = contract(pre_b, c_stack, 1, 0).reshape(seq_count, blk_len, 2 * state_count)
    c_grad = contract(pre_b, states_b, 0, 0)
    back_local = lax.associative_scan(
        combine,
        (full_re, -full_im, state_grad[..., :state_count], state_grad[..., state_count:]),
        axis=1,
        reverse=True,
    )
    later_adj = carried_in(
        (pow_re[-1:], -pow_im[-1:], back_local[2][:, 0], back_local[3][:, 0]),
        "ctx",
        combine,
        identity,
        True,
    )
    rev_re = pow_re[::-1]
    rev_im = -pow_im[::-1]
    next_re = later_adj[2][:, None, :]
    next_im = later_adj[3][:, None, :]
    adj_re = back_local[2] + rev_re * next_re - rev_im * next_im
    adj_im = back_local[3] + rev_re * next_im + rev_im * next_re
    prev_re = jnp.concatenate([in_re, state_re[:, :-1]], 1)
    prev_im = jnp.concatenate([in_im, state_im[:, :-1]], 1)
    decay_grad_re = jnp.sum(adj_re * prev_re + adj_im * prev_im, (0, 1))
    decay_grad_im = jnp.sum(adj_im * prev_re - adj_re * prev_im, (0, 1))
    adj_b = (
        jnp.concatenate([adj_re, adj_im], -1)
        .reshape(row_count, 2 * state_count)
        .astype(jnp.bfloat16)
    )
    bar_grad = contract(adj_b, normed_b, 0, 0)
    normed_part = contract(adj_b, bar_b, 1, 0)
    normed_sum = lax.psum(normed_part.astype(jnp.bfloat16), "tp").astype(jnp.float32)
    normed_grad = normed_sum + skip_full * pre_grad
    token_grad, gain_grad = norm_pull(normed_grad)
    input_grad = (
        valid_mask * cotangent + lax.dynamic_slice_in_dim(token_grad, unit_start, unit_count, 1)
    ).reshape(seq_count, blk_len, unit_count)
    grad_cre = c_grad[:, :state_count]
    grad_cim = -c_grad[:, state_count:]
    lre_grad, lim_grad, step_grad, bre_grad, bim_grad = disc_pull(
        (decay_grad_re, decay_grad_im, bar_grad)
    )
    shards = (
        lax.psum_scatter(
            gain_grad.astype(jnp.bfloat16), "dp", scatter_dimension=0, tiled=True
        ).astype(jnp.float32),
        lax.psum_scatter(
            skip_grad.astype(jnp.bfloat16), "dp", scatter_dimension=0, tiled=True
        ).astype(jnp.float32),
        lax.psum_scatter(
            lre_grad.astype(jnp.bfloat16), "dp", scatter_dimension=0, tiled=True
        ).astype(jnp.float32),
        lax.psum_scatter(
            lim_grad.astype(jnp.bfloat16), "dp", scatter_dimension=0, tiled=True
        ).astype(jnp.float32),
        lax.psum_scatter(
            step_grad.astype(jnp.bfloat16), "dp", scatter_dimension=0, tiled=True
        ).astype(jnp.float32),
        lax.psum_scatter(
            bias_grad.astype(jnp.bfloat16), "dp", scatter_dimension=0, tiled=True
        ).astype(jnp.float32),
        lax.psum_scatter(
            bre_grad.astype(jnp.bfloat16), "dp", scatter_dimension=1, tiled=True
        ).astype(jnp.float32),
        lax.psum_scatter(
            bim_grad.astype(jnp.bfloat16), "dp", scatter_dimension=1, tiled=True
        ).astype(jnp.float32),
        lax.psum_scatter(
            grad_cre.astype(jnp.bfloat16), "dp", scatter_dimension=0, tiled=True
        ).astype(jnp.float32),
        lax.psum_scatter(
            grad_cim.astype(jnp.bfloat16), "dp", scatter_dimension=0, tiled=True
        ).astype(jnp.float32),
        lax.psum_scatter(
            glu_grad.astype(jnp.bfloat16), "dp", scatter_dimension=0, tiled=True
        ).astype(jnp.float32),
    )
    summed = (
        lax.psum(shards[0].astype(jnp.bfloat16), "ctx").astype(jnp.float32),
        lax.psum(shards[1].astype(jnp.bfloat16), "ctx").astype(jnp.float32),
        lax.psum(shards[2].astype(jnp.bfloat16), "ctx").astype(jnp.float32),
        lax.psum(shards[3].astype(jnp.bfloat16), "ctx").astype(jnp.float32),
        lax.psum(shards[4].astype(jnp.bfloat16), "ctx").astype(jnp.float32),
        lax.psum(shards[5].astype(jnp.bfloat16), "ctx").astype(jnp.float32),
        lax.psum(shards[6].astype(jnp.bfloat16), "ctx").astype(jnp.float32),
        lax.psum(shards[7].astype(jnp.bfloat16), "ctx").astype(jnp.float32),
        lax.psum(shards[8].astype(jnp.bfloat16), "ctx").astype(jnp.float32),
        lax.psum(shards[9].astype(jnp.bfloat16), "ctx").astype(jnp.float32),
        lax.psum(shards[10].astype(jnp.bfloat16), "ctx").astype(jnp.float32),
    )
    return (
        output,
        input_grad,
        summed[0],
        summed[1],
        summed[2],
        summed[3],
        summed[4],
        summed[6],
        summed[7],
        summed[8],
        summed[9],
        summed[10],
        summed[5],
    )


MESH = pl.DeviceIdType.MESH
SQ2PI = 0.7978845608028654


def nt(a, b):
    return lax.dot_general(a, b, (((1,), (1,)), ((), ())), preferred_element_type=jnp.float32)


def nn(a, b):
    return lax.dot_general(a, b, (((1,), (0,)), ((), ())), preferred_element_type=jnp.float32)


def tn(a, b):
    return lax.dot_general(a, b, (((0,), (0,)), ((), ())), preferred_element_type=jnp.float32)


def cmul(ar, ai, br, bi):
    return ar * br - ai * bi, ar * bi + ai * br


def lane(start, size):
    return pl.ds(pl.multiple_of(start, 128), size)


def fused_body(geo, *refs):
    D, C, T, S, L, H, N, U = geo
    R = S * L
    NS = N // T
    HD = H // D
    f32, bf16 = jnp.float32, jnp.bfloat16
    (len_ref, x_hbm, og_hbm, bre, bim, cre, cim, glu_hbm, gain_h, skip_h, lre_h, lim_h, stp_h, bias_h,
     out_hbm, tg_hbm, fc_ref, fg_ref, fb_ref, fv_ref) = refs[:20]
    (xv, nrm, xh, rs, raw, st, sb, tmp, act, gp, sig, ogv, ob, gl, pg, plb, mu, nb, tgb,
     xe, nrme, rawe, sbe, acte, tmpe, obe,
     w4, gt, smr, cst, ce, cer, cin, gc, gg, gb, r1c, r1g, r1b, s1c, s1g, s1b, r2c, r2g, r2b,
     s2c, s2g, s2b, r3c, r3g, r3b, s3c, s3g, s3b, r4c, r4g, r4b,
     vv, vr1, vr2, vr3, vf, accv, pk, sm_ref, glu, gain_in, skip_in, lre_in, lim_in, stp_in, bias_in,
     lsem, ssem, rsem) = refs[20:]
    d, c, t = lax.axis_index("dp"), lax.axis_index("ctx"), lax.axis_index("tp")
    half = t // 2
    t1 = t + 1 - 2 * lax.rem(t, 2)
    t2 = t + 2 - 4 * half
    t3 = T - 1 - t
    z1, z2, z3 = (d, c, t1), (d, c, t2), (d, c, t3)
    zpeer = [(d, c, lax.rem(t + k, T)) for k in range(1, T)]
    cpeer = [(d, lax.rem(c + k, C), t) for k in range(1, C)]
    sib = (1 - d, c, t)
    xpeer = [(1 - d, c, lax.rem(t + k, T)) for k in range(1, T)]
    everyone = zpeer + cpeer + [sib] + xpeer
    erank = [t2, t3]

    count = [0]
    started = []

    def remote(src, dst, peer):
        i = count[0]
        count[0] += 1
        cp = pltpu.make_async_remote_copy(
            src_ref=src, dst_ref=dst, send_sem=ssem.at[i], recv_sem=rsem.at[i],
            device_id=peer, device_id_type=MESH)
        cp.start()
        started.append(cp)
        return cp

    def arrived(*cps):
        for cp in cps:
            cp.wait_recv()

    nlocal = [0]

    def local(src, dst):
        cp = pltpu.make_async_copy(src, dst, lsem.at[nlocal[0]])
        nlocal[0] += 1
        cp.start()
        return cp

    def rows_at(start, size):
        return pl.ds(pl.multiple_of(start, size), size)

    barrier = pltpu.get_barrier_semaphore()
    for p in everyone:
        pl.semaphore_signal(barrier, inc=1, device_id=p, device_id_type=MESH)
    cp_small = [local(a, b) for a, b in (
        (lre_h, lre_in), (lim_h, lim_in), (stp_h, stp_in), (bias_h, bias_in), (gain_h, gain_in), (skip_h, skip_in))]
    mine = rows_at(R * t, R)
    cp_pk = [local(a, pk.at[k]) for k, a in enumerate((bre, bim, cre, cim))] + [local(glu_hbm, glu)]
    cx = local(x_hbm.at[mine], xv)
    cxe = [local(x_hbm.at[rows_at(R * e, R)], xe.at[pl.ds(R * k, R)]) for k, e in enumerate(erank)]
    co = local(og_hbm.at[mine], ogv.at[:, lane(U * t, U)])
    dl = lane(HD * d, HD)
    dr_ = rows_at(HD * d, HD)
    tl = lane(U * t, U)
    sm_ref[...] = jnp.zeros_like(sm_ref)
    for cp in cp_small:
        cp.wait()
    own = coefficients(lre_in[...], lim_in[...], stp_in[...])
    for k in range(4):
        sm_ref[k:k + 1, 0:NS // D] = own[k]
    sm_ref[4:5, 0:U // D] = bias_in[...]
    sm_ref[5:6, :] = gain_in[...]
    sm_ref[6:7, :] = skip_in[...]
    me8 = d * T + t
    smr[me8] = sm_ref[...]
    accv[...] = jnp.zeros_like(accv)
    vv[...] = jnp.zeros_like(vv)
    for cp in cp_pk:
        cp.wait()
    for k in range(4):
        w4[k, t, :, dl] = pk[k]
    gt[dr_, tl] = glu[...]
    cx.wait()

    def standard(x):
        cen = x - jnp.mean(x, -1, keepdims=True)
        rstd = lax.rsqrt(jnp.mean(cen * cen, -1, keepdims=True) + epsilon)
        return cen * rstd, rstd

    def ln_tile(i, _):
        for u in range(4):
            rows = rows_at(i * 128 + u * 32, 32)
            xn, rstd = standard(xv[rows, :].astype(f32))
            xh[rows, :] = xn
            rs[rows, :] = jnp.broadcast_to(rstd, (32, 128))
        return 0

    lax.fori_loop(0, R // 128, ln_tile, 0)
    pl.semaphore_wait(barrier, len(everyone))

    gq, hq = c // 2, lax.rem(c, 2)
    ql = lane(128 * hq, 128)
    wl = lane(HD * d + 128 * hq, 128)
    uq = HD // C
    gown = rows_at(uq * c, uq)
    grow = rows_at(HD * d + uq * c, uq)
    pair = rows_at(2 - 2 * half, 2)
    pairl = lane(2 * U * (1 - half), 2 * U)

    def first(k):
        q = 2 * k + gq
        return [remote(pk.at[q, :, ql], w4.at[q, t, :, wl], p) for p in (z1, z2)]

    small = [remote(sm_ref, smr.at[me8], p) for p in zpeer + [sib] + xpeer]
    w1b = first(0)
    w3b = [remote(pk.at[0:2], w4.at[0:2, t, :, dl], sib)]

    def pass_on(cp, blk):
        arrived(cp)
        return remote(blk, blk, z1)

    def spread(blk, *cps):
        arrived(*cps)
        return [remote(blk, blk, p) for p in cpeer]

    qb, qc = gq, 2 + gq
    gl1, gl2 = lane(U * t1, U), lane(U * t2, U)
    w1b3 = pass_on(w1b[1], w4.at[qb, t2, :, wl])
    w2b = [spread(w4.at[qb, t1, :, wl], w1b[0])]
    w1c = first(1)
    w1g = [remote(glu.at[gown], gt.at[grow, tl], p) for p in (z1, z2)]
    w3c = [remote(pk.at[2:4], w4.at[2:4, t, :, dl], sib)]
    w3g = [remote(glu, gt.at[dr_, tl], sib)]

    def cot_send(s):
        return [remote(og_hbm.at[rows_at(R * p[2] + L * s, L)], ogv.at[pl.ds(L * s, L), tl], p) for p in zpeer]

    arrived(*small)
    zero = jnp.zeros((8, H - HD), f32)
    vec = jnp.zeros((8, H), f32)
    bias = jnp.zeros((8, H), f32)
    for dd in range(D):
        for tt in range(T):
            ext = jnp.concatenate([smr[dd * T + tt], zero], 1)
            place = tt * D + dd
            vec = vec + (pltpu.roll(ext, place * (NS // D), 1) if place else ext)
            bias = bias + (pltpu.roll(ext, place * (U // D), 1) if place else ext)
    both = jnp.concatenate([smr[t], smr[T + t]], 1)
    gain_r, skip_r, bias_r = both[5:6, :], both[6:7, :], bias[4:5, :]

    w2b.append(spread(w4.at[qb, pair, :, wl], w1b3))
    row8 = lax.broadcasted_iota(jnp.int32, (8, N), 0)
    full = lambda v, k, n: jnp.broadcast_to(v[k:k + 1, :n], (8, n))
    dr, di = full(vec, 0, N), full(vec, 1, N)
    cr, ci = full(vec, 2, N), full(vec, 3, N)
    pows = {1: (dr, di)}
    for k in range(2, 9):
        pows[k] = cmul(*pows[k - 1], dr, di)
    for n_, k in ((0, 1), (1, 2), (2, 4)):
        keep = row8 >= k
        cst[2 * n_] = jnp.where(keep, pows[k][0], 0.0)
        cst[2 * n_ + 1] = jnp.where(keep, pows[k][1], 0.0)
        keep = row8 < 8 - k
        cst[8 + 2 * n_] = jnp.where(keep, pows[k][0], 0.0)
        cst[8 + 2 * n_ + 1] = jnp.where(keep, -pows[k][1], 0.0)
    pr, pi, qr, qi = pows[1][0], pows[1][1], pows[8][0], -pows[8][1]
    for r in range(1, 8):
        pr = jnp.where(row8 == r, pows[r + 1][0], pr)
        pi = jnp.where(row8 == r, pows[r + 1][1], pi)
        qr = jnp.where(row8 == r, pows[8 - r][0], qr)
        qi = jnp.where(row8 == r, -pows[8 - r][1], qi)
    cst[6], cst[7], cst[14], cst[15] = pr, pi, qr, qi
    cst[16], cst[17] = pows[8]
    cst[18], cst[19] = cr, ci
    big = pows[8]
    n_ = 8
    while n_ < L:
        big = cmul(*big, *big)
        n_ *= 2
    cst[20], cst[21] = big

    def nrm_tile(i, _):
        rows = rows_at(i * 32, 32)
        nrm[rows, :] = (xh[rows, :] * gain_r).astype(bf16)
        return 0

    lax.fori_loop(0, R // 32, nrm_tile, 0)
    w1c3 = pass_on(w1c[1], w4.at[qc, t2, :, wl])
    w2c = [spread(w4.at[qc, t1, :, wl], w1c[0])]
    w1g3 = pass_on(w1g[1], gt.at[grow, gl2])
    w2g = [spread(gt.at[grow, gl1], w1g[0])]
    og = [cot_send(0)]

    def lne_tile(i, _):
        for u in range(4):
            rows = rows_at(i * 128 + u * 32, 32)
            nrme[rows, :] = (standard(xe[rows, :].astype(f32))[0] * gain_r).astype(bf16)
        return 0

    for cp in cxe:
        cp.wait()
    lax.fori_loop(0, R // 128, lne_tile, 0)
    w2c.append(spread(w4.at[qc, pair, :, wl], w1c3))
    w2g.append(spread(gt.at[grow, pairl], w1g3))
    og.append(cot_send(1))
    arrived(*w2b[0])
    w3b.append(remote(w4.at[0:2, t1, :, dl], w4.at[0:2, t1, :, dl], sib))
    og.append(cot_send(2))
    lax.fori_loop(R // 128, 2 * R // 128, lne_tile, 0)
    arrived(*w2b[1])
    w3b.append(remote(w4.at[0:2, pair, :, dl], w4.at[0:2, pair, :, dl], sib))

    def seq_rows(s):
        return rows_at(s * L, L)

    def drive(src, dst, lo, hi, off):
        def step(s, _):
            dst[seq_rows(s), :] = nt(src[seq_rows(s + off), :], w4[0:2].reshape(2 * N, H))
            return 0

        lax.fori_loop(lo, hi, step, 0)

    def scan(src, dst, groups, base, coef, reverse):
        e = 0 if reverse else 7

        def tile(i, carry):
            carry = list(carry)
            ii = L // 32 - 1 - i if reverse else i
            for g, (rb, l0) in enumerate(groups):
                lr_, li_ = lane(l0, 128), lane(N + l0, 128)
                con = [cst[base + k, :, lr_] for k in range(8)]
                e0 = cst[16, :, lr_]
                e1 = -cst[17, :, lr_] if reverse else cst[17, :, lr_]
                loc = []
                for u in range(4):
                    uu = 3 - u if reverse else u
                    rows = rows_at(rb + ii * 32 + uu * 8, 8)
                    ar, ai = src[rows, lr_], src[rows, li_]
                    if coef:
                        ar, ai = cmul(cst[18, :, lr_], cst[19, :, lr_], ar, ai)
                    else:
                        ai = -ai
                    for n_, k in ((0, 1), (1, 2), (2, 4)):
                        sh = 8 - k if reverse else k
                        br, bi = pltpu.roll(ar, sh, 0), pltpu.roll(ai, sh, 0)
                        mr, mi = con[2 * n_], con[2 * n_ + 1]
                        ar, ai = ar + mr * br - mi * bi, ai + mr * bi + mi * br
                    loc.append((rows, ar, ai))
                kr, ki = carry[2 * g], carry[2 * g + 1]
                for rows, ar, ai in loc:
                    dst[rows, lr_] = ar + con[6] * kr - con[7] * ki
                    dst[rows, li_] = ai + con[6] * ki + con[7] * kr
                    endr = jnp.broadcast_to(ar[e:e + 1, :], (8, 128))
                    endi = jnp.broadcast_to(ai[e:e + 1, :], (8, 128))
                    kr, ki = endr + e0 * kr - e1 * ki, endi + e0 * ki + e1 * kr
                carry[2 * g], carry[2 * g + 1] = kr, ki
            return tuple(carry)

        z = jnp.zeros((8, 128), f32)
        return lax.fori_loop(0, L // 32, tile, (z,) * (2 * len(groups)))

    def scan_batch(src, dst, slot):
        def lanes_step(j, _):
            fin = scan(src, dst, [(s * L, 128 * j) for s in range(S)], 0, True, False)
            for s in range(S):
                ce[slot, pl.ds(s, 1), lane(128 * j, 128)] = fin[2 * s][0:1, :]
                ce[slot, pl.ds(S + s, 1), lane(128 * j, 128)] = fin[2 * s + 1][0:1, :]
            return 0

        lax.fori_loop(0, N // 128, lanes_step, 0)
        return [remote(ce.at[slot], cer.at[slot, k], p) for k, p in enumerate(cpeer)]

    def incoming(slot, cps, n, forward):
        arrived(*cps)
        bg = (cst[20, 0:1, :], cst[21, 0:1, :])
        wt = (jnp.ones((1, N), f32), jnp.zeros((1, N), f32))
        accr = jnp.zeros((n, N), f32)
        acci = jnp.zeros((n, N), f32)
        for k in range(1, C):
            got = cer[slot, k - 1] if forward else cer[slot, C - 1 - k]
            has = (c >= k) if forward else (c + k < C)
            w = jnp.where(has, 1.0, 0.0)
            wi = wt[1] if forward else -wt[1]
            ur, ui = cmul(wt[0], wi, got[0:n, :], got[n:2 * n, :])
            accr = accr + w * ur
            acci = acci + w * ui
            wt = cmul(*wt, *bg)
        cin[slot, 0:n, :] = accr
        cin[slot, n:2 * n, :] = acci

    def entering(slot, k, lanes):
        return jnp.broadcast_to(cin[slot, pl.ds(k, 1), lanes], (8, 128))

    def fix_batch(ref, dst, slot, keep):
        def fix_lanes(j, _):
            lr_, li_ = lane(128 * j, 128), lane(N + 128 * j, 128)
            p0, p1 = cst[6, :, lr_], cst[7, :, lr_]
            e0, e1 = cst[16, :, lr_], cst[17, :, lr_]
            q0 = tuple(entering(slot, k * S + s, lr_) for s in range(S) for k in range(2))

            def tile(i, q):
                q = list(q)
                for s in range(S):
                    rr, ri = [], []
                    for h in range(2):
                        rows = rows_at(s * L + i * 16 + 8 * h, 8)
                        vr, vi = cmul(p0, p1, q[2 * s], q[2 * s + 1])
                        ar, ai = ref[rows, lr_] + vr, ref[rows, li_] + vi
                        if keep:
                            ref[rows, lr_] = ar
                            ref[rows, li_] = ai
                        rr.append(ar)
                        ri.append(ai)
                        q[2 * s], q[2 * s + 1] = cmul(q[2 * s], q[2 * s + 1], e0, e1)
                    rows = rows_at(s * L + i * 16, 16)
                    dst[rows, lr_] = jnp.concatenate(rr, 0).astype(bf16)
                    dst[rows, li_] = (-jnp.concatenate(ri, 0)).astype(bf16)
                return tuple(q)

            lax.fori_loop(0, L // 16, tile, q0)
            return 0

        lax.fori_loop(0, N // 128, fix_lanes, 0)

    def each_seq(f):
        def step(s, _):
            f(seq_rows(s))
            return 0

        lax.fori_loop(0, S, step, 0)

    def tiles(f, lo=0, hi=R // 32):
        def step(i, _):
            f(i, rows_at(i * 32, 32))
            return 0

        lax.fori_loop(lo, hi, step, 0)

    def valid_of(i, rank):
        s = i // (L // 32)
        pos = c * L + lax.rem(i, L // 32) * 32 + lax.broadcasted_iota(jnp.int32, (32, 1), 0)
        return jnp.where(pos < len_ref[S * rank + s], 1.0, 0.0)

    def logistic(v):
        return 0.5 + 0.5 * jnp.tanh(0.5 * v)

    arrived(*w3b)
    drive(nrm, raw, 0, S, 0)
    fce = [scan_batch(raw, st, 0)]
    arrived(*w2c[0])
    w3c.append(remote(w4.at[2:4, t1, :, dl], w4.at[2:4, t1, :, dl], sib))
    arrived(*w2c[1])
    w3c.append(remote(w4.at[2:4, pair, :, dl], w4.at[2:4, pair, :, dl], sib))
    arrived(*w2g[0], *w2g[1])
    blk = gt.at[dr_, lane(U * t1, U)]
    w3g.append(remote(blk, blk, sib))
    blk = gt.at[dr_, pairl]
    w3g.append(remote(blk, blk, sib))

    def extra_start(k):
        drive(nrme, rawe.at[k], 0, S, S * k)
        fce.append(scan_batch(rawe.at[k], rawe.at[k], 1 + k))

    extra_start(0)
    incoming(0, fce[0], S, True)
    fix_batch(st, sb, 0, True)
    arrived(*w3c)

    def ssm_own(rows):
        tmp[rows, :] = nn(sb[rows, :], w4[2:4].reshape(2 * N, H))

    each_seq(ssm_own)

    def gelu_tile(i, rows):
        pre = tmp[rows, :] + skip_r * nrm[rows, :].astype(f32)
        sq = pre * pre
        th = jnp.tanh(pre * (SQ2PI + (SQ2PI * 0.044715) * sq))
        hf = 0.5 + 0.5 * th
        act[rows, :] = (pre * hf).astype(bf16)
        gp[rows, :] = hf + 0.5 * pre * (1.0 - th * th) * (SQ2PI + (3 * 0.044715 * SQ2PI) * sq)

    tiles(gelu_tile)
    arrived(*w3g)

    def gate_own(rows):
        tmp[rows, :] = nn(act[rows, :], gt[...])

    each_seq(gate_own)

    def out_tile(i, rows):
        sg = logistic(tmp[rows, :] + bias_r)
        sig[rows, :] = sg
        o = valid_of(i, t) * (xv[rows, :].astype(f32) + act[rows, :].astype(f32) * sg)
        ob[rows, :] = o.astype(bf16)

    tiles(out_tile)
    outc = [remote(ob.at[:, lane(U * t1, U)], out_hbm.at[mine, :], z1)]
    locals_ = [local(ob.at[:, tl], out_hbm.at[mine, :])]

    def fold(v):
        return jnp.sum(v.reshape(4, 8, v.shape[-1]), 0)

    def seq_tiles(s, f):
        def step(i, acc):
            return acc + fold(f(i, rows_at(i * 32, 32)))

        return lax.fori_loop(s * (L // 32), (s + 1) * (L // 32), step, jnp.zeros((8, H), f32))

    co.wait()

    def gate_tile(i, rows):
        sg = sig[rows, :]
        direct = valid_of(i, t) * ogv[rows, :].astype(f32) * sg
        g = direct * act[rows, :].astype(f32) * (1.0 - sg)
        gl[rows, :] = g.astype(bf16)
        sig[rows, :] = direct
        return g

    def pre_tile(i, rows):
        p = (tmp[rows, :] + sig[rows, :]) * gp[rows, :]
        pg[rows, :] = p
        plb[rows, :] = p.astype(bf16)
        return p * nrm[rows, :].astype(f32)

    def back_one(s):
        arrived(*og[s])
        rows = pl.ds(s * L, L)
        accv[0] += seq_tiles(s, gate_tile)
        tmp[rows, :] = nt(gl[rows, :], gt[...])
        accv[1] += seq_tiles(s, pre_tile)
        mu[rows, :] = nt(plb[rows, :], w4[2:4].reshape(2 * N, H))
        fin = scan(mu, mu, [(s * L, 128 * j) for j in range(N // 128)], 8, False, True)
        for j in range(N // 128):
            ce[3 + s, 0:1, 128 * j:128 * j + 128] = fin[2 * j][0:1, :]
            ce[3 + s, 1:2, 128 * j:128 * j + 128] = fin[2 * j + 1][0:1, :]
        return [remote(ce.at[3 + s], cer.at[3 + s, k], p) for k, p in enumerate(cpeer)]

    row1 = lax.broadcasted_iota(jnp.int32, (8, 128), 0)

    def back_two(s, cps):
        incoming(3 + s, cps, 1, False)
        nj = N // 128
        q0 = tuple(entering(3 + s, k, lane(128 * j, 128)) for j in range(nj) for k in range(2))
        z = jnp.zeros((8, 128), f32)

        def tile(i, carry):
            q, m, acc = list(carry[:2 * nj]), list(carry[2 * nj:4 * nj]), list(carry[4 * nj:])
            ii = L // 16 - 1 - i
            for j in range(nj):
                lr_, li_ = lane(128 * j, 128), lane(N + 128 * j, 128)
                p0, p1 = cst[14, :, lr_], cst[15, :, lr_]
                e0, e1 = cst[16, :, lr_], -cst[17, :, lr_]
                cfr, cfi = cst[18, :, lr_], cst[19, :, lr_]
                rr, ri = [None, None], [None, None]
                for h in (1, 0):
                    rows = rows_at(s * L + ii * 16 + 8 * h, 8)
                    vr, vi = cmul(p0, p1, q[2 * j], q[2 * j + 1])
                    ar, ai = mu[rows, lr_] + vr, mu[rows, li_] + vi
                    q[2 * j], q[2 * j + 1] = cmul(q[2 * j], q[2 * j + 1], e0, e1)
                    nr = jnp.where(row1 == 7, m[2 * j], pltpu.roll(ar, 7, 0))
                    ni = jnp.where(row1 == 7, m[2 * j + 1], pltpu.roll(ai, 7, 0))
                    m[2 * j] = jnp.broadcast_to(ar[0:1, :], (8, 128))
                    m[2 * j + 1] = jnp.broadcast_to(ai[0:1, :], (8, 128))
                    xr, xi = st[rows, lr_], st[rows, li_]
                    ur, ui = raw[rows, lr_], raw[rows, li_]
                    acc[4 * j] = acc[4 * j] + nr * xr + ni * xi
                    acc[4 * j + 1] = acc[4 * j + 1] + ni * xr - nr * xi
                    acc[4 * j + 2] = acc[4 * j + 2] + ar * ur + ai * ui
                    acc[4 * j + 3] = acc[4 * j + 3] + ai * ur - ar * ui
                    rr[h] = cfr * ar + cfi * ai
                    ri[h] = cfr * ai - cfi * ar
                rows = rows_at(s * L + ii * 16, 16)
                nb[rows, lr_] = jnp.concatenate(rr, 0).astype(bf16)
                nb[rows, li_] = jnp.concatenate(ri, 0).astype(bf16)
            return tuple(q) + tuple(m) + tuple(acc)

        fin = lax.fori_loop(0, L // 16, tile, q0 + q0 + (z,) * (4 * nj))
        for j in range(nj):
            for k in range(4):
                vv[3 + k:4 + k, 128 * j:128 * j + 128] += jnp.sum(fin[4 * nj + 4 * j + k], 0, keepdims=True)
        rows = pl.ds(s * L, L)
        tmp[rows, :] = nn(nb[rows, :], w4[0:2].reshape(2 * N, H))

        def tok_tile(i, acc):
            for u in range(4):
                rows = rows_at(s * L + i * 128 + u * 32, 32)
                n = tmp[rows, :] + skip_r * pg[rows, :]
                xt = xh[rows, :]
                h = n * gain_r
                m1 = jnp.mean(h, -1, keepdims=True)
                m2 = jnp.mean(h * xt, -1, keepdims=True)
                tgb[rows, :] = ((h - m1 - xt * m2) * rs[rows, 0:1]).astype(bf16)
                acc = acc + fold(n * xt)
            return acc

        accv[2] += lax.fori_loop(0, L // 128, tok_tile, jnp.zeros((8, H), f32))
        there = rows_at(R * t + L * s, L)
        locals_.append(local(tgb.at[rows, tl], tg_hbm.at[there, :]))
        return [remote(tgb.at[rows, lane(U * p[2], U)], tg_hbm.at[there, :], p) for p in zpeer]

    b0 = back_one(0)
    b1 = back_one(1)
    tgc = back_two(0, b0)
    b2 = back_one(2)

    gcf, gbf = gc.reshape(2 * N, H), gb.reshape(2 * N, H)
    ol = lane(HD * (1 - d), HD)

    def gc_step(j, _):
        gcf[rows_at(j * 256, 256), :] = tn(sb[:, lane(j * 256, 256)], plb[...]).astype(bf16)
        return 0

    lax.fori_loop(0, 2 * N // 256, gc_step, 0)
    d1c = remote(gc.at[:, :, :, ol], r1c, sib)

    def gg_step(j, _):
        gg[rows_at(j * 256, 256), :] = tn(act[:, lane(j * 256, 256)], gl[...]).astype(bf16)
        return 0

    lax.fori_loop(0, H // 256, gg_step, 0)
    d1g = remote(gg.at[rows_at(HD * (1 - d), HD), :], r1g, sib)
    tgc += back_two(1, b1)

    def gb_step(j, _):
        gbf[rows_at(j * 256, 256), :] = tn(nb[:, lane(j * 256, 256)], nrm[...]).astype(bf16)
        return 0

    hs = NS // 2

    def rs_ctx(p):
        return p // 2, rows_at(hs * lax.rem(p, 2), hs)

    gr = lambda p: rows_at(uq * p, uq)

    def add2(a, b):
        return (a.astype(f32) + b.astype(f32)).astype(bf16)

    def total(first_, buf, n):
        acc = first_.astype(f32)
        for k in range(n):
            acc = acc + buf[k].astype(f32)
        return acc

    def two_states(g, d1, r1, s1, r2):
        arrived(d1)
        s1[...] = add2(g[:, :, :, dl], r1[...])
        return [remote(s1.at[rs_ctx(p[1])[0], :, rs_ctx(p[1])[1], :], r2.at[k], p) for k, p in enumerate(cpeer)]

    def three_states(d2, s1, r2, s2, r3):
        arrived(*d2)
        s2[...] = total(s1[rs_ctx(c)[0], :, rs_ctx(c)[1], :], r2, C - 1).astype(bf16)
        return [remote(s2.at[t1], r3.at[0], z1), remote(s2.at[t3], r3.at[1], z1)]

    def four_states(d3, s2, r3, s3, r4):
        arrived(*d3)
        s3[0] = add2(s2[t], r3[0])
        s3[1] = add2(s2[t2], r3[1])
        return remote(s3.at[1], r4, z2)

    def five(d4, s3, r4, out):
        arrived(d4)
        out[c] = add2(s3[0], r4[...])
        return [remote(out.at[c], out.at[c], p) for p in cpeer]

    def extra_fix(k):
        incoming(1 + k, fce[1 + k], S, True)
        fix_batch(rawe.at[k], sbe, 1 + k, False)

    def extra_act(k):
        def ssm(rows):
            tmpe[rows, :] = nn(sbe[rows, :], w4[2:4].reshape(2 * N, H))

        each_seq(ssm)

        def gelu(i, rows):
            pre = tmpe[rows, :] + skip_r * nrme[rows_at(R * k + i * 32, 32), :].astype(f32)
            acte[rows, :] = (pre * (0.5 + 0.5 * jnp.tanh(pre * (SQ2PI + (SQ2PI * 0.044715) * (pre * pre))))).astype(bf16)

        tiles(gelu)

    def extra_out(k):
        rank = erank[k]

        def gate(rows):
            tmpe[rows, 0:U] = nn(acte[rows, :], gt[:, tl])

        each_seq(gate)
        bias_u = jnp.sum(jnp.where(lax.broadcasted_iota(jnp.int32, (T, U), 0) == t, bias_t, 0.0), 0, keepdims=True)

        def fin(i, rows):
            here = rows_at(R * k + i * 32, 32)
            sg = logistic(tmpe[rows, 0:U] + bias_u)
            o = valid_of(i, rank) * (xe[here, tl].astype(f32) + acte[rows, tl].astype(f32) * sg)
            obe[here, :] = o.astype(bf16)

        tiles(fin)
        locals_.append(local(obe.at[pl.ds(R * k, R)], out_hbm.at[rows_at(R * rank, R), :]))

    bias_t = jnp.concatenate([bias_r[:, U * k:U * k + U] for k in range(T)], 0)
    d2c = two_states(gc, d1c, r1c, s1c, r2c)
    arrived(d1g)
    s1g[...] = add2(gg[dr_, :], r1g[...])
    d2g = [remote(s1g.at[gr(p[1]), :], r2g.at[k], p) for k, p in enumerate(cpeer)]
    tgc += back_two(2, b2)
    lax.fori_loop(0, 2 * N // 256, gb_step, 0)
    d1b = remote(gb.at[:, :, :, ol], r1b, sib)
    for k, row in ((2, 0), (1, 1), (0, 2)):
        vv[row:row + 1, :] = jnp.sum(accv[k], 0, keepdims=True)
    d1v = remote(vv, vr1, sib)
    extra_fix(0)
    d2b = two_states(gb, d1b, r1b, s1b, r2b)
    arrived(d1v)
    vr2[0] = vv[...] + vr1[...]
    d2v = [remote(vr2.at[0], vr2.at[k + 1], p) for k, p in enumerate(cpeer)]
    extra_start(1)
    extra_act(0)
    extra_out(0)
    d3c = three_states(d2c, s1c, r2c, s2c, r3c)
    arrived(*d2g)
    s2g[...] = total(s1g[gr(c), :], r2g, C - 1).astype(bf16)
    d3g = [remote(s2g.at[:, gl1], r3g.at[0], z1), remote(s2g.at[:, lane(U * t3, U)], r3g.at[1], z1)]
    d3b = three_states(d2b, s1b, r2b, s2b, r3b)
    arrived(*d2v)
    vr3[0] = vr2[0] + vr2[1] + vr2[2] + vr2[3]
    d3v = [remote(vr3.at[0], vr3.at[k + 1], p) for k, p in enumerate(zpeer)]
    extra_fix(1)
    d4c = four_states(d3c, s2c, r3c, s3c, r4c)
    arrived(*d3g)
    s3g[0] = add2(s2g[:, tl], r3g[0])
    s3g[1] = add2(s2g[:, gl2], r3g[1])
    d4g = remote(s3g.at[1], r4g, z2)
    d4b = four_states(d3b, s2b, r3b, s3b, r4b)
    extra_act(1)
    d5 = five(d4c, s3c, r4c, fc_ref) + five(d4g, s3g, r4g, fg_ref) + five(d4b, s3b, r4b, fb_ref)
    extra_out(1)

    arrived(*d3v)
    vf[...] = vr3[0] + vr3[1] + vr3[2] + vr3[3]
    place = t * D + d
    back = lambda n: lax.rem(H - n * place, H)
    st8 = pltpu.roll(vf[...], back(NS // D), 1)[:, 0:NS // D]
    ub8 = pltpu.roll(vf[...], back(U // D), 1)[:, 0:U // D]
    lr1, li1, step1 = lre_in[...], lim_in[...], jnp.exp(stp_in[...])
    dr1, di1, cr1, ci1 = (sm_ref[k:k + 1, 0:NS // D] for k in range(4))
    gdr, gdi, gcr, gci = (st8[k:k + 1] for k in range(3, 7))
    inv = 1.0 / (lr1 * lr1 + li1 * li1)
    hdr = gdr + (gcr * lr1 - gci * li1) * inv
    hdi = gdi + (gcr * li1 + gci * lr1) * inv
    pull = 2.0 * (gcr * cr1 + gci * ci1)
    e1, e2 = dr1 - 1.0, hdr * dr1 + hdi * di1
    e3 = hdi * dr1 - hdr * di1
    fv_ref[...] = jnp.zeros_like(fv_ref)
    fv_ref[0:1, :] = vf[0:1, dl]
    fv_ref[1:2, :] = vf[1:2, dl]
    fv_ref[2:3, 0:U // D] = ub8[2:3]
    fv_ref[3:4, 0:NS // D] = (gcr * e1 + gci * di1 - pull * lr1) * inv + step1 * e2
    fv_ref[4:5, 0:NS // D] = (gcr * di1 - gci * e1 - pull * li1) * inv + step1 * e3
    fv_ref[5:6, 0:NS // D] = step1 * (lr1 * e2 + li1 * e3)
    arrived(*d5, *tgc, *outc)
    for cp in locals_:
        cp.wait()
    for cp in started:
        cp.wait_send()
    assert count[0] == NSEM and nlocal[0] == NLOCAL, (count[0], nlocal[0])


NSEM, NLOCAL = 117, 21


def fused_call(geo, lens, x2, og2, *params):
    D, C, T, S, L, H, N, U = geo
    R, NS, HD = S * L, N // T, H // D
    f32, bf16 = jnp.float32, jnp.bfloat16
    uq, hs = HD // C, NS // 2
    V = pltpu.VMEM
    any_, vm = pl.BlockSpec(memory_space=pl.ANY), pl.BlockSpec(memory_space=pltpu.VMEM)
    scratch = [
        V((R, H), bf16), V((R, H), bf16), V((R, H), f32), V((R, 128), f32),
        V((R, 2 * N), f32), V((R, 2 * N), f32), V((R, 2 * N), bf16),
        V((R, H), f32), V((R, H), bf16), V((R, H), f32), V((R, H), f32),
        V((R, H), bf16), V((R, H), bf16), V((R, H), bf16), V((R, H), f32), V((R, H), bf16),
        V((R, 2 * N), f32), V((R, 2 * N), bf16), V((R, H), bf16),
        V((2 * R, H), bf16), V((2 * R, H), bf16), V((2, R, 2 * N), f32), V((R, 2 * N), bf16),
        V((R, H), bf16), V((R, H), f32), V((2 * R, U), bf16),
        V((4, T, NS, H), bf16), V((H, H), bf16), V((D * T, 8, HD), f32),
        V((22, 8, N), f32), V((6, 8, N), f32), V((6, C - 1, 8, N), f32), V((6, 8, N), f32),
        V((2, T, NS, H), bf16), V((H, H), bf16), V((2, T, NS, H), bf16),
        V((2, T, NS, HD), bf16), V((HD, H), bf16), V((2, T, NS, HD), bf16),
        V((2, T, NS, HD), bf16), V((HD, H), bf16), V((2, T, NS, HD), bf16),
        V((C - 1, T, hs, HD), bf16), V((C - 1, uq, H), bf16), V((C - 1, T, hs, HD), bf16),
        V((T, hs, HD), bf16), V((uq, H), bf16), V((T, hs, HD), bf16),
        V((2, hs, HD), bf16), V((2, uq, U), bf16), V((2, hs, HD), bf16),
        V((2, hs, HD), bf16), V((2, uq, U), bf16), V((2, hs, HD), bf16),
        V((hs, HD), bf16), V((uq, U), bf16), V((hs, HD), bf16),
        V((8, H), f32), V((8, H), f32), V((C, 8, H), f32), V((T, 8, H), f32), V((8, H), f32), V((3, 8, H), f32),
        V((4, NS, HD), bf16), V((8, HD), f32), V((HD, U), bf16), V((1, HD), f32), V((1, HD), f32),
        V((1, NS // D), f32), V((1, NS // D), f32), V((1, NS // D), f32), V((1, U // D), f32),
        pltpu.SemaphoreType.DMA((NLOCAL,)), pltpu.SemaphoreType.DMA((NSEM,)), pltpu.SemaphoreType.DMA((NSEM,)),
    ]
    rows = x2.shape[0]
    return pl.pallas_call(
        functools.partial(fused_body, geo),
        out_shape=(
            jax.ShapeDtypeStruct((rows, U), bf16), jax.ShapeDtypeStruct((rows, U), bf16),
            jax.ShapeDtypeStruct((C, hs, HD), bf16), jax.ShapeDtypeStruct((C, uq, U), bf16),
            jax.ShapeDtypeStruct((C, hs, HD), bf16), jax.ShapeDtypeStruct((8, HD), f32)),
        in_specs=[pl.BlockSpec(memory_space=pltpu.SMEM), any_, any_] + [any_] * 11,
        out_specs=(any_, any_, vm, vm, vm, vm),
        scratch_shapes=scratch,
        compiler_params=pltpu.CompilerParams(
            collective_id=0, has_side_effects=True, vmem_limit_bytes=60 * 1024 * 1024),
        name="block",
    )(lens, x2, og2, *params)


def finish_body(geo, len_ref, out_in, tok_in, og_in, fc_in, fg_in, fb_in, fv, out, ingrad, gain_g, skip_g,
                lre_g, lim_g, step_g, bre_g, bim_g, cre_g, cim_g, glu_g, bias_g,
                tokv, ogv, outv, fc, fg, fb, bre, bim, cre, cim, glu, res, sem, gsem, osem):
    D, C, T, S, L, H, N, U = geo
    NS = N // T
    f32 = jnp.float32

    def move(src, dst, s):
        cp = pltpu.make_async_copy(src, dst, s)
        cp.start()
        return cp

    part = [pl.ds(S * k, S) for k in range(T)]
    loads = [(move(tok_in.at[part[k]], tokv.at[part[k]], sem.at[0, k]),
              move(og_in.at[part[k]], ogv.at[part[k]], sem.at[1, k])) for k in range(T)]
    params = [move(a, b, gsem.at[k]) for k, (a, b) in enumerate(((fc_in, fc), (fg_in, fg), (fb_in, fb)))]
    passes = [move(out_in.at[part[k]], outv.at[part[k]], sem.at[2, k]) for k in range(T)]
    base = lax.axis_index("ctx") * L
    stores = []
    for k in range(T):
        for cp in loads[k]:
            cp.wait()

        def tile(i, _):
            s = S * k + i // (L // 32)
            r0 = lax.rem(i, L // 32) * 32
            rows = pl.ds(pl.multiple_of(r0, 32), 32)
            pos = base + r0 + lax.broadcasted_iota(jnp.int32, (32, 1), 0)
            keep = jnp.where(pos < len_ref[s], 1.0, 0.0)
            res[s, rows, :] = keep * ogv[s, rows, :].astype(f32) + tokv[s, rows, :].astype(f32)
            return 0

        lax.fori_loop(0, S * L // 32, tile, 0)
        stores.append(move(res.at[part[k]], ingrad.at[part[k]], osem.at[k]))
    for cp in params:
        cp.wait()
    h = C // 2
    for k in range(C):
        rows = pl.ds((k % h) * (NS // h), NS // h)
        (bre if k < h else bim)[rows, :] = fb[k].astype(f32)
        (cre if k < h else cim)[rows, :] = fc[k].astype(f32)
    glu[...] = fg[...].reshape(glu.shape).astype(f32)
    pairs = ((bre, bre_g), (bim, bim_g), (cre, cre_g), (cim, cim_g), (glu, glu_g))
    stores += [move(a, b, osem.at[2 * T + k]) for k, (a, b) in enumerate(pairs)]
    for k in range(T):
        passes[k].wait()
        stores.append(move(outv.at[part[k]], out.at[part[k]], osem.at[T + k]))
    gain_g[...] = fv[0:1, :]
    skip_g[...] = fv[1:2, :]
    bias_g[...] = fv[2:3, 0:U // D]
    lre_g[...] = fv[3:4, 0:NS // D]
    lim_g[...] = fv[4:5, 0:NS // D]
    step_g[...] = fv[5:6, 0:NS // D]
    for cp in stores:
        cp.wait()


def finish_call(geo, lens, out, tok, og, fc, fg, fb, fv):
    D, C, T, S, L, H, N, U = geo
    NS, HD = N // T, H // D
    f32, bf16 = jnp.float32, jnp.bfloat16
    seqs = S * T
    any_, vm = pl.BlockSpec(memory_space=pl.ANY), pl.BlockSpec(memory_space=pltpu.VMEM)
    V = pltpu.VMEM
    small = [(1, HD), (1, HD)] + [(1, NS // D)] * 3 + [(NS, HD)] * 4 + [(HD, U), (1, U // D)]
    return pl.pallas_call(
        functools.partial(finish_body, geo),
        out_shape=[jax.ShapeDtypeStruct((seqs, L, U), bf16), jax.ShapeDtypeStruct((seqs, L, U), f32)]
        + [jax.ShapeDtypeStruct(s, f32) for s in small],
        in_specs=[pl.BlockSpec(memory_space=pltpu.SMEM)] + [any_] * 6 + [vm],
        out_specs=[any_, any_] + [vm] * 5 + [any_] * 5 + [vm],
        scratch_shapes=[V((seqs, L, U), bf16)] * 3 + [V(a.shape, a.dtype) for a in (fc, fg, fb)]
        + [V((NS, HD), f32)] * 4 + [V((HD, U), f32), V((seqs, L, U), f32)]
        + [pltpu.SemaphoreType.DMA((3, T)), pltpu.SemaphoreType.DMA((3,)), pltpu.SemaphoreType.DMA((2 * T + 5,))],
        compiler_params=pltpu.CompilerParams(vmem_limit_bytes=60 * 1024 * 1024),
        name="finish",
    )(lens, out.reshape(seqs, L, U), tok.reshape(seqs, L, U), og, fc, fg, fb, fv)


def coefficients(lam_re, lam_im, step_log):
    step = jnp.exp(step_log)
    magnitude = jnp.exp(lam_re * step)
    decay_re = magnitude * jnp.cos(lam_im * step)
    decay_im = magnitude * jnp.sin(lam_im * step)
    inv = 1.0 / (lam_re * lam_re + lam_im * lam_im)
    coef_re = ((decay_re - 1.0) * lam_re + decay_im * lam_im) * inv
    coef_im = (decay_im * lam_re - (decay_re - 1.0) * lam_im) * inv
    return decay_re, decay_im, coef_re, coef_im


def token_split(sizes, inputs, lengths, norm_gain, skip_weight, lambda_re, lambda_im, log_step,
                b_re, b_im, c_re, c_im, glu_weight, glu_bias, out_grad):
    D, C, T = sizes
    seqs, L, H = inputs.shape
    NS, HD = b_re.shape
    U = glu_weight.shape[1]
    geo = (D, C, T, seqs // T, L, H, NS * T, U)
    row = lambda v: v.reshape(1, -1)
    out, tok, fc, fg, fb, fv = fused_call(
        geo, lengths, inputs.reshape(seqs * L, H), out_grad.reshape(seqs * L, U),
        b_re, b_im, c_re.T, c_im.T, glu_weight,
        *(row(v) for v in (norm_gain, skip_weight, lambda_re, lambda_im, log_step, glu_bias)))
    res = finish_call(geo, lengths, out, tok, out_grad, fc, fg, fb, fv)
    out, ingrad, gain_g, skip_g, lre_g, lim_g, step_g, bre_g, bim_g, cre_g, cim_g, glu_g, bias_g = res
    flat = lambda v: v.reshape(-1)
    return (out, ingrad, flat(gain_g), flat(skip_g), flat(lre_g), flat(lim_g), flat(step_g),
            bre_g, bim_g, cre_g.T, cim_g.T, glu_g, flat(bias_g))


def solution(mesh):
    in_specs = (
        P("dp", "ctx", None),
        P("dp"),
        P("dp"),
        P("dp"),
        P(("tp", "dp")),
        P(("tp", "dp")),
        P(("tp", "dp")),
        P("tp", "dp"),
        P("tp", "dp"),
        P("dp", "tp"),
        P("dp", "tp"),
        P("dp", "tp"),
        P(("tp", "dp")),
        P("dp", "ctx", "tp"),
    )
    out_specs = (
        P("dp", "ctx", "tp"),
        P("dp", "ctx", "tp"),
        P("dp"),
        P("dp"),
        P(("tp", "dp")),
        P(("tp", "dp")),
        P(("tp", "dp")),
        P("tp", "dp"),
        P("tp", "dp"),
        P("dp", "tp"),
        P("dp", "tp"),
        P("dp", "tp"),
        P(("tp", "dp")),
    )
    sizes = tuple(mesh.shape[name] for name in ("dp", "ctx", "tp"))

    def block(*args):
        seqs, _, feat = args[0].shape
        units = args[11].shape[1]
        if sizes == (2, 4, 4) and seqs % sizes[2] == 0 and units % 128 == 0:
            return token_split(sizes, *args)
        return on_device(*args)

    return jax.shard_map(
        block, mesh=mesh, in_specs=in_specs, out_specs=out_specs, check_vma=False
    )
```

```python
import functools

import jax
import jax.numpy as jnp
from jax import lax
from jax.experimental import pallas as pl
from jax.experimental.pallas import tpu as pltpu
from jax.sharding import PartitionSpec as P

epsilon = 1e-05


def carried_in(value, axis, combine, identity, reverse):
    count, index = (lax.axis_size(axis), lax.axis_index(axis))
    everything = jax.tree.map(lambda part: lax.all_gather(part, axis), value)
    start = jax.tree.map(
        lambda part, zero: jnp.broadcast_to(jnp.asarray(zero, part.dtype), part.shape),
        value,
        identity,
    )

    def lap(k, before):
        at = count - 1 - k if reverse else k
        reached = at > index if reverse else at < index
        new = combine(before, jax.tree.map(lambda part: part[at], everything))
        return jax.tree.map(lambda a, b: jnp.where(reached, a, b), new, before)

    return lax.fori_loop(0, count, lap, start)


def contract(left, right, left_dim, right_dim):
    return lax.dot_general(
        left, right, (((left_dim,), (right_dim,)), ((), ())), preferred_element_type=jnp.float32
    )


def combine(earlier, later):
    e_re, e_im, eb_re, eb_im = earlier
    l_re, l_im, lb_re, lb_im = later
    return (
        e_re * l_re - e_im * l_im,
        e_re * l_im + e_im * l_re,
        l_re * eb_re - l_im * eb_im + lb_re,
        l_re * eb_im + l_im * eb_re + lb_im,
    )


def discretize(lam_re, lam_im, step_log, mat_re, mat_im):
    step = jnp.exp(step_log)
    magnitude = jnp.exp(lam_re * step)
    decay_re = magnitude * jnp.cos(lam_im * step)
    decay_im = magnitude * jnp.sin(lam_im * step)
    denom = lam_re * lam_re + lam_im * lam_im
    coef_re = ((decay_re - 1.0) * lam_re + decay_im * lam_im) / denom
    coef_im = (decay_im * lam_re - (decay_re - 1.0) * lam_im) / denom
    bar_re = coef_re[:, None] * mat_re - coef_im[:, None] * mat_im
    bar_im = coef_re[:, None] * mat_im + coef_im[:, None] * mat_re
    return (decay_re, decay_im, jnp.concatenate([bar_re, bar_im], 0))


def normalize(tokens, gain):
    mean_val = jnp.mean(tokens, -1, keepdims=True)
    centered = tokens - mean_val
    var_val = jnp.mean(centered * centered, -1, keepdims=True)
    return centered * lax.rsqrt(var_val + epsilon) * gain


def powers(lam_re, lam_im, step_log, count):
    step = jnp.exp(step_log)
    exponent = (jnp.arange(count, dtype=jnp.float32) + 1.0)[:, None]
    magnitude = jnp.exp(exponent * lam_re * step)
    return (
        magnitude * jnp.cos(exponent * lam_im * step),
        magnitude * jnp.sin(exponent * lam_im * step),
    )


def on_device(
    inputs,
    lengths,
    norm_gain,
    skip_weight,
    lambda_re,
    lambda_im,
    log_step,
    b_re,
    b_im,
    c_re,
    c_im,
    glu_weight,
    glu_bias,
    out_grad,
):
    full_bre, full_bim, full_cre, full_cim, full_glu = (
        lax.all_gather(b_re, "dp", axis=1, tiled=True),
        lax.all_gather(b_im, "dp", axis=1, tiled=True),
        lax.all_gather(c_re, "dp", axis=0, tiled=True),
        lax.all_gather(c_im, "dp", axis=0, tiled=True),
        lax.all_gather(glu_weight, "dp", axis=0, tiled=True),
    )
    gain, skip_full, lam_re, lam_im, step_log, bias_vec = (
        lax.all_gather(norm_gain, "dp", axis=0, tiled=True),
        lax.all_gather(skip_weight, "dp", axis=0, tiled=True),
        lax.all_gather(lambda_re, "dp", axis=0, tiled=True),
        lax.all_gather(lambda_im, "dp", axis=0, tiled=True),
        lax.all_gather(log_step, "dp", axis=0, tiled=True),
        lax.all_gather(glu_bias, "dp", axis=0, tiled=True),
    )
    seq_count, blk_len, feat_dim = inputs.shape
    row_count = seq_count * blk_len
    state_count = full_bre.shape[0]
    unit_count = full_glu.shape[1]
    tp_rank = lax.axis_index("tp")
    unit_start = tp_rank * unit_count
    positions = lax.axis_index("ctx") * blk_len + jnp.arange(blk_len, dtype=jnp.int32)
    valid_mask = (positions[None, :] < lengths[:, None]).astype(jnp.float32).reshape(row_count, 1)
    tokens = inputs.astype(jnp.float32).reshape(row_count, feat_dim)
    tokens_mine = lax.dynamic_slice_in_dim(tokens, unit_start, unit_count, 1)
    cotangent = out_grad.astype(jnp.float32).reshape(row_count, unit_count)
    normed_f, norm_pull = jax.vjp(normalize, tokens, gain)
    normed_b = normed_f.astype(jnp.bfloat16)
    normed_r = normed_b.astype(jnp.float32)
    (decay_re, decay_im, bar_full), disc_pull = jax.vjp(
        discretize,
        lam_re,
        lam_im,
        step_log,
        full_bre.astype(jnp.float32),
        full_bim.astype(jnp.float32),
    )
    bar_b = bar_full.astype(jnp.bfloat16)
    drive = contract(normed_b, bar_b, 1, 1).reshape(seq_count, blk_len, 2 * state_count)
    full_re = jnp.broadcast_to(decay_re, (seq_count, blk_len, state_count))
    full_im = jnp.broadcast_to(decay_im, (seq_count, blk_len, state_count))
    local_states = lax.associative_scan(
        combine, (full_re, full_im, drive[..., :state_count], drive[..., state_count:]), axis=1
    )
    pow_re, pow_im = powers(lam_re, lam_im, step_log, blk_len)
    identity = (
        jnp.ones((1, state_count), jnp.float32),
        jnp.zeros((1, state_count), jnp.float32),
        jnp.zeros((seq_count, state_count), jnp.float32),
        jnp.zeros((seq_count, state_count), jnp.float32),
    )
    incoming = carried_in(
        (pow_re[-1:], pow_im[-1:], local_states[2][:, -1], local_states[3][:, -1]),
        "ctx",
        combine,
        identity,
        False,
    )
    in_re = incoming[2][:, None, :]
    in_im = incoming[3][:, None, :]
    state_re = local_states[2] + pow_re * in_re - pow_im * in_im
    state_im = local_states[3] + pow_re * in_im + pow_im * in_re
    states_b = (
        jnp.concatenate([state_re, state_im], -1)
        .reshape(row_count, 2 * state_count)
        .astype(jnp.bfloat16)
    )
    c_stack = jnp.concatenate([full_cre, -full_cim], 1)
    ssm_part = contract(states_b, c_stack, 1, 1)
    ssm_full = lax.psum(ssm_part.astype(jnp.bfloat16), "tp").astype(jnp.float32)
    pre_full = ssm_full + skip_full * normed_r
    gelu_full, gelu_pull = jax.vjp(jax.nn.gelu, pre_full)
    gelu_b = gelu_full.astype(jnp.bfloat16)
    gelu_part = lax.dynamic_slice_in_dim(gelu_b, unit_start, unit_count, 1)
    gelu_mine = gelu_part.astype(jnp.float32)
    gate = contract(gelu_b, full_glu, 1, 0) + bias_vec
    gate_sig = jax.nn.sigmoid(gate)
    output = (
        (valid_mask * (tokens_mine + gelu_mine * gate_sig))
        .astype(jnp.bfloat16)
        .reshape(seq_count, blk_len, unit_count)
    )
    branch_grad = valid_mask * cotangent
    gate_grad = branch_grad * gelu_mine * gate_sig * (1.0 - gate_sig)
    bias_grad = jnp.sum(gate_grad, 0)
    gate_b = gate_grad.astype(jnp.bfloat16)
    glu_grad = contract(gelu_b, gate_b, 0, 0)
    gelu_grad = contract(gate_b, full_glu, 1, 1)
    own_cols = (
        lax.dynamic_slice_in_dim(gelu_grad, unit_start, unit_count, 1) + branch_grad * gate_sig
    )
    gelu_grad = lax.dynamic_update_slice_in_dim(gelu_grad, own_cols, unit_start, 1)
    gelu_back = lax.psum(gelu_grad, "tp")
    (pre_grad,) = gelu_pull(gelu_back)
    skip_grad = jnp.sum(pre_grad * normed_r, 0)
    pre_b = pre_grad.astype(jnp.bfloat16)
    state_grad = contract(pre_b, c_stack, 1, 0).reshape(seq_count, blk_len, 2 * state_count)
    c_grad = contract(pre_b, states_b, 0, 0)
    back_local = lax.associative_scan(
        combine,
        (full_re, -full_im, state_grad[..., :state_count], state_grad[..., state_count:]),
        axis=1,
        reverse=True,
    )
    later_adj = carried_in(
        (pow_re[-1:], -pow_im[-1:], back_local[2][:, 0], back_local[3][:, 0]),
        "ctx",
        combine,
        identity,
        True,
    )
    rev_re = pow_re[::-1]
    rev_im = -pow_im[::-1]
    next_re = later_adj[2][:, None, :]
    next_im = later_adj[3][:, None, :]
    adj_re = back_local[2] + rev_re * next_re - rev_im * next_im
    adj_im = back_local[3] + rev_re * next_im + rev_im * next_re
    prev_re = jnp.concatenate([in_re, state_re[:, :-1]], 1)
    prev_im = jnp.concatenate([in_im, state_im[:, :-1]], 1)
    decay_grad_re = jnp.sum(adj_re * prev_re + adj_im * prev_im, (0, 1))
    decay_grad_im = jnp.sum(adj_im * prev_re - adj_re * prev_im, (0, 1))
    adj_b = (
        jnp.concatenate([adj_re, adj_im], -1)
        .reshape(row_count, 2 * state_count)
        .astype(jnp.bfloat16)
    )
    bar_grad = contract(adj_b, normed_b, 0, 0)
    normed_part = contract(adj_b, bar_b, 1, 0)
    normed_sum = lax.psum(normed_part.astype(jnp.bfloat16), "tp").astype(jnp.float32)
    normed_grad = normed_sum + skip_full * pre_grad
    token_grad, gain_grad = norm_pull(normed_grad)
    input_grad = (
        valid_mask * cotangent + lax.dynamic_slice_in_dim(token_grad, unit_start, unit_count, 1)
    ).reshape(seq_count, blk_len, unit_count)
    grad_cre = c_grad[:, :state_count]
    grad_cim = -c_grad[:, state_count:]
    lre_grad, lim_grad, step_grad, bre_grad, bim_grad = disc_pull(
        (decay_grad_re, decay_grad_im, bar_grad)
    )
    shards = (
        lax.psum_scatter(
            gain_grad.astype(jnp.bfloat16), "dp", scatter_dimension=0, tiled=True
        ).astype(jnp.float32),
        lax.psum_scatter(
            skip_grad.astype(jnp.bfloat16), "dp", scatter_dimension=0, tiled=True
        ).astype(jnp.float32),
        lax.psum_scatter(
            lre_grad.astype(jnp.bfloat16), "dp", scatter_dimension=0, tiled=True
        ).astype(jnp.float32),
        lax.psum_scatter(
            lim_grad.astype(jnp.bfloat16), "dp", scatter_dimension=0, tiled=True
        ).astype(jnp.float32),
        lax.psum_scatter(
            step_grad.astype(jnp.bfloat16), "dp", scatter_dimension=0, tiled=True
        ).astype(jnp.float32),
        lax.psum_scatter(
            bias_grad.astype(jnp.bfloat16), "dp", scatter_dimension=0, tiled=True
        ).astype(jnp.float32),
        lax.psum_scatter(
            bre_grad.astype(jnp.bfloat16), "dp", scatter_dimension=1, tiled=True
        ).astype(jnp.float32),
        lax.psum_scatter(
            bim_grad.astype(jnp.bfloat16), "dp", scatter_dimension=1, tiled=True
        ).astype(jnp.float32),
        lax.psum_scatter(
            grad_cre.astype(jnp.bfloat16), "dp", scatter_dimension=0, tiled=True
        ).astype(jnp.float32),
        lax.psum_scatter(
            grad_cim.astype(jnp.bfloat16), "dp", scatter_dimension=0, tiled=True
        ).astype(jnp.float32),
        lax.psum_scatter(
            glu_grad.astype(jnp.bfloat16), "dp", scatter_dimension=0, tiled=True
        ).astype(jnp.float32),
    )
    summed = (
        lax.psum(shards[0].astype(jnp.bfloat16), "ctx").astype(jnp.float32),
        lax.psum(shards[1].astype(jnp.bfloat16), "ctx").astype(jnp.float32),
        lax.psum(shards[2].astype(jnp.bfloat16), "ctx").astype(jnp.float32),
        lax.psum(shards[3].astype(jnp.bfloat16), "ctx").astype(jnp.float32),
        lax.psum(shards[4].astype(jnp.bfloat16), "ctx").astype(jnp.float32),
        lax.psum(shards[5].astype(jnp.bfloat16), "ctx").astype(jnp.float32),
        lax.psum(shards[6].astype(jnp.bfloat16), "ctx").astype(jnp.float32),
        lax.psum(shards[7].astype(jnp.bfloat16), "ctx").astype(jnp.float32),
        lax.psum(shards[8].astype(jnp.bfloat16), "ctx").astype(jnp.float32),
        lax.psum(shards[9].astype(jnp.bfloat16), "ctx").astype(jnp.float32),
        lax.psum(shards[10].astype(jnp.bfloat16), "ctx").astype(jnp.float32),
    )
    return (
        output,
        input_grad,
        summed[0],
        summed[1],
        summed[2],
        summed[3],
        summed[4],
        summed[6],
        summed[7],
        summed[8],
        summed[9],
        summed[10],
        summed[5],
    )


MESH = pl.DeviceIdType.MESH
SQ2PI = 0.7978845608028654


def nt(a, b):
    return lax.dot_general(a, b, (((1,), (1,)), ((), ())), preferred_element_type=jnp.float32)


def nn(a, b):
    return lax.dot_general(a, b, (((1,), (0,)), ((), ())), preferred_element_type=jnp.float32)


def tn(a, b):
    return lax.dot_general(a, b, (((0,), (0,)), ((), ())), preferred_element_type=jnp.float32)


def cmul(ar, ai, br, bi):
    return ar * br - ai * bi, ar * bi + ai * br


def lane(start, size):
    return pl.ds(pl.multiple_of(start, 128), size)


def fused_body(geo, *refs):
    D, C, T, S, L, H, N, U = geo
    R = S * L
    NS = N // T
    HD = H // D
    f32, bf16 = jnp.float32, jnp.bfloat16
    (len_ref, x_hbm, og_hbm, bre, bim, cre, cim, glu_hbm, gain_h, skip_h, lre_h, lim_h, stp_h, bias_h,
     out_hbm, tg_hbm, fc_ref, fg_ref, fb_ref, fv_ref) = refs[:20]
    (xv, nrm, xh, rs, raw, st, sb, tmp, act, gp, sig, ogv, ob, gl, pg, plb, mu, nb, tgb,
     xe, nrme, rawe, sbe, acte, tmpe, obe,
     w4, gt, smr, cst, ce, cer, cin, gc, gg, gb, r1c, r1g, r1b, s1c, s1g, s1b, r2c, r2g, r2b,
     s2c, s2g, s2b, r3c, r3g, r3b, s3c, s3g, r4c, r4g,
     vv, vr1, vr2, vr3, vf, accv, pk, sm_ref, glu, gain_in, skip_in, lre_in, lim_in, stp_in, bias_in,
     lsem, ssem, rsem) = refs[20:]
    d, c, t = lax.axis_index("dp"), lax.axis_index("ctx"), lax.axis_index("tp")
    half = t // 2
    t1 = t + 1 - 2 * lax.rem(t, 2)
    t2 = t + 2 - 4 * half
    t3 = T - 1 - t
    z1, z2, z3 = (d, c, t1), (d, c, t2), (d, c, t3)
    zpeer = [(d, c, lax.rem(t + k, T)) for k in range(1, T)]
    cpeer = [(d, lax.rem(c + k, C), t) for k in range(1, C)]
    sib = (1 - d, c, t)
    xpeer = [(1 - d, c, lax.rem(t + k, T)) for k in range(1, T)]
    everyone = zpeer + cpeer + [sib] + xpeer
    erank = [t2]

    count = [0]
    started = []

    def remote(src, dst, peer):
        i = count[0]
        count[0] += 1
        cp = pltpu.make_async_remote_copy(
            src_ref=src, dst_ref=dst, send_sem=ssem.at[i], recv_sem=rsem.at[i],
            device_id=peer, device_id_type=MESH)
        cp.start()
        started.append(cp)
        return cp

    def arrived(*cps):
        for cp in cps:
            cp.wait_recv()

    nlocal = [0]

    def local(src, dst):
        cp = pltpu.make_async_copy(src, dst, lsem.at[nlocal[0]])
        nlocal[0] += 1
        cp.start()
        return cp

    def rows_at(start, size):
        return pl.ds(pl.multiple_of(start, size), size)

    barrier = pltpu.get_barrier_semaphore()
    for p in everyone:
        pl.semaphore_signal(barrier, inc=1, device_id=p, device_id_type=MESH)
    cp_small = [local(a, b) for a, b in (
        (lre_h, lre_in), (lim_h, lim_in), (stp_h, stp_in), (bias_h, bias_in), (gain_h, gain_in), (skip_h, skip_in))]
    mine = rows_at(R * t, R)
    cp_pk = [local(a, pk.at[k]) for k, a in enumerate((bre, bim, cre, cim))] + [local(glu_hbm, glu)]
    cx = local(x_hbm.at[mine], xv)
    cxe = [local(x_hbm.at[rows_at(R * e, R)], xe.at[pl.ds(R * k, R)]) for k, e in enumerate(erank)]
    co = local(og_hbm.at[mine], ogv.at[:, lane(U * t, U)])
    dl = lane(HD * d, HD)
    dr_ = rows_at(HD * d, HD)
    tl = lane(U * t, U)
    sm_ref[...] = jnp.zeros_like(sm_ref)
    for cp in cp_small:
        cp.wait()
    own = coefficients(lre_in[...], lim_in[...], stp_in[...])
    for k in range(4):
        sm_ref[k:k + 1, 0:NS // D] = own[k]
    sm_ref[4:5, 0:U // D] = bias_in[...]
    sm_ref[5:6, :] = gain_in[...]
    sm_ref[6:7, :] = skip_in[...]
    me8 = d * T + t
    smr[me8] = sm_ref[...]
    accv[...] = jnp.zeros_like(accv)
    vv[...] = jnp.zeros_like(vv)
    for cp in cp_pk:
        cp.wait()
    for k in range(4):
        w4[k, t, :, dl] = pk[k]
    gt[dr_, tl] = glu[...]
    cx.wait()

    def standard(x):
        cen = x - jnp.mean(x, -1, keepdims=True)
        rstd = lax.rsqrt(jnp.mean(cen * cen, -1, keepdims=True) + epsilon)
        return cen * rstd, rstd

    def ln_tile(i, _):
        for u in range(4):
            rows = rows_at(i * 128 + u * 32, 32)
            xn, rstd = standard(xv[rows, :].astype(f32))
            xh[rows, :] = xn
            rs[rows, :] = jnp.broadcast_to(rstd, (32, 128))
        return 0

    lax.fori_loop(0, R // 128, ln_tile, 0)
    pl.semaphore_wait(barrier, len(everyone))

    gq, hq = c // 2, lax.rem(c, 2)
    ql = lane(128 * hq, 128)
    wl = lane(HD * d + 128 * hq, 128)
    uq = HD // C
    gown = rows_at(uq * c, uq)
    grow = rows_at(HD * d + uq * c, uq)
    pair = rows_at(2 - 2 * half, 2)
    pairl = lane(2 * U * (1 - half), 2 * U)

    qb, qc = gq, 2 + gq
    far_b = [remote(pk.at[qb, :, ql], w4.at[qb, t, :, wl], p) for p in (z3, z2)]
    small = [remote(sm_ref, smr.at[me8], p) for p in zpeer + [sib] + xpeer]
    near_b = remote(pk.at[0:2], w4.at[0:2, t, :, dl], z1)
    w3b = [remote(pk.at[0:2], w4.at[0:2, t, :, dl], sib)]

    def spread(blk, *cps):
        arrived(*cps)
        return [remote(blk, blk, p) for p in cpeer]

    gl1, gl2 = lane(U * t1, U), lane(U * t2, U)
    w2b = spread(w4.at[qb, pair, :, wl], *far_b)
    far_c = [remote(pk.at[qc, :, ql], w4.at[qc, t, :, wl], p) for p in (z3, z2)]
    far_g = [remote(glu.at[gown], gt.at[grow, tl], p) for p in (z3, z2)]
    near_c = remote(pk.at[2:4], w4.at[2:4, t, :, dl], z1)
    near_g = remote(glu, gt.at[dr_, tl], z1)
    w3c = [remote(pk.at[2:4], w4.at[2:4, t, :, dl], sib)]
    w3g = [remote(glu, gt.at[dr_, tl], sib)]

    def cot_send(s):
        return [remote(og_hbm.at[rows_at(R * p[2] + L * s, L)], ogv.at[pl.ds(L * s, L), tl], p) for p in zpeer]

    arrived(*small)
    zero = jnp.zeros((8, H - HD), f32)
    vec = jnp.zeros((8, H), f32)
    bias = jnp.zeros((8, H), f32)
    for dd in range(D):
        for tt in range(T):
            ext = jnp.concatenate([smr[dd * T + tt], zero], 1)
            place = tt * D + dd
            vec = vec + (pltpu.roll(ext, place * (NS // D), 1) if place else ext)
            bias = bias + (pltpu.roll(ext, place * (U // D), 1) if place else ext)
    both = jnp.concatenate([smr[t], smr[T + t]], 1)
    gain_r, skip_r, bias_r = both[5:6, :], both[6:7, :], bias[4:5, :]

    arrived(near_b)
    w3b.append(remote(w4.at[0:2, t1, :, dl], w4.at[0:2, t1, :, dl], sib))
    row8 = lax.broadcasted_iota(jnp.int32, (8, N), 0)
    full = lambda v, k, n: jnp.broadcast_to(v[k:k + 1, :n], (8, n))
    dr, di = full(vec, 0, N), full(vec, 1, N)
    cr, ci = full(vec, 2, N), full(vec, 3, N)
    pows = {1: (dr, di)}
    for k in range(2, 9):
        pows[k] = cmul(*pows[k - 1], dr, di)
    for n_, k in ((0, 1), (1, 2), (2, 4)):
        keep = row8 >= k
        cst[2 * n_] = jnp.where(keep, pows[k][0], 0.0)
        cst[2 * n_ + 1] = jnp.where(keep, pows[k][1], 0.0)
        keep = row8 < 8 - k
        cst[8 + 2 * n_] = jnp.where(keep, pows[k][0], 0.0)
        cst[8 + 2 * n_ + 1] = jnp.where(keep, -pows[k][1], 0.0)
    pr, pi, qr, qi = pows[1][0], pows[1][1], pows[8][0], -pows[8][1]
    for r in range(1, 8):
        pr = jnp.where(row8 == r, pows[r + 1][0], pr)
        pi = jnp.where(row8 == r, pows[r + 1][1], pi)
        qr = jnp.where(row8 == r, pows[8 - r][0], qr)
        qi = jnp.where(row8 == r, -pows[8 - r][1], qi)
    cst[6], cst[7], cst[14], cst[15] = pr, pi, qr, qi
    cst[16], cst[17] = pows[8]
    cst[18], cst[19] = cr, ci
    big = pows[8]
    n_ = 8
    while n_ < L:
        big = cmul(*big, *big)
        n_ *= 2
    cst[20], cst[21] = big

    def nrm_tile(i, _):
        rows = rows_at(i * 32, 32)
        nrm[rows, :] = (xh[rows, :] * gain_r).astype(bf16)
        return 0

    lax.fori_loop(0, R // 32, nrm_tile, 0)
    og = [cot_send(0)]

    def lne_tile(i, _):
        for u in range(4):
            rows = rows_at(i * 128 + u * 32, 32)
            nrme[rows, :] = (standard(xe[rows, :].astype(f32))[0] * gain_r).astype(bf16)
        return 0

    def seq_rows(s):
        return rows_at(s * L, L)

    wv = w4.reshape(4, N, H)

    def drive(src, off, dst, j):
        rows = rows_at(128 * j, 128)
        both_ = nt(src[pl.ds(off, R), :], jnp.concatenate([wv[0, rows, :], wv[1, rows, :]], 0))
        dst[:, lane(128 * j, 128)] = both_[:, 0:128]
        dst[:, lane(N + 128 * j, 128)] = both_[:, 128:256]

    def scan(src, dst, groups, base, coef, reverse):
        e = 0 if reverse else 7

        def tile(i, carry):
            carry = list(carry)
            ii = L // 32 - 1 - i if reverse else i
            for g, (rb, l0) in enumerate(groups):
                lr_, li_ = lane(l0, 128), lane(N + l0, 128)
                con = [cst[base + k, :, lr_] for k in range(8)]
                e0 = cst[16, :, lr_]
                e1 = -cst[17, :, lr_] if reverse else cst[17, :, lr_]
                loc = []
                for u in range(4):
                    uu = 3 - u if reverse else u
                    rows = rows_at(rb + ii * 32 + uu * 8, 8)
                    ar, ai = src[rows, lr_], src[rows, li_]
                    if coef:
                        ar, ai = cmul(cst[18, :, lr_], cst[19, :, lr_], ar, ai)
                    else:
                        ai = -ai
                    for n_, k in ((0, 1), (1, 2), (2, 4)):
                        sh = 8 - k if reverse else k
                        br, bi = pltpu.roll(ar, sh, 0), pltpu.roll(ai, sh, 0)
                        mr, mi = con[2 * n_], con[2 * n_ + 1]
                        ar, ai = ar + mr * br - mi * bi, ai + mr * bi + mi * br
                    loc.append((rows, ar, ai))
                kr, ki = carry[2 * g], carry[2 * g + 1]
                for rows, ar, ai in loc:
                    dst[rows, lr_] = ar + con[6] * kr - con[7] * ki
                    dst[rows, li_] = ai + con[6] * ki + con[7] * kr
                    endr = jnp.broadcast_to(ar[e:e + 1, :], (8, 128))
                    endi = jnp.broadcast_to(ai[e:e + 1, :], (8, 128))
                    kr, ki = endr + e0 * kr - e1 * ki, endi + e0 * ki + e1 * kr
                carry[2 * g], carry[2 * g + 1] = kr, ki
            return tuple(carry)

        z = jnp.zeros((8, 128), f32)
        return lax.fori_loop(0, L // 32, tile, (z,) * (2 * len(groups)))

    def begin(src, off, dst, out, slot, j):
        drive(src, off, dst, j)
        fin = scan(dst, out, [(s * L, 128 * j) for s in range(S)], 0, True, False)
        for s in range(S):
            ce[slot, pl.ds(s, 1), lane(128 * j, 128)] = fin[2 * s][0:1, :]
            ce[slot, pl.ds(S + s, 1), lane(128 * j, 128)] = fin[2 * s + 1][0:1, :]

    def rest(*what):
        def step(k, _):
            begin(*what, 1 + k * (1 - 2 * half))
            return 0

        lax.fori_loop(0, 2, step, 0)
        slot = what[4 - 0]
        return [remote(ce.at[slot], cer.at[slot, k], p) for k, p in enumerate(cpeer)]

    def incoming(slot, cps, n, forward):
        arrived(*cps)
        bg = (cst[20, 0:1, :], cst[21, 0:1, :])
        wt = (jnp.ones((1, N), f32), jnp.zeros((1, N), f32))
        accr = jnp.zeros((n, N), f32)
        acci = jnp.zeros((n, N), f32)
        for k in range(1, C):
            got = cer[slot, k - 1] if forward else cer[slot, C - 1 - k]
            has = (c >= k) if forward else (c + k < C)
            w = jnp.where(has, 1.0, 0.0)
            wi = wt[1] if forward else -wt[1]
            ur, ui = cmul(wt[0], wi, got[0:n, :], got[n:2 * n, :])
            accr = accr + w * ur
            acci = acci + w * ui
            wt = cmul(*wt, *bg)
        cin[slot, 0:n, :] = accr
        cin[slot, n:2 * n, :] = acci

    def entering(slot, k, lanes):
        return jnp.broadcast_to(cin[slot, pl.ds(k, 1), lanes], (8, 128))

    def fix_batch(ref, dst, slot, keep):
        def fix_lanes(j, _):
            lr_, li_ = lane(128 * j, 128), lane(N + 128 * j, 128)
            p0, p1 = cst[6, :, lr_], cst[7, :, lr_]
            e0, e1 = cst[16, :, lr_], cst[17, :, lr_]
            q0 = tuple(entering(slot, k * S + s, lr_) for s in range(S) for k in range(2))

            def tile(i, q):
                q = list(q)
                for s in range(S):
                    rr, ri = [], []
                    for h in range(2):
                        rows = rows_at(s * L + i * 16 + 8 * h, 8)
                        vr, vi = cmul(p0, p1, q[2 * s], q[2 * s + 1])
                        ar, ai = ref[rows, lr_] + vr, ref[rows, li_] + vi
                        if keep:
                            ref[rows, lr_] = ar
                            ref[rows, li_] = ai
                        rr.append(ar)
                        ri.append(ai)
                        q[2 * s], q[2 * s + 1] = cmul(q[2 * s], q[2 * s + 1], e0, e1)
                    rows = rows_at(s * L + i * 16, 16)
                    dst[rows, lr_] = jnp.concatenate(rr, 0).astype(bf16)
                    dst[rows, li_] = (-jnp.concatenate(ri, 0)).astype(bf16)
                return tuple(q)

            lax.fori_loop(0, L // 16, tile, q0)
            return 0

        lax.fori_loop(0, N // 128, fix_lanes, 0)

    def each_seq(f):
        f(pl.ds(0, R))

    def tiles(f, lo=0, hi=R // 32):
        def step(i, _):
            f(i, rows_at(i * 32, 32))
            return 0

        lax.fori_loop(lo, hi, step, 0)

    def valid_of(i, rank):
        s = i // (L // 32)
        pos = c * L + lax.rem(i, L // 32) * 32 + lax.broadcasted_iota(jnp.int32, (32, 1), 0)
        return jnp.where(pos < len_ref[S * rank + s], 1.0, 0.0)

    def logistic(v):
        return 0.5 + 0.5 * jnp.tanh(0.5 * v)

    batches = [(nrm, 0, raw, st, 0)] + [(nrme, R * k, rawe.at[k], rawe.at[k], 1 + k) for k in range(len(erank))]
    arrived(*w3b)
    begin(*batches[0], 2 * half)
    w2c = spread(w4.at[qc, pair, :, wl], *far_c)
    w2g = spread(gt.at[grow, pairl], *far_g)
    og.append(cot_send(1))
    for cp in cxe:
        cp.wait()
    lax.fori_loop(0, R // 128, lne_tile, 0)
    arrived(*w2b)
    w3b2 = remote(w4.at[0:2, pair, :, dl], w4.at[0:2, pair, :, dl], sib)
    og.append(cot_send(2))
    begin(*batches[1], 2 * half)
    arrived(w3b2)
    fce = [rest(*batches[0])]
    arrived(near_c)
    w3c.append(remote(w4.at[2:4, t1, :, dl], w4.at[2:4, t1, :, dl], sib))
    arrived(near_g)
    blk = gt.at[dr_, gl1]
    w3g.append(remote(blk, blk, sib))
    arrived(*w2c)
    w3c.append(remote(w4.at[2:4, pair, :, dl], w4.at[2:4, pair, :, dl], sib))
    arrived(*w2g)
    blk = gt.at[dr_, pairl]
    w3g.append(remote(blk, blk, sib))
    fce.append(rest(*batches[1]))
    if len(erank) > 1:
        lax.fori_loop(R // 128, 2 * R // 128, lne_tile, 0)
        begin(*batches[2], 2 * half)
    incoming(0, fce[0], S, True)
    fix_batch(st, sb, 0, True)
    arrived(*w3c)

    def ssm_own(rows):
        tmp[rows, :] = nn(sb[rows, :], w4[2:4].reshape(2 * N, H))

    each_seq(ssm_own)

    def gelu_tile(i, rows):
        pre = tmp[rows, :] + skip_r * nrm[rows, :].astype(f32)
        sq = pre * pre
        th = jnp.tanh(pre * (SQ2PI + (SQ2PI * 0.044715) * sq))
        hf = 0.5 + 0.5 * th
        act[rows, :] = (pre * hf).astype(bf16)
        gp[rows, :] = hf + 0.5 * pre * (1.0 - th * th) * (SQ2PI + (3 * 0.044715 * SQ2PI) * sq)

    tiles(gelu_tile)
    arrived(*w3g)

    def gate_own(rows):
        tmp[rows, :] = nn(act[rows, :], gt[...])

    each_seq(gate_own)

    def out_tile(i, rows):
        sg = logistic(tmp[rows, :] + bias_r)
        sig[rows, :] = sg
        o = valid_of(i, t) * (xv[rows, :].astype(f32) + act[rows, :].astype(f32) * sg)
        ob[rows, :] = o.astype(bf16)

    tiles(out_tile)
    outc = [remote(ob.at[:, lane(U * q, U)], out_hbm.at[mine, :], p) for q, p in ((t1, z1), (t3, z3))]
    locals_ = [local(ob.at[:, tl], out_hbm.at[mine, :])]

    def fold(v):
        return jnp.sum(v.reshape(4, 8, v.shape[-1]), 0)

    def seq_tiles(s, f):
        def step(i, acc):
            return acc + fold(f(i, rows_at(i * 32, 32)))

        return lax.fori_loop(s * (L // 32), (s + 1) * (L // 32), step, jnp.zeros((8, H), f32))

    co.wait()

    def gate_tile(i, rows):
        sg = sig[rows, :]
        direct = valid_of(i, t) * ogv[rows, :].astype(f32) * sg
        g = direct * act[rows, :].astype(f32) * (1.0 - sg)
        gl[rows, :] = g.astype(bf16)
        sig[rows, :] = direct
        return g

    def pre_tile(i, rows):
        p = (tmp[rows, :] + sig[rows, :]) * gp[rows, :]
        pg[rows, :] = p
        plb[rows, :] = p.astype(bf16)
        return p * nrm[rows, :].astype(f32)

    def back_one(s):
        arrived(*og[s])
        rows = pl.ds(s * L, L)
        accv[0] += seq_tiles(s, gate_tile)
        tmp[rows, :] = nt(gl[rows, :], gt[...])
        accv[1] += seq_tiles(s, pre_tile)
        mu[rows, :] = nt(plb[rows, :], w4[2:4].reshape(2 * N, H))
        fin = scan(mu, mu, [(s * L, 128 * j) for j in range(N // 128)], 8, False, True)
        for j in range(N // 128):
            ce[3 + s, 0:1, 128 * j:128 * j + 128] = fin[2 * j][0:1, :]
            ce[3 + s, 1:2, 128 * j:128 * j + 128] = fin[2 * j + 1][0:1, :]
        return [remote(ce.at[3 + s], cer.at[3 + s, k], p) for k, p in enumerate(cpeer)]

    row1 = lax.broadcasted_iota(jnp.int32, (8, 128), 0)

    def back_two(s, cps):
        incoming(3 + s, cps, 1, False)
        nj = N // 128
        q0 = tuple(entering(3 + s, k, lane(128 * j, 128)) for j in range(nj) for k in range(2))
        z = jnp.zeros((8, 128), f32)

        def tile(i, carry):
            q, m, acc = list(carry[:2 * nj]), list(carry[2 * nj:4 * nj]), list(carry[4 * nj:])
            ii = L // 16 - 1 - i
            for j in range(nj):
                lr_, li_ = lane(128 * j, 128), lane(N + 128 * j, 128)
                p0, p1 = cst[14, :, lr_], cst[15, :, lr_]
                e0, e1 = cst[16, :, lr_], -cst[17, :, lr_]
                cfr, cfi = cst[18, :, lr_], cst[19, :, lr_]
                rr, ri = [None, None], [None, None]
                for h in (1, 0):
                    rows = rows_at(s * L + ii * 16 + 8 * h, 8)
                    vr, vi = cmul(p0, p1, q[2 * j], q[2 * j + 1])
                    ar, ai = mu[rows, lr_] + vr, mu[rows, li_] + vi
                    q[2 * j], q[2 * j + 1] = cmul(q[2 * j], q[2 * j + 1], e0, e1)
                    nr = jnp.where(row1 == 7, m[2 * j], pltpu.roll(ar, 7, 0))
                    ni = jnp.where(row1 == 7, m[2 * j + 1], pltpu.roll(ai, 7, 0))
                    m[2 * j] = jnp.broadcast_to(ar[0:1, :], (8, 128))
                    m[2 * j + 1] = jnp.broadcast_to(ai[0:1, :], (8, 128))
                    xr, xi = st[rows, lr_], st[rows, li_]
                    ur, ui = raw[rows, lr_], raw[rows, li_]
                    acc[4 * j] = acc[4 * j] + nr * xr + ni * xi
                    acc[4 * j + 1] = acc[4 * j + 1] + ni * xr - nr * xi
                    acc[4 * j + 2] = acc[4 * j + 2] + ar * ur + ai * ui
                    acc[4 * j + 3] = acc[4 * j + 3] + ai * ur - ar * ui
                    rr[h] = cfr * ar + cfi * ai
                    ri[h] = cfr * ai - cfi * ar
                rows = rows_at(s * L + ii * 16, 16)
                nb[rows, lr_] = jnp.concatenate(rr, 0).astype(bf16)
                nb[rows, li_] = jnp.concatenate(ri, 0).astype(bf16)
            return tuple(q) + tuple(m) + tuple(acc)

        fin = lax.fori_loop(0, L // 16, tile, q0 + q0 + (z,) * (4 * nj))
        for j in range(nj):
            for k in range(4):
                vv[3 + k:4 + k, 128 * j:128 * j + 128] += jnp.sum(fin[4 * nj + 4 * j + k], 0, keepdims=True)
        rows = pl.ds(s * L, L)
        tmp[rows, :] = nn(nb[rows, :], w4[0:2].reshape(2 * N, H))

        def tok_tile(i, acc):
            for u in range(4):
                rows = rows_at(s * L + i * 128 + u * 32, 32)
                n = tmp[rows, :] + skip_r * pg[rows, :]
                xt = xh[rows, :]
                h = n * gain_r
                m1 = jnp.mean(h, -1, keepdims=True)
                m2 = jnp.mean(h * xt, -1, keepdims=True)
                tgb[rows, :] = ((h - m1 - xt * m2) * rs[rows, 0:1]).astype(bf16)
                acc = acc + fold(n * xt)
            return acc

        accv[2] += lax.fori_loop(0, L // 128, tok_tile, jnp.zeros((8, H), f32))
        there = rows_at(R * t + L * s, L)
        locals_.append(local(tgb.at[rows, tl], tg_hbm.at[there, :]))
        return [remote(tgb.at[rows, lane(U * p[2], U)], tg_hbm.at[there, :], p) for p in zpeer]

    bs = [back_one(s) for s in range(S)]

    gcf, gbf = gc.reshape(2 * N, H), gb.reshape(2 * N, H)
    ol = lane(HD * (1 - d), HD)

    def gc_step(j, _):
        gcf[rows_at(j * 256, 256), :] = tn(sb[:, lane(j * 256, 256)], plb[...]).astype(bf16)
        return 0

    lax.fori_loop(0, 2 * N // 256, gc_step, 0)
    d1c = remote(gc.at[:, :, :, ol], r1c, sib)

    def gg_step(j, _):
        gg[rows_at(j * 256, 256), :] = tn(act[:, lane(j * 256, 256)], gl[...]).astype(bf16)
        return 0

    lax.fori_loop(0, H // 256, gg_step, 0)
    d1g = remote(gg.at[rows_at(HD * (1 - d), HD), :], r1g, sib)

    def gb_step(j, _):
        gbf[rows_at(j * 256, 256), :] = tn(nb[:, lane(j * 256, 256)], nrm[...]).astype(bf16)
        return 0

    hs = NS // 2

    def rs_ctx(p):
        return p // 2, rows_at(hs * lax.rem(p, 2), hs)

    gr = lambda p: rows_at(uq * p, uq)

    def add2(a, b):
        return (a.astype(f32) + b.astype(f32)).astype(bf16)

    def total(first_, buf, n):
        acc = first_.astype(f32)
        for k in range(n):
            acc = acc + buf[k].astype(f32)
        return acc

    def two_states(g, d1, r1, s1, r2):
        arrived(d1)
        s1[...] = add2(g[:, :, :, dl], r1[...])
        return [remote(s1.at[rs_ctx(p[1])[0], :, rs_ctx(p[1])[1], :], r2.at[k], p) for k, p in enumerate(cpeer)]

    def three_states(d2, s1, r2, s2, r3):
        arrived(*d2)
        s2[...] = total(s1[rs_ctx(c)[0], :, rs_ctx(c)[1], :], r2, C - 1).astype(bf16)
        return [remote(s2.at[t1], r3.at[0], z1), remote(s2.at[t3], r3.at[1], z1)]

    def four_states(d3, s2, r3, s3, r4):
        arrived(*d3)
        s3[0] = add2(s2[t], r3[0])
        s3[1] = add2(s2[t2], r3[1])
        return remote(s3.at[1], r4, z2)

    def five(d4, s3, r4, out):
        arrived(d4)
        out[c] = add2(s3[0], r4[...])
        return [remote(out.at[c], out.at[c], p) for p in cpeer]

    def extra_fix(k):
        incoming(1 + k, fce[1 + k], S, True)
        fix_batch(rawe.at[k], sbe, 1 + k, False)

    def extra_act(k):
        def ssm(rows):
            tmpe[rows, :] = nn(sbe[rows, :], w4[2:4].reshape(2 * N, H))

        each_seq(ssm)

        def gelu(i, rows):
            pre = tmpe[rows, :] + skip_r * nrme[rows_at(R * k + i * 32, 32), :].astype(f32)
            acte[rows, :] = (pre * (0.5 + 0.5 * jnp.tanh(pre * (SQ2PI + (SQ2PI * 0.044715) * (pre * pre))))).astype(bf16)

        tiles(gelu)

    def extra_out(k):
        rank = erank[k]

        def gate(rows):
            tmpe[rows, 0:U] = nn(acte[rows, :], gt[:, tl])

        each_seq(gate)
        bias_u = jnp.sum(jnp.where(lax.broadcasted_iota(jnp.int32, (T, U), 0) == t, bias_t, 0.0), 0, keepdims=True)

        def fin(i, rows):
            here = rows_at(R * k + i * 32, 32)
            sg = logistic(tmpe[rows, 0:U] + bias_u)
            o = valid_of(i, rank) * (xe[here, tl].astype(f32) + acte[rows, tl].astype(f32) * sg)
            obe[here, :] = o.astype(bf16)

        tiles(fin)
        locals_.append(local(obe.at[pl.ds(R * k, R)], out_hbm.at[rows_at(R * rank, R), :]))

    bias_t = jnp.concatenate([bias_r[:, U * k:U * k + U] for k in range(T)], 0)
    tgc = back_two(0, bs[0])
    d2c = two_states(gc, d1c, r1c, s1c, r2c)
    arrived(d1g)
    s1g[...] = add2(gg[dr_, :], r1g[...])
    d2g = [remote(s1g.at[gr(p[1]), :], r2g.at[k], p) for k, p in enumerate(cpeer)]
    for k in range(1, S):
        tgc += back_two(k, bs[k])
    lax.fori_loop(0, 2 * N // 256, gb_step, 0)
    d1b = remote(gb.at[:, :, :, ol], r1b, sib)
    for k, row in ((2, 0), (1, 1), (0, 2)):
        vv[row:row + 1, :] = jnp.sum(accv[k], 0, keepdims=True)
    d1v = remote(vv, vr1, sib)
    if erank:
        extra_fix(0)
    d2b = two_states(gb, d1b, r1b, s1b, r2b)
    arrived(d1v)
    vr2[0] = vv[...] + vr1[...]
    d2v = [remote(vr2.at[0], vr2.at[k + 1], p) for k, p in enumerate(cpeer)]
    if len(erank) > 1:
        fce.append(rest(*batches[2]))
    d3c = three_states(d2c, s1c, r2c, s2c, r3c)
    arrived(*d2g)
    s2g[...] = total(s1g[gr(c), :], r2g, C - 1).astype(bf16)
    d3g = [remote(s2g.at[:, gl1], r3g.at[0], z1), remote(s2g.at[:, lane(U * t3, U)], r3g.at[1], z1)]
    if erank:
        extra_act(0)
    d4c = four_states(d3c, s2c, r3c, s3c, r4c)
    arrived(*d3g)
    s3g[0] = add2(s2g[:, tl], r3g[0])
    s3g[1] = add2(s2g[:, gl2], r3g[1])
    d4g = remote(s3g.at[1], r4g, z2)
    if erank:
        extra_out(0)
    arrived(*d2b)
    s2b[...] = total(s1b[rs_ctx(c)[0], :, rs_ctx(c)[1], :], r2b, C - 1).astype(bf16)
    d3b = [remote(s2b.at[p[2]], r3b.at[k], p) for k, p in enumerate(zpeer)]
    arrived(*d2v)
    vr3[0] = vr2[0] + vr2[1] + vr2[2] + vr2[3]
    d3v = [remote(vr3.at[0], vr3.at[k + 1], p) for k, p in enumerate(zpeer)]
    if len(erank) > 1:
        extra_fix(1)
    d5 = five(d4c, s3c, r4c, fc_ref) + five(d4g, s3g, r4g, fg_ref)
    if len(erank) > 1:
        extra_act(1)
    arrived(*d3b)
    fb_ref[c] = total(s2b[t], r3b, T - 1).astype(bf16)
    d5 += [remote(fb_ref.at[c], fb_ref.at[c], p) for p in cpeer]
    if len(erank) > 1:
        extra_out(1)

    arrived(*d3v)
    vf[...] = vr3[0] + vr3[1] + vr3[2] + vr3[3]
    place = t * D + d
    back = lambda n: lax.rem(H - n * place, H)
    st8 = pltpu.roll(vf[...], back(NS // D), 1)[:, 0:NS // D]
    ub8 = pltpu.roll(vf[...], back(U // D), 1)[:, 0:U // D]
    lr1, li1, step1 = lre_in[...], lim_in[...], jnp.exp(stp_in[...])
    dr1, di1, cr1, ci1 = (sm_ref[k:k + 1, 0:NS // D] for k in range(4))
    gdr, gdi, gcr, gci = (st8[k:k + 1] for k in range(3, 7))
    inv = 1.0 / (lr1 * lr1 + li1 * li1)
    hdr = gdr + (gcr * lr1 - gci * li1) * inv
    hdi = gdi + (gcr * li1 + gci * lr1) * inv
    pull = 2.0 * (gcr * cr1 + gci * ci1)
    e1, e2 = dr1 - 1.0, hdr * dr1 + hdi * di1
    e3 = hdi * dr1 - hdr * di1
    fv_ref[...] = jnp.zeros_like(fv_ref)
    fv_ref[0:1, :] = vf[0:1, dl]
    fv_ref[1:2, :] = vf[1:2, dl]
    fv_ref[2:3, 0:U // D] = ub8[2:3]
    fv_ref[3:4, 0:NS // D] = (gcr * e1 + gci * di1 - pull * lr1) * inv + step1 * e2
    fv_ref[4:5, 0:NS // D] = (gcr * di1 - gci * e1 - pull * li1) * inv + step1 * e3
    fv_ref[5:6, 0:NS // D] = step1 * (lr1 * e2 + li1 * e3)
    arrived(*d5, *tgc, *outc)
    for cp in locals_:
        cp.wait()
    for cp in started:
        cp.wait_send()
    assert count[0] == NSEM and nlocal[0] == NLOCAL, (count[0], nlocal[0])


NSEM, NLOCAL = 106, 19


def fused_call(geo, lens, x2, og2, *params):
    D, C, T, S, L, H, N, U = geo
    R, NS, HD = S * L, N // T, H // D
    f32, bf16 = jnp.float32, jnp.bfloat16
    uq, hs = HD // C, NS // 2
    V = pltpu.VMEM
    any_, vm = pl.BlockSpec(memory_space=pl.ANY), pl.BlockSpec(memory_space=pltpu.VMEM)
    scratch = [
        V((R, H), bf16), V((R, H), bf16), V((R, H), f32), V((R, 128), f32),
        V((R, 2 * N), f32), V((R, 2 * N), f32), V((R, 2 * N), bf16),
        V((R, H), f32), V((R, H), bf16), V((R, H), f32), V((R, H), f32),
        V((R, H), bf16), V((R, H), bf16), V((R, H), bf16), V((R, H), f32), V((R, H), bf16),
        V((R, 2 * N), f32), V((R, 2 * N), bf16), V((R, H), bf16),
        V((2 * R, H), bf16), V((2 * R, H), bf16), V((2, R, 2 * N), f32), V((R, 2 * N), bf16),
        V((R, H), bf16), V((R, H), f32), V((2 * R, U), bf16),
        V((4, T, NS, H), bf16), V((H, H), bf16), V((D * T, 8, HD), f32),
        V((22, 8, N), f32), V((6, 8, N), f32), V((6, C - 1, 8, N), f32), V((6, 8, N), f32),
        V((2, T, NS, H), bf16), V((H, H), bf16), V((2, T, NS, H), bf16),
        V((2, T, NS, HD), bf16), V((HD, H), bf16), V((2, T, NS, HD), bf16),
        V((2, T, NS, HD), bf16), V((HD, H), bf16), V((2, T, NS, HD), bf16),
        V((C - 1, T, hs, HD), bf16), V((C - 1, uq, H), bf16), V((C - 1, T, hs, HD), bf16),
        V((T, hs, HD), bf16), V((uq, H), bf16), V((T, hs, HD), bf16),
        V((2, hs, HD), bf16), V((2, uq, U), bf16), V((T - 1, hs, HD), bf16),
        V((2, hs, HD), bf16), V((2, uq, U), bf16), V((hs, HD), bf16), V((uq, U), bf16),
        V((8, H), f32), V((8, H), f32), V((C, 8, H), f32), V((T, 8, H), f32), V((8, H), f32), V((3, 8, H), f32),
        V((4, NS, HD), bf16), V((8, HD), f32), V((HD, U), bf16), V((1, HD), f32), V((1, HD), f32),
        V((1, NS // D), f32), V((1, NS // D), f32), V((1, NS // D), f32), V((1, U // D), f32),
        pltpu.SemaphoreType.DMA((NLOCAL,)), pltpu.SemaphoreType.DMA((NSEM,)), pltpu.SemaphoreType.DMA((NSEM,)),
    ]
    rows = x2.shape[0]
    return pl.pallas_call(
        functools.partial(fused_body, geo),
        out_shape=(
            jax.ShapeDtypeStruct((rows, U), bf16), jax.ShapeDtypeStruct((rows, U), bf16),
            jax.ShapeDtypeStruct((C, hs, HD), bf16), jax.ShapeDtypeStruct((C, uq, U), bf16),
            jax.ShapeDtypeStruct((C, hs, HD), bf16), jax.ShapeDtypeStruct((8, HD), f32)),
        in_specs=[pl.BlockSpec(memory_space=pltpu.SMEM), any_, any_] + [any_] * 11,
        out_specs=(any_, any_, vm, vm, vm, vm),
        scratch_shapes=scratch,
        compiler_params=pltpu.CompilerParams(
            collective_id=0, has_side_effects=True, vmem_limit_bytes=60 * 1024 * 1024),
        name="block",
    )(lens, x2, og2, *params)


def finish_body(geo, len_ref, out_in, tok_in, og_in, fc_in, fg_in, fb_in, fv, out, ingrad, gain_g, skip_g,
                lre_g, lim_g, step_g, bre_g, bim_g, cre_g, cim_g, glu_g, bias_g,
                tokv, ogv, outv, fc, fg, fb, bre, bim, cre, cim, glu, res, sem, gsem, osem):
    D, C, T, S, L, H, N, U = geo
    NS = N // T
    f32 = jnp.float32

    def move(src, dst, s):
        cp = pltpu.make_async_copy(src, dst, s)
        cp.start()
        return cp

    part = [pl.ds(S * k, S) for k in range(T)]
    loads = [(move(tok_in.at[part[k]], tokv.at[part[k]], sem.at[0, k]),
              move(og_in.at[part[k]], ogv.at[part[k]], sem.at[1, k])) for k in range(T)]
    params = [move(a, b, gsem.at[k]) for k, (a, b) in enumerate(((fc_in, fc), (fg_in, fg), (fb_in, fb)))]
    passes = [move(out_in.at[part[k]], outv.at[part[k]], sem.at[2, k]) for k in range(T)]
    base = lax.axis_index("ctx") * L
    stores = []
    for k in range(T):
        for cp in loads[k]:
            cp.wait()

        def tile(i, _):
            s = S * k + i // (L // 32)
            r0 = lax.rem(i, L // 32) * 32
            rows = pl.ds(pl.multiple_of(r0, 32), 32)
            pos = base + r0 + lax.broadcasted_iota(jnp.int32, (32, 1), 0)
            keep = jnp.where(pos < len_ref[s], 1.0, 0.0)
            res[s, rows, :] = keep * ogv[s, rows, :].astype(f32) + tokv[s, rows, :].astype(f32)
            return 0

        lax.fori_loop(0, S * L // 32, tile, 0)
        stores.append(move(res.at[part[k]], ingrad.at[part[k]], osem.at[k]))
    for cp in params:
        cp.wait()
    h = C // 2
    for k in range(C):
        rows = pl.ds((k % h) * (NS // h), NS // h)
        (bre if k < h else bim)[rows, :] = fb[k].astype(f32)
        (cre if k < h else cim)[rows, :] = fc[k].astype(f32)
    glu[...] = fg[...].reshape(glu.shape).astype(f32)
    pairs = ((bre, bre_g), (bim, bim_g), (cre, cre_g), (cim, cim_g), (glu, glu_g))
    stores += [move(a, b, osem.at[2 * T + k]) for k, (a, b) in enumerate(pairs)]
    for k in range(T):
        passes[k].wait()
        stores.append(move(outv.at[part[k]], out.at[part[k]], osem.at[T + k]))
    gain_g[...] = fv[0:1, :]
    skip_g[...] = fv[1:2, :]
    bias_g[...] = fv[2:3, 0:U // D]
    lre_g[...] = fv[3:4, 0:NS // D]
    lim_g[...] = fv[4:5, 0:NS // D]
    step_g[...] = fv[5:6, 0:NS // D]
    for cp in stores:
        cp.wait()


def finish_call(geo, lens, out, tok, og, fc, fg, fb, fv):
    D, C, T, S, L, H, N, U = geo
    NS, HD = N // T, H // D
    f32, bf16 = jnp.float32, jnp.bfloat16
    seqs = S * T
    any_, vm = pl.BlockSpec(memory_space=pl.ANY), pl.BlockSpec(memory_space=pltpu.VMEM)
    V = pltpu.VMEM
    small = [(1, HD), (1, HD)] + [(1, NS // D)] * 3 + [(NS, HD)] * 4 + [(HD, U), (1, U // D)]
    return pl.pallas_call(
        functools.partial(finish_body, geo),
        out_shape=[jax.ShapeDtypeStruct((seqs, L, U), bf16), jax.ShapeDtypeStruct((seqs, L, U), f32)]
        + [jax.ShapeDtypeStruct(s, f32) for s in small],
        in_specs=[pl.BlockSpec(memory_space=pltpu.SMEM)] + [any_] * 6 + [vm],
        out_specs=[any_, any_] + [vm] * 5 + [any_] * 5 + [vm],
        scratch_shapes=[V((seqs, L, U), bf16)] * 3 + [V(a.shape, a.dtype) for a in (fc, fg, fb)]
        + [V((NS, HD), f32)] * 4 + [V((HD, U), f32), V((seqs, L, U), f32)]
        + [pltpu.SemaphoreType.DMA((3, T)), pltpu.SemaphoreType.DMA((3,)), pltpu.SemaphoreType.DMA((2 * T + 5,))],
        compiler_params=pltpu.CompilerParams(vmem_limit_bytes=60 * 1024 * 1024),
        name="finish",
    )(lens, out.reshape(seqs, L, U), tok.reshape(seqs, L, U), og, fc, fg, fb, fv)


def coefficients(lam_re, lam_im, step_log):
    step = jnp.exp(step_log)
    magnitude = jnp.exp(lam_re * step)
    decay_re = magnitude * jnp.cos(lam_im * step)
    decay_im = magnitude * jnp.sin(lam_im * step)
    inv = 1.0 / (lam_re * lam_re + lam_im * lam_im)
    coef_re = ((decay_re - 1.0) * lam_re + decay_im * lam_im) * inv
    coef_im = (decay_im * lam_re - (decay_re - 1.0) * lam_im) * inv
    return decay_re, decay_im, coef_re, coef_im


def token_split(sizes, inputs, lengths, norm_gain, skip_weight, lambda_re, lambda_im, log_step,
                b_re, b_im, c_re, c_im, glu_weight, glu_bias, out_grad):
    D, C, T = sizes
    seqs, L, H = inputs.shape
    NS, HD = b_re.shape
    U = glu_weight.shape[1]
    geo = (D, C, T, seqs // T, L, H, NS * T, U)
    row = lambda v: v.reshape(1, -1)
    out, tok, fc, fg, fb, fv = fused_call(
        geo, lengths, inputs.reshape(seqs * L, H), out_grad.reshape(seqs * L, U),
        b_re, b_im, c_re.T, c_im.T, glu_weight,
        *(row(v) for v in (norm_gain, skip_weight, lambda_re, lambda_im, log_step, glu_bias)))
    res = finish_call(geo, lengths, out, tok, out_grad, fc, fg, fb, fv)
    out, ingrad, gain_g, skip_g, lre_g, lim_g, step_g, bre_g, bim_g, cre_g, cim_g, glu_g, bias_g = res
    flat = lambda v: v.reshape(-1)
    return (out, ingrad, flat(gain_g), flat(skip_g), flat(lre_g), flat(lim_g), flat(step_g),
            bre_g, bim_g, cre_g.T, cim_g.T, glu_g, flat(bias_g))


def solution(mesh):
    in_specs = (
        P("dp", "ctx", None),
        P("dp"),
        P("dp"),
        P("dp"),
        P(("tp", "dp")),
        P(("tp", "dp")),
        P(("tp", "dp")),
        P("tp", "dp"),
        P("tp", "dp"),
        P("dp", "tp"),
        P("dp", "tp"),
        P("dp", "tp"),
        P(("tp", "dp")),
        P("dp", "ctx", "tp"),
    )
    out_specs = (
        P("dp", "ctx", "tp"),
        P("dp", "ctx", "tp"),
        P("dp"),
        P("dp"),
        P(("tp", "dp")),
        P(("tp", "dp")),
        P(("tp", "dp")),
        P("tp", "dp"),
        P("tp", "dp"),
        P("dp", "tp"),
        P("dp", "tp"),
        P("dp", "tp"),
        P(("tp", "dp")),
    )
    sizes = tuple(mesh.shape[name] for name in ("dp", "ctx", "tp"))

    def block(*args):
        seqs, _, feat = args[0].shape
        units = args[11].shape[1]
        if sizes == (2, 4, 4) and seqs % sizes[2] == 0 and units % 128 == 0:
            return token_split(sizes, *args)
        return on_device(*args)

    return jax.shard_map(
        block, mesh=mesh, in_specs=in_specs, out_specs=out_specs, check_vma=False
    )
```

```python
import functools

import jax
import jax.numpy as jnp
from jax import lax
from jax.experimental import pallas as pl
from jax.experimental.pallas import tpu as pltpu
from jax.sharding import PartitionSpec as P

epsilon = 1e-05


def carried_in(value, axis, combine, identity, reverse):
    count, index = (lax.axis_size(axis), lax.axis_index(axis))
    everything = jax.tree.map(lambda part: lax.all_gather(part, axis), value)
    start = jax.tree.map(
        lambda part, zero: jnp.broadcast_to(jnp.asarray(zero, part.dtype), part.shape),
        value,
        identity,
    )

    def lap(k, before):
        at = count - 1 - k if reverse else k
        reached = at > index if reverse else at < index
        new = combine(before, jax.tree.map(lambda part: part[at], everything))
        return jax.tree.map(lambda a, b: jnp.where(reached, a, b), new, before)

    return lax.fori_loop(0, count, lap, start)


def contract(left, right, left_dim, right_dim):
    return lax.dot_general(
        left, right, (((left_dim,), (right_dim,)), ((), ())), preferred_element_type=jnp.float32
    )


def combine(earlier, later):
    e_re, e_im, eb_re, eb_im = earlier
    l_re, l_im, lb_re, lb_im = later
    return (
        e_re * l_re - e_im * l_im,
        e_re * l_im + e_im * l_re,
        l_re * eb_re - l_im * eb_im + lb_re,
        l_re * eb_im + l_im * eb_re + lb_im,
    )


def discretize(lam_re, lam_im, step_log, mat_re, mat_im):
    step = jnp.exp(step_log)
    magnitude = jnp.exp(lam_re * step)
    decay_re = magnitude * jnp.cos(lam_im * step)
    decay_im = magnitude * jnp.sin(lam_im * step)
    denom = lam_re * lam_re + lam_im * lam_im
    coef_re = ((decay_re - 1.0) * lam_re + decay_im * lam_im) / denom
    coef_im = (decay_im * lam_re - (decay_re - 1.0) * lam_im) / denom
    bar_re = coef_re[:, None] * mat_re - coef_im[:, None] * mat_im
    bar_im = coef_re[:, None] * mat_im + coef_im[:, None] * mat_re
    return (decay_re, decay_im, jnp.concatenate([bar_re, bar_im], 0))


def normalize(tokens, gain):
    mean_val = jnp.mean(tokens, -1, keepdims=True)
    centered = tokens - mean_val
    var_val = jnp.mean(centered * centered, -1, keepdims=True)
    return centered * lax.rsqrt(var_val + epsilon) * gain


def powers(lam_re, lam_im, step_log, count):
    step = jnp.exp(step_log)
    exponent = (jnp.arange(count, dtype=jnp.float32) + 1.0)[:, None]
    magnitude = jnp.exp(exponent * lam_re * step)
    return (
        magnitude * jnp.cos(exponent * lam_im * step),
        magnitude * jnp.sin(exponent * lam_im * step),
    )


def on_device(
    inputs,
    lengths,
    norm_gain,
    skip_weight,
    lambda_re,
    lambda_im,
    log_step,
    b_re,
    b_im,
    c_re,
    c_im,
    glu_weight,
    glu_bias,
    out_grad,
):
    full_bre, full_bim, full_cre, full_cim, full_glu = (
        lax.all_gather(b_re, "dp", axis=1, tiled=True),
        lax.all_gather(b_im, "dp", axis=1, tiled=True),
        lax.all_gather(c_re, "dp", axis=0, tiled=True),
        lax.all_gather(c_im, "dp", axis=0, tiled=True),
        lax.all_gather(glu_weight, "dp", axis=0, tiled=True),
    )
    gain, skip_full, lam_re, lam_im, step_log, bias_vec = (
        lax.all_gather(norm_gain, "dp", axis=0, tiled=True),
        lax.all_gather(skip_weight, "dp", axis=0, tiled=True),
        lax.all_gather(lambda_re, "dp", axis=0, tiled=True),
        lax.all_gather(lambda_im, "dp", axis=0, tiled=True),
        lax.all_gather(log_step, "dp", axis=0, tiled=True),
        lax.all_gather(glu_bias, "dp", axis=0, tiled=True),
    )
    seq_count, blk_len, feat_dim = inputs.shape
    row_count = seq_count * blk_len
    state_count = full_bre.shape[0]
    unit_count = full_glu.shape[1]
    tp_rank = lax.axis_index("tp")
    unit_start = tp_rank * unit_count
    positions = lax.axis_index("ctx") * blk_len + jnp.arange(blk_len, dtype=jnp.int32)
    valid_mask = (positions[None, :] < lengths[:, None]).astype(jnp.float32).reshape(row_count, 1)
    tokens = inputs.astype(jnp.float32).reshape(row_count, feat_dim)
    tokens_mine = lax.dynamic_slice_in_dim(tokens, unit_start, unit_count, 1)
    cotangent = out_grad.astype(jnp.float32).reshape(row_count, unit_count)
    normed_f, norm_pull = jax.vjp(normalize, tokens, gain)
    normed_b = normed_f.astype(jnp.bfloat16)
    normed_r = normed_b.astype(jnp.float32)
    (decay_re, decay_im, bar_full), disc_pull = jax.vjp(
        discretize,
        lam_re,
        lam_im,
        step_log,
        full_bre.astype(jnp.float32),
        full_bim.astype(jnp.float32),
    )
    bar_b = bar_full.astype(jnp.bfloat16)
    drive = contract(normed_b, bar_b, 1, 1).reshape(seq_count, blk_len, 2 * state_count)
    full_re = jnp.broadcast_to(decay_re, (seq_count, blk_len, state_count))
    full_im = jnp.broadcast_to(decay_im, (seq_count, blk_len, state_count))
    local_states = lax.associative_scan(
        combine, (full_re, full_im, drive[..., :state_count], drive[..., state_count:]), axis=1
    )
    pow_re, pow_im = powers(lam_re, lam_im, step_log, blk_len)
    identity = (
        jnp.ones((1, state_count), jnp.float32),
        jnp.zeros((1, state_count), jnp.float32),
        jnp.zeros((seq_count, state_count), jnp.float32),
        jnp.zeros((seq_count, state_count), jnp.float32),
    )
    incoming = carried_in(
        (pow_re[-1:], pow_im[-1:], local_states[2][:, -1], local_states[3][:, -1]),
        "ctx",
        combine,
        identity,
        False,
    )
    in_re = incoming[2][:, None, :]
    in_im = incoming[3][:, None, :]
    state_re = local_states[2] + pow_re * in_re - pow_im * in_im
    state_im = local_states[3] + pow_re * in_im + pow_im * in_re
    states_b = (
        jnp.concatenate([state_re, state_im], -1)
        .reshape(row_count, 2 * state_count)
        .astype(jnp.bfloat16)
    )
    c_stack = jnp.concatenate([full_cre, -full_cim], 1)
    ssm_part = contract(states_b, c_stack, 1, 1)
    ssm_full = lax.psum(ssm_part.astype(jnp.bfloat16), "tp").astype(jnp.float32)
    pre_full = ssm_full + skip_full * normed_r
    gelu_full, gelu_pull = jax.vjp(jax.nn.gelu, pre_full)
    gelu_b = gelu_full.astype(jnp.bfloat16)
    gelu_part = lax.dynamic_slice_in_dim(gelu_b, unit_start, unit_count, 1)
    gelu_mine = gelu_part.astype(jnp.float32)
    gate = contract(gelu_b, full_glu, 1, 0) + bias_vec
    gate_sig = jax.nn.sigmoid(gate)
    output = (
        (valid_mask * (tokens_mine + gelu_mine * gate_sig))
        .astype(jnp.bfloat16)
        .reshape(seq_count, blk_len, unit_count)
    )
    branch_grad = valid_mask * cotangent
    gate_grad = branch_grad * gelu_mine * gate_sig * (1.0 - gate_sig)
    bias_grad = jnp.sum(gate_grad, 0)
    gate_b = gate_grad.astype(jnp.bfloat16)
    glu_grad = contract(gelu_b, gate_b, 0, 0)
    gelu_grad = contract(gate_b, full_glu, 1, 1)
    own_cols = (
        lax.dynamic_slice_in_dim(gelu_grad, unit_start, unit_count, 1) + branch_grad * gate_sig
    )
    gelu_grad = lax.dynamic_update_slice_in_dim(gelu_grad, own_cols, unit_start, 1)
    gelu_back = lax.psum(gelu_grad, "tp")
    (pre_grad,) = gelu_pull(gelu_back)
    skip_grad = jnp.sum(pre_grad * normed_r, 0)
    pre_b = pre_grad.astype(jnp.bfloat16)
    state_grad = contract(pre_b, c_stack, 1, 0).reshape(seq_count, blk_len, 2 * state_count)
    c_grad = contract(pre_b, states_b, 0, 0)
    back_local = lax.associative_scan(
        combine,
        (full_re, -full_im, state_grad[..., :state_count], state_grad[..., state_count:]),
        axis=1,
        reverse=True,
    )
    later_adj = carried_in(
        (pow_re[-1:], -pow_im[-1:], back_local[2][:, 0], back_local[3][:, 0]),
        "ctx",
        combine,
        identity,
        True,
    )
    rev_re = pow_re[::-1]
    rev_im = -pow_im[::-1]
    next_re = later_adj[2][:, None, :]
    next_im = later_adj[3][:, None, :]
    adj_re = back_local[2] + rev_re * next_re - rev_im * next_im
    adj_im = back_local[3] + rev_re * next_im + rev_im * next_re
    prev_re = jnp.concatenate([in_re, state_re[:, :-1]], 1)
    prev_im = jnp.concatenate([in_im, state_im[:, :-1]], 1)
    decay_grad_re = jnp.sum(adj_re * prev_re + adj_im * prev_im, (0, 1))
    decay_grad_im = jnp.sum(adj_im * prev_re - adj_re * prev_im, (0, 1))
    adj_b = (
        jnp.concatenate([adj_re, adj_im], -1)
        .reshape(row_count, 2 * state_count)
        .astype(jnp.bfloat16)
    )
    bar_grad = contract(adj_b, normed_b, 0, 0)
    normed_part = contract(adj_b, bar_b, 1, 0)
    normed_sum = lax.psum(normed_part.astype(jnp.bfloat16), "tp").astype(jnp.float32)
    normed_grad = normed_sum + skip_full * pre_grad
    token_grad, gain_grad = norm_pull(normed_grad)
    input_grad = (
        valid_mask * cotangent + lax.dynamic_slice_in_dim(token_grad, unit_start, unit_count, 1)
    ).reshape(seq_count, blk_len, unit_count)
    grad_cre = c_grad[:, :state_count]
    grad_cim = -c_grad[:, state_count:]
    lre_grad, lim_grad, step_grad, bre_grad, bim_grad = disc_pull(
        (decay_grad_re, decay_grad_im, bar_grad)
    )
    shards = (
        lax.psum_scatter(
            gain_grad.astype(jnp.bfloat16), "dp", scatter_dimension=0, tiled=True
        ).astype(jnp.float32),
        lax.psum_scatter(
            skip_grad.astype(jnp.bfloat16), "dp", scatter_dimension=0, tiled=True
        ).astype(jnp.float32),
        lax.psum_scatter(
            lre_grad.astype(jnp.bfloat16), "dp", scatter_dimension=0, tiled=True
        ).astype(jnp.float32),
        lax.psum_scatter(
            lim_grad.astype(jnp.bfloat16), "dp", scatter_dimension=0, tiled=True
        ).astype(jnp.float32),
        lax.psum_scatter(
            step_grad.astype(jnp.bfloat16), "dp", scatter_dimension=0, tiled=True
        ).astype(jnp.float32),
        lax.psum_scatter(
            bias_grad.astype(jnp.bfloat16), "dp", scatter_dimension=0, tiled=True
        ).astype(jnp.float32),
        lax.psum_scatter(
            bre_grad.astype(jnp.bfloat16), "dp", scatter_dimension=1, tiled=True
        ).astype(jnp.float32),
        lax.psum_scatter(
            bim_grad.astype(jnp.bfloat16), "dp", scatter_dimension=1, tiled=True
        ).astype(jnp.float32),
        lax.psum_scatter(
            grad_cre.astype(jnp.bfloat16), "dp", scatter_dimension=0, tiled=True
        ).astype(jnp.float32),
        lax.psum_scatter(
            grad_cim.astype(jnp.bfloat16), "dp", scatter_dimension=0, tiled=True
        ).astype(jnp.float32),
        lax.psum_scatter(
            glu_grad.astype(jnp.bfloat16), "dp", scatter_dimension=0, tiled=True
        ).astype(jnp.float32),
    )
    summed = (
        lax.psum(shards[0].astype(jnp.bfloat16), "ctx").astype(jnp.float32),
        lax.psum(shards[1].astype(jnp.bfloat16), "ctx").astype(jnp.float32),
        lax.psum(shards[2].astype(jnp.bfloat16), "ctx").astype(jnp.float32),
        lax.psum(shards[3].astype(jnp.bfloat16), "ctx").astype(jnp.float32),
        lax.psum(shards[4].astype(jnp.bfloat16), "ctx").astype(jnp.float32),
        lax.psum(shards[5].astype(jnp.bfloat16), "ctx").astype(jnp.float32),
        lax.psum(shards[6].astype(jnp.bfloat16), "ctx").astype(jnp.float32),
        lax.psum(shards[7].astype(jnp.bfloat16), "ctx").astype(jnp.float32),
        lax.psum(shards[8].astype(jnp.bfloat16), "ctx").astype(jnp.float32),
        lax.psum(shards[9].astype(jnp.bfloat16), "ctx").astype(jnp.float32),
        lax.psum(shards[10].astype(jnp.bfloat16), "ctx").astype(jnp.float32),
    )
    return (
        output,
        input_grad,
        summed[0],
        summed[1],
        summed[2],
        summed[3],
        summed[4],
        summed[6],
        summed[7],
        summed[8],
        summed[9],
        summed[10],
        summed[5],
    )


MESH = pl.DeviceIdType.MESH
SQ2PI = 0.7978845608028654


def nt(a, b):
    return lax.dot_general(a, b, (((1,), (1,)), ((), ())), preferred_element_type=jnp.float32)


def nn(a, b):
    return lax.dot_general(a, b, (((1,), (0,)), ((), ())), preferred_element_type=jnp.float32)


def tn(a, b):
    return lax.dot_general(a, b, (((0,), (0,)), ((), ())), preferred_element_type=jnp.float32)


def cmul(ar, ai, br, bi):
    return ar * br - ai * bi, ar * bi + ai * br


def lane(start, size):
    return pl.ds(pl.multiple_of(start, 128), size)


def fused_body(geo, extra, *refs):
    D, C, T, S, L, H, N, U = geo
    R = S * L
    NS = N // T
    HD = H // D
    f32, bf16 = jnp.float32, jnp.bfloat16
    (len_ref, x_hbm, og_hbm, bre, bim, cre, cim, glu_hbm, gain_h, skip_h, lre_h, lim_h, stp_h, bias_h,
     out_hbm, tg_hbm, fc_hbm, fg_hbm, fb_hbm, fv_hbm) = refs[:20]
    (xv, nrm, xh, rs, raw, st, sb, tmp, act, gp, sig, ogv, ob, gl, pg, plb, mu, nb, tgb,
     xe, nrme, rawe, sbe, acte, tmpe, obe,
     w4, gt, smr, cst, ce, cer, cin, gc, gg, gb, r1c, r1g, r1b, s1c, s1g, s1b, r2c, r2g, r2b,
     s2c, s2g, s2b, r3c, r3g, r3b, s3c, s3g, r4c, r4g,
     q5c, q5g, q5b, vv, vr1, vr2, vr3, accv, pk, sm_ref, glu, gain_in, skip_in, lre_in, lim_in, stp_in, bias_in,
     lsem, ssem, rsem) = refs[20:]
    d, c, t = lax.axis_index("dp"), lax.axis_index("ctx"), lax.axis_index("tp")
    half = t // 2
    t1 = t + 1 - 2 * lax.rem(t, 2)
    t2 = t + 2 - 4 * half
    t3 = T - 1 - t
    z1, z2, z3 = (d, c, t1), (d, c, t2), (d, c, t3)
    zpeer = [(d, c, lax.rem(t + k, T)) for k in range(1, T)]
    cpeer = [(d, lax.rem(c + k, C), t) for k in range(1, C)]
    sib = (1 - d, c, t)
    xpeer = [(1 - d, c, lax.rem(t + k, T)) for k in range(1, T)]
    everyone = zpeer + cpeer + [sib] + xpeer
    erank = [t2, t3][:len(extra)]
    eoff = [L * sum(extra[:k]) for k in range(len(extra))]

    count = [0]
    started = []

    def remote(src, dst, peer):
        i = count[0]
        count[0] += 1
        cp = pltpu.make_async_remote_copy(
            src_ref=src, dst_ref=dst, send_sem=ssem.at[i], recv_sem=rsem.at[i],
            device_id=peer, device_id_type=MESH)
        cp.start()
        started.append(cp)
        return cp

    def arrived(*cps):
        for cp in cps:
            cp.wait_recv()

    nlocal = [0]

    def local(src, dst):
        cp = pltpu.make_async_copy(src, dst, lsem.at[nlocal[0]])
        nlocal[0] += 1
        cp.start()
        return cp

    def rows_at(start, size):
        return pl.ds(pl.multiple_of(start, size), size)

    barrier = pltpu.get_barrier_semaphore()
    for p in everyone:
        pl.semaphore_signal(barrier, inc=1, device_id=p, device_id_type=MESH)
    cp_small = [local(a, b) for a, b in (
        (lre_h, lre_in), (lim_h, lim_in), (stp_h, stp_in), (bias_h, bias_in), (gain_h, gain_in), (skip_h, skip_in))]
    mine = rows_at(R * t, R)
    cp_pk = [local(a, pk.at[k]) for k, a in enumerate((bre, bim, cre, cim))] + [local(glu_hbm, glu)]
    cx = local(x_hbm.at[mine], xv)
    cxe = [local(x_hbm.at[pl.ds(pl.multiple_of(R * e, R), L * n)], xe.at[pl.ds(o, L * n)])
           for e, n, o in zip(erank, extra, eoff)]
    co = local(og_hbm.at[mine], ogv.at[:, lane(U * t, U)])
    dl = lane(HD * d, HD)
    dr_ = rows_at(HD * d, HD)
    tl = lane(U * t, U)
    sm_ref[...] = jnp.zeros_like(sm_ref)
    for cp in cp_small:
        cp.wait()
    own = coefficients(lre_in[...], lim_in[...], stp_in[...])
    for k in range(4):
        sm_ref[k:k + 1, 0:NS // D] = own[k]
    sm_ref[4:5, 0:U // D] = bias_in[...]
    sm_ref[5:6, :] = gain_in[...]
    sm_ref[6:7, :] = skip_in[...]
    me8 = d * T + t
    smr[me8] = sm_ref[...]
    accv[...] = jnp.zeros_like(accv)
    vv[...] = jnp.zeros_like(vv)
    for cp in cp_pk:
        cp.wait()
    for k in range(4):
        w4[k, t, :, dl] = pk[k]
    gt[dr_, tl] = glu[...]
    cx.wait()

    def standard(x):
        cen = x - jnp.mean(x, -1, keepdims=True)
        rstd = lax.rsqrt(jnp.mean(cen * cen, -1, keepdims=True) + epsilon)
        return cen * rstd, rstd

    def ln_tile(i, _):
        for u in range(4):
            rows = rows_at(i * 128 + u * 32, 32)
            xn, rstd = standard(xv[rows, :].astype(f32))
            xh[rows, :] = xn
            rs[rows, :] = jnp.broadcast_to(rstd, (32, 128))
        return 0

    lax.fori_loop(0, R // 128, ln_tile, 0)
    pl.semaphore_wait(barrier, len(everyone))

    gq, hq = c // 2, lax.rem(c, 2)
    ql = lane(128 * hq, 128)
    wl = lane(HD * d + 128 * hq, 128)
    uq = HD // C
    gown = rows_at(uq * c, uq)
    grow = rows_at(HD * d + uq * c, uq)
    pair = rows_at(2 - 2 * half, 2)
    pairl = lane(2 * U * (1 - half), 2 * U)

    qb, qc = gq, 2 + gq
    far_b = [remote(pk.at[qb, :, ql], w4.at[qb, t, :, wl], p) for p in (z3, z2)]
    small = [remote(sm_ref, smr.at[me8], p) for p in zpeer + [sib] + xpeer]
    near_b = remote(pk.at[0:2], w4.at[0:2, t, :, dl], z1)
    w3b = [remote(pk.at[0:2], w4.at[0:2, t, :, dl], sib)]

    def spread(blk, *cps):
        arrived(*cps)
        return [remote(blk, blk, p) for p in cpeer]

    gl1, gl2 = lane(U * t1, U), lane(U * t2, U)
    w2b = spread(w4.at[qb, pair, :, wl], *far_b)
    far_c = [remote(pk.at[qc, :, ql], w4.at[qc, t, :, wl], p) for p in (z3, z2)]
    far_g = [remote(glu.at[gown], gt.at[grow, tl], p) for p in (z3, z2)]
    near_c = remote(pk.at[2:4], w4.at[2:4, t, :, dl], z1)
    near_g = remote(glu, gt.at[dr_, tl], z1)
    w3c = [remote(pk.at[2:4], w4.at[2:4, t, :, dl], sib)]
    w3g = [remote(glu, gt.at[dr_, tl], sib)]

    def cot_send(s):
        return [remote(og_hbm.at[rows_at(R * p[2] + L * s, L)], ogv.at[pl.ds(L * s, L), tl], p) for p in zpeer]

    arrived(*small)
    zero = jnp.zeros((8, H - HD), f32)
    vec = jnp.zeros((8, H), f32)
    bias = jnp.zeros((8, H), f32)
    for dd in range(D):
        for tt in range(T):
            ext = jnp.concatenate([smr[dd * T + tt], zero], 1)
            place = tt * D + dd
            vec = vec + (pltpu.roll(ext, place * (NS // D), 1) if place else ext)
            bias = bias + (pltpu.roll(ext, place * (U // D), 1) if place else ext)
    both = jnp.concatenate([smr[t], smr[T + t]], 1)
    gain_r, skip_r, bias_r = both[5:6, :], both[6:7, :], bias[4:5, :]

    arrived(near_b)
    w3b.append(remote(w4.at[0:2, t1, :, dl], w4.at[0:2, t1, :, dl], sib))
    row8 = lax.broadcasted_iota(jnp.int32, (8, N), 0)
    full = lambda v, k, n: jnp.broadcast_to(v[k:k + 1, :n], (8, n))
    dr, di = full(vec, 0, N), full(vec, 1, N)
    cr, ci = full(vec, 2, N), full(vec, 3, N)
    pows = {1: (dr, di)}
    for k in range(2, 9):
        pows[k] = cmul(*pows[k - 1], dr, di)
    for n_, k in ((0, 1), (1, 2), (2, 4)):
        keep = row8 >= k
        cst[2 * n_] = jnp.where(keep, pows[k][0], 0.0)
        cst[2 * n_ + 1] = jnp.where(keep, pows[k][1], 0.0)
        keep = row8 < 8 - k
        cst[8 + 2 * n_] = jnp.where(keep, pows[k][0], 0.0)
        cst[8 + 2 * n_ + 1] = jnp.where(keep, -pows[k][1], 0.0)
    pr, pi, qr, qi = pows[1][0], pows[1][1], pows[8][0], -pows[8][1]
    for r in range(1, 8):
        pr = jnp.where(row8 == r, pows[r + 1][0], pr)
        pi = jnp.where(row8 == r, pows[r + 1][1], pi)
        qr = jnp.where(row8 == r, pows[8 - r][0], qr)
        qi = jnp.where(row8 == r, -pows[8 - r][1], qi)
    cst[6], cst[7], cst[14], cst[15] = pr, pi, qr, qi
    cst[16], cst[17] = pows[8]
    cst[18], cst[19] = cr, ci
    big = pows[8]
    n_ = 8
    while n_ < L:
        big = cmul(*big, *big)
        n_ *= 2
    cst[20], cst[21] = big

    def nrm_tile(i, _):
        rows = rows_at(i * 32, 32)
        nrm[rows, :] = (xh[rows, :] * gain_r).astype(bf16)
        return 0

    lax.fori_loop(0, R // 32, nrm_tile, 0)
    og = [cot_send(0)]

    def lne_tile(i, _):
        for u in range(4):
            rows = rows_at(i * 128 + u * 32, 32)
            nrme[rows, :] = (standard(xe[rows, :].astype(f32))[0] * gain_r).astype(bf16)
        return 0

    def seq_rows(s):
        return rows_at(s * L, L)

    wv = w4.reshape(4, N, H)

    def drive(src, off, dst, n, j):
        rows = rows_at(128 * j, 128)
        both_ = nt(src[pl.ds(off, n * L), :], jnp.concatenate([wv[0, rows, :], wv[1, rows, :]], 0))
        dst[pl.ds(0, n * L), lane(128 * j, 128)] = both_[:, 0:128]
        dst[pl.ds(0, n * L), lane(N + 128 * j, 128)] = both_[:, 128:256]

    def scan(src, dst, groups, base, coef, reverse):
        e = 0 if reverse else 7

        def tile(i, carry):
            carry = list(carry)
            ii = L // 32 - 1 - i if reverse else i
            for g, (rb, l0) in enumerate(groups):
                lr_, li_ = lane(l0, 128), lane(N + l0, 128)
                con = [cst[base + k, :, lr_] for k in range(8)]
                e0 = cst[16, :, lr_]
                e1 = -cst[17, :, lr_] if reverse else cst[17, :, lr_]
                loc = []
                for u in range(4):
                    uu = 3 - u if reverse else u
                    rows = rows_at(rb + ii * 32 + uu * 8, 8)
                    ar, ai = src[rows, lr_], src[rows, li_]
                    if coef:
                        ar, ai = cmul(cst[18, :, lr_], cst[19, :, lr_], ar, ai)
                    else:
                        ai = -ai
                    for n_, k in ((0, 1), (1, 2), (2, 4)):
                        sh = 8 - k if reverse else k
                        br, bi = pltpu.roll(ar, sh, 0), pltpu.roll(ai, sh, 0)
                        mr, mi = con[2 * n_], con[2 * n_ + 1]
                        ar, ai = ar + mr * br - mi * bi, ai + mr * bi + mi * br
                    loc.append((rows, ar, ai))
                kr, ki = carry[2 * g], carry[2 * g + 1]
                for rows, ar, ai in loc:
                    dst[rows, lr_] = ar + con[6] * kr - con[7] * ki
                    dst[rows, li_] = ai + con[6] * ki + con[7] * kr
                    endr = jnp.broadcast_to(ar[e:e + 1, :], (8, 128))
                    endi = jnp.broadcast_to(ai[e:e + 1, :], (8, 128))
                    kr, ki = endr + e0 * kr - e1 * ki, endi + e0 * ki + e1 * kr
                carry[2 * g], carry[2 * g + 1] = kr, ki
            return tuple(carry)

        z = jnp.zeros((8, 128), f32)
        return lax.fori_loop(0, L // 32, tile, (z,) * (2 * len(groups)))

    def begin(src, off, dst, out, slot, n, j):
        drive(src, off, dst, n, j)
        fin = scan(dst, out, [(s * L, 128 * j) for s in range(n)], 0, True, False)
        for s in range(n):
            ce[slot, pl.ds(s, 1), lane(128 * j, 128)] = fin[2 * s][0:1, :]
            ce[slot, pl.ds(n + s, 1), lane(128 * j, 128)] = fin[2 * s + 1][0:1, :]

    def rest(what, tiles_=2):
        def step(k, _):
            begin(*what, 1 + k * (1 - 2 * half) if tiles_ == 2 else k)
            return 0

        lax.fori_loop(0, tiles_, step, 0)
        slot = what[4]
        return [remote(ce.at[slot], cer.at[slot, k], p) for k, p in enumerate(cpeer)]

    def incoming(slot, cps, n, forward):
        arrived(*cps)
        bg = (cst[20, 0:1, :], cst[21, 0:1, :])
        wt = (jnp.ones((1, N), f32), jnp.zeros((1, N), f32))
        accr = jnp.zeros((n, N), f32)
        acci = jnp.zeros((n, N), f32)
        for k in range(1, C):
            got = cer[slot, k - 1] if forward else cer[slot, C - 1 - k]
            has = (c >= k) if forward else (c + k < C)
            w = jnp.where(has, 1.0, 0.0)
            wi = wt[1] if forward else -wt[1]
            ur, ui = cmul(wt[0], wi, got[0:n, :], got[n:2 * n, :])
            accr = accr + w * ur
            acci = acci + w * ui
            wt = cmul(*wt, *bg)
        cin[slot, 0:n, :] = accr
        cin[slot, n:2 * n, :] = acci

    def entering(slot, k, lanes):
        return jnp.broadcast_to(cin[slot, pl.ds(k, 1), lanes], (8, 128))

    def fix_batch(ref, dst, slot, keep, n):
        def fix_lanes(j, _):
            lr_, li_ = lane(128 * j, 128), lane(N + 128 * j, 128)
            p0, p1 = cst[6, :, lr_], cst[7, :, lr_]
            e0, e1 = cst[16, :, lr_], cst[17, :, lr_]
            q0 = tuple(entering(slot, k * n + s, lr_) for s in range(n) for k in range(2))

            def tile(i, q):
                q = list(q)
                for s in range(n):
                    rr, ri = [], []
                    for h in range(2):
                        rows = rows_at(s * L + i * 16 + 8 * h, 8)
                        vr, vi = cmul(p0, p1, q[2 * s], q[2 * s + 1])
                        ar, ai = ref[rows, lr_] + vr, ref[rows, li_] + vi
                        if keep:
                            ref[rows, lr_] = ar
                            ref[rows, li_] = ai
                        rr.append(ar)
                        ri.append(ai)
                        q[2 * s], q[2 * s + 1] = cmul(q[2 * s], q[2 * s + 1], e0, e1)
                    rows = rows_at(s * L + i * 16, 16)
                    dst[rows, lr_] = jnp.concatenate(rr, 0).astype(bf16)
                    dst[rows, li_] = (-jnp.concatenate(ri, 0)).astype(bf16)
                return tuple(q)

            lax.fori_loop(0, L // 16, tile, q0)
            return 0

        lax.fori_loop(0, N // 128, fix_lanes, 0)

    def each_seq(f, n=S):
        f(pl.ds(0, n * L))

    def tiles(f, lo=0, hi=R // 32):
        def step(i, _):
            f(i, rows_at(i * 32, 32))
            return 0

        lax.fori_loop(lo, hi, step, 0)

    def valid_of(i, rank):
        s = i // (L // 32)
        pos = c * L + lax.rem(i, L // 32) * 32 + lax.broadcasted_iota(jnp.int32, (32, 1), 0)
        return jnp.where(pos < len_ref[S * rank + s], 1.0, 0.0)

    def logistic(v):
        return 0.5 + 0.5 * jnp.tanh(0.5 * v)

    batches = [(nrm, 0, raw, st, 0, S)] + [
        (nrme, eoff[k], rawe.at[k], rawe.at[k], 1 + k, extra[k]) for k in range(len(extra))]
    arrived(*w3b)
    begin(*batches[0], 2 * half)
    w2c = spread(w4.at[qc, pair, :, wl], *far_c)
    w2g = spread(gt.at[grow, pairl], *far_g)
    og.append(cot_send(1))
    for cp in cxe:
        cp.wait()
    lax.fori_loop(0, extra[0] * L // 128, lne_tile, 0)
    arrived(*w2b)
    w3b2 = remote(w4.at[0:2, pair, :, dl], w4.at[0:2, pair, :, dl], sib)
    og.append(cot_send(2))
    begin(*batches[1], 2 * half)
    arrived(w3b2)
    fce = [rest(batches[0])]
    arrived(near_c)
    w3c.append(remote(w4.at[2:4, t1, :, dl], w4.at[2:4, t1, :, dl], sib))
    arrived(near_g)
    blk = gt.at[dr_, gl1]
    w3g.append(remote(blk, blk, sib))
    arrived(*w2c)
    w3c.append(remote(w4.at[2:4, pair, :, dl], w4.at[2:4, pair, :, dl], sib))
    arrived(*w2g)
    blk = gt.at[dr_, pairl]
    w3g.append(remote(blk, blk, sib))
    fce.append(rest(batches[1]))
    if len(extra) > 1:
        lax.fori_loop(eoff[1] // 128, (eoff[1] + extra[1] * L) // 128, lne_tile, 0)
    incoming(0, fce[0], S, True)
    fix_batch(st, sb, 0, True, S)
    arrived(*w3c)

    def ssm_own(rows):
        tmp[rows, :] = nn(sb[rows, :], w4[2:4].reshape(2 * N, H))

    each_seq(ssm_own)

    def gelu_tile(i, rows):
        pre = tmp[rows, :] + skip_r * nrm[rows, :].astype(f32)
        sq = pre * pre
        th = jnp.tanh(pre * (SQ2PI + (SQ2PI * 0.044715) * sq))
        hf = 0.5 + 0.5 * th
        act[rows, :] = (pre * hf).astype(bf16)
        gp[rows, :] = hf + 0.5 * pre * (1.0 - th * th) * (SQ2PI + (3 * 0.044715 * SQ2PI) * sq)

    tiles(gelu_tile)
    arrived(*w3g)

    def gate_own(rows):
        tmp[rows, :] = nn(act[rows, :], gt[...])

    each_seq(gate_own)

    def out_tile(i, rows):
        sg = logistic(tmp[rows, :] + bias_r)
        sig[rows, :] = sg
        o = valid_of(i, t) * (xv[rows, :].astype(f32) + act[rows, :].astype(f32) * sg)
        ob[rows, :] = o.astype(bf16)

    tiles(out_tile)
    outc = [remote(ob.at[:, lane(U * t1, U)], out_hbm.at[mine, :], z1)]
    done3 = extra[1] if len(extra) > 1 else 0
    if done3 < S:
        part = pl.ds(done3 * L, (S - done3) * L)
        there3 = pl.ds(pl.multiple_of(R * t + done3 * L, L), (S - done3) * L)
        outc.append(remote(ob.at[part, lane(U * t3, U)], out_hbm.at[there3, :], z3))
    locals_ = [local(ob.at[:, tl], out_hbm.at[mine, :])]

    def fold(v):
        return jnp.sum(v.reshape(4, 8, v.shape[-1]), 0)

    def seq_tiles(s, f):
        def step(i, acc):
            return acc + fold(f(i, rows_at(i * 32, 32)))

        return lax.fori_loop(s * (L // 32), (s + 1) * (L // 32), step, jnp.zeros((8, H), f32))

    co.wait()

    def gate_tile(i, rows):
        sg = sig[rows, :]
        direct = valid_of(i, t) * ogv[rows, :].astype(f32) * sg
        g = direct * act[rows, :].astype(f32) * (1.0 - sg)
        gl[rows, :] = g.astype(bf16)
        sig[rows, :] = direct
        return g

    def pre_tile(i, rows):
        p = (tmp[rows, :] + sig[rows, :]) * gp[rows, :]
        pg[rows, :] = p
        plb[rows, :] = p.astype(bf16)
        return p * nrm[rows, :].astype(f32)

    def back_one(s):
        arrived(*og[s])
        rows = pl.ds(s * L, L)
        accv[0] += seq_tiles(s, gate_tile)
        tmp[rows, :] = nt(gl[rows, :], gt[...])
        accv[1] += seq_tiles(s, pre_tile)
        mu[rows, :] = nt(plb[rows, :], w4[2:4].reshape(2 * N, H))
        fin = scan(mu, mu, [(s * L, 128 * j) for j in range(N // 128)], 8, False, True)
        for j in range(N // 128):
            ce[3 + s, 0:1, 128 * j:128 * j + 128] = fin[2 * j][0:1, :]
            ce[3 + s, 1:2, 128 * j:128 * j + 128] = fin[2 * j + 1][0:1, :]
        return [remote(ce.at[3 + s], cer.at[3 + s, k], p) for k, p in enumerate(cpeer)]

    row1 = lax.broadcasted_iota(jnp.int32, (8, 128), 0)

    def back_two(s, cps):
        incoming(3 + s, cps, 1, False)
        nj = N // 128
        q0 = tuple(entering(3 + s, k, lane(128 * j, 128)) for j in range(nj) for k in range(2))
        z = jnp.zeros((8, 128), f32)

        def tile(i, carry):
            q, m, acc = list(carry[:2 * nj]), list(carry[2 * nj:4 * nj]), list(carry[4 * nj:])
            ii = L // 16 - 1 - i
            for j in range(nj):
                lr_, li_ = lane(128 * j, 128), lane(N + 128 * j, 128)
                p0, p1 = cst[14, :, lr_], cst[15, :, lr_]
                e0, e1 = cst[16, :, lr_], -cst[17, :, lr_]
                cfr, cfi = cst[18, :, lr_], cst[19, :, lr_]
                rr, ri = [None, None], [None, None]
                for h in (1, 0):
                    rows = rows_at(s * L + ii * 16 + 8 * h, 8)
                    vr, vi = cmul(p0, p1, q[2 * j], q[2 * j + 1])
                    ar, ai = mu[rows, lr_] + vr, mu[rows, li_] + vi
                    q[2 * j], q[2 * j + 1] = cmul(q[2 * j], q[2 * j + 1], e0, e1)
                    nr = jnp.where(row1 == 7, m[2 * j], pltpu.roll(ar, 7, 0))
                    ni = jnp.where(row1 == 7, m[2 * j + 1], pltpu.roll(ai, 7, 0))
                    m[2 * j] = jnp.broadcast_to(ar[0:1, :], (8, 128))
                    m[2 * j + 1] = jnp.broadcast_to(ai[0:1, :], (8, 128))
                    xr, xi = st[rows, lr_], st[rows, li_]
                    ur, ui = raw[rows, lr_], raw[rows, li_]
                    acc[4 * j] = acc[4 * j] + nr * xr + ni * xi
                    acc[4 * j + 1] = acc[4 * j + 1] + ni * xr - nr * xi
                    acc[4 * j + 2] = acc[4 * j + 2] + ar * ur + ai * ui
                    acc[4 * j + 3] = acc[4 * j + 3] + ai * ur - ar * ui
                    rr[h] = cfr * ar + cfi * ai
                    ri[h] = cfr * ai - cfi * ar
                rows = rows_at(s * L + ii * 16, 16)
                nb[rows, lr_] = jnp.concatenate(rr, 0).astype(bf16)
                nb[rows, li_] = jnp.concatenate(ri, 0).astype(bf16)
            return tuple(q) + tuple(m) + tuple(acc)

        fin = lax.fori_loop(0, L // 16, tile, q0 + q0 + (z,) * (4 * nj))
        for j in range(nj):
            for k in range(4):
                vv[3 + k:4 + k, 128 * j:128 * j + 128] += jnp.sum(fin[4 * nj + 4 * j + k], 0, keepdims=True)
        rows = pl.ds(s * L, L)
        tmp[rows, :] = nn(nb[rows, :], w4[0:2].reshape(2 * N, H))

        def tok_tile(i, acc):
            for u in range(4):
                rows = rows_at(s * L + i * 128 + u * 32, 32)
                n = tmp[rows, :] + skip_r * pg[rows, :]
                xt = xh[rows, :]
                h = n * gain_r
                m1 = jnp.mean(h, -1, keepdims=True)
                m2 = jnp.mean(h * xt, -1, keepdims=True)
                tgb[rows, :] = ((h - m1 - xt * m2) * rs[rows, 0:1]).astype(bf16)
                acc = acc + fold(n * xt)
            return acc

        accv[2] += lax.fori_loop(0, L // 128, tok_tile, jnp.zeros((8, H), f32))
        there = rows_at(R * t + L * s, L)
        locals_.append(local(tgb.at[rows, tl], tg_hbm.at[there, :]))

    def tok_send(s):
        there = rows_at(R * t + L * s, L)
        return [remote(tgb.at[pl.ds(s * L, L), lane(U * p[2], U)], tg_hbm.at[there, :], p) for p in (z3, z2, z1)]

    gcf, gbf = gc.reshape(2 * N, H), gb.reshape(2 * N, H)
    ol = lane(HD * (1 - d), HD)

    def gc_step(j, _):
        gcf[rows_at(j * 256, 256), :] = tn(sb[:, lane(j * 256, 256)], plb[...]).astype(bf16)
        return 0

    def gg_step(j, _):
        gg[rows_at(j * 256, 256), :] = tn(act[:, lane(j * 256, 256)], gl[...]).astype(bf16)
        return 0

    def gb_step(j, _):
        gbf[rows_at(j * 256, 256), :] = tn(nb[:, lane(j * 256, 256)], nrm[...]).astype(bf16)
        return 0

    hs = NS // 2

    def rs_ctx(p):
        return p // 2, rows_at(hs * lax.rem(p, 2), hs)

    gr = lambda p: rows_at(uq * p, uq)

    def add2(a, b):
        return (a.astype(f32) + b.astype(f32)).astype(bf16)

    def total(first_, buf, n):
        acc = first_.astype(f32)
        for k in range(n):
            acc = acc + buf[k].astype(f32)
        return acc

    def two_states(g, d1, r1, s1, r2):
        arrived(d1)
        s1[...] = add2(g[:, :, :, dl], r1[...])
        return [remote(s1.at[rs_ctx(p[1])[0], :, rs_ctx(p[1])[1], :], r2.at[k], p) for k, p in enumerate(cpeer)]

    def three_states(d2, s1, r2, s2, r3):
        arrived(*d2)
        s2[...] = total(s1[rs_ctx(c)[0], :, rs_ctx(c)[1], :], r2, C - 1).astype(bf16)
        return [remote(s2.at[t1], r3.at[0], z1), remote(s2.at[t3], r3.at[1], z1)]

    def four_states(d3, s2, r3, s3, r4):
        arrived(*d3)
        s3[0] = add2(s2[t], r3[0])
        s3[1] = add2(s2[t2], r3[1])
        return remote(s3.at[1], r4, z2)

    def spread_out(stage, out):
        locals_.append(local(stage, out.at[c]))
        return [remote(stage, out.at[c], p) for p in cpeer]

    def five(d4, s3, r4, stage, out):
        arrived(d4)
        stage[...] = add2(s3[0], r4[...])
        return spread_out(stage, out)

    def extra_fix(k):
        incoming(1 + k, fce[1 + k], extra[k], True)
        fix_batch(rawe.at[k], sbe, 1 + k, False, extra[k])

    def extra_act(k):
        def ssm(rows):
            tmpe[rows, :] = nn(sbe[rows, :], w4[2:4].reshape(2 * N, H))

        each_seq(ssm, extra[k])

        def gelu(i, rows):
            pre = tmpe[rows, :] + skip_r * nrme[rows_at(eoff[k] + i * 32, 32), :].astype(f32)
            acte[rows, :] = (pre * (0.5 + 0.5 * jnp.tanh(pre * (SQ2PI + (SQ2PI * 0.044715) * (pre * pre))))).astype(bf16)

        tiles(gelu, 0, extra[k] * L // 32)

    def extra_out(k):
        rank = erank[k]

        def gate(rows):
            tmpe[rows, 0:U] = nn(acte[rows, :], gt[:, tl])

        each_seq(gate, extra[k])
        bias_u = jnp.sum(jnp.where(lax.broadcasted_iota(jnp.int32, (T, U), 0) == t, bias_t, 0.0), 0, keepdims=True)

        def fin(i, rows):
            here = rows_at(eoff[k] + i * 32, 32)
            sg = logistic(tmpe[rows, 0:U] + bias_u)
            o = valid_of(i, rank) * (xe[here, tl].astype(f32) + acte[rows, tl].astype(f32) * sg)
            obe[here, :] = o.astype(bf16)

        tiles(fin, 0, extra[k] * L // 32)
        locals_.append(local(
            obe.at[pl.ds(eoff[k], extra[k] * L)], out_hbm.at[pl.ds(pl.multiple_of(R * rank, R), extra[k] * L), :]))

    bias_t = jnp.concatenate([bias_r[:, U * k:U * k + U] for k in range(T)], 0)
    bs, tgc = [], []
    bs.append(back_one(0))
    bs.append(back_one(1))
    bs.append(back_one(2))
    lax.fori_loop(0, 2 * N // 256, gc_step, 0)
    d1c = remote(gc.at[:, :, :, ol], r1c, sib)
    lax.fori_loop(0, H // 256, gg_step, 0)
    d1g = remote(gg.at[rows_at(HD * (1 - d), HD), :], r1g, sib)
    back_two(0, bs[0])
    tgc += tok_send(0)
    d2c = two_states(gc, d1c, r1c, s1c, r2c)
    arrived(d1g)
    s1g[...] = add2(gg[dr_, :], r1g[...])
    d2g = [remote(s1g.at[gr(p[1]), :], r2g.at[k], p) for k, p in enumerate(cpeer)]
    back_two(1, bs[1])
    tgc += tok_send(1)
    back_two(2, bs[2])
    tgc += tok_send(2)
    lax.fori_loop(0, 2 * N // 256, gb_step, 0)
    d1b = remote(gb.at[:, :, :, ol], r1b, sib)
    for k, row in ((2, 0), (1, 1), (0, 2)):
        vv[row:row + 1, :] = jnp.sum(accv[k], 0, keepdims=True)
    d1v = remote(vv, vr1, sib)
    extra_fix(0)
    d2b = two_states(gb, d1b, r1b, s1b, r2b)
    arrived(d1v)
    vr2[0] = vv[...] + vr1[...]
    d2v = [remote(vr2.at[0], vr2.at[k + 1], p) for k, p in enumerate(cpeer)]
    d3c = three_states(d2c, s1c, r2c, s2c, r3c)
    arrived(*d2g)
    s2g[...] = total(s1g[gr(c), :], r2g, C - 1).astype(bf16)
    d3g = [remote(s2g.at[:, gl1], r3g.at[0], z1), remote(s2g.at[:, lane(U * t3, U)], r3g.at[1], z1)]
    extra_act(0)
    d4c = four_states(d3c, s2c, r3c, s3c, r4c)
    arrived(*d3g)
    s3g[0] = add2(s2g[:, tl], r3g[0])
    s3g[1] = add2(s2g[:, gl2], r3g[1])
    d4g = remote(s3g.at[1], r4g, z2)
    extra_out(0)
    arrived(*d2b)
    s2b[...] = total(s1b[rs_ctx(c)[0], :, rs_ctx(c)[1], :], r2b, C - 1).astype(bf16)
    d3b = [remote(s2b.at[p[2]], r3b.at[k], p) for k, p in enumerate(zpeer)]
    arrived(*d2v)
    vr3[...] = vr2[0] + vr2[1] + vr2[2] + vr2[3]
    locals_.append(local(vr3, fv_hbm.at[0]))
    d3v = [remote(vr3, fv_hbm.at[k + 1], p) for k, p in enumerate(zpeer)]
    d5 = five(d4c, s3c, r4c, q5c, fc_hbm) + five(d4g, s3g, r4g, q5g, fg_hbm)
    arrived(*d3b)
    q5b[...] = total(s2b[t], r3b, T - 1).astype(bf16)
    d5 += spread_out(q5b, fb_hbm)

    arrived(*d5, *d3v, *tgc, *outc)
    for cp in locals_:
        cp.wait()
    for cp in started:
        cp.wait_send()
    assert count[0] == NSEM and nlocal[0] == NLOCAL, (count[0], nlocal[0])


EXTRA = (3,)
NSEM, NLOCAL = 106, 23


def fused_call(geo, lens, x2, og2, *params):
    D, C, T, S, L, H, N, U = geo
    R, NS, HD = S * L, N // T, H // D
    f32, bf16 = jnp.float32, jnp.bfloat16
    uq, hs = HD // C, NS // 2
    V = pltpu.VMEM
    any_ = pl.BlockSpec(memory_space=pl.ANY)
    scratch = [
        V((R, H), bf16), V((R, H), bf16), V((R, H), f32), V((R, 128), f32),
        V((R, 2 * N), f32), V((R, 2 * N), f32), V((R, 2 * N), bf16),
        V((R, H), f32), V((R, H), bf16), V((R, H), f32), V((R, H), f32),
        V((R, H), bf16), V((R, H), bf16), V((R, H), bf16), V((R, H), f32), V((R, H), bf16),
        V((R, 2 * N), f32), V((R, 2 * N), bf16), V((R, H), bf16),
        V((2 * R, H), bf16), V((2 * R, H), bf16), V((2, R, 2 * N), f32), V((R, 2 * N), bf16),
        V((R, H), bf16), V((R, H), f32), V((2 * R, U), bf16),
        V((4, T, NS, H), bf16), V((H, H), bf16), V((D * T, 8, HD), f32),
        V((22, 8, N), f32), V((6, 8, N), f32), V((6, C - 1, 8, N), f32), V((6, 8, N), f32),
        V((2, T, NS, H), bf16), V((H, H), bf16), V((2, T, NS, H), bf16),
        V((2, T, NS, HD), bf16), V((HD, H), bf16), V((2, T, NS, HD), bf16),
        V((2, T, NS, HD), bf16), V((HD, H), bf16), V((2, T, NS, HD), bf16),
        V((C - 1, T, hs, HD), bf16), V((C - 1, uq, H), bf16), V((C - 1, T, hs, HD), bf16),
        V((T, hs, HD), bf16), V((uq, H), bf16), V((T, hs, HD), bf16),
        V((2, hs, HD), bf16), V((2, uq, U), bf16), V((T - 1, hs, HD), bf16),
        V((2, hs, HD), bf16), V((2, uq, U), bf16), V((hs, HD), bf16), V((uq, U), bf16),
        V((hs, HD), bf16), V((uq, U), bf16), V((hs, HD), bf16),
        V((8, H), f32), V((8, H), f32), V((C, 8, H), f32), V((8, H), f32), V((3, 8, H), f32),
        V((4, NS, HD), bf16), V((8, HD), f32), V((HD, U), bf16), V((1, HD), f32), V((1, HD), f32),
        V((1, NS // D), f32), V((1, NS // D), f32), V((1, NS // D), f32), V((1, U // D), f32),
        pltpu.SemaphoreType.DMA((NLOCAL,)), pltpu.SemaphoreType.DMA((NSEM,)), pltpu.SemaphoreType.DMA((NSEM,)),
    ]
    rows = x2.shape[0]
    return pl.pallas_call(
        functools.partial(fused_body, geo, EXTRA),
        out_shape=(
            jax.ShapeDtypeStruct((rows, U), bf16), jax.ShapeDtypeStruct((rows, U), bf16),
            jax.ShapeDtypeStruct((C, hs, HD), bf16), jax.ShapeDtypeStruct((C, uq, U), bf16),
            jax.ShapeDtypeStruct((C, hs, HD), bf16), jax.ShapeDtypeStruct((T, 8, H), f32)),
        in_specs=[pl.BlockSpec(memory_space=pltpu.SMEM), any_, any_] + [any_] * 11,
        out_specs=(any_,) * 6,
        scratch_shapes=scratch,
        compiler_params=pltpu.CompilerParams(
            collective_id=0, has_side_effects=True, vmem_limit_bytes=60 * 1024 * 1024),
        name="block",
    )(lens, x2, og2, *params)


def finish_body(geo, len_ref, out_in, tok_in, og_in, fc_in, fg_in, fb_in, fv_in, lre_in, lim_in, stp_in, *refs):
    D, C, T, S, L, H, N, U = geo
    NS = N // T
    f32 = jnp.float32
    out, ingrad = refs[:2]
    small_out, big_out = refs[2:8], refs[8:13]
    tokv, ogv, outv, fc, fg, fb, fv, lre, lim, stp = refs[13:23]
    small, big = refs[23:29], refs[29:34]
    res, vf, sem, gsem, osem = refs[34:]
    d, c, t = lax.axis_index("dp"), lax.axis_index("ctx"), lax.axis_index("tp")

    def move(src, dst, s):
        cp = pltpu.make_async_copy(src, dst, s)
        cp.start()
        return cp

    part = [pl.ds(S * k, S) for k in range(T)]
    loads = [(move(tok_in.at[part[k]], tokv.at[part[k]], sem.at[0, k]),
              move(og_in.at[part[k]], ogv.at[part[k]], sem.at[1, k])) for k in range(T)]
    params = [move(a, b, gsem.at[k]) for k, (a, b) in enumerate((
        (fv_in, fv), (lre_in, lre), (lim_in, lim), (stp_in, stp), (fc_in, fc), (fg_in, fg), (fb_in, fb)))]
    passes = [move(out_in.at[part[k]], outv.at[part[k]], sem.at[2, k]) for k in range(T)]
    pos = c * L + lax.broadcasted_iota(jnp.int32, (L, 1), 0)
    stores = []
    for k in range(T):
        for cp in loads[k]:
            cp.wait()
        for s in range(S * k, S * k + S):
            keep = jnp.where(pos < len_ref[s], 1.0, 0.0)
            res[s] = keep * ogv[s].astype(f32) + tokv[s].astype(f32)
        stores.append(move(res.at[part[k]], ingrad.at[part[k]], osem.at[k]))
    for cp in params:
        cp.wait()
    h = C // 2
    for k in range(C):
        rows = pl.ds((k % h) * (NS // h), NS // h)
        big[0 if k < h else 1][rows, :] = fb[k].astype(f32)
        big[2 if k < h else 3][rows, :] = fc[k].astype(f32)
    big[4][...] = fg[...].reshape(big[4].shape).astype(f32)
    stores += [move(a, b, osem.at[2 * T + k]) for k, (a, b) in enumerate(zip(big, big_out))]
    for k in range(T):
        passes[k].wait()
        stores.append(move(outv.at[part[k]], out.at[part[k]], osem.at[T + k]))
    acc = fv[0]
    for k in range(1, T):
        acc = acc + fv[k]
    vf[...] = acc
    place = t * D + d
    back = lambda n: lax.rem(H - n * place, H)
    st8 = pltpu.roll(acc, back(NS // D), 1)[:, 0:NS // D]
    ub8 = pltpu.roll(acc, back(U // D), 1)[:, 0:U // D]
    lr1, li1 = lre[...], lim[...]
    dr1, di1, cr1, ci1 = coefficients(lr1, li1, stp[...])
    step1 = jnp.exp(stp[...])
    gdr, gdi, gcr, gci = (st8[k:k + 1] for k in range(3, 7))
    inv = 1.0 / (lr1 * lr1 + li1 * li1)
    hdr = gdr + (gcr * lr1 - gci * li1) * inv
    hdi = gdi + (gcr * li1 + gci * lr1) * inv
    pull = 2.0 * (gcr * cr1 + gci * ci1)
    e1, e2 = dr1 - 1.0, hdr * dr1 + hdi * di1
    e3 = hdi * dr1 - hdr * di1
    dl = lane(H // D * d, H // D)
    small[0][...] = vf[0:1, dl]
    small[1][...] = vf[1:2, dl]
    small[2][...] = (gcr * e1 + gci * di1 - pull * lr1) * inv + step1 * e2
    small[3][...] = (gcr * di1 - gci * e1 - pull * li1) * inv + step1 * e3
    small[4][...] = step1 * (lr1 * e2 + li1 * e3)
    small[5][...] = ub8[2:3]
    stores += [move(a, b, osem.at[2 * T + 5 + k]) for k, (a, b) in enumerate(zip(small, small_out))]
    for cp in stores:
        cp.wait()


def finish_call(geo, lens, out, tok, og, fc, fg, fb, fv, lre, lim, stp):
    D, C, T, S, L, H, N, U = geo
    NS, HD = N // T, H // D
    f32, bf16 = jnp.float32, jnp.bfloat16
    seqs = S * T
    any_ = pl.BlockSpec(memory_space=pl.ANY)
    V = pltpu.VMEM
    sizes = [(1, HD), (1, HD)] + [(1, NS // D)] * 3 + [(1, U // D)] + [(NS, HD)] * 4 + [(HD, U)]
    return pl.pallas_call(
        functools.partial(finish_body, geo),
        out_shape=[jax.ShapeDtypeStruct((seqs, L, U), bf16), jax.ShapeDtypeStruct((seqs, L, U), f32)]
        + [jax.ShapeDtypeStruct(s, f32) for s in sizes],
        in_specs=[pl.BlockSpec(memory_space=pltpu.SMEM)] + [any_] * 10,
        out_specs=[any_] * 13,
        scratch_shapes=[V((seqs, L, U), bf16)] * 3 + [V(a.shape, a.dtype) for a in (fc, fg, fb, fv, lre, lim, stp)]
        + [V(s, f32) for s in sizes] + [V((seqs, L, U), f32), V((8, H), f32)]
        + [pltpu.SemaphoreType.DMA((3, T)), pltpu.SemaphoreType.DMA((7,)), pltpu.SemaphoreType.DMA((2 * T + 11,))],
        compiler_params=pltpu.CompilerParams(vmem_limit_bytes=60 * 1024 * 1024),
        name="finish",
    )(lens, out.reshape(seqs, L, U), tok.reshape(seqs, L, U), og, fc, fg, fb, fv, lre, lim, stp)


def coefficients(lam_re, lam_im, step_log):
    step = jnp.exp(step_log)
    magnitude = jnp.exp(lam_re * step)
    decay_re = magnitude * jnp.cos(lam_im * step)
    decay_im = magnitude * jnp.sin(lam_im * step)
    inv = 1.0 / (lam_re * lam_re + lam_im * lam_im)
    coef_re = ((decay_re - 1.0) * lam_re + decay_im * lam_im) * inv
    coef_im = (decay_im * lam_re - (decay_re - 1.0) * lam_im) * inv
    return decay_re, decay_im, coef_re, coef_im


def token_split(sizes, inputs, lengths, norm_gain, skip_weight, lambda_re, lambda_im, log_step,
                b_re, b_im, c_re, c_im, glu_weight, glu_bias, out_grad):
    D, C, T = sizes
    seqs, L, H = inputs.shape
    NS, HD = b_re.shape
    U = glu_weight.shape[1]
    geo = (D, C, T, seqs // T, L, H, NS * T, U)
    rows = [v.reshape(1, -1) for v in (norm_gain, skip_weight, lambda_re, lambda_im, log_step, glu_bias)]
    out, tok, fc, fg, fb, fv = fused_call(
        geo, lengths, inputs.reshape(seqs * L, H), out_grad.reshape(seqs * L, U),
        b_re, b_im, c_re.T, c_im.T, glu_weight, *rows)
    res = finish_call(geo, lengths, out, tok, out_grad, fc, fg, fb, fv, *rows[2:5])
    out, ingrad, gain_g, skip_g, lre_g, lim_g, step_g, bias_g, bre_g, bim_g, cre_g, cim_g, glu_g = res
    flat = lambda v: v.reshape(-1)
    return (out, ingrad, flat(gain_g), flat(skip_g), flat(lre_g), flat(lim_g), flat(step_g),
            bre_g, bim_g, cre_g.T, cim_g.T, glu_g, flat(bias_g))


def solution(mesh):
    in_specs = (
        P("dp", "ctx", None),
        P("dp"),
        P("dp"),
        P("dp"),
        P(("tp", "dp")),
        P(("tp", "dp")),
        P(("tp", "dp")),
        P("tp", "dp"),
        P("tp", "dp"),
        P("dp", "tp"),
        P("dp", "tp"),
        P("dp", "tp"),
        P(("tp", "dp")),
        P("dp", "ctx", "tp"),
    )
    out_specs = (
        P("dp", "ctx", "tp"),
        P("dp", "ctx", "tp"),
        P("dp"),
        P("dp"),
        P(("tp", "dp")),
        P(("tp", "dp")),
        P(("tp", "dp")),
        P("tp", "dp"),
        P("tp", "dp"),
        P("dp", "tp"),
        P("dp", "tp"),
        P("dp", "tp"),
        P(("tp", "dp")),
    )
    sizes = tuple(mesh.shape[name] for name in ("dp", "ctx", "tp"))

    def block(*args):
        seqs, _, feat = args[0].shape
        units = args[11].shape[1]
        if sizes == (2, 4, 4) and seqs % sizes[2] == 0 and units % 128 == 0:
            return token_split(sizes, *args)
        return on_device(*args)

    return jax.shard_map(
        block, mesh=mesh, in_specs=in_specs, out_specs=out_specs, check_vma=False
    )
```

```python
import functools

import jax
import jax.numpy as jnp
from jax import lax
from jax.experimental import pallas as pl
from jax.experimental.pallas import tpu as pltpu
from jax.sharding import PartitionSpec as P

epsilon = 1e-05


def carried_in(value, axis, combine, identity, reverse):
    count, index = (lax.axis_size(axis), lax.axis_index(axis))
    everything = jax.tree.map(lambda part: lax.all_gather(part, axis), value)
    start = jax.tree.map(
        lambda part, zero: jnp.broadcast_to(jnp.asarray(zero, part.dtype), part.shape),
        value,
        identity,
    )

    def lap(k, before):
        at = count - 1 - k if reverse else k
        reached = at > index if reverse else at < index
        new = combine(before, jax.tree.map(lambda part: part[at], everything))
        return jax.tree.map(lambda a, b: jnp.where(reached, a, b), new, before)

    return lax.fori_loop(0, count, lap, start)


def contract(left, right, left_dim, right_dim):
    return lax.dot_general(
        left, right, (((left_dim,), (right_dim,)), ((), ())), preferred_element_type=jnp.float32
    )


def combine(earlier, later):
    e_re, e_im, eb_re, eb_im = earlier
    l_re, l_im, lb_re, lb_im = later
    return (
        e_re * l_re - e_im * l_im,
        e_re * l_im + e_im * l_re,
        l_re * eb_re - l_im * eb_im + lb_re,
        l_re * eb_im + l_im * eb_re + lb_im,
    )


def discretize(lam_re, lam_im, step_log, mat_re, mat_im):
    step = jnp.exp(step_log)
    magnitude = jnp.exp(lam_re * step)
    decay_re = magnitude * jnp.cos(lam_im * step)
    decay_im = magnitude * jnp.sin(lam_im * step)
    denom = lam_re * lam_re + lam_im * lam_im
    coef_re = ((decay_re - 1.0) * lam_re + decay_im * lam_im) / denom
    coef_im = (decay_im * lam_re - (decay_re - 1.0) * lam_im) / denom
    bar_re = coef_re[:, None] * mat_re - coef_im[:, None] * mat_im
    bar_im = coef_re[:, None] * mat_im + coef_im[:, None] * mat_re
    return (decay_re, decay_im, jnp.concatenate([bar_re, bar_im], 0))


def normalize(tokens, gain):
    mean_val = jnp.mean(tokens, -1, keepdims=True)
    centered = tokens - mean_val
    var_val = jnp.mean(centered * centered, -1, keepdims=True)
    return centered * lax.rsqrt(var_val + epsilon) * gain


def powers(lam_re, lam_im, step_log, count):
    step = jnp.exp(step_log)
    exponent = (jnp.arange(count, dtype=jnp.float32) + 1.0)[:, None]
    magnitude = jnp.exp(exponent * lam_re * step)
    return (
        magnitude * jnp.cos(exponent * lam_im * step),
        magnitude * jnp.sin(exponent * lam_im * step),
    )


def on_device(
    inputs,
    lengths,
    norm_gain,
    skip_weight,
    lambda_re,
    lambda_im,
    log_step,
    b_re,
    b_im,
    c_re,
    c_im,
    glu_weight,
    glu_bias,
    out_grad,
):
    full_bre, full_bim, full_cre, full_cim, full_glu = (
        lax.all_gather(b_re, "dp", axis=1, tiled=True),
        lax.all_gather(b_im, "dp", axis=1, tiled=True),
        lax.all_gather(c_re, "dp", axis=0, tiled=True),
        lax.all_gather(c_im, "dp", axis=0, tiled=True),
        lax.all_gather(glu_weight, "dp", axis=0, tiled=True),
    )
    gain, skip_full, lam_re, lam_im, step_log, bias_vec = (
        lax.all_gather(norm_gain, "dp", axis=0, tiled=True),
        lax.all_gather(skip_weight, "dp", axis=0, tiled=True),
        lax.all_gather(lambda_re, "dp", axis=0, tiled=True),
        lax.all_gather(lambda_im, "dp", axis=0, tiled=True),
        lax.all_gather(log_step, "dp", axis=0, tiled=True),
        lax.all_gather(glu_bias, "dp", axis=0, tiled=True),
    )
    seq_count, blk_len, feat_dim = inputs.shape
    row_count = seq_count * blk_len
    state_count = full_bre.shape[0]
    unit_count = full_glu.shape[1]
    tp_rank = lax.axis_index("tp")
    unit_start = tp_rank * unit_count
    positions = lax.axis_index("ctx") * blk_len + jnp.arange(blk_len, dtype=jnp.int32)
    valid_mask = (positions[None, :] < lengths[:, None]).astype(jnp.float32).reshape(row_count, 1)
    tokens = inputs.astype(jnp.float32).reshape(row_count, feat_dim)
    tokens_mine = lax.dynamic_slice_in_dim(tokens, unit_start, unit_count, 1)
    cotangent = out_grad.astype(jnp.float32).reshape(row_count, unit_count)
    normed_f, norm_pull = jax.vjp(normalize, tokens, gain)
    normed_b = normed_f.astype(jnp.bfloat16)
    normed_r = normed_b.astype(jnp.float32)
    (decay_re, decay_im, bar_full), disc_pull = jax.vjp(
        discretize,
        lam_re,
        lam_im,
        step_log,
        full_bre.astype(jnp.float32),
        full_bim.astype(jnp.float32),
    )
    bar_b = bar_full.astype(jnp.bfloat16)
    drive = contract(normed_b, bar_b, 1, 1).reshape(seq_count, blk_len, 2 * state_count)
    full_re = jnp.broadcast_to(decay_re, (seq_count, blk_len, state_count))
    full_im = jnp.broadcast_to(decay_im, (seq_count, blk_len, state_count))
    local_states = lax.associative_scan(
        combine, (full_re, full_im, drive[..., :state_count], drive[..., state_count:]), axis=1
    )
    pow_re, pow_im = powers(lam_re, lam_im, step_log, blk_len)
    identity = (
        jnp.ones((1, state_count), jnp.float32),
        jnp.zeros((1, state_count), jnp.float32),
        jnp.zeros((seq_count, state_count), jnp.float32),
        jnp.zeros((seq_count, state_count), jnp.float32),
    )
    incoming = carried_in(
        (pow_re[-1:], pow_im[-1:], local_states[2][:, -1], local_states[3][:, -1]),
        "ctx",
        combine,
        identity,
        False,
    )
    in_re = incoming[2][:, None, :]
    in_im = incoming[3][:, None, :]
    state_re = local_states[2] + pow_re * in_re - pow_im * in_im
    state_im = local_states[3] + pow_re * in_im + pow_im * in_re
    states_b = (
        jnp.concatenate([state_re, state_im], -1)
        .reshape(row_count, 2 * state_count)
        .astype(jnp.bfloat16)
    )
    c_stack = jnp.concatenate([full_cre, -full_cim], 1)
    ssm_part = contract(states_b, c_stack, 1, 1)
    ssm_full = lax.psum(ssm_part.astype(jnp.bfloat16), "tp").astype(jnp.float32)
    pre_full = ssm_full + skip_full * normed_r
    gelu_full, gelu_pull = jax.vjp(jax.nn.gelu, pre_full)
    gelu_b = gelu_full.astype(jnp.bfloat16)
    gelu_part = lax.dynamic_slice_in_dim(gelu_b, unit_start, unit_count, 1)
    gelu_mine = gelu_part.astype(jnp.float32)
    gate = contract(gelu_b, full_glu, 1, 0) + bias_vec
    gate_sig = jax.nn.sigmoid(gate)
    output = (
        (valid_mask * (tokens_mine + gelu_mine * gate_sig))
        .astype(jnp.bfloat16)
        .reshape(seq_count, blk_len, unit_count)
    )
    branch_grad = valid_mask * cotangent
    gate_grad = branch_grad * gelu_mine * gate_sig * (1.0 - gate_sig)
    bias_grad = jnp.sum(gate_grad, 0)
    gate_b = gate_grad.astype(jnp.bfloat16)
    glu_grad = contract(gelu_b, gate_b, 0, 0)
    gelu_grad = contract(gate_b, full_glu, 1, 1)
    own_cols = (
        lax.dynamic_slice_in_dim(gelu_grad, unit_start, unit_count, 1) + branch_grad * gate_sig
    )
    gelu_grad = lax.dynamic_update_slice_in_dim(gelu_grad, own_cols, unit_start, 1)
    gelu_back = lax.psum(gelu_grad, "tp")
    (pre_grad,) = gelu_pull(gelu_back)
    skip_grad = jnp.sum(pre_grad * normed_r, 0)
    pre_b = pre_grad.astype(jnp.bfloat16)
    state_grad = contract(pre_b, c_stack, 1, 0).reshape(seq_count, blk_len, 2 * state_count)
    c_grad = contract(pre_b, states_b, 0, 0)
    back_local = lax.associative_scan(
        combine,
        (full_re, -full_im, state_grad[..., :state_count], state_grad[..., state_count:]),
        axis=1,
        reverse=True,
    )
    later_adj = carried_in(
        (pow_re[-1:], -pow_im[-1:], back_local[2][:, 0], back_local[3][:, 0]),
        "ctx",
        combine,
        identity,
        True,
    )
    rev_re = pow_re[::-1]
    rev_im = -pow_im[::-1]
    next_re = later_adj[2][:, None, :]
    next_im = later_adj[3][:, None, :]
    adj_re = back_local[2] + rev_re * next_re - rev_im * next_im
    adj_im = back_local[3] + rev_re * next_im + rev_im * next_re
    prev_re = jnp.concatenate([in_re, state_re[:, :-1]], 1)
    prev_im = jnp.concatenate([in_im, state_im[:, :-1]], 1)
    decay_grad_re = jnp.sum(adj_re * prev_re + adj_im * prev_im, (0, 1))
    decay_grad_im = jnp.sum(adj_im * prev_re - adj_re * prev_im, (0, 1))
    adj_b = (
        jnp.concatenate([adj_re, adj_im], -1)
        .reshape(row_count, 2 * state_count)
        .astype(jnp.bfloat16)
    )
    bar_grad = contract(adj_b, normed_b, 0, 0)
    normed_part = contract(adj_b, bar_b, 1, 0)
    normed_sum = lax.psum(normed_part.astype(jnp.bfloat16), "tp").astype(jnp.float32)
    normed_grad = normed_sum + skip_full * pre_grad
    token_grad, gain_grad = norm_pull(normed_grad)
    input_grad = (
        valid_mask * cotangent + lax.dynamic_slice_in_dim(token_grad, unit_start, unit_count, 1)
    ).reshape(seq_count, blk_len, unit_count)
    grad_cre = c_grad[:, :state_count]
    grad_cim = -c_grad[:, state_count:]
    lre_grad, lim_grad, step_grad, bre_grad, bim_grad = disc_pull(
        (decay_grad_re, decay_grad_im, bar_grad)
    )
    shards = (
        lax.psum_scatter(
            gain_grad.astype(jnp.bfloat16), "dp", scatter_dimension=0, tiled=True
        ).astype(jnp.float32),
        lax.psum_scatter(
            skip_grad.astype(jnp.bfloat16), "dp", scatter_dimension=0, tiled=True
        ).astype(jnp.float32),
        lax.psum_scatter(
            lre_grad.astype(jnp.bfloat16), "dp", scatter_dimension=0, tiled=True
        ).astype(jnp.float32),
        lax.psum_scatter(
            lim_grad.astype(jnp.bfloat16), "dp", scatter_dimension=0, tiled=True
        ).astype(jnp.float32),
        lax.psum_scatter(
            step_grad.astype(jnp.bfloat16), "dp", scatter_dimension=0, tiled=True
        ).astype(jnp.float32),
        lax.psum_scatter(
            bias_grad.astype(jnp.bfloat16), "dp", scatter_dimension=0, tiled=True
        ).astype(jnp.float32),
        lax.psum_scatter(
            bre_grad.astype(jnp.bfloat16), "dp", scatter_dimension=1, tiled=True
        ).astype(jnp.float32),
        lax.psum_scatter(
            bim_grad.astype(jnp.bfloat16), "dp", scatter_dimension=1, tiled=True
        ).astype(jnp.float32),
        lax.psum_scatter(
            grad_cre.astype(jnp.bfloat16), "dp", scatter_dimension=0, tiled=True
        ).astype(jnp.float32),
        lax.psum_scatter(
            grad_cim.astype(jnp.bfloat16), "dp", scatter_dimension=0, tiled=True
        ).astype(jnp.float32),
        lax.psum_scatter(
            glu_grad.astype(jnp.bfloat16), "dp", scatter_dimension=0, tiled=True
        ).astype(jnp.float32),
    )
    summed = (
        lax.psum(shards[0].astype(jnp.bfloat16), "ctx").astype(jnp.float32),
        lax.psum(shards[1].astype(jnp.bfloat16), "ctx").astype(jnp.float32),
        lax.psum(shards[2].astype(jnp.bfloat16), "ctx").astype(jnp.float32),
        lax.psum(shards[3].astype(jnp.bfloat16), "ctx").astype(jnp.float32),
        lax.psum(shards[4].astype(jnp.bfloat16), "ctx").astype(jnp.float32),
        lax.psum(shards[5].astype(jnp.bfloat16), "ctx").astype(jnp.float32),
        lax.psum(shards[6].astype(jnp.bfloat16), "ctx").astype(jnp.float32),
        lax.psum(shards[7].astype(jnp.bfloat16), "ctx").astype(jnp.float32),
        lax.psum(shards[8].astype(jnp.bfloat16), "ctx").astype(jnp.float32),
        lax.psum(shards[9].astype(jnp.bfloat16), "ctx").astype(jnp.float32),
        lax.psum(shards[10].astype(jnp.bfloat16), "ctx").astype(jnp.float32),
    )
    return (
        output,
        input_grad,
        summed[0],
        summed[1],
        summed[2],
        summed[3],
        summed[4],
        summed[6],
        summed[7],
        summed[8],
        summed[9],
        summed[10],
        summed[5],
    )


MESH = pl.DeviceIdType.MESH
SQ2PI = 0.7978845608028654


def nt(a, b):
    return lax.dot_general(a, b, (((1,), (1,)), ((), ())), preferred_element_type=jnp.float32)


def nn(a, b):
    return lax.dot_general(a, b, (((1,), (0,)), ((), ())), preferred_element_type=jnp.float32)


def tn(a, b):
    return lax.dot_general(a, b, (((0,), (0,)), ((), ())), preferred_element_type=jnp.float32)


def cmul(ar, ai, br, bi):
    return ar * br - ai * bi, ar * bi + ai * br


def lane(start, size):
    return pl.ds(pl.multiple_of(start, 128), size)


def fused_body(geo, extra, *refs):
    D, C, T, S, L, H, N, U = geo
    R = S * L
    NS = N // T
    HD = H // D
    f32, bf16 = jnp.float32, jnp.bfloat16
    (len_ref, x_hbm, og_hbm, bre, bim, cre, cim, glu_hbm, gain_h, skip_h, lre_h, lim_h, stp_h, bias_h,
     out_hbm, tg_hbm, fc_hbm, fg_hbm, fb_hbm, fv_hbm) = refs[:20]
    (xv, nrm, xh, rs, raw, st, sb, tmp, act, gp, sig, ogv, ob, gl, pg, plb, mu, nb, tgb,
     xe, nrme, rawe, sbe, acte, tmpe, obe,
     w4, gt, smr, cst, ce, cer, cin, gc, gg, gb, r1c, r1g, r1b, s1c, s1g, s1b, r2c, r2g, r2b,
     s2c, s2g, s2b, r3c, r3g, r3b, s3c, s3g, r4c, r4g,
     q5c, q5g, q5b, vv, vr1, vr2, vr3, accv, pk, sm_ref, glu, gain_in, skip_in, lre_in, lim_in, stp_in, bias_in,
     lsem, ssem, rsem) = refs[20:]
    d, c, t = lax.axis_index("dp"), lax.axis_index("ctx"), lax.axis_index("tp")
    half = t // 2
    t1 = t + 1 - 2 * lax.rem(t, 2)
    t2 = t + 2 - 4 * half
    t3 = T - 1 - t
    z1, z2, z3 = (d, c, t1), (d, c, t2), (d, c, t3)
    zpeer = [(d, c, lax.rem(t + k, T)) for k in range(1, T)]
    cpeer = [(d, lax.rem(c + k, C), t) for k in range(1, C)]
    sib = (1 - d, c, t)
    xpeer = [(1 - d, c, lax.rem(t + k, T)) for k in range(1, T)]
    everyone = zpeer + cpeer + [sib] + xpeer
    erank = [t2, t3][:len(extra)]
    eoff = [L * sum(extra[:k]) for k in range(len(extra))]

    count = [0]
    started = []

    def remote(src, dst, peer):
        i = count[0]
        count[0] += 1
        cp = pltpu.make_async_remote_copy(
            src_ref=src, dst_ref=dst, send_sem=ssem.at[i], recv_sem=rsem.at[i],
            device_id=peer, device_id_type=MESH)
        cp.start()
        started.append(cp)
        return cp

    def arrived(*cps):
        for cp in cps:
            cp.wait_recv()

    nlocal = [0]

    def local(src, dst):
        cp = pltpu.make_async_copy(src, dst, lsem.at[nlocal[0]])
        nlocal[0] += 1
        cp.start()
        return cp

    def rows_at(start, size):
        return pl.ds(pl.multiple_of(start, size), size)

    barrier = pltpu.get_barrier_semaphore()
    for p in everyone:
        pl.semaphore_signal(barrier, inc=1, device_id=p, device_id_type=MESH)
    cp_small = [local(a, b) for a, b in (
        (lre_h, lre_in), (lim_h, lim_in), (stp_h, stp_in), (bias_h, bias_in), (gain_h, gain_in), (skip_h, skip_in))]
    mine = rows_at(R * t, R)
    cp_pk = [local(a, pk.at[k]) for k, a in enumerate((bre, bim, cre, cim))] + [local(glu_hbm, glu)]
    cx = local(x_hbm.at[mine], xv)
    cxe = [local(x_hbm.at[pl.ds(pl.multiple_of(R * e, R), L * n)], xe.at[pl.ds(o, L * n)])
           for e, n, o in zip(erank, extra, eoff)]
    co = local(og_hbm.at[mine], ogv.at[:, lane(U * t, U)])
    dl = lane(HD * d, HD)
    dr_ = rows_at(HD * d, HD)
    tl = lane(U * t, U)
    sm_ref[...] = jnp.zeros_like(sm_ref)
    for cp in cp_small:
        cp.wait()
    own = coefficients(lre_in[...], lim_in[...], stp_in[...])
    for k in range(4):
        sm_ref[k:k + 1, 0:NS // D] = own[k]
    sm_ref[4:5, 0:U // D] = bias_in[...]
    sm_ref[5:6, :] = gain_in[...]
    sm_ref[6:7, :] = skip_in[...]
    me8 = d * T + t
    smr[me8] = sm_ref[...]
    accv[...] = jnp.zeros_like(accv)
    vv[...] = jnp.zeros_like(vv)
    for cp in cp_pk:
        cp.wait()
    for k in range(4):
        w4[k, t, :, dl] = pk[k]
    gt[dr_, tl] = glu[...]
    cx.wait()

    def standard(x):
        cen = x - jnp.mean(x, -1, keepdims=True)
        rstd = lax.rsqrt(jnp.mean(cen * cen, -1, keepdims=True) + epsilon)
        return cen * rstd, rstd

    def ln_tile(i, _):
        for u in range(4):
            rows = rows_at(i * 128 + u * 32, 32)
            xn, rstd = standard(xv[rows, :].astype(f32))
            xh[rows, :] = xn
            rs[rows, :] = jnp.broadcast_to(rstd, (32, 128))
        return 0

    lax.fori_loop(0, R // 128, ln_tile, 0)
    pl.semaphore_wait(barrier, len(everyone))

    gq, hq = c // 2, lax.rem(c, 2)
    ql = lane(128 * hq, 128)
    wl = lane(HD * d + 128 * hq, 128)
    uq = HD // C
    gown = rows_at(uq * c, uq)
    grow = rows_at(HD * d + uq * c, uq)
    pair = rows_at(2 - 2 * half, 2)
    pairl = lane(2 * U * (1 - half), 2 * U)

    qb, qc = gq, 2 + gq
    far_b = [remote(pk.at[qb, :, ql], w4.at[qb, t, :, wl], p) for p in (z3, z2)]
    small = [remote(sm_ref, smr.at[me8], p) for p in zpeer + [sib] + xpeer]
    near_b = remote(pk.at[0:2], w4.at[0:2, t, :, dl], z1)
    w3b = [remote(pk.at[0:2], w4.at[0:2, t, :, dl], sib)]

    def spread(blk, *cps):
        arrived(*cps)
        return [remote(blk, blk, p) for p in cpeer]

    gl1, gl2 = lane(U * t1, U), lane(U * t2, U)
    w2b = spread(w4.at[qb, pair, :, wl], *far_b)
    far_c = [remote(pk.at[qc, :, ql], w4.at[qc, t, :, wl], p) for p in (z3, z2)]
    far_g = [remote(glu.at[gown], gt.at[grow, tl], p) for p in (z3, z2)]
    near_c = remote(pk.at[2:4], w4.at[2:4, t, :, dl], z1)
    near_g = remote(glu, gt.at[dr_, tl], z1)
    w3c = [remote(pk.at[2:4], w4.at[2:4, t, :, dl], sib)]
    w3g = [remote(glu, gt.at[dr_, tl], sib)]

    def cot_send(s):
        return [remote(og_hbm.at[rows_at(R * p[2] + L * s, L)], ogv.at[pl.ds(L * s, L), tl], p) for p in zpeer]

    arrived(*small)
    zero = jnp.zeros((8, H - HD), f32)
    vec = jnp.zeros((8, H), f32)
    bias = jnp.zeros((8, H), f32)
    for dd in range(D):
        for tt in range(T):
            ext = jnp.concatenate([smr[dd * T + tt], zero], 1)
            place = tt * D + dd
            vec = vec + (pltpu.roll(ext, place * (NS // D), 1) if place else ext)
            bias = bias + (pltpu.roll(ext, place * (U // D), 1) if place else ext)
    both = jnp.concatenate([smr[t], smr[T + t]], 1)
    gain_r, skip_r, bias_r = both[5:6, :], both[6:7, :], bias[4:5, :]

    arrived(near_b)
    w3b.append(remote(w4.at[0:2, t1, :, dl], w4.at[0:2, t1, :, dl], sib))
    row8 = lax.broadcasted_iota(jnp.int32, (8, N), 0)
    full = lambda v, k, n: jnp.broadcast_to(v[k:k + 1, :n], (8, n))
    dr, di = full(vec, 0, N), full(vec, 1, N)
    cr, ci = full(vec, 2, N), full(vec, 3, N)
    pows = {1: (dr, di)}
    for k in range(2, 9):
        pows[k] = cmul(*pows[k - 1], dr, di)
    for n_, k in ((0, 1), (1, 2), (2, 4)):
        keep = row8 >= k
        cst[2 * n_] = jnp.where(keep, pows[k][0], 0.0)
        cst[2 * n_ + 1] = jnp.where(keep, pows[k][1], 0.0)
        keep = row8 < 8 - k
        cst[8 + 2 * n_] = jnp.where(keep, pows[k][0], 0.0)
        cst[8 + 2 * n_ + 1] = jnp.where(keep, -pows[k][1], 0.0)
    pr, pi, qr, qi = pows[1][0], pows[1][1], pows[8][0], -pows[8][1]
    for r in range(1, 8):
        pr = jnp.where(row8 == r, pows[r + 1][0], pr)
        pi = jnp.where(row8 == r, pows[r + 1][1], pi)
        qr = jnp.where(row8 == r, pows[8 - r][0], qr)
        qi = jnp.where(row8 == r, -pows[8 - r][1], qi)
    cst[6], cst[7], cst[14], cst[15] = pr, pi, qr, qi
    cst[16], cst[17] = pows[8]
    cst[18], cst[19] = cr, ci
    big = pows[8]
    n_ = 8
    while n_ < L:
        big = cmul(*big, *big)
        n_ *= 2
    cst[20], cst[21] = big

    def nrm_tile(i, _):
        rows = rows_at(i * 32, 32)
        nrm[rows, :] = (xh[rows, :] * gain_r).astype(bf16)
        return 0

    lax.fori_loop(0, R // 32, nrm_tile, 0)
    og = [cot_send(0)]

    def lne_tile(i, _):
        for u in range(4):
            rows = rows_at(i * 128 + u * 32, 32)
            nrme[rows, :] = (standard(xe[rows, :].astype(f32))[0] * gain_r).astype(bf16)
        return 0

    def seq_rows(s):
        return rows_at(s * L, L)

    wv = w4.reshape(4, N, H)

    def drive(src, off, dst, n, j):
        rows = rows_at(128 * j, 128)
        both_ = nt(src[pl.ds(off, n * L), :], jnp.concatenate([wv[0, rows, :], wv[1, rows, :]], 0))
        dst[pl.ds(0, n * L), lane(128 * j, 128)] = both_[:, 0:128]
        dst[pl.ds(0, n * L), lane(N + 128 * j, 128)] = both_[:, 128:256]

    def scan(src, dst, groups, base, coef, reverse):
        e = 0 if reverse else 7

        def tile(i, carry):
            carry = list(carry)
            ii = L // 32 - 1 - i if reverse else i
            for g, (rb, l0) in enumerate(groups):
                lr_, li_ = lane(l0, 128), lane(N + l0, 128)
                con = [cst[base + k, :, lr_] for k in range(8)]
                e0 = cst[16, :, lr_]
                e1 = -cst[17, :, lr_] if reverse else cst[17, :, lr_]
                loc = []
                for u in range(4):
                    uu = 3 - u if reverse else u
                    rows = rows_at(rb + ii * 32 + uu * 8, 8)
                    ar, ai = src[rows, lr_], src[rows, li_]
                    if coef:
                        ar, ai = cmul(cst[18, :, lr_], cst[19, :, lr_], ar, ai)
                    else:
                        ai = -ai
                    for n_, k in ((0, 1), (1, 2), (2, 4)):
                        sh = 8 - k if reverse else k
                        br, bi = pltpu.roll(ar, sh, 0), pltpu.roll(ai, sh, 0)
                        mr, mi = con[2 * n_], con[2 * n_ + 1]
                        ar, ai = ar + mr * br - mi * bi, ai + mr * bi + mi * br
                    loc.append((rows, ar, ai))
                kr, ki = carry[2 * g], carry[2 * g + 1]
                for rows, ar, ai in loc:
                    dst[rows, lr_] = ar + con[6] * kr - con[7] * ki
                    dst[rows, li_] = ai + con[6] * ki + con[7] * kr
                    endr = jnp.broadcast_to(ar[e:e + 1, :], (8, 128))
                    endi = jnp.broadcast_to(ai[e:e + 1, :], (8, 128))
                    kr, ki = endr + e0 * kr - e1 * ki, endi + e0 * ki + e1 * kr
                carry[2 * g], carry[2 * g + 1] = kr, ki
            return tuple(carry)

        z = jnp.zeros((8, 128), f32)
        return lax.fori_loop(0, L // 32, tile, (z,) * (2 * len(groups)))

    def begin(src, off, dst, out, slot, n, j):
        drive(src, off, dst, n, j)
        fin = scan(dst, out, [(s * L, 128 * j) for s in range(n)], 0, True, False)
        for s in range(n):
            ce[slot, pl.ds(s, 1), lane(128 * j, 128)] = fin[2 * s][0:1, :]
            ce[slot, pl.ds(n + s, 1), lane(128 * j, 128)] = fin[2 * s + 1][0:1, :]

    def rest(what, tiles_=2):
        def step(k, _):
            begin(*what, 1 + k * (1 - 2 * half) if tiles_ == 2 else k)
            return 0

        lax.fori_loop(0, tiles_, step, 0)
        slot = what[4]
        return [remote(ce.at[slot], cer.at[slot, k], p) for k, p in enumerate(cpeer)]

    def incoming(slot, cps, n, forward):
        arrived(*cps)
        bg = (cst[20, 0:1, :], cst[21, 0:1, :])
        wt = (jnp.ones((1, N), f32), jnp.zeros((1, N), f32))
        accr = jnp.zeros((n, N), f32)
        acci = jnp.zeros((n, N), f32)
        for k in range(1, C):
            got = cer[slot, k - 1] if forward else cer[slot, C - 1 - k]
            has = (c >= k) if forward else (c + k < C)
            w = jnp.where(has, 1.0, 0.0)
            wi = wt[1] if forward else -wt[1]
            ur, ui = cmul(wt[0], wi, got[0:n, :], got[n:2 * n, :])
            accr = accr + w * ur
            acci = acci + w * ui
            wt = cmul(*wt, *bg)
        cin[slot, 0:n, :] = accr
        cin[slot, n:2 * n, :] = acci

    def entering(slot, k, lanes):
        return jnp.broadcast_to(cin[slot, pl.ds(k, 1), lanes], (8, 128))

    def fix_batch(ref, dst, slot, keep, n):
        def fix_lanes(j, _):
            lr_, li_ = lane(128 * j, 128), lane(N + 128 * j, 128)
            p0, p1 = cst[6, :, lr_], cst[7, :, lr_]
            e0, e1 = cst[16, :, lr_], cst[17, :, lr_]
            q0 = tuple(entering(slot, k * n + s, lr_) for s in range(n) for k in range(2))

            def tile(i, q):
                q = list(q)
                for s in range(n):
                    rr, ri = [], []
                    for h in range(2):
                        rows = rows_at(s * L + i * 16 + 8 * h, 8)
                        vr, vi = cmul(p0, p1, q[2 * s], q[2 * s + 1])
                        ar, ai = ref[rows, lr_] + vr, ref[rows, li_] + vi
                        if keep:
                            ref[rows, lr_] = ar
                            ref[rows, li_] = ai
                        rr.append(ar)
                        ri.append(ai)
                        q[2 * s], q[2 * s + 1] = cmul(q[2 * s], q[2 * s + 1], e0, e1)
                    rows = rows_at(s * L + i * 16, 16)
                    dst[rows, lr_] = jnp.concatenate(rr, 0).astype(bf16)
                    dst[rows, li_] = (-jnp.concatenate(ri, 0)).astype(bf16)
                return tuple(q)

            lax.fori_loop(0, L // 16, tile, q0)
            return 0

        lax.fori_loop(0, N // 128, fix_lanes, 0)

    def each_seq(f, n=S):
        f(pl.ds(0, n * L))

    def tiles(f, lo=0, hi=R // 32):
        def step(i, _):
            f(i, rows_at(i * 32, 32))
            return 0

        lax.fori_loop(lo, hi, step, 0)

    def valid_of(i, rank):
        s = i // (L // 32)
        pos = c * L + lax.rem(i, L // 32) * 32 + lax.broadcasted_iota(jnp.int32, (32, 1), 0)
        return jnp.where(pos < len_ref[S * rank + s], 1.0, 0.0)

    def logistic(v):
        return 0.5 + 0.5 * jnp.tanh(0.5 * v)

    batches = [(nrm, 0, raw, st, 0, S)] + [
        (nrme, eoff[k], rawe.at[k], rawe.at[k], 1 + k, extra[k]) for k in range(len(extra))]
    arrived(*w3b)
    begin(*batches[0], 2 * half)
    w2c = spread(w4.at[qc, pair, :, wl], *far_c)
    w2g = spread(gt.at[grow, pairl], *far_g)
    og.append(cot_send(1))
    for cp in cxe:
        cp.wait()
    lax.fori_loop(0, extra[0] * L // 128, lne_tile, 0)
    arrived(*w2b)
    w3b2 = remote(w4.at[0:2, pair, :, dl], w4.at[0:2, pair, :, dl], sib)
    og.append(cot_send(2))
    begin(*batches[1], 2 * half)
    arrived(w3b2)
    fce = [rest(batches[0])]
    arrived(near_c)
    w3c.append(remote(w4.at[2:4, t1, :, dl], w4.at[2:4, t1, :, dl], sib))
    arrived(near_g)
    blk = gt.at[dr_, gl1]
    w3g.append(remote(blk, blk, sib))
    arrived(*w2c)
    w3c.append(remote(w4.at[2:4, pair, :, dl], w4.at[2:4, pair, :, dl], sib))
    arrived(*w2g)
    blk = gt.at[dr_, pairl]
    w3g.append(remote(blk, blk, sib))
    fce.append(rest(batches[1]))
    incoming(0, fce[0], S, True)
    fix_batch(st, sb, 0, True, S)
    arrived(*w3c)

    def ssm_own(rows):
        tmp[rows, :] = nn(sb[rows, :], w4[2:4].reshape(2 * N, H))

    each_seq(ssm_own)

    def gelu_tile(i, rows):
        pre = tmp[rows, :] + skip_r * nrm[rows, :].astype(f32)
        sq = pre * pre
        th = jnp.tanh(pre * (SQ2PI + (SQ2PI * 0.044715) * sq))
        hf = 0.5 + 0.5 * th
        act[rows, :] = (pre * hf).astype(bf16)
        gp[rows, :] = hf + 0.5 * pre * (1.0 - th * th) * (SQ2PI + (3 * 0.044715 * SQ2PI) * sq)

    tiles(gelu_tile)
    arrived(*w3g)

    def gate_own(rows):
        tmp[rows, :] = nn(act[rows, :], gt[...])

    each_seq(gate_own)

    def out_tile(i, rows):
        sg = logistic(tmp[rows, :] + bias_r)
        sig[rows, :] = sg
        o = valid_of(i, t) * (xv[rows, :].astype(f32) + act[rows, :].astype(f32) * sg)
        ob[rows, :] = o.astype(bf16)

    tiles(out_tile)
    outc = [remote(ob.at[:, lane(U * t1, U)], out_hbm.at[mine, :], z1)]
    done3 = extra[1] if len(extra) > 1 else 0
    if done3 < S:
        part = pl.ds(done3 * L, (S - done3) * L)
        there3 = pl.ds(pl.multiple_of(R * t + done3 * L, L), (S - done3) * L)
        outc.append(remote(ob.at[part, lane(U * t3, U)], out_hbm.at[there3, :], z3))
    locals_ = [local(ob.at[:, tl], out_hbm.at[mine, :])]

    def fold(v):
        return jnp.sum(v.reshape(4, 8, v.shape[-1]), 0)

    def seq_tiles(s, f):
        def step(i, acc):
            return acc + fold(f(i, rows_at(i * 32, 32)))

        return lax.fori_loop(s * (L // 32), (s + 1) * (L // 32), step, jnp.zeros((8, H), f32))

    co.wait()

    def gate_tile(i, rows):
        sg = sig[rows, :]
        direct = valid_of(i, t) * ogv[rows, :].astype(f32) * sg
        g = direct * act[rows, :].astype(f32) * (1.0 - sg)
        gl[rows, :] = g.astype(bf16)
        sig[rows, :] = direct
        return g

    def pre_tile(i, rows):
        p = (tmp[rows, :] + sig[rows, :]) * gp[rows, :]
        pg[rows, :] = p
        plb[rows, :] = p.astype(bf16)
        return p * nrm[rows, :].astype(f32)

    def back_one(s):
        arrived(*og[s])
        rows = pl.ds(s * L, L)
        accv[0] += seq_tiles(s, gate_tile)
        tmp[rows, :] = nt(gl[rows, :], gt[...])
        accv[1] += seq_tiles(s, pre_tile)
        mu[rows, :] = nt(plb[rows, :], w4[2:4].reshape(2 * N, H))
        fin = scan(mu, mu, [(s * L, 128 * j) for j in range(N // 128)], 8, False, True)
        for j in range(N // 128):
            ce[3 + s, 0:1, 128 * j:128 * j + 128] = fin[2 * j][0:1, :]
            ce[3 + s, 1:2, 128 * j:128 * j + 128] = fin[2 * j + 1][0:1, :]
        return [remote(ce.at[3 + s], cer.at[3 + s, k], p) for k, p in enumerate(cpeer)]

    row1 = lax.broadcasted_iota(jnp.int32, (8, 128), 0)

    def back_two(s, cps):
        incoming(3 + s, cps, 1, False)
        nj = N // 128
        q0 = tuple(entering(3 + s, k, lane(128 * j, 128)) for j in range(nj) for k in range(2))
        z = jnp.zeros((8, 128), f32)

        def tile(i, carry):
            q, m, acc = list(carry[:2 * nj]), list(carry[2 * nj:4 * nj]), list(carry[4 * nj:])
            ii = L // 16 - 1 - i
            for j in range(nj):
                lr_, li_ = lane(128 * j, 128), lane(N + 128 * j, 128)
                p0, p1 = cst[14, :, lr_], cst[15, :, lr_]
                e0, e1 = cst[16, :, lr_], -cst[17, :, lr_]
                cfr, cfi = cst[18, :, lr_], cst[19, :, lr_]
                rr, ri = [None, None], [None, None]
                for h in (1, 0):
                    rows = rows_at(s * L + ii * 16 + 8 * h, 8)
                    vr, vi = cmul(p0, p1, q[2 * j], q[2 * j + 1])
                    ar, ai = mu[rows, lr_] + vr, mu[rows, li_] + vi
                    q[2 * j], q[2 * j + 1] = cmul(q[2 * j], q[2 * j + 1], e0, e1)
                    nr = jnp.where(row1 == 7, m[2 * j], pltpu.roll(ar, 7, 0))
                    ni = jnp.where(row1 == 7, m[2 * j + 1], pltpu.roll(ai, 7, 0))
                    m[2 * j] = jnp.broadcast_to(ar[0:1, :], (8, 128))
                    m[2 * j + 1] = jnp.broadcast_to(ai[0:1, :], (8, 128))
                    xr, xi = st[rows, lr_], st[rows, li_]
                    ur, ui = raw[rows, lr_], raw[rows, li_]
                    acc[4 * j] = acc[4 * j] + nr * xr + ni * xi
                    acc[4 * j + 1] = acc[4 * j + 1] + ni * xr - nr * xi
                    acc[4 * j + 2] = acc[4 * j + 2] + ar * ur + ai * ui
                    acc[4 * j + 3] = acc[4 * j + 3] + ai * ur - ar * ui
                    rr[h] = cfr * ar + cfi * ai
                    ri[h] = cfr * ai - cfi * ar
                rows = rows_at(s * L + ii * 16, 16)
                nb[rows, lr_] = jnp.concatenate(rr, 0).astype(bf16)
                nb[rows, li_] = jnp.concatenate(ri, 0).astype(bf16)
            return tuple(q) + tuple(m) + tuple(acc)

        fin = lax.fori_loop(0, L // 16, tile, q0 + q0 + (z,) * (4 * nj))
        for j in range(nj):
            for k in range(4):
                vv[3 + k:4 + k, 128 * j:128 * j + 128] += jnp.sum(fin[4 * nj + 4 * j + k], 0, keepdims=True)
        rows = pl.ds(s * L, L)
        tmp[rows, :] = nn(nb[rows, :], w4[0:2].reshape(2 * N, H))

        def tok_tile(i, acc):
            for u in range(4):
                rows = rows_at(s * L + i * 128 + u * 32, 32)
                n = tmp[rows, :] + skip_r * pg[rows, :]
                xt = xh[rows, :]
                h = n * gain_r
                m1 = jnp.mean(h, -1, keepdims=True)
                m2 = jnp.mean(h * xt, -1, keepdims=True)
                tgb[rows, :] = ((h - m1 - xt * m2) * rs[rows, 0:1]).astype(bf16)
                acc = acc + fold(n * xt)
            return acc

        accv[2] += lax.fori_loop(0, L // 128, tok_tile, jnp.zeros((8, H), f32))
        there = rows_at(R * t + L * s, L)
        locals_.append(local(tgb.at[rows, tl], tg_hbm.at[there, :]))

    def tok_send(s):
        there = rows_at(R * t + L * s, L)
        return [remote(tgb.at[pl.ds(s * L, L), lane(U * p[2], U)], tg_hbm.at[there, :], p) for p in (z3, z2, z1)]

    gcf, gbf = gc.reshape(2 * N, H), gb.reshape(2 * N, H)
    ol = lane(HD * (1 - d), HD)

    def gc_step(j, _):
        gcf[rows_at(j * 256, 256), :] = tn(sb[:, lane(j * 256, 256)], plb[...]).astype(bf16)
        return 0

    def gg_step(j, _):
        gg[rows_at(j * 256, 256), :] = tn(act[:, lane(j * 256, 256)], gl[...]).astype(bf16)
        return 0

    def gb_step(j, _):
        gbf[rows_at(j * 256, 256), :] = tn(nb[:, lane(j * 256, 256)], nrm[...]).astype(bf16)
        return 0

    hs = NS // 2

    def rs_ctx(p):
        return p // 2, rows_at(hs * lax.rem(p, 2), hs)

    gr = lambda p: rows_at(uq * p, uq)

    def add2(a, b):
        return (a.astype(f32) + b.astype(f32)).astype(bf16)

    def total(first_, buf, n):
        acc = first_.astype(f32)
        for k in range(n):
            acc = acc + buf[k].astype(f32)
        return acc

    def two_states(g, d1, r1, s1, r2):
        arrived(d1)
        s1[...] = add2(g[:, :, :, dl], r1[...])
        return [remote(s1.at[rs_ctx(p[1])[0], :, rs_ctx(p[1])[1], :], r2.at[k], p) for k, p in enumerate(cpeer)]

    def three_states(d2, s1, r2, s2, r3):
        arrived(*d2)
        s2[...] = total(s1[rs_ctx(c)[0], :, rs_ctx(c)[1], :], r2, C - 1).astype(bf16)
        return [remote(s2.at[t1], r3.at[0], z1), remote(s2.at[t3], r3.at[1], z1)]

    def four_states(d3, s2, r3, s3, r4):
        arrived(*d3)
        s3[0] = add2(s2[t], r3[0])
        s3[1] = add2(s2[t2], r3[1])
        return remote(s3.at[1], r4, z2)

    def spread_out(stage, out):
        locals_.append(local(stage, out.at[c]))
        return [remote(stage, out.at[c], p) for p in cpeer]

    def five(d4, s3, r4, stage, out):
        arrived(d4)
        stage[...] = add2(s3[0], r4[...])
        return spread_out(stage, out)

    def extra_fix(k):
        incoming(1 + k, fce[1 + k], extra[k], True)
        fix_batch(rawe.at[k], sbe, 1 + k, False, extra[k])

    def extra_act(k):
        def ssm(rows):
            tmpe[rows, :] = nn(sbe[rows, :], w4[2:4].reshape(2 * N, H))

        each_seq(ssm, extra[k])

        def gelu(i, rows):
            pre = tmpe[rows, :] + skip_r * nrme[rows_at(eoff[k] + i * 32, 32), :].astype(f32)
            acte[rows, :] = (pre * (0.5 + 0.5 * jnp.tanh(pre * (SQ2PI + (SQ2PI * 0.044715) * (pre * pre))))).astype(bf16)

        tiles(gelu, 0, extra[k] * L // 32)

    def extra_out(k):
        rank = erank[k]

        def gate(rows):
            tmpe[rows, 0:U] = nn(acte[rows, :], gt[:, tl])

        each_seq(gate, extra[k])
        bias_u = jnp.sum(jnp.where(lax.broadcasted_iota(jnp.int32, (T, U), 0) == t, bias_t, 0.0), 0, keepdims=True)

        def fin(i, rows):
            here = rows_at(eoff[k] + i * 32, 32)
            sg = logistic(tmpe[rows, 0:U] + bias_u)
            o = valid_of(i, rank) * (xe[here, tl].astype(f32) + acte[rows, tl].astype(f32) * sg)
            obe[here, :] = o.astype(bf16)

        tiles(fin, 0, extra[k] * L // 32)
        locals_.append(local(
            obe.at[pl.ds(eoff[k], extra[k] * L)], out_hbm.at[pl.ds(pl.multiple_of(R * rank, R), extra[k] * L), :]))

    bias_t = jnp.concatenate([bias_r[:, U * k:U * k + U] for k in range(T)], 0)
    bs, tgc = [], []
    bs.append(back_one(0))
    bs.append(back_one(1))
    back_two(0, bs[0])
    tgc += tok_send(0)
    bs.append(back_one(2))
    lax.fori_loop(0, 2 * N // 256, gc_step, 0)
    d1c = remote(gc.at[:, :, :, ol], r1c, sib)
    lax.fori_loop(0, H // 256, gg_step, 0)
    d1g = remote(gg.at[rows_at(HD * (1 - d), HD), :], r1g, sib)
    d2c = two_states(gc, d1c, r1c, s1c, r2c)
    back_two(1, bs[1])
    tgc += tok_send(1)
    arrived(d1g)
    s1g[...] = add2(gg[dr_, :], r1g[...])
    d2g = [remote(s1g.at[gr(p[1]), :], r2g.at[k], p) for k, p in enumerate(cpeer)]
    back_two(2, bs[2])
    tgc += tok_send(2)
    lax.fori_loop(0, 2 * N // 256, gb_step, 0)
    d1b = remote(gb.at[:, :, :, ol], r1b, sib)
    for k, row in ((2, 0), (1, 1), (0, 2)):
        vv[row:row + 1, :] = jnp.sum(accv[k], 0, keepdims=True)
    d1v = remote(vv, vr1, sib)
    d2b = two_states(gb, d1b, r1b, s1b, r2b)
    arrived(d1v)
    vr2[0] = vv[...] + vr1[...]
    d2v = [remote(vr2.at[0], vr2.at[k + 1], p) for k, p in enumerate(cpeer)]
    extra_fix(0)
    extra_act(0)
    d3c = three_states(d2c, s1c, r2c, s2c, r3c)
    arrived(*d2g)
    s2g[...] = total(s1g[gr(c), :], r2g, C - 1).astype(bf16)
    d3g = [remote(s2g.at[:, gl1], r3g.at[0], z1), remote(s2g.at[:, lane(U * t3, U)], r3g.at[1], z1)]
    extra_out(0)
    lax.fori_loop(eoff[1] // 128, (eoff[1] + extra[1] * L) // 128, lne_tile, 0)
    fce.append(rest(batches[2], N // 128))
    d4c = four_states(d3c, s2c, r3c, s3c, r4c)
    arrived(*d3g)
    s3g[0] = add2(s2g[:, tl], r3g[0])
    s3g[1] = add2(s2g[:, gl2], r3g[1])
    d4g = remote(s3g.at[1], r4g, z2)
    arrived(*d2b)
    s2b[...] = total(s1b[rs_ctx(c)[0], :, rs_ctx(c)[1], :], r2b, C - 1).astype(bf16)
    d3b = [remote(s2b.at[p[2]], r3b.at[k], p) for k, p in enumerate(zpeer)]
    arrived(*d2v)
    vr3[...] = vr2[0] + vr2[1] + vr2[2] + vr2[3]
    locals_.append(local(vr3, fv_hbm.at[0]))
    d3v = [remote(vr3, fv_hbm.at[k + 1], p) for k, p in enumerate(zpeer)]
    extra_fix(1)
    d5 = five(d4c, s3c, r4c, q5c, fc_hbm) + five(d4g, s3g, r4g, q5g, fg_hbm)
    extra_act(1)
    arrived(*d3b)
    q5b[...] = total(s2b[t], r3b, T - 1).astype(bf16)
    d5 += spread_out(q5b, fb_hbm)
    extra_out(1)

    arrived(*d5, *d3v, *tgc, *outc)
    for cp in locals_:
        cp.wait()
    for cp in started:
        cp.wait_send()
    assert count[0] == NSEM and nlocal[0] == NLOCAL, (count[0], nlocal[0])


EXTRA = (3, 1,)
NSEM, NLOCAL = 109, 25


def fused_call(geo, lens, x2, og2, *params):
    D, C, T, S, L, H, N, U = geo
    R, NS, HD = S * L, N // T, H // D
    f32, bf16 = jnp.float32, jnp.bfloat16
    uq, hs = HD // C, NS // 2
    V = pltpu.VMEM
    any_ = pl.BlockSpec(memory_space=pl.ANY)
    scratch = [
        V((R, H), bf16), V((R, H), bf16), V((R, H), f32), V((R, 128), f32),
        V((R, 2 * N), f32), V((R, 2 * N), f32), V((R, 2 * N), bf16),
        V((R, H), f32), V((R, H), bf16), V((R, H), f32), V((R, H), f32),
        V((R, H), bf16), V((R, H), bf16), V((R, H), bf16), V((R, H), f32), V((R, H), bf16),
        V((R, 2 * N), f32), V((R, 2 * N), bf16), V((R, H), bf16),
        V((2 * R, H), bf16), V((2 * R, H), bf16), V((2, R, 2 * N), f32), V((R, 2 * N), bf16),
        V((R, H), bf16), V((R, H), f32), V((2 * R, U), bf16),
        V((4, T, NS, H), bf16), V((H, H), bf16), V((D * T, 8, HD), f32),
        V((22, 8, N), f32), V((6, 8, N), f32), V((6, C - 1, 8, N), f32), V((6, 8, N), f32),
        V((2, T, NS, H), bf16), V((H, H), bf16), V((2, T, NS, H), bf16),
        V((2, T, NS, HD), bf16), V((HD, H), bf16), V((2, T, NS, HD), bf16),
        V((2, T, NS, HD), bf16), V((HD, H), bf16), V((2, T, NS, HD), bf16),
        V((C - 1, T, hs, HD), bf16), V((C - 1, uq, H), bf16), V((C - 1, T, hs, HD), bf16),
        V((T, hs, HD), bf16), V((uq, H), bf16), V((T, hs, HD), bf16),
        V((2, hs, HD), bf16), V((2, uq, U), bf16), V((T - 1, hs, HD), bf16),
        V((2, hs, HD), bf16), V((2, uq, U), bf16), V((hs, HD), bf16), V((uq, U), bf16),
        V((hs, HD), bf16), V((uq, U), bf16), V((hs, HD), bf16),
        V((8, H), f32), V((8, H), f32), V((C, 8, H), f32), V((8, H), f32), V((3, 8, H), f32),
        V((4, NS, HD), bf16), V((8, HD), f32), V((HD, U), bf16), V((1, HD), f32), V((1, HD), f32),
        V((1, NS // D), f32), V((1, NS // D), f32), V((1, NS // D), f32), V((1, U // D), f32),
        pltpu.SemaphoreType.DMA((NLOCAL,)), pltpu.SemaphoreType.DMA((NSEM,)), pltpu.SemaphoreType.DMA((NSEM,)),
    ]
    rows = x2.shape[0]
    return pl.pallas_call(
        functools.partial(fused_body, geo, EXTRA),
        out_shape=(
            jax.ShapeDtypeStruct((rows, U), bf16), jax.ShapeDtypeStruct((rows, U), bf16),
            jax.ShapeDtypeStruct((C, hs, HD), bf16), jax.ShapeDtypeStruct((C, uq, U), bf16),
            jax.ShapeDtypeStruct((C, hs, HD), bf16), jax.ShapeDtypeStruct((T, 8, H), f32)),
        in_specs=[pl.BlockSpec(memory_space=pltpu.SMEM), any_, any_] + [any_] * 11,
        out_specs=(any_,) * 6,
        scratch_shapes=scratch,
        compiler_params=pltpu.CompilerParams(
            collective_id=0, has_side_effects=True, vmem_limit_bytes=60 * 1024 * 1024),
        name="block",
    )(lens, x2, og2, *params)


def finish_body(geo, len_ref, out_in, tok_in, og_in, fc_in, fg_in, fb_in, fv_in, lre_in, lim_in, stp_in, *refs):
    D, C, T, S, L, H, N, U = geo
    NS = N // T
    f32 = jnp.float32
    out, ingrad = refs[:2]
    small_out, big_out = refs[2:8], refs[8:13]
    tokv, ogv, outv, fc, fg, fb, fv, lre, lim, stp = refs[13:23]
    small, big = refs[23:29], refs[29:34]
    res, vf, sem, gsem, osem = refs[34:]
    d, c, t = lax.axis_index("dp"), lax.axis_index("ctx"), lax.axis_index("tp")

    def move(src, dst, s):
        cp = pltpu.make_async_copy(src, dst, s)
        cp.start()
        return cp

    part = [pl.ds(S * k, S) for k in range(T)]
    loads = [(move(tok_in.at[part[k]], tokv.at[part[k]], sem.at[0, k]),
              move(og_in.at[part[k]], ogv.at[part[k]], sem.at[1, k])) for k in range(T)]
    params = [move(a, b, gsem.at[k]) for k, (a, b) in enumerate((
        (fv_in, fv), (lre_in, lre), (lim_in, lim), (stp_in, stp), (fc_in, fc), (fg_in, fg), (fb_in, fb)))]
    passes = [move(out_in.at[part[k]], outv.at[part[k]], sem.at[2, k]) for k in range(T)]
    pos = c * L + lax.broadcasted_iota(jnp.int32, (L, 1), 0)
    stores = []
    for k in range(T):
        for cp in loads[k]:
            cp.wait()
        for s in range(S * k, S * k + S):
            keep = jnp.where(pos < len_ref[s], 1.0, 0.0)
            res[s] = keep * ogv[s].astype(f32) + tokv[s].astype(f32)
        stores.append(move(res.at[part[k]], ingrad.at[part[k]], osem.at[k]))
    for cp in params:
        cp.wait()
    h = C // 2
    for k in range(C):
        rows = pl.ds((k % h) * (NS // h), NS // h)
        big[0 if k < h else 1][rows, :] = fb[k].astype(f32)
        big[2 if k < h else 3][rows, :] = fc[k].astype(f32)
    big[4][...] = fg[...].reshape(big[4].shape).astype(f32)
    stores += [move(a, b, osem.at[2 * T + k]) for k, (a, b) in enumerate(zip(big, big_out))]
    for k in range(T):
        passes[k].wait()
        stores.append(move(outv.at[part[k]], out.at[part[k]], osem.at[T + k]))
    acc = fv[0]
    for k in range(1, T):
        acc = acc + fv[k]
    vf[...] = acc
    place = t * D + d
    back = lambda n: lax.rem(H - n * place, H)
    st8 = pltpu.roll(acc, back(NS // D), 1)[:, 0:NS // D]
    ub8 = pltpu.roll(acc, back(U // D), 1)[:, 0:U // D]
    lr1, li1 = lre[...], lim[...]
    dr1, di1, cr1, ci1 = coefficients(lr1, li1, stp[...])
    step1 = jnp.exp(stp[...])
    gdr, gdi, gcr, gci = (st8[k:k + 1] for k in range(3, 7))
    inv = 1.0 / (lr1 * lr1 + li1 * li1)
    hdr = gdr + (gcr * lr1 - gci * li1) * inv
    hdi = gdi + (gcr * li1 + gci * lr1) * inv
    pull = 2.0 * (gcr * cr1 + gci * ci1)
    e1, e2 = dr1 - 1.0, hdr * dr1 + hdi * di1
    e3 = hdi * dr1 - hdr * di1
    dl = lane(H // D * d, H // D)
    small[0][...] = vf[0:1, dl]
    small[1][...] = vf[1:2, dl]
    small[2][...] = (gcr * e1 + gci * di1 - pull * lr1) * inv + step1 * e2
    small[3][...] = (gcr * di1 - gci * e1 - pull * li1) * inv + step1 * e3
    small[4][...] = step1 * (lr1 * e2 + li1 * e3)
    small[5][...] = ub8[2:3]
    stores += [move(a, b, osem.at[2 * T + 5 + k]) for k, (a, b) in enumerate(zip(small, small_out))]
    for cp in stores:
        cp.wait()


def finish_call(geo, lens, out, tok, og, fc, fg, fb, fv, lre, lim, stp):
    D, C, T, S, L, H, N, U = geo
    NS, HD = N // T, H // D
    f32, bf16 = jnp.float32, jnp.bfloat16
    seqs = S * T
    any_ = pl.BlockSpec(memory_space=pl.ANY)
    V = pltpu.VMEM
    sizes = [(1, HD), (1, HD)] + [(1, NS // D)] * 3 + [(1, U // D)] + [(NS, HD)] * 4 + [(HD, U)]
    return pl.pallas_call(
        functools.partial(finish_body, geo),
        out_shape=[jax.ShapeDtypeStruct((seqs, L, U), bf16), jax.ShapeDtypeStruct((seqs, L, U), f32)]
        + [jax.ShapeDtypeStruct(s, f32) for s in sizes],
        in_specs=[pl.BlockSpec(memory_space=pltpu.SMEM)] + [any_] * 10,
        out_specs=[any_] * 13,
        scratch_shapes=[V((seqs, L, U), bf16)] * 3 + [V(a.shape, a.dtype) for a in (fc, fg, fb, fv, lre, lim, stp)]
        + [V(s, f32) for s in sizes] + [V((seqs, L, U), f32), V((8, H), f32)]
        + [pltpu.SemaphoreType.DMA((3, T)), pltpu.SemaphoreType.DMA((7,)), pltpu.SemaphoreType.DMA((2 * T + 11,))],
        compiler_params=pltpu.CompilerParams(vmem_limit_bytes=60 * 1024 * 1024),
        name="finish",
    )(lens, out.reshape(seqs, L, U), tok.reshape(seqs, L, U), og, fc, fg, fb, fv, lre, lim, stp)


def coefficients(lam_re, lam_im, step_log):
    step = jnp.exp(step_log)
    magnitude = jnp.exp(lam_re * step)
    decay_re = magnitude * jnp.cos(lam_im * step)
    decay_im = magnitude * jnp.sin(lam_im * step)
    inv = 1.0 / (lam_re * lam_re + lam_im * lam_im)
    coef_re = ((decay_re - 1.0) * lam_re + decay_im * lam_im) * inv
    coef_im = (decay_im * lam_re - (decay_re - 1.0) * lam_im) * inv
    return decay_re, decay_im, coef_re, coef_im


def token_split(sizes, inputs, lengths, norm_gain, skip_weight, lambda_re, lambda_im, log_step,
                b_re, b_im, c_re, c_im, glu_weight, glu_bias, out_grad):
    D, C, T = sizes
    seqs, L, H = inputs.shape
    NS, HD = b_re.shape
    U = glu_weight.shape[1]
    geo = (D, C, T, seqs // T, L, H, NS * T, U)
    rows = [v.reshape(1, -1) for v in (norm_gain, skip_weight, lambda_re, lambda_im, log_step, glu_bias)]
    out, tok, fc, fg, fb, fv = fused_call(
        geo, lengths, inputs.reshape(seqs * L, H), out_grad.reshape(seqs * L, U),
        b_re, b_im, c_re.T, c_im.T, glu_weight, *rows)
    res = finish_call(geo, lengths, out, tok, out_grad, fc, fg, fb, fv, *rows[2:5])
    out, ingrad, gain_g, skip_g, lre_g, lim_g, step_g, bias_g, bre_g, bim_g, cre_g, cim_g, glu_g = res
    flat = lambda v: v.reshape(-1)
    return (out, ingrad, flat(gain_g), flat(skip_g), flat(lre_g), flat(lim_g), flat(step_g),
            bre_g, bim_g, cre_g.T, cim_g.T, glu_g, flat(bias_g))


def solution(mesh):
    in_specs = (
        P("dp", "ctx", None),
        P("dp"),
        P("dp"),
        P("dp"),
        P(("tp", "dp")),
        P(("tp", "dp")),
        P(("tp", "dp")),
        P("tp", "dp"),
        P("tp", "dp"),
        P("dp", "tp"),
        P("dp", "tp"),
        P("dp", "tp"),
        P(("tp", "dp")),
        P("dp", "ctx", "tp"),
    )
    out_specs = (
        P("dp", "ctx", "tp"),
        P("dp", "ctx", "tp"),
        P("dp"),
        P("dp"),
        P(("tp", "dp")),
        P(("tp", "dp")),
        P(("tp", "dp")),
        P("tp", "dp"),
        P("tp", "dp"),
        P("dp", "tp"),
        P("dp", "tp"),
        P("dp", "tp"),
        P(("tp", "dp")),
    )
    sizes = tuple(mesh.shape[name] for name in ("dp", "ctx", "tp"))

    def block(*args):
        seqs, _, feat = args[0].shape
        units = args[11].shape[1]
        if sizes == (2, 4, 4) and seqs % sizes[2] == 0 and units % 128 == 0:
            return token_split(sizes, *args)
        return on_device(*args)

    return jax.shard_map(
        block, mesh=mesh, in_specs=in_specs, out_specs=out_specs, check_vma=False
    )
```

```python
import functools

import jax
import jax.numpy as jnp
from jax import lax
from jax.experimental import pallas as pl
from jax.experimental.pallas import tpu as pltpu
from jax.sharding import PartitionSpec as P

epsilon = 1e-05


def carried_in(value, axis, combine, identity, reverse):
    count, index = (lax.axis_size(axis), lax.axis_index(axis))
    everything = jax.tree.map(lambda part: lax.all_gather(part, axis), value)
    start = jax.tree.map(
        lambda part, zero: jnp.broadcast_to(jnp.asarray(zero, part.dtype), part.shape),
        value,
        identity,
    )

    def lap(k, before):
        at = count - 1 - k if reverse else k
        reached = at > index if reverse else at < index
        new = combine(before, jax.tree.map(lambda part: part[at], everything))
        return jax.tree.map(lambda a, b: jnp.where(reached, a, b), new, before)

    return lax.fori_loop(0, count, lap, start)


def contract(left, right, left_dim, right_dim):
    return lax.dot_general(
        left, right, (((left_dim,), (right_dim,)), ((), ())), preferred_element_type=jnp.float32
    )


def combine(earlier, later):
    e_re, e_im, eb_re, eb_im = earlier
    l_re, l_im, lb_re, lb_im = later
    return (
        e_re * l_re - e_im * l_im,
        e_re * l_im + e_im * l_re,
        l_re * eb_re - l_im * eb_im + lb_re,
        l_re * eb_im + l_im * eb_re + lb_im,
    )


def discretize(lam_re, lam_im, step_log, mat_re, mat_im):
    step = jnp.exp(step_log)
    magnitude = jnp.exp(lam_re * step)
    decay_re = magnitude * jnp.cos(lam_im * step)
    decay_im = magnitude * jnp.sin(lam_im * step)
    denom = lam_re * lam_re + lam_im * lam_im
    coef_re = ((decay_re - 1.0) * lam_re + decay_im * lam_im) / denom
    coef_im = (decay_im * lam_re - (decay_re - 1.0) * lam_im) / denom
    bar_re = coef_re[:, None] * mat_re - coef_im[:, None] * mat_im
    bar_im = coef_re[:, None] * mat_im + coef_im[:, None] * mat_re
    return (decay_re, decay_im, jnp.concatenate([bar_re, bar_im], 0))


def normalize(tokens, gain):
    mean_val = jnp.mean(tokens, -1, keepdims=True)
    centered = tokens - mean_val
    var_val = jnp.mean(centered * centered, -1, keepdims=True)
    return centered * lax.rsqrt(var_val + epsilon) * gain


def powers(lam_re, lam_im, step_log, count):
    step = jnp.exp(step_log)
    exponent = (jnp.arange(count, dtype=jnp.float32) + 1.0)[:, None]
    magnitude = jnp.exp(exponent * lam_re * step)
    return (
        magnitude * jnp.cos(exponent * lam_im * step),
        magnitude * jnp.sin(exponent * lam_im * step),
    )


def on_device(
    inputs,
    lengths,
    norm_gain,
    skip_weight,
    lambda_re,
    lambda_im,
    log_step,
    b_re,
    b_im,
    c_re,
    c_im,
    glu_weight,
    glu_bias,
    out_grad,
):
    full_bre, full_bim, full_cre, full_cim, full_glu = (
        lax.all_gather(b_re, "dp", axis=1, tiled=True),
        lax.all_gather(b_im, "dp", axis=1, tiled=True),
        lax.all_gather(c_re, "dp", axis=0, tiled=True),
        lax.all_gather(c_im, "dp", axis=0, tiled=True),
        lax.all_gather(glu_weight, "dp", axis=0, tiled=True),
    )
    gain, skip_full, lam_re, lam_im, step_log, bias_vec = (
        lax.all_gather(norm_gain, "dp", axis=0, tiled=True),
        lax.all_gather(skip_weight, "dp", axis=0, tiled=True),
        lax.all_gather(lambda_re, "dp", axis=0, tiled=True),
        lax.all_gather(lambda_im, "dp", axis=0, tiled=True),
        lax.all_gather(log_step, "dp", axis=0, tiled=True),
        lax.all_gather(glu_bias, "dp", axis=0, tiled=True),
    )
    seq_count, blk_len, feat_dim = inputs.shape
    row_count = seq_count * blk_len
    state_count = full_bre.shape[0]
    unit_count = full_glu.shape[1]
    tp_rank = lax.axis_index("tp")
    unit_start = tp_rank * unit_count
    positions = lax.axis_index("ctx") * blk_len + jnp.arange(blk_len, dtype=jnp.int32)
    valid_mask = (positions[None, :] < lengths[:, None]).astype(jnp.float32).reshape(row_count, 1)
    tokens = inputs.astype(jnp.float32).reshape(row_count, feat_dim)
    tokens_mine = lax.dynamic_slice_in_dim(tokens, unit_start, unit_count, 1)
    cotangent = out_grad.astype(jnp.float32).reshape(row_count, unit_count)
    normed_f, norm_pull = jax.vjp(normalize, tokens, gain)
    normed_b = normed_f.astype(jnp.bfloat16)
    normed_r = normed_b.astype(jnp.float32)
    (decay_re, decay_im, bar_full), disc_pull = jax.vjp(
        discretize,
        lam_re,
        lam_im,
        step_log,
        full_bre.astype(jnp.float32),
        full_bim.astype(jnp.float32),
    )
    bar_b = bar_full.astype(jnp.bfloat16)
    drive = contract(normed_b, bar_b, 1, 1).reshape(seq_count, blk_len, 2 * state_count)
    full_re = jnp.broadcast_to(decay_re, (seq_count, blk_len, state_count))
    full_im = jnp.broadcast_to(decay_im, (seq_count, blk_len, state_count))
    local_states = lax.associative_scan(
        combine, (full_re, full_im, drive[..., :state_count], drive[..., state_count:]), axis=1
    )
    pow_re, pow_im = powers(lam_re, lam_im, step_log, blk_len)
    identity = (
        jnp.ones((1, state_count), jnp.float32),
        jnp.zeros((1, state_count), jnp.float32),
        jnp.zeros((seq_count, state_count), jnp.float32),
        jnp.zeros((seq_count, state_count), jnp.float32),
    )
    incoming = carried_in(
        (pow_re[-1:], pow_im[-1:], local_states[2][:, -1], local_states[3][:, -1]),
        "ctx",
        combine,
        identity,
        False,
    )
    in_re = incoming[2][:, None, :]
    in_im = incoming[3][:, None, :]
    state_re = local_states[2] + pow_re * in_re - pow_im * in_im
    state_im = local_states[3] + pow_re * in_im + pow_im * in_re
    states_b = (
        jnp.concatenate([state_re, state_im], -1)
        .reshape(row_count, 2 * state_count)
        .astype(jnp.bfloat16)
    )
    c_stack = jnp.concatenate([full_cre, -full_cim], 1)
    ssm_part = contract(states_b, c_stack, 1, 1)
    ssm_full = lax.psum(ssm_part.astype(jnp.bfloat16), "tp").astype(jnp.float32)
    pre_full = ssm_full + skip_full * normed_r
    gelu_full, gelu_pull = jax.vjp(jax.nn.gelu, pre_full)
    gelu_b = gelu_full.astype(jnp.bfloat16)
    gelu_part = lax.dynamic_slice_in_dim(gelu_b, unit_start, unit_count, 1)
    gelu_mine = gelu_part.astype(jnp.float32)
    gate = contract(gelu_b, full_glu, 1, 0) + bias_vec
    gate_sig = jax.nn.sigmoid(gate)
    output = (
        (valid_mask * (tokens_mine + gelu_mine * gate_sig))
        .astype(jnp.bfloat16)
        .reshape(seq_count, blk_len, unit_count)
    )
    branch_grad = valid_mask * cotangent
    gate_grad = branch_grad * gelu_mine * gate_sig * (1.0 - gate_sig)
    bias_grad = jnp.sum(gate_grad, 0)
    gate_b = gate_grad.astype(jnp.bfloat16)
    glu_grad = contract(gelu_b, gate_b, 0, 0)
    gelu_grad = contract(gate_b, full_glu, 1, 1)
    own_cols = (
        lax.dynamic_slice_in_dim(gelu_grad, unit_start, unit_count, 1) + branch_grad * gate_sig
    )
    gelu_grad = lax.dynamic_update_slice_in_dim(gelu_grad, own_cols, unit_start, 1)
    gelu_back = lax.psum(gelu_grad, "tp")
    (pre_grad,) = gelu_pull(gelu_back)
    skip_grad = jnp.sum(pre_grad * normed_r, 0)
    pre_b = pre_grad.astype(jnp.bfloat16)
    state_grad = contract(pre_b, c_stack, 1, 0).reshape(seq_count, blk_len, 2 * state_count)
    c_grad = contract(pre_b, states_b, 0, 0)
    back_local = lax.associative_scan(
        combine,
        (full_re, -full_im, state_grad[..., :state_count], state_grad[..., state_count:]),
        axis=1,
        reverse=True,
    )
    later_adj = carried_in(
        (pow_re[-1:], -pow_im[-1:], back_local[2][:, 0], back_local[3][:, 0]),
        "ctx",
        combine,
        identity,
        True,
    )
    rev_re = pow_re[::-1]
    rev_im = -pow_im[::-1]
    next_re = later_adj[2][:, None, :]
    next_im = later_adj[3][:, None, :]
    adj_re = back_local[2] + rev_re * next_re - rev_im * next_im
    adj_im = back_local[3] + rev_re * next_im + rev_im * next_re
    prev_re = jnp.concatenate([in_re, state_re[:, :-1]], 1)
    prev_im = jnp.concatenate([in_im, state_im[:, :-1]], 1)
    decay_grad_re = jnp.sum(adj_re * prev_re + adj_im * prev_im, (0, 1))
    decay_grad_im = jnp.sum(adj_im * prev_re - adj_re * prev_im, (0, 1))
    adj_b = (
        jnp.concatenate([adj_re, adj_im], -1)
        .reshape(row_count, 2 * state_count)
        .astype(jnp.bfloat16)
    )
    bar_grad = contract(adj_b, normed_b, 0, 0)
    normed_part = contract(adj_b, bar_b, 1, 0)
    normed_sum = lax.psum(normed_part.astype(jnp.bfloat16), "tp").astype(jnp.float32)
    normed_grad = normed_sum + skip_full * pre_grad
    token_grad, gain_grad = norm_pull(normed_grad)
    input_grad = (
        valid_mask * cotangent + lax.dynamic_slice_in_dim(token_grad, unit_start, unit_count, 1)
    ).reshape(seq_count, blk_len, unit_count)
    grad_cre = c_grad[:, :state_count]
    grad_cim = -c_grad[:, state_count:]
    lre_grad, lim_grad, step_grad, bre_grad, bim_grad = disc_pull(
        (decay_grad_re, decay_grad_im, bar_grad)
    )
    shards = (
        lax.psum_scatter(
            gain_grad.astype(jnp.bfloat16), "dp", scatter_dimension=0, tiled=True
        ).astype(jnp.float32),
        lax.psum_scatter(
            skip_grad.astype(jnp.bfloat16), "dp", scatter_dimension=0, tiled=True
        ).astype(jnp.float32),
        lax.psum_scatter(
            lre_grad.astype(jnp.bfloat16), "dp", scatter_dimension=0, tiled=True
        ).astype(jnp.float32),
        lax.psum_scatter(
            lim_grad.astype(jnp.bfloat16), "dp", scatter_dimension=0, tiled=True
        ).astype(jnp.float32),
        lax.psum_scatter(
            step_grad.astype(jnp.bfloat16), "dp", scatter_dimension=0, tiled=True
        ).astype(jnp.float32),
        lax.psum_scatter(
            bias_grad.astype(jnp.bfloat16), "dp", scatter_dimension=0, tiled=True
        ).astype(jnp.float32),
        lax.psum_scatter(
            bre_grad.astype(jnp.bfloat16), "dp", scatter_dimension=1, tiled=True
        ).astype(jnp.float32),
        lax.psum_scatter(
            bim_grad.astype(jnp.bfloat16), "dp", scatter_dimension=1, tiled=True
        ).astype(jnp.float32),
        lax.psum_scatter(
            grad_cre.astype(jnp.bfloat16), "dp", scatter_dimension=0, tiled=True
        ).astype(jnp.float32),
        lax.psum_scatter(
            grad_cim.astype(jnp.bfloat16), "dp", scatter_dimension=0, tiled=True
        ).astype(jnp.float32),
        lax.psum_scatter(
            glu_grad.astype(jnp.bfloat16), "dp", scatter_dimension=0, tiled=True
        ).astype(jnp.float32),
    )
    summed = (
        lax.psum(shards[0].astype(jnp.bfloat16), "ctx").astype(jnp.float32),
        lax.psum(shards[1].astype(jnp.bfloat16), "ctx").astype(jnp.float32),
        lax.psum(shards[2].astype(jnp.bfloat16), "ctx").astype(jnp.float32),
        lax.psum(shards[3].astype(jnp.bfloat16), "ctx").astype(jnp.float32),
        lax.psum(shards[4].astype(jnp.bfloat16), "ctx").astype(jnp.float32),
        lax.psum(shards[5].astype(jnp.bfloat16), "ctx").astype(jnp.float32),
        lax.psum(shards[6].astype(jnp.bfloat16), "ctx").astype(jnp.float32),
        lax.psum(shards[7].astype(jnp.bfloat16), "ctx").astype(jnp.float32),
        lax.psum(shards[8].astype(jnp.bfloat16), "ctx").astype(jnp.float32),
        lax.psum(shards[9].astype(jnp.bfloat16), "ctx").astype(jnp.float32),
        lax.psum(shards[10].astype(jnp.bfloat16), "ctx").astype(jnp.float32),
    )
    return (
        output,
        input_grad,
        summed[0],
        summed[1],
        summed[2],
        summed[3],
        summed[4],
        summed[6],
        summed[7],
        summed[8],
        summed[9],
        summed[10],
        summed[5],
    )


MESH = pl.DeviceIdType.MESH
SQ2PI = 0.7978845608028654


def nt(a, b):
    return lax.dot_general(a, b, (((1,), (1,)), ((), ())), preferred_element_type=jnp.float32)


def nn(a, b):
    return lax.dot_general(a, b, (((1,), (0,)), ((), ())), preferred_element_type=jnp.float32)


def tn(a, b):
    return lax.dot_general(a, b, (((0,), (0,)), ((), ())), preferred_element_type=jnp.float32)


def cmul(ar, ai, br, bi):
    return ar * br - ai * bi, ar * bi + ai * br


def lane(start, size):
    return pl.ds(pl.multiple_of(start, 128), size)


def fused_body(geo, extra, *refs):
    D, C, T, S, L, H, N, U = geo
    R = S * L
    NS = N // T
    HD = H // D
    f32, bf16 = jnp.float32, jnp.bfloat16
    (len_ref, x_hbm, og_hbm, bre, bim, cre, cim, glu_hbm, gain_h, skip_h, lre_h, lim_h, stp_h, bias_h,
     out_hbm, tg_hbm, fc_hbm, fg_hbm, fb_hbm, fv_hbm) = refs[:20]
    (xv, nrm, xh, rs, raw, st, sb, tmp, act, gp, sig, ogv, ob, gl, pg, plb, mu, nb, tgb,
     xe, nrme, rawe, sbe, acte, tmpe, obe,
     w4, gt, smr, cst, ce, cer, cin, gc, gg, gb, r1c, r1g, r1b, s1c, s1g, s1b, r2c, r2g, r2b,
     s2c, s2g, s2b, r3c, r3g, r3b, s3c, s3g, r4c, r4g,
     q5c, q5g, q5b, vv, vr1, vr2, vr3, accv, pk, sm_ref, glu, gain_in, skip_in, lre_in, lim_in, stp_in, bias_in,
     lsem, ssem, rsem) = refs[20:]
    d, c, t = lax.axis_index("dp"), lax.axis_index("ctx"), lax.axis_index("tp")
    half = t // 2
    t1 = t + 1 - 2 * lax.rem(t, 2)
    t2 = t + 2 - 4 * half
    t3 = T - 1 - t
    z1, z2, z3 = (d, c, t1), (d, c, t2), (d, c, t3)
    zpeer = [(d, c, lax.rem(t + k, T)) for k in range(1, T)]
    cpeer = [(d, lax.rem(c + k, C), t) for k in range(1, C)]
    sib = (1 - d, c, t)
    xpeer = [(1 - d, c, lax.rem(t + k, T)) for k in range(1, T)]
    everyone = zpeer + cpeer + [sib] + xpeer
    erank = [t2, t3][:len(extra)]
    eoff = [L * sum(extra[:k]) for k in range(len(extra))]

    count = [0]
    started = []

    def remote(src, dst, peer):
        i = count[0]
        count[0] += 1
        cp = pltpu.make_async_remote_copy(
            src_ref=src, dst_ref=dst, send_sem=ssem.at[i], recv_sem=rsem.at[i],
            device_id=peer, device_id_type=MESH)
        cp.start()
        started.append(cp)
        return cp

    def arrived(*cps):
        for cp in cps:
            cp.wait_recv()

    nlocal = [0]

    def local(src, dst):
        cp = pltpu.make_async_copy(src, dst, lsem.at[nlocal[0]])
        nlocal[0] += 1
        cp.start()
        return cp

    def rows_at(start, size):
        return pl.ds(pl.multiple_of(start, size), size)

    barrier = pltpu.get_barrier_semaphore()
    for p in everyone:
        pl.semaphore_signal(barrier, inc=1, device_id=p, device_id_type=MESH)
    cp_small = [local(a, b) for a, b in (
        (lre_h, lre_in), (lim_h, lim_in), (stp_h, stp_in), (bias_h, bias_in), (gain_h, gain_in), (skip_h, skip_in))]
    mine = rows_at(R * t, R)
    cp_pk = [local(a, pk.at[k]) for k, a in enumerate((bre, bim, cre, cim))] + [local(glu_hbm, glu)]
    cx = local(x_hbm.at[mine], xv)
    cxe = [local(x_hbm.at[pl.ds(pl.multiple_of(R * e, R), L * n)], xe.at[pl.ds(o, L * n)])
           for e, n, o in zip(erank, extra, eoff)]
    co = local(og_hbm.at[mine], ogv.at[:, lane(U * t, U)])
    dl = lane(HD * d, HD)
    dr_ = rows_at(HD * d, HD)
    tl = lane(U * t, U)
    sm_ref[...] = jnp.zeros_like(sm_ref)
    for cp in cp_small:
        cp.wait()
    own = coefficients(lre_in[...], lim_in[...], stp_in[...])
    for k in range(4):
        sm_ref[k:k + 1, 0:NS // D] = own[k]
    sm_ref[4:5, 0:U // D] = bias_in[...]
    sm_ref[5:6, :] = gain_in[...]
    sm_ref[6:7, :] = skip_in[...]
    me8 = d * T + t
    smr[me8] = sm_ref[...]
    accv[...] = jnp.zeros_like(accv)
    vv[...] = jnp.zeros_like(vv)
    for cp in cp_pk:
        cp.wait()
    for k in range(4):
        w4[k, t, :, dl] = pk[k]
    gt[dr_, tl] = glu[...]
    cx.wait()

    def standard(x):
        cen = x - jnp.mean(x, -1, keepdims=True)
        rstd = lax.rsqrt(jnp.mean(cen * cen, -1, keepdims=True) + epsilon)
        return cen * rstd, rstd

    def ln_tile(i, _):
        for u in range(4):
            rows = rows_at(i * 128 + u * 32, 32)
            xn, rstd = standard(xv[rows, :].astype(f32))
            xh[rows, :] = xn
            rs[rows, :] = jnp.broadcast_to(rstd, (32, 128))
        return 0

    lax.fori_loop(0, R // 128, ln_tile, 0)
    pl.semaphore_wait(barrier, len(everyone))

    gq, hq = c // 2, lax.rem(c, 2)
    ql = lane(128 * hq, 128)
    wl = lane(HD * d + 128 * hq, 128)
    uq = HD // C
    gown = rows_at(uq * c, uq)
    grow = rows_at(HD * d + uq * c, uq)
    pair = rows_at(2 - 2 * half, 2)
    pairl = lane(2 * U * (1 - half), 2 * U)

    qb, qc = gq, 2 + gq
    far_b = [remote(pk.at[qb, :, ql], w4.at[qb, t, :, wl], p) for p in (z3, z2)]
    small = [remote(sm_ref, smr.at[me8], p) for p in zpeer + [sib] + xpeer]
    near_b = remote(pk.at[0:2], w4.at[0:2, t, :, dl], z1)
    w3b = [remote(pk.at[0:2], w4.at[0:2, t, :, dl], sib)]

    def spread(blk, *cps):
        arrived(*cps)
        return [remote(blk, blk, p) for p in cpeer]

    gl1, gl2 = lane(U * t1, U), lane(U * t2, U)
    w2b = spread(w4.at[qb, pair, :, wl], *far_b)
    far_c = [remote(pk.at[qc, :, ql], w4.at[qc, t, :, wl], p) for p in (z3, z2)]
    far_g = [remote(glu.at[gown], gt.at[grow, tl], p) for p in (z3, z2)]
    near_c = remote(pk.at[2:4], w4.at[2:4, t, :, dl], z1)
    near_g = remote(glu, gt.at[dr_, tl], z1)
    w3c = [remote(pk.at[2:4], w4.at[2:4, t, :, dl], sib)]
    w3g = [remote(glu, gt.at[dr_, tl], sib)]

    def cot_send(s):
        return [remote(og_hbm.at[rows_at(R * p[2] + L * s, L)], ogv.at[pl.ds(L * s, L), tl], p) for p in zpeer]

    arrived(*small)
    zero = jnp.zeros((8, H - HD), f32)
    vec = jnp.zeros((8, H), f32)
    bias = jnp.zeros((8, H), f32)
    for dd in range(D):
        for tt in range(T):
            ext = jnp.concatenate([smr[dd * T + tt], zero], 1)
            place = tt * D + dd
            vec = vec + (pltpu.roll(ext, place * (NS // D), 1) if place else ext)
            bias = bias + (pltpu.roll(ext, place * (U // D), 1) if place else ext)
    both = jnp.concatenate([smr[t], smr[T + t]], 1)
    gain_r, skip_r, bias_r = both[5:6, :], both[6:7, :], bias[4:5, :]

    arrived(near_b)
    w3b.append(remote(w4.at[0:2, t1, :, dl], w4.at[0:2, t1, :, dl], sib))
    row8 = lax.broadcasted_iota(jnp.int32, (8, N), 0)
    full = lambda v, k, n: jnp.broadcast_to(v[k:k + 1, :n], (8, n))
    dr, di = full(vec, 0, N), full(vec, 1, N)
    cr, ci = full(vec, 2, N), full(vec, 3, N)
    pows = {1: (dr, di)}
    for k in range(2, 9):
        pows[k] = cmul(*pows[k - 1], dr, di)
    for n_, k in ((0, 1), (1, 2), (2, 4)):
        keep = row8 >= k
        cst[2 * n_] = jnp.where(keep, pows[k][0], 0.0)
        cst[2 * n_ + 1] = jnp.where(keep, pows[k][1], 0.0)
        keep = row8 < 8 - k
        cst[8 + 2 * n_] = jnp.where(keep, pows[k][0], 0.0)
        cst[8 + 2 * n_ + 1] = jnp.where(keep, -pows[k][1], 0.0)
    pr, pi, qr, qi = pows[1][0], pows[1][1], pows[8][0], -pows[8][1]
    for r in range(1, 8):
        pr = jnp.where(row8 == r, pows[r + 1][0], pr)
        pi = jnp.where(row8 == r, pows[r + 1][1], pi)
        qr = jnp.where(row8 == r, pows[8 - r][0], qr)
        qi = jnp.where(row8 == r, -pows[8 - r][1], qi)
    cst[6], cst[7], cst[14], cst[15] = pr, pi, qr, qi
    cst[16], cst[17] = pows[8]
    cst[18], cst[19] = cr, ci
    big = pows[8]
    n_ = 8
    while n_ < L:
        big = cmul(*big, *big)
        n_ *= 2
    cst[20], cst[21] = big

    def nrm_tile(i, _):
        rows = rows_at(i * 32, 32)
        nrm[rows, :] = (xh[rows, :] * gain_r).astype(bf16)
        return 0

    lax.fori_loop(0, R // 32, nrm_tile, 0)
    og = [cot_send(0)]

    def lne_tile(i, _):
        for u in range(4):
            rows = rows_at(i * 128 + u * 32, 32)
            nrme[rows, :] = (standard(xe[rows, :].astype(f32))[0] * gain_r).astype(bf16)
        return 0

    def seq_rows(s):
        return rows_at(s * L, L)

    wv = w4.reshape(4, N, H)

    def drive(src, off, dst, n, j):
        rows = rows_at(128 * j, 128)
        both_ = nt(src[pl.ds(off, n * L), :], jnp.concatenate([wv[0, rows, :], wv[1, rows, :]], 0))
        dst[pl.ds(0, n * L), lane(128 * j, 128)] = both_[:, 0:128]
        dst[pl.ds(0, n * L), lane(N + 128 * j, 128)] = both_[:, 128:256]

    def scan(src, dst, groups, base, coef, reverse):
        e = 0 if reverse else 7

        def tile(i, carry):
            carry = list(carry)
            ii = L // 32 - 1 - i if reverse else i
            for g, (rb, l0) in enumerate(groups):
                lr_, li_ = lane(l0, 128), lane(N + l0, 128)
                con = [cst[base + k, :, lr_] for k in range(8)]
                e0 = cst[16, :, lr_]
                e1 = -cst[17, :, lr_] if reverse else cst[17, :, lr_]
                loc = []
                for u in range(4):
                    uu = 3 - u if reverse else u
                    rows = rows_at(rb + ii * 32 + uu * 8, 8)
                    ar, ai = src[rows, lr_], src[rows, li_]
                    if coef:
                        ar, ai = cmul(cst[18, :, lr_], cst[19, :, lr_], ar, ai)
                    else:
                        ai = -ai
                    for n_, k in ((0, 1), (1, 2), (2, 4)):
                        sh = 8 - k if reverse else k
                        br, bi = pltpu.roll(ar, sh, 0), pltpu.roll(ai, sh, 0)
                        mr, mi = con[2 * n_], con[2 * n_ + 1]
                        ar, ai = ar + mr * br - mi * bi, ai + mr * bi + mi * br
                    loc.append((rows, ar, ai))
                kr, ki = carry[2 * g], carry[2 * g + 1]
                for rows, ar, ai in loc:
                    dst[rows, lr_] = ar + con[6] * kr - con[7] * ki
                    dst[rows, li_] = ai + con[6] * ki + con[7] * kr
                    endr = jnp.broadcast_to(ar[e:e + 1, :], (8, 128))
                    endi = jnp.broadcast_to(ai[e:e + 1, :], (8, 128))
                    kr, ki = endr + e0 * kr - e1 * ki, endi + e0 * ki + e1 * kr
                carry[2 * g], carry[2 * g + 1] = kr, ki
            return tuple(carry)

        z = jnp.zeros((8, 128), f32)
        return lax.fori_loop(0, L // 32, tile, (z,) * (2 * len(groups)))

    def begin(src, off, dst, out, slot, n, j):
        drive(src, off, dst, n, j)
        fin = scan(dst, out, [(s * L, 128 * j) for s in range(n)], 0, True, False)
        for s in range(n):
            ce[slot, pl.ds(s, 1), lane(128 * j, 128)] = fin[2 * s][0:1, :]
            ce[slot, pl.ds(n + s, 1), lane(128 * j, 128)] = fin[2 * s + 1][0:1, :]

    def rest(what, tiles_=2):
        def step(k, _):
            begin(*what, 1 + k * (1 - 2 * half) if tiles_ == 2 else k)
            return 0

        lax.fori_loop(0, tiles_, step, 0)
        slot = what[4]
        return [remote(ce.at[slot], cer.at[slot, k], p) for k, p in enumerate(cpeer)]

    def incoming(slot, cps, n, forward):
        arrived(*cps)
        bg = (cst[20, 0:1, :], cst[21, 0:1, :])
        wt = (jnp.ones((1, N), f32), jnp.zeros((1, N), f32))
        accr = jnp.zeros((n, N), f32)
        acci = jnp.zeros((n, N), f32)
        for k in range(1, C):
            got = cer[slot, k - 1] if forward else cer[slot, C - 1 - k]
            has = (c >= k) if forward else (c + k < C)
            w = jnp.where(has, 1.0, 0.0)
            wi = wt[1] if forward else -wt[1]
            ur, ui = cmul(wt[0], wi, got[0:n, :], got[n:2 * n, :])
            accr = accr + w * ur
            acci = acci + w * ui
            wt = cmul(*wt, *bg)
        cin[slot, 0:n, :] = accr
        cin[slot, n:2 * n, :] = acci

    def entering(slot, k, lanes):
        return jnp.broadcast_to(cin[slot, pl.ds(k, 1), lanes], (8, 128))

    def fix_batch(ref, dst, slot, keep, n):
        def fix_lanes(j, _):
            lr_, li_ = lane(128 * j, 128), lane(N + 128 * j, 128)
            p0, p1 = cst[6, :, lr_], cst[7, :, lr_]
            e0, e1 = cst[16, :, lr_], cst[17, :, lr_]
            q0 = tuple(entering(slot, k * n + s, lr_) for s in range(n) for k in range(2))

            def tile(i, q):
                q = list(q)
                for s in range(n):
                    rr, ri = [], []
                    for h in range(2):
                        rows = rows_at(s * L + i * 16 + 8 * h, 8)
                        vr, vi = cmul(p0, p1, q[2 * s], q[2 * s + 1])
                        ar, ai = ref[rows, lr_] + vr, ref[rows, li_] + vi
                        if keep:
                            ref[rows, lr_] = ar
                            ref[rows, li_] = ai
                        rr.append(ar)
                        ri.append(ai)
                        q[2 * s], q[2 * s + 1] = cmul(q[2 * s], q[2 * s + 1], e0, e1)
                    rows = rows_at(s * L + i * 16, 16)
                    dst[rows, lr_] = jnp.concatenate(rr, 0).astype(bf16)
                    dst[rows, li_] = (-jnp.concatenate(ri, 0)).astype(bf16)
                return tuple(q)

            lax.fori_loop(0, L // 16, tile, q0)
            return 0

        lax.fori_loop(0, N // 128, fix_lanes, 0)

    def each_seq(f, n=S):
        f(pl.ds(0, n * L))

    def tiles(f, lo=0, hi=R // 32):
        def step(i, _):
            f(i, rows_at(i * 32, 32))
            return 0

        lax.fori_loop(lo, hi, step, 0)

    def valid_of(i, rank):
        s = i // (L // 32)
        pos = c * L + lax.rem(i, L // 32) * 32 + lax.broadcasted_iota(jnp.int32, (32, 1), 0)
        return jnp.where(pos < len_ref[S * rank + s], 1.0, 0.0)

    def logistic(v):
        return 0.5 + 0.5 * jnp.tanh(0.5 * v)

    batches = [(nrm, 0, raw, st, 0, S)] + [
        (nrme, eoff[k], rawe.at[k], rawe.at[k], 1 + k, extra[k]) for k in range(len(extra))]
    arrived(*w3b)
    begin(*batches[0], 2 * half)
    w2c = spread(w4.at[qc, pair, :, wl], *far_c)
    w2g = spread(gt.at[grow, pairl], *far_g)
    og.append(cot_send(1))
    for cp in cxe:
        cp.wait()
    lax.fori_loop(0, extra[0] * L // 128, lne_tile, 0)
    arrived(*w2b)
    w3b2 = remote(w4.at[0:2, pair, :, dl], w4.at[0:2, pair, :, dl], sib)
    og.append(cot_send(2))
    begin(*batches[1], 2 * half)
    arrived(w3b2)
    fce = [rest(batches[0])]
    arrived(near_c)
    w3c.append(remote(w4.at[2:4, t1, :, dl], w4.at[2:4, t1, :, dl], sib))
    arrived(near_g)
    blk = gt.at[dr_, gl1]
    w3g.append(remote(blk, blk, sib))
    arrived(*w2c)
    w3c.append(remote(w4.at[2:4, pair, :, dl], w4.at[2:4, pair, :, dl], sib))
    arrived(*w2g)
    blk = gt.at[dr_, pairl]
    w3g.append(remote(blk, blk, sib))
    fce.append(rest(batches[1]))
    incoming(0, fce[0], S, True)
    fix_batch(st, sb, 0, True, S)
    arrived(*w3c)

    def ssm_own(rows):
        tmp[rows, :] = nn(sb[rows, :], w4[2:4].reshape(2 * N, H))

    each_seq(ssm_own)

    def gelu_tile(i, rows):
        pre = tmp[rows, :] + skip_r * nrm[rows, :].astype(f32)
        sq = pre * pre
        th = jnp.tanh(pre * (SQ2PI + (SQ2PI * 0.044715) * sq))
        hf = 0.5 + 0.5 * th
        act[rows, :] = (pre * hf).astype(bf16)
        gp[rows, :] = hf + 0.5 * pre * (1.0 - th * th) * (SQ2PI + (3 * 0.044715 * SQ2PI) * sq)

    tiles(gelu_tile)
    arrived(*w3g)

    def gate_own(rows):
        tmp[rows, :] = nn(act[rows, :], gt[...])

    each_seq(gate_own)

    def out_tile(i, rows):
        sg = logistic(tmp[rows, :] + bias_r)
        sig[rows, :] = sg
        o = valid_of(i, t) * (xv[rows, :].astype(f32) + act[rows, :].astype(f32) * sg)
        ob[rows, :] = o.astype(bf16)

    tiles(out_tile)
    outc = [remote(ob.at[:, lane(U * t1, U)], out_hbm.at[mine, :], z1)]
    done3 = extra[1] if len(extra) > 1 else 0
    if done3 < S:
        part = pl.ds(done3 * L, (S - done3) * L)
        there3 = pl.ds(pl.multiple_of(R * t + done3 * L, L), (S - done3) * L)
        outc.append(remote(ob.at[part, lane(U * t3, U)], out_hbm.at[there3, :], z3))
    locals_ = [local(ob.at[:, tl], out_hbm.at[mine, :])]

    def fold(v):
        return jnp.sum(v.reshape(4, 8, v.shape[-1]), 0)

    def seq_tiles(s, f):
        def step(i, acc):
            return acc + fold(f(i, rows_at(i * 32, 32)))

        return lax.fori_loop(s * (L // 32), (s + 1) * (L // 32), step, jnp.zeros((8, H), f32))

    co.wait()

    def gate_tile(i, rows):
        sg = sig[rows, :]
        direct = valid_of(i, t) * ogv[rows, :].astype(f32) * sg
        g = direct * act[rows, :].astype(f32) * (1.0 - sg)
        gl[rows, :] = g.astype(bf16)
        sig[rows, :] = direct
        return g

    def pre_tile(i, rows):
        p = (tmp[rows, :] + sig[rows, :]) * gp[rows, :]
        pg[rows, :] = p
        plb[rows, :] = p.astype(bf16)
        return p * nrm[rows, :].astype(f32)

    def back_one(s):
        arrived(*og[s])
        rows = pl.ds(s * L, L)
        accv[0] += seq_tiles(s, gate_tile)
        tmp[rows, :] = nt(gl[rows, :], gt[...])
        accv[1] += seq_tiles(s, pre_tile)
        mu[rows, :] = nt(plb[rows, :], w4[2:4].reshape(2 * N, H))
        fin = scan(mu, mu, [(s * L, 128 * j) for j in range(N // 128)], 8, False, True)
        for j in range(N // 128):
            ce[3 + s, 0:1, 128 * j:128 * j + 128] = fin[2 * j][0:1, :]
            ce[3 + s, 1:2, 128 * j:128 * j + 128] = fin[2 * j + 1][0:1, :]
        return [remote(ce.at[3 + s], cer.at[3 + s, k], p) for k, p in enumerate(cpeer)]

    row1 = lax.broadcasted_iota(jnp.int32, (8, 128), 0)

    def back_two(s, cps):
        incoming(3 + s, cps, 1, False)
        nj = N // 128
        q0 = tuple(entering(3 + s, k, lane(128 * j, 128)) for j in range(nj) for k in range(2))
        z = jnp.zeros((8, 128), f32)

        def tile(i, carry):
            q, m, acc = list(carry[:2 * nj]), list(carry[2 * nj:4 * nj]), list(carry[4 * nj:])
            ii = L // 16 - 1 - i
            for j in range(nj):
                lr_, li_ = lane(128 * j, 128), lane(N + 128 * j, 128)
                p0, p1 = cst[14, :, lr_], cst[15, :, lr_]
                e0, e1 = cst[16, :, lr_], -cst[17, :, lr_]
                cfr, cfi = cst[18, :, lr_], cst[19, :, lr_]
                rr, ri = [None, None], [None, None]
                for h in (1, 0):
                    rows = rows_at(s * L + ii * 16 + 8 * h, 8)
                    vr, vi = cmul(p0, p1, q[2 * j], q[2 * j + 1])
                    ar, ai = mu[rows, lr_] + vr, mu[rows, li_] + vi
                    q[2 * j], q[2 * j + 1] = cmul(q[2 * j], q[2 * j + 1], e0, e1)
                    nr = jnp.where(row1 == 7, m[2 * j], pltpu.roll(ar, 7, 0))
                    ni = jnp.where(row1 == 7, m[2 * j + 1], pltpu.roll(ai, 7, 0))
                    m[2 * j] = jnp.broadcast_to(ar[0:1, :], (8, 128))
                    m[2 * j + 1] = jnp.broadcast_to(ai[0:1, :], (8, 128))
                    xr, xi = st[rows, lr_], st[rows, li_]
                    ur, ui = raw[rows, lr_], raw[rows, li_]
                    acc[4 * j] = acc[4 * j] + nr * xr + ni * xi
                    acc[4 * j + 1] = acc[4 * j + 1] + ni * xr - nr * xi
                    acc[4 * j + 2] = acc[4 * j + 2] + ar * ur + ai * ui
                    acc[4 * j + 3] = acc[4 * j + 3] + ai * ur - ar * ui
                    rr[h] = cfr * ar + cfi * ai
                    ri[h] = cfr * ai - cfi * ar
                rows = rows_at(s * L + ii * 16, 16)
                nb[rows, lr_] = jnp.concatenate(rr, 0).astype(bf16)
                nb[rows, li_] = jnp.concatenate(ri, 0).astype(bf16)
            return tuple(q) + tuple(m) + tuple(acc)

        fin = lax.fori_loop(0, L // 16, tile, q0 + q0 + (z,) * (4 * nj))
        for j in range(nj):
            for k in range(4):
                vv[3 + k:4 + k, 128 * j:128 * j + 128] += jnp.sum(fin[4 * nj + 4 * j + k], 0, keepdims=True)
        rows = pl.ds(s * L, L)
        tmp[rows, :] = nn(nb[rows, :], w4[0:2].reshape(2 * N, H))

        def tok_tile(i, acc):
            for u in range(4):
                rows = rows_at(s * L + i * 128 + u * 32, 32)
                n = tmp[rows, :] + skip_r * pg[rows, :]
                xt = xh[rows, :]
                h = n * gain_r
                m1 = jnp.mean(h, -1, keepdims=True)
                m2 = jnp.mean(h * xt, -1, keepdims=True)
                tgb[rows, :] = ((h - m1 - xt * m2) * rs[rows, 0:1]).astype(bf16)
                acc = acc + fold(n * xt)
            return acc

        accv[2] += lax.fori_loop(0, L // 128, tok_tile, jnp.zeros((8, H), f32))
        there = rows_at(R * t + L * s, L)
        locals_.append(local(tgb.at[rows, tl], tg_hbm.at[there, :]))

    def tok_send(s):
        there = rows_at(R * t + L * s, L)
        return [remote(tgb.at[pl.ds(s * L, L), lane(U * p[2], U)], tg_hbm.at[there, :], p) for p in (z3, z2, z1)]

    gcf, gbf = gc.reshape(2 * N, H), gb.reshape(2 * N, H)
    ol = lane(HD * (1 - d), HD)

    def gc_step(j, _):
        gcf[rows_at(j * 256, 256), :] = tn(sb[:, lane(j * 256, 256)], plb[...]).astype(bf16)
        return 0

    def gg_step(j, _):
        gg[rows_at(j * 256, 256), :] = tn(act[:, lane(j * 256, 256)], gl[...]).astype(bf16)
        return 0

    def gb_step(j, _):
        gbf[rows_at(j * 256, 256), :] = tn(nb[:, lane(j * 256, 256)], nrm[...]).astype(bf16)
        return 0

    hs = NS // 2

    def rs_ctx(p):
        return p // 2, rows_at(hs * lax.rem(p, 2), hs)

    gr = lambda p: rows_at(uq * p, uq)

    def add2(a, b):
        return (a.astype(f32) + b.astype(f32)).astype(bf16)

    def total(first_, buf, n):
        acc = first_.astype(f32)
        for k in range(n):
            acc = acc + buf[k].astype(f32)
        return acc

    def two_states(g, d1, r1, s1, r2):
        arrived(d1)
        s1[...] = add2(g[:, :, :, dl], r1[...])
        return [remote(s1.at[rs_ctx(p[1])[0], :, rs_ctx(p[1])[1], :], r2.at[k], p) for k, p in enumerate(cpeer)]

    def three_states(d2, s1, r2, s2, r3):
        arrived(*d2)
        s2[...] = total(s1[rs_ctx(c)[0], :, rs_ctx(c)[1], :], r2, C - 1).astype(bf16)
        return [remote(s2.at[t1], r3.at[0], z1), remote(s2.at[t3], r3.at[1], z1)]

    def four_states(d3, s2, r3, s3, r4):
        arrived(*d3)
        s3[0] = add2(s2[t], r3[0])
        s3[1] = add2(s2[t2], r3[1])
        return remote(s3.at[1], r4, z2)

    def spread_out(stage, out):
        locals_.append(local(stage, out.at[c]))
        return [remote(stage, out.at[c], p) for p in cpeer]

    def five(d4, s3, r4, stage, out):
        arrived(d4)
        stage[...] = add2(s3[0], r4[...])
        return spread_out(stage, out)

    def extra_fix(k):
        incoming(1 + k, fce[1 + k], extra[k], True)
        fix_batch(rawe.at[k], sbe, 1 + k, False, extra[k])

    def extra_act(k):
        def ssm(rows):
            tmpe[rows, :] = nn(sbe[rows, :], w4[2:4].reshape(2 * N, H))

        each_seq(ssm, extra[k])

        def gelu(i, rows):
            pre = tmpe[rows, :] + skip_r * nrme[rows_at(eoff[k] + i * 32, 32), :].astype(f32)
            acte[rows, :] = (pre * (0.5 + 0.5 * jnp.tanh(pre * (SQ2PI + (SQ2PI * 0.044715) * (pre * pre))))).astype(bf16)

        tiles(gelu, 0, extra[k] * L // 32)

    def extra_out(k):
        rank = erank[k]

        def gate(rows):
            tmpe[rows, 0:U] = nn(acte[rows, :], gt[:, tl])

        each_seq(gate, extra[k])
        bias_u = jnp.sum(jnp.where(lax.broadcasted_iota(jnp.int32, (T, U), 0) == t, bias_t, 0.0), 0, keepdims=True)

        def fin(i, rows):
            here = rows_at(eoff[k] + i * 32, 32)
            sg = logistic(tmpe[rows, 0:U] + bias_u)
            o = valid_of(i, rank) * (xe[here, tl].astype(f32) + acte[rows, tl].astype(f32) * sg)
            obe[here, :] = o.astype(bf16)

        tiles(fin, 0, extra[k] * L // 32)
        locals_.append(local(
            obe.at[pl.ds(eoff[k], extra[k] * L)], out_hbm.at[pl.ds(pl.multiple_of(R * rank, R), extra[k] * L), :]))

    bias_t = jnp.concatenate([bias_r[:, U * k:U * k + U] for k in range(T)], 0)
    bs, tgc = [], []
    bs.append(back_one(0))
    bs.append(back_one(1))
    extra_fix(0)
    back_two(0, bs[0])
    tgc += tok_send(0)
    bs.append(back_one(2))
    lax.fori_loop(0, 2 * N // 256, gc_step, 0)
    d1c = remote(gc.at[:, :, :, ol], r1c, sib)
    lax.fori_loop(0, H // 256, gg_step, 0)
    d1g = remote(gg.at[rows_at(HD * (1 - d), HD), :], r1g, sib)
    d2c = two_states(gc, d1c, r1c, s1c, r2c)
    back_two(1, bs[1])
    tgc += tok_send(1)
    arrived(d1g)
    s1g[...] = add2(gg[dr_, :], r1g[...])
    d2g = [remote(s1g.at[gr(p[1]), :], r2g.at[k], p) for k, p in enumerate(cpeer)]
    back_two(2, bs[2])
    tgc += tok_send(2)
    lax.fori_loop(0, 2 * N // 256, gb_step, 0)
    d1b = remote(gb.at[:, :, :, ol], r1b, sib)
    for k, row in ((2, 0), (1, 1), (0, 2)):
        vv[row:row + 1, :] = jnp.sum(accv[k], 0, keepdims=True)
    d1v = remote(vv, vr1, sib)
    d2b = two_states(gb, d1b, r1b, s1b, r2b)
    arrived(d1v)
    vr2[0] = vv[...] + vr1[...]
    d2v = [remote(vr2.at[0], vr2.at[k + 1], p) for k, p in enumerate(cpeer)]
    extra_act(0)
    extra_out(0)
    d3c = three_states(d2c, s1c, r2c, s2c, r3c)
    arrived(*d2g)
    s2g[...] = total(s1g[gr(c), :], r2g, C - 1).astype(bf16)
    d3g = [remote(s2g.at[:, gl1], r3g.at[0], z1), remote(s2g.at[:, lane(U * t3, U)], r3g.at[1], z1)]
    lax.fori_loop(eoff[1] // 128, (eoff[1] + extra[1] * L) // 128, lne_tile, 0)
    fce.append(rest(batches[2], N // 128))
    d4c = four_states(d3c, s2c, r3c, s3c, r4c)
    arrived(*d3g)
    s3g[0] = add2(s2g[:, tl], r3g[0])
    s3g[1] = add2(s2g[:, gl2], r3g[1])
    d4g = remote(s3g.at[1], r4g, z2)
    arrived(*d2b)
    s2b[...] = total(s1b[rs_ctx(c)[0], :, rs_ctx(c)[1], :], r2b, C - 1).astype(bf16)
    d3b = [remote(s2b.at[p[2]], r3b.at[k], p) for k, p in enumerate(zpeer)]
    arrived(*d2v)
    vr3[...] = vr2[0] + vr2[1] + vr2[2] + vr2[3]
    locals_.append(local(vr3, fv_hbm.at[0]))
    d3v = [remote(vr3, fv_hbm.at[k + 1], p) for k, p in enumerate(zpeer)]
    extra_fix(1)
    d5 = five(d4c, s3c, r4c, q5c, fc_hbm) + five(d4g, s3g, r4g, q5g, fg_hbm)
    extra_act(1)
    arrived(*d3b)
    q5b[...] = total(s2b[t], r3b, T - 1).astype(bf16)
    d5 += spread_out(q5b, fb_hbm)
    extra_out(1)

    arrived(*d5, *d3v, *tgc, *outc)
    for cp in locals_:
        cp.wait()
    for cp in started:
        cp.wait_send()
    assert count[0] == NSEM and nlocal[0] == NLOCAL, (count[0], nlocal[0])


EXTRA = (3, 1,)
NSEM, NLOCAL = 109, 25


def fused_call(geo, lens, x2, og2, *params):
    D, C, T, S, L, H, N, U = geo
    R, NS, HD = S * L, N // T, H // D
    f32, bf16 = jnp.float32, jnp.bfloat16
    uq, hs = HD // C, NS // 2
    V = pltpu.VMEM
    any_ = pl.BlockSpec(memory_space=pl.ANY)
    scratch = [
        V((R, H), bf16), V((R, H), bf16), V((R, H), f32), V((R, 128), f32),
        V((R, 2 * N), f32), V((R, 2 * N), f32), V((R, 2 * N), bf16),
        V((R, H), f32), V((R, H), bf16), V((R, H), f32), V((R, H), f32),
        V((R, H), bf16), V((R, H), bf16), V((R, H), bf16), V((R, H), f32), V((R, H), bf16),
        V((R, 2 * N), f32), V((R, 2 * N), bf16), V((R, H), bf16),
        V((2 * R, H), bf16), V((2 * R, H), bf16), V((2, R, 2 * N), f32), V((R, 2 * N), bf16),
        V((R, H), bf16), V((R, H), f32), V((2 * R, U), bf16),
        V((4, T, NS, H), bf16), V((H, H), bf16), V((D * T, 8, HD), f32),
        V((22, 8, N), f32), V((6, 8, N), f32), V((6, C - 1, 8, N), f32), V((6, 8, N), f32),
        V((2, T, NS, H), bf16), V((H, H), bf16), V((2, T, NS, H), bf16),
        V((2, T, NS, HD), bf16), V((HD, H), bf16), V((2, T, NS, HD), bf16),
        V((2, T, NS, HD), bf16), V((HD, H), bf16), V((2, T, NS, HD), bf16),
        V((C - 1, T, hs, HD), bf16), V((C - 1, uq, H), bf16), V((C - 1, T, hs, HD), bf16),
        V((T, hs, HD), bf16), V((uq, H), bf16), V((T, hs, HD), bf16),
        V((2, hs, HD), bf16), V((2, uq, U), bf16), V((T - 1, hs, HD), bf16),
        V((2, hs, HD), bf16), V((2, uq, U), bf16), V((hs, HD), bf16), V((uq, U), bf16),
        V((hs, HD), bf16), V((uq, U), bf16), V((hs, HD), bf16),
        V((8, H), f32), V((8, H), f32), V((C, 8, H), f32), V((8, H), f32), V((3, 8, H), f32),
        V((4, NS, HD), bf16), V((8, HD), f32), V((HD, U), bf16), V((1, HD), f32), V((1, HD), f32),
        V((1, NS // D), f32), V((1, NS // D), f32), V((1, NS // D), f32), V((1, U // D), f32),
        pltpu.SemaphoreType.DMA((NLOCAL,)), pltpu.SemaphoreType.DMA((NSEM,)), pltpu.SemaphoreType.DMA((NSEM,)),
    ]
    rows = x2.shape[0]
    return pl.pallas_call(
        functools.partial(fused_body, geo, EXTRA),
        out_shape=(
            jax.ShapeDtypeStruct((rows, U), bf16), jax.ShapeDtypeStruct((rows, U), bf16),
            jax.ShapeDtypeStruct((C, hs, HD), bf16), jax.ShapeDtypeStruct((C, uq, U), bf16),
            jax.ShapeDtypeStruct((C, hs, HD), bf16), jax.ShapeDtypeStruct((T, 8, H), f32)),
        in_specs=[pl.BlockSpec(memory_space=pltpu.SMEM), any_, any_] + [any_] * 11,
        out_specs=(any_,) * 6,
        scratch_shapes=scratch,
        compiler_params=pltpu.CompilerParams(
            collective_id=0, has_side_effects=True, vmem_limit_bytes=60 * 1024 * 1024),
        name="block",
    )(lens, x2, og2, *params)


def finish_body(geo, len_ref, out_in, tok_in, og_in, fc_in, fg_in, fb_in, fv_in, lre_in, lim_in, stp_in, *refs):
    D, C, T, S, L, H, N, U = geo
    NS = N // T
    f32 = jnp.float32
    out, ingrad = refs[:2]
    small_out, big_out = refs[2:8], refs[8:13]
    tokv, ogv, outv, fc, fg, fb, fv, lre, lim, stp = refs[13:23]
    small, big = refs[23:29], refs[29:34]
    res, vf, sem, gsem, osem = refs[34:]
    d, c, t = lax.axis_index("dp"), lax.axis_index("ctx"), lax.axis_index("tp")

    def move(src, dst, s):
        cp = pltpu.make_async_copy(src, dst, s)
        cp.start()
        return cp

    part = [pl.ds(S * k, S) for k in range(T)]
    loads = [(move(tok_in.at[part[k]], tokv.at[part[k]], sem.at[0, k]),
              move(og_in.at[part[k]], ogv.at[part[k]], sem.at[1, k])) for k in range(T)]
    params = [move(a, b, gsem.at[k]) for k, (a, b) in enumerate((
        (fv_in, fv), (lre_in, lre), (lim_in, lim), (stp_in, stp), (fc_in, fc), (fg_in, fg), (fb_in, fb)))]
    passes = [move(out_in.at[part[k]], outv.at[part[k]], sem.at[2, k]) for k in range(T)]
    pos = c * L + lax.broadcasted_iota(jnp.int32, (L, 1), 0)
    stores = []
    for k in range(T):
        for cp in loads[k]:
            cp.wait()
        for s in range(S * k, S * k + S):
            keep = jnp.where(pos < len_ref[s], 1.0, 0.0)
            res[s] = keep * ogv[s].astype(f32) + tokv[s].astype(f32)
        stores.append(move(res.at[part[k]], ingrad.at[part[k]], osem.at[k]))
    for cp in params:
        cp.wait()
    h = C // 2
    for k in range(C):
        rows = pl.ds((k % h) * (NS // h), NS // h)
        big[0 if k < h else 1][rows, :] = fb[k].astype(f32)
        big[2 if k < h else 3][rows, :] = fc[k].astype(f32)
    big[4][...] = fg[...].reshape(big[4].shape).astype(f32)
    stores += [move(a, b, osem.at[2 * T + k]) for k, (a, b) in enumerate(zip(big, big_out))]
    for k in range(T):
        passes[k].wait()
        stores.append(move(outv.at[part[k]], out.at[part[k]], osem.at[T + k]))
    acc = fv[0]
    for k in range(1, T):
        acc = acc + fv[k]
    vf[...] = acc
    place = t * D + d
    back = lambda n: lax.rem(H - n * place, H)
    st8 = pltpu.roll(acc, back(NS // D), 1)[:, 0:NS // D]
    ub8 = pltpu.roll(acc, back(U // D), 1)[:, 0:U // D]
    lr1, li1 = lre[...], lim[...]
    dr1, di1, cr1, ci1 = coefficients(lr1, li1, stp[...])
    step1 = jnp.exp(stp[...])
    gdr, gdi, gcr, gci = (st8[k:k + 1] for k in range(3, 7))
    inv = 1.0 / (lr1 * lr1 + li1 * li1)
    hdr = gdr + (gcr * lr1 - gci * li1) * inv
    hdi = gdi + (gcr * li1 + gci * lr1) * inv
    pull = 2.0 * (gcr * cr1 + gci * ci1)
    e1, e2 = dr1 - 1.0, hdr * dr1 + hdi * di1
    e3 = hdi * dr1 - hdr * di1
    dl = lane(H // D * d, H // D)
    small[0][...] = vf[0:1, dl]
    small[1][...] = vf[1:2, dl]
    small[2][...] = (gcr * e1 + gci * di1 - pull * lr1) * inv + step1 * e2
    small[3][...] = (gcr * di1 - gci * e1 - pull * li1) * inv + step1 * e3
    small[4][...] = step1 * (lr1 * e2 + li1 * e3)
    small[5][...] = ub8[2:3]
    stores += [move(a, b, osem.at[2 * T + 5 + k]) for k, (a, b) in enumerate(zip(small, small_out))]
    for cp in stores:
        cp.wait()


def finish_call(geo, lens, out, tok, og, fc, fg, fb, fv, lre, lim, stp):
    D, C, T, S, L, H, N, U = geo
    NS, HD = N // T, H // D
    f32, bf16 = jnp.float32, jnp.bfloat16
    seqs = S * T
    any_ = pl.BlockSpec(memory_space=pl.ANY)
    V = pltpu.VMEM
    sizes = [(1, HD), (1, HD)] + [(1, NS // D)] * 3 + [(1, U // D)] + [(NS, HD)] * 4 + [(HD, U)]
    return pl.pallas_call(
        functools.partial(finish_body, geo),
        out_shape=[jax.ShapeDtypeStruct((seqs, L, U), bf16), jax.ShapeDtypeStruct((seqs, L, U), f32)]
        + [jax.ShapeDtypeStruct(s, f32) for s in sizes],
        in_specs=[pl.BlockSpec(memory_space=pltpu.SMEM)] + [any_] * 10,
        out_specs=[any_] * 13,
        scratch_shapes=[V((seqs, L, U), bf16)] * 3 + [V(a.shape, a.dtype) for a in (fc, fg, fb, fv, lre, lim, stp)]
        + [V(s, f32) for s in sizes] + [V((seqs, L, U), f32), V((8, H), f32)]
        + [pltpu.SemaphoreType.DMA((3, T)), pltpu.SemaphoreType.DMA((7,)), pltpu.SemaphoreType.DMA((2 * T + 11,))],
        compiler_params=pltpu.CompilerParams(vmem_limit_bytes=60 * 1024 * 1024),
        name="finish",
    )(lens, out.reshape(seqs, L, U), tok.reshape(seqs, L, U), og, fc, fg, fb, fv, lre, lim, stp)


def coefficients(lam_re, lam_im, step_log):
    step = jnp.exp(step_log)
    magnitude = jnp.exp(lam_re * step)
    decay_re = magnitude * jnp.cos(lam_im * step)
    decay_im = magnitude * jnp.sin(lam_im * step)
    inv = 1.0 / (lam_re * lam_re + lam_im * lam_im)
    coef_re = ((decay_re - 1.0) * lam_re + decay_im * lam_im) * inv
    coef_im = (decay_im * lam_re - (decay_re - 1.0) * lam_im) * inv
    return decay_re, decay_im, coef_re, coef_im


def token_split(sizes, inputs, lengths, norm_gain, skip_weight, lambda_re, lambda_im, log_step,
                b_re, b_im, c_re, c_im, glu_weight, glu_bias, out_grad):
    D, C, T = sizes
    seqs, L, H = inputs.shape
    NS, HD = b_re.shape
    U = glu_weight.shape[1]
    geo = (D, C, T, seqs // T, L, H, NS * T, U)
    rows = [v.reshape(1, -1) for v in (norm_gain, skip_weight, lambda_re, lambda_im, log_step, glu_bias)]
    out, tok, fc, fg, fb, fv = fused_call(
        geo, lengths, inputs.reshape(seqs * L, H), out_grad.reshape(seqs * L, U),
        b_re, b_im, c_re.T, c_im.T, glu_weight, *rows)
    res = finish_call(geo, lengths, out, tok, out_grad, fc, fg, fb, fv, *rows[2:5])
    out, ingrad, gain_g, skip_g, lre_g, lim_g, step_g, bias_g, bre_g, bim_g, cre_g, cim_g, glu_g = res
    flat = lambda v: v.reshape(-1)
    return (out, ingrad, flat(gain_g), flat(skip_g), flat(lre_g), flat(lim_g), flat(step_g),
            bre_g, bim_g, cre_g.T, cim_g.T, glu_g, flat(bias_g))


def solution(mesh):
    in_specs = (
        P("dp", "ctx", None),
        P("dp"),
        P("dp"),
        P("dp"),
        P(("tp", "dp")),
        P(("tp", "dp")),
        P(("tp", "dp")),
        P("tp", "dp"),
        P("tp", "dp"),
        P("dp", "tp"),
        P("dp", "tp"),
        P("dp", "tp"),
        P(("tp", "dp")),
        P("dp", "ctx", "tp"),
    )
    out_specs = (
        P("dp", "ctx", "tp"),
        P("dp", "ctx", "tp"),
        P("dp"),
        P("dp"),
        P(("tp", "dp")),
        P(("tp", "dp")),
        P(("tp", "dp")),
        P("tp", "dp"),
        P("tp", "dp"),
        P("dp", "tp"),
        P("dp", "tp"),
        P("dp", "tp"),
        P(("tp", "dp")),
    )
    sizes = tuple(mesh.shape[name] for name in ("dp", "ctx", "tp"))

    def block(*args):
        seqs, _, feat = args[0].shape
        units = args[11].shape[1]
        if sizes == (2, 4, 4) and seqs % sizes[2] == 0 and units % 128 == 0:
            return token_split(sizes, *args)
        return on_device(*args)

    return jax.shard_map(
        block, mesh=mesh, in_specs=in_specs, out_specs=out_specs, check_vma=False
    )
```
